32 devices in a mesh: dp: 8 (over y, x, core), tensor: 4 (over z).
Axes of the slice: x: 2, y: 2, z: 4, core: 2. Of those that a mesh axis runs over, the one named last changes fastest.
Arguments:
- tokens: bfloat16 [4096, 2048], P(('dp', 'tensor')), may hold values from -6 to 6
- file_ids: int32 [8, 512], P('dp'), may hold values from 0 to 7, never falling along the last dimension, each value on 1 to 256 neighbouring positions
- expert_ids: int32 [4096, 8], P(('dp', 'tensor')), may hold values from 0 to 15, all different within a row; in each aligned block of 128 rows (0 to 127, 128 to 255, ...) at most 72 rows name the same one
- attention_norm_gain: float32 [2048], replicated, may hold values from 0.5 to 1.5
- w_query: bfloat16 [2048, 2048], P(None, 'tensor'), as said below
- w_key: bfloat16 [2048, 2048], P(None, 'tensor'), as said below
- w_value: bfloat16 [2048, 2048], P(None, 'tensor'), may hold values from -0.125 to 0.125
- query_gain: float32 [2048], P('tensor'), may hold values from 0.5 to 1.5
- key_gain: float32 [2048], P('tensor'), may hold values from 0.5 to 1.5
- w_output: bfloat16 [2048, 2048], P('tensor'), may hold values from -1 to 1
- expert_norm_gain: float32 [2048], replicated, may hold values from 0.5 to 1.5
- w_router: bfloat16 [2048, 16], replicated, may hold values from -0.0625 to 0.0625
- w_gate: bfloat16 [16, 2048, 1024], P('dp', None, 'tensor'), may hold values from -0.125 to 0.125
- w_up: bfloat16 [16, 2048, 1024], P('dp', None, 'tensor'), may hold values from -0.125 to 0.125
- w_down: bfloat16 [16, 1024, 2048], P('dp', 'tensor'), may hold values from -3.59375 to 3.59375
- grad_output: bfloat16 [4096, 2048], P(('dp', 'tensor')), may hold values from -6 to 6
Outputs:
- out: bfloat16 [4096, 2048], P(('dp', 'tensor'))
- grad_tokens: bfloat16 [4096, 2048], P(('dp', 'tensor'))
- grad_w_query: float32 [2048, 2048], P(None, 'tensor')
- grad_w_key: float32 [2048, 2048], P(None, 'tensor')
- grad_w_value: float32 [2048, 2048], P(None, 'tensor')
- grad_w_output: float32 [2048, 2048], P('tensor')
- grad_query_gain: float32 [2048], P('tensor')
- grad_key_gain: float32 [2048], P('tensor')
- grad_attn_gain: float32 [2048], replicated
- grad_ffn_gain: float32 [2048], replicated
- grad_w_router: float32 [2048, 16], replicated
- grad_w_gate: float32 [16, 2048, 1024], P('dp', None, 'tensor')
- grad_w_up: float32 [16, 2048, 1024], P('dp', None, 'tensor')
- grad_w_down: float32 [16, 1024, 2048], P('dp', 'tensor')
The draws below stay inside these ranges and needn't reach their ends.
Inputs may be any that keep to these rules, and one draw needn't show every extreme that they name: `expert_ids`: each row names 8 different experts; the 128 rows of one device (aligned blocks) name no expert more than 72 times, a bound that some block reaches. `file_ids`: along each row the ids never fall; equal ids mark one file; no file is longer than 256 tokens. `w_query`: drawn independently, columns of unequal scale. `w_key`: drawn independently, columns of unequal scale.
All inputs are finite; a program needn't handle non-finite values.
Results may differ from the reference program's by a relative error of at most 0.022.
Values may be sent and summed in bfloat16 or wider, within the bound.
A program may use at most 320 MiB of HBM per device.

```python
import math
import jax
import jax.numpy as jnp
import numpy as np
from jax import lax

D = 2048
HEADS = 16
HEAD_DIM = 128
FFE = 1024
TOPK = 8
FILES = 8
TOK_DEV = 128
EXPERTS = 16
SEQ = 512
TOKENS = 4096
MOST = 72
N_DP = 8
N_TENSOR = 4


def column_scaled(key, salt_value):
    base_draw = jax.random.normal(jax.random.fold_in(key, salt_value), (D, D), jnp.float32) / math.sqrt(D)
    column_ramp = jnp.arange(D, dtype=jnp.float32) / (D - 1)
    factor = 3.0 ** (0.5 * column_ramp)
    return (base_draw * factor[None, :]).astype(jnp.bfloat16)


def draw_w_query(key, part):
    return column_scaled(key, 11)


def draw_w_key(key, part):
    return column_scaled(key, 23)


def steps_of(rng, extent, split, least, top_value):
    loudness = 1.0
    for axis_at, blocks in split:
        draws = jax.random.uniform(jax.random.fold_in(jax.random.fold_in(rng, 6), axis_at), (blocks,), jnp.float32, least / len(split), top_value / len(split))
        loudness = loudness * jnp.repeat(jnp.exp(draws), extent[axis_at] // blocks).reshape((-1,) + (1,) * (len(extent) - 1 - axis_at))
    return loudness


def split_up(count, total, bound, slope):
    portions = [(1 << 20) // math.isqrt(rank ** slope) + 1 for rank in range(2, count + 1)]
    surplus, counts = total - bound - (count - 1), [1] * (count - 1)
    while surplus > 0:
        candidates = [i for i in range(count - 1) if counts[i] < bound]
        mass, left = sum([portions[i] for i in candidates]), surplus
        for i in candidates:
            addition = min(bound - counts[i], max(1, left * portions[i] // mass), surplus)
            counts[i] = counts[i] + addition
            surplus = surplus - addition
    return np.array([bound] + counts)


def uneven_parts(rng, number_of, total, most, skew):
    if number_of == 2:
        one = jax.random.randint(rng, (), max(1, total - most), min(most, total - 1) + 1)
        return jnp.stack([one, total - one])
    lengths = jnp.asarray(split_up(number_of, total, most, skew), jnp.int32)
    twos = (number_of - 1) // 2
    source_of, receiver = lengths[1:1 + 2 * twos:2], lengths[2:2 + 2 * twos:2]
    slack = jnp.minimum(source_of - 1, most - receiver)
    passed = jax.random.randint(jax.random.fold_in(rng, 1), (twos,), 0, 1 << 20) % (slack + 1)
    lengths = lengths.at[1:1 + 2 * twos:2].set(source_of - passed).at[2:2 + 2 * twos:2].set(receiver + passed)
    return lengths[jax.random.permutation(jax.random.fold_in(rng, 2), number_of)]


def routed_block(rng, own, number, rows, number_of, top, limit, skew):
    sequence = jax.random.permutation(rng, number_of)
    heavy_load, ordinary = load_shares(number_of, rows * top, limit, skew, True), load_shares(number_of, rows * top, limit, skew, False)
    places = jnp.arange(number_of)

    def named(tallies, offset_by):
        used = int((tallies > 0).sum())
        fixed = max(1, used // 4)
        shifted = fixed + (places - fixed + offset_by * (used - fixed)) % max(1, number_of - fixed)
        return jnp.zeros((number_of,), jnp.int32).at[sequence[jnp.where(places < fixed, places, shifted)]].set(jnp.asarray(tallies, jnp.int32))

    tallies = jnp.where(number % 4 == 0, named(heavy_load, number // 4), named(ordinary, number - number // 4 - 1))
    mixed = jax.random.permutation(jax.random.fold_in(own, 3), number_of)
    donor, sink = mixed[0:number_of // 2 * 2:2], mixed[1:number_of // 2 * 2:2]
    room = jnp.minimum(tallies[donor] - 1, limit - tallies[sink]) // 2
    room = jnp.where((donor == sequence[0]) | (sink == sequence[0]) | (tallies[sink] == 0), 0, jnp.maximum(room, 0))
    shifted = jax.random.randint(jax.random.fold_in(own, 4), (number_of // 2,), 0, 1 << 20) % (room + 1)
    tallies = tallies.at[donor].add(-shifted).at[sink].add(shifted)
    items = jnp.searchsorted(jnp.cumsum(tallies), jnp.arange(rows * top), side="right").astype(jnp.int32)
    table = items.reshape(top, rows).T
    table = table[jax.random.permutation(jax.random.fold_in(own, 1), rows)]
    offset_by = jax.random.randint(jax.random.fold_in(own, 2), (rows, 1), 0, top)
    return jnp.take_along_axis(table, (jnp.arange(top)[None, :] + offset_by) % top, axis=1)


def load_shares(amount, total, limit, lean, full):
    portions = [(1 << 20) // math.isqrt(grade ** lean) + 1 for grade in range(1, amount + 1)]
    largest = limit if full else min(limit, max(-(-total // amount), total * portions[0] // sum(portions)))
    least = 1 if total - largest >= amount - 1 else 0
    counts, rest = [largest] + [least] * (amount - 1), total - largest - least * (amount - 1)
    while rest > 0:
        free = [i for i in range(1, amount) if counts[i] < largest] or [i for i in range(1, amount) if counts[i] < limit]
        whole, remaining = sum([portions[i] for i in free]), rest
        for i in free:
            more = min(limit - counts[i], max(1, remaining * portions[i] // whole), rest)
            counts[i] = counts[i] + more
            rest = rest - more
    return np.array(counts)


def normal_values(own_key, shape, scale, limit, split=(), kind=jnp.bfloat16):
    values = jax.random.normal(own_key, shape, jnp.float32) * scale
    if len(split) > 0:
        values = steps_of(own_key, shape, split, -0.22, 0.18) * values
    return jnp.clip(values, min=-limit, max=limit).astype(kind)


def setup_inputs(seed: int = 0) -> dict:
    arg_keys = jax.random.split(jax.random.key(seed), 17)
    tokens = normal_values(arg_keys[0], (TOKENS, D), 1.0, 6.0, ((0, 32),))
    file_ids = jax.vmap(lambda own: jnp.searchsorted(jnp.cumsum(uneven_parts(own, FILES, SEQ, SEQ // 2, 2)), jnp.arange(SEQ), side="right"))(jax.random.split(arg_keys[1], N_DP)).reshape((N_DP, SEQ)).astype(jnp.int32)
    expert_ids_keys = jax.random.split(jax.random.fold_in(arg_keys[2], 1), TOKENS // TOK_DEV)
    expert_ids_turns = jax.random.permutation(jax.random.fold_in(arg_keys[2], 3), TOKENS // TOK_DEV)
    expert_ids = jax.vmap(lambda own, number: routed_block(jax.random.fold_in(arg_keys[2], 2), own, number, TOK_DEV, EXPERTS, TOPK, MOST, 1))(expert_ids_keys, expert_ids_turns).reshape((TOKENS, TOPK))
    attention_norm_gain = jnp.clip(1.0 + 0.1 * jax.random.normal(arg_keys[3], (D,), jnp.float32), 0.5, 1.5)
    w_query = draw_w_query(jax.random.fold_in(arg_keys[16], 71), 0)
    w_key = draw_w_key(jax.random.fold_in(arg_keys[16], 71), 0)
    w_value = normal_values(arg_keys[6], (D, D), D ** -0.5, 0.125, ((1, 4),))
    query_gain = jnp.clip(1.0 + 0.1 * jax.random.normal(arg_keys[7], (D,), jnp.float32), 0.5, 1.5)
    key_gain = jnp.clip(1.0 + 0.1 * jax.random.normal(arg_keys[8], (D,), jnp.float32), 0.5, 1.5)
    w_output = normal_values(arg_keys[9], (D, D), (D // 64) ** -0.5, 1.0, ((0, 4),))
    expert_norm_gain = jnp.clip(1.0 + 0.1 * jax.random.normal(arg_keys[10], (D,), jnp.float32), 0.5, 1.5)
    w_router = normal_values(arg_keys[11], (D, EXPERTS), (4 * D) ** -0.5, 0.0625)
    w_gate = normal_values(arg_keys[12], (EXPERTS, D, FFE), D ** -0.5, 0.125, ((0, 8), (2, 4)))
    w_up = normal_values(arg_keys[13], (EXPERTS, D, FFE), D ** -0.5, 0.125, ((0, 8), (2, 4)))
    w_down = normal_values(arg_keys[14], (EXPERTS, FFE, D), 0.6, 3.59375, ((0, 8), (1, 4)))
    grad_output = normal_values(arg_keys[15], (TOKENS, D), 1.0, 6.0, ((0, 32),))
    return {"tokens": tokens, "file_ids": file_ids, "expert_ids": expert_ids, "attention_norm_gain": attention_norm_gain, "w_query": w_query, "w_key": w_key, "w_value": w_value, "query_gain": query_gain, "key_gain": key_gain, "w_output": w_output, "expert_norm_gain": expert_norm_gain, "w_router": w_router, "w_gate": w_gate, "w_up": w_up, "w_down": w_down, "grad_output": grad_output}


@jax.custom_vjp
def low(v):
    return lax.optimization_barrier(v.astype(jnp.bfloat16)).astype(jnp.float32)

@jax.custom_vjp
def low_back(v):
    return v

def low_keep(v):
    return (low(v), None)

def low_pass(kept, grad):
    return (grad,)

def back_keep(v):
    return (v, None)

def back_low(kept, grad):
    return (low(grad),)
low.defvjp(low_keep, low_pass)
low_back.defvjp(back_keep, back_low)
EPSILON = 1e-05
THETA = 10000.0
NEG_LARGE = -1e+30
HIGH = lax.Precision.HIGHEST

def root_mean_square_scale(values):
    return lax.rsqrt(lax.optimization_barrier(jnp.mean(values * values, axis=-1, keepdims=True)) + EPSILON)

def rope_tables(length, head_dim):
    half_dim = head_dim // 2
    freq_index = jnp.arange(half_dim, dtype=jnp.float32)
    frequency = THETA ** (-(2.0 * freq_index) / head_dim)
    angles = jnp.arange(length, dtype=jnp.float32)[:, None] * frequency[None, :]
    cosine = jnp.concatenate([jnp.cos(angles), jnp.cos(angles)], axis=1)
    sine_table = jnp.concatenate([jnp.sin(angles), jnp.sin(angles)], axis=1)
    return (cosine[:, None, :], sine_table[:, None, :])

def rotate(values, cosine, sine_table):
    half_dim = values.shape[-1] // 2
    turned = jnp.concatenate([-values[..., half_dim:], values[..., :half_dim]], axis=-1)
    return values * cosine + turned * sine_table

def slot_positions(ids, experts):
    flat_ids = ids.reshape(-1)
    onehot = (flat_ids[:, None] == jnp.arange(experts, dtype=jnp.int32)[None, :]).astype(jnp.int32)
    running = jnp.cumsum(onehot, axis=0)
    return (flat_ids, lax.optimization_barrier(jnp.sum(running * onehot, axis=1)) - 1)

def reference(tokens, file_ids, expert_ids, attention_norm_gain, w_query, w_key, w_value, query_gain, key_gain, w_output, expert_norm_gain, w_router, w_gate, w_up, w_down, grad_output):
    floats = [arr.astype(jnp.float32) for arr in (tokens, attention_norm_gain, w_query, w_key, w_value, query_gain, key_gain, w_output, expert_norm_gain, w_router, w_gate, w_up, w_down)]

    def forward(input_tensors, attention_gain_local, wq_mat, wk_mat, wv_mat, q_gain, k_gain, wo_mat, expert_gain_local, router_mat, gate_mat, up_mat, down_mat):
        cosine, sine_table = rope_tables(SEQ, HEAD_DIM)
        score_scale = 1.0 / math.sqrt(HEAD_DIM)

        def attend(mapped):
            row_values, row_files = mapped
            first_unit_rows = row_values * root_mean_square_scale(row_values)
            first_normalized = low(first_unit_rows * attention_gain_local)
            query_raw = low_back(jnp.dot(first_normalized, wq_mat, precision=HIGH))
            key_raw = low_back(jnp.dot(first_normalized, wk_mat, precision=HIGH))
            value_rows = low(low_back(jnp.dot(first_normalized, wv_mat, precision=HIGH))).reshape(SEQ, HEADS, HEAD_DIM)
            query_normed = query_raw * root_mean_square_scale(query_raw) * q_gain
            key_normed = key_raw * root_mean_square_scale(key_raw) * k_gain
            queries = low(rotate(query_normed.reshape(SEQ, HEADS, HEAD_DIM), cosine, sine_table))
            key_rows = low(rotate(key_normed.reshape(SEQ, HEADS, HEAD_DIM), cosine, sine_table))
            raw_scores = low_back(jnp.einsum('qhd,khd->hqk', queries, key_rows, precision=HIGH) * score_scale)
            positions = jnp.arange(SEQ, dtype=jnp.int32)
            allowed = (positions[None, :] <= positions[:, None]) & (row_files[None, :] == row_files[:, None])
            scores = jnp.where(allowed[None], raw_scores, NEG_LARGE)
            attn_probs = low(jnp.exp(scores - jax.nn.logsumexp(scores, axis=-1, keepdims=True)))
            context = jnp.einsum('hqk,khd->qhd', attn_probs, value_rows, precision=HIGH).reshape(SEQ, D)
            context = low(low_back(context))
            attn_out = low_back(jnp.dot(context, wo_mat, precision=HIGH))
            return row_values + attn_out
        row_blocks = input_tensors.reshape(N_DP, SEQ, D)
        hidden_after_attention = lax.map(jax.checkpoint(attend), (row_blocks, file_ids)).reshape(TOKENS, D)
        quarter = FFE // N_TENSOR

        def experts_block(mapped):
            block_hidden_rows, block_ids = mapped
            second_unit_rows = block_hidden_rows * root_mean_square_scale(block_hidden_rows)
            second_normalized = low(second_unit_rows * expert_gain_local)
            logits = low_back(jnp.dot(second_normalized, router_mat, precision=HIGH))
            route_probs = jax.nn.softmax(logits, axis=-1)
            chosen = block_ids[:, :, None] == jnp.arange(EXPERTS, dtype=jnp.int32)[None, None, :]
            gate_values = lax.optimization_barrier(jnp.sum(jnp.where(chosen, route_probs[:, None, :], 0.0), axis=-1))
            flat_ids, pair_rank = slot_positions(block_ids, EXPERTS)
            pair_slot = flat_ids * MOST + pair_rank
            pair_count = TOK_DEV * TOPK
            slot_owner = jnp.full((EXPERTS * MOST,), pair_count, jnp.int32).at[pair_slot].set(jnp.arange(pair_count, dtype=jnp.int32))
            padded = jnp.concatenate([second_normalized, jnp.zeros((1, D), jnp.float32)], axis=0)
            sent_rows = padded[slot_owner // TOPK].reshape(EXPERTS, MOST, D)
            total = jnp.zeros((EXPERTS, MOST, D), jnp.float32)
            for quarter_index in range(N_TENSOR):
                lo_col = quarter_index * quarter
                hi_col = lo_col + quarter
                expert_in = low_back(sent_rows)
                gate_pre = low_back(jnp.einsum('emd,edf->emf', expert_in, gate_mat[:, :, lo_col:hi_col], precision=HIGH))
                up_pre = low_back(jnp.einsum('emd,edf->emf', expert_in, up_mat[:, :, lo_col:hi_col], precision=HIGH))
                hidden = low(jax.nn.silu(gate_pre) * up_pre)
                total = total + low(jnp.einsum('emf,efd->emd', hidden, down_mat[:, lo_col:hi_col, :], precision=HIGH))
            expert_out = low_back(total).reshape(EXPERTS * MOST, D)[pair_slot].reshape(TOK_DEV, TOPK, D)
            return block_hidden_rows + lax.optimization_barrier(jnp.sum(gate_values[:, :, None] * expert_out, axis=1))
        device_blocks = hidden_after_attention.reshape(N_DP * N_TENSOR, TOK_DEV, D)
        id_blocks = expert_ids.reshape(N_DP * N_TENSOR, TOK_DEV, TOPK)
        return lax.map(jax.checkpoint(experts_block), (device_blocks, id_blocks)).reshape(TOKENS, D)
    result, pullback = jax.vjp(forward, *floats)
    grads = pullback(grad_output.astype(jnp.float32))
    return (result.astype(jnp.bfloat16), grads[0].astype(jnp.bfloat16), grads[2], grads[3], grads[4], grads[7], grads[5], grads[6], grads[1], grads[8], grads[9], grads[10], grads[11], grads[12])
```

```python
import functools
import math

import jax
import jax.numpy as jnp
from jax import lax
from jax.experimental import pallas as pl
from jax.experimental.pallas import tpu as pltpu
from jax.sharding import PartitionSpec as P

HEAD_DIM = 128


EPSILON = 1e-05
THETA = 10000.0
NEG_LARGE = -1e30


def root_mean_square_scale(values):
    return lax.rsqrt(jnp.mean(values * values, axis=-1, keepdims=True) + EPSILON)


def rope_tables(length, head_dim):
    half_dim = head_dim // 2
    freq_index = jnp.arange(half_dim, dtype=jnp.float32)
    frequency = THETA ** (-(2.0 * freq_index) / head_dim)
    angles = jnp.arange(length, dtype=jnp.float32)[:, None] * frequency[None, :]
    cosine = jnp.concatenate([jnp.cos(angles), jnp.cos(angles)], axis=1)
    sine_table = jnp.concatenate([jnp.sin(angles), jnp.sin(angles)], axis=1)
    return (cosine[:, None, :], sine_table[:, None, :])


def rotate(values, cosine, sine_table):
    half_dim = values.shape[-1] // 2
    turned = jnp.concatenate([-values[..., half_dim:], values[..., :half_dim]], axis=-1)
    return values * cosine + turned * sine_table


def unrotate(grad_rows, cosine, sine_table):
    half_dim = grad_rows.shape[-1] // 2
    scaled = grad_rows * sine_table
    turned = jnp.concatenate([scaled[..., half_dim:], -scaled[..., :half_dim]], axis=-1)
    return grad_rows * cosine + turned


def slot_positions(ids, experts):
    flat_ids = ids.reshape(-1)
    onehot = (flat_ids[:, None] == jnp.arange(experts, dtype=jnp.int32)[None, :]).astype(jnp.int32)
    running = jnp.cumsum(onehot, axis=0)
    return (flat_ids, jnp.sum(running * onehot, axis=1) - 1)


def block_scores(query_block, key_rows, file_row, block_start, score_scale):
    block_rows = query_block.shape[0]
    raw_scores = (
        jnp.einsum("qhd,khd->hqk", query_block, key_rows, preferred_element_type=jnp.float32)
        * score_scale
    )
    rows_at = block_start + jnp.arange(block_rows, dtype=jnp.int32)
    cols_at = jnp.arange(key_rows.shape[0], dtype=jnp.int32)
    allowed = (cols_at[None, :] <= rows_at[:, None]) & (file_row[None, :] == file_row[:, None])
    return jnp.where(allowed[None], raw_scores, NEG_LARGE)


MESH = pl.DeviceIdType.MESH
VMEM_LIMIT = 60 * 2**20


def greet(dp, z, nz):
    barrier = pltpu.get_barrier_semaphore()
    for flip in (1, 2, 4):
        pl.semaphore_signal(barrier, 1, device_id=(dp ^ flip, z), device_id_type=MESH)

    @pl.when(z > 0)
    def _():
        pl.semaphore_signal(barrier, 1, device_id=(dp, z - 1), device_id_type=MESH)

    @pl.when(z < nz - 1)
    def _():
        pl.semaphore_signal(barrier, 1, device_id=(dp, z + 1), device_id_type=MESH)

    ends = jnp.where(z > 0, 1, 0) + jnp.where(z < nz - 1, 1, 0)
    pl.semaphore_wait(barrier, 3 + ends)


def gather_kernel(nz, x_ref, out_ref, local_sem, sz, sx, sy, sda, sdb, sc, rz, rx, ry, rda, rdb, rc):
    dp, z = lax.axis_index("dp"), lax.axis_index("tensor")
    half = x_ref.shape[0] // 2
    greet(dp, z, nz)

    def at(flip, zz):
        return out_ref.at[(dp ^ flip) * nz + zz]

    def remote(src, dst, send, recv, device):
        return pltpu.make_async_remote_copy(
            src_ref=src, dst_ref=dst, send_sem=send, recv_sem=recv, device_id=device, device_id_type=MESH
        )

    def z_copy(zz, step, own):
        src = x_ref if own else at(0, zz)
        return remote(src, at(0, zz), sz.at[(step + 1) // 2, zz], rz.at[zz], (dp, z + step))

    def x_copy(zz, own):
        return remote(x_ref if own else at(0, zz), at(0, zz), sx.at[zz], rx.at[zz], (dp ^ 2, z))

    def y_copy(zz, own):
        return remote(x_ref if own else at(0, zz), at(0, zz), sy.at[zz], ry.at[zz], (dp ^ 4, z))

    def a_copy(zz):
        ref = at(4, zz).at[pl.ds(0, half)]
        return remote(ref, ref, sda.at[zz], rda.at[zz], (dp ^ 2, z))

    def b_copy(zz):
        ref = at(2, zz).at[pl.ds(half, half)]
        return remote(ref, ref, sdb.at[zz], rdb.at[zz], (dp ^ 4, z))

    def c_copy(kind, zz, own=False):
        if kind < 3:
            dst = at((0, 2, 4)[kind], zz)
        else:
            dst = at(6, zz).at[pl.ds((kind - 3) * half, half)]
        return remote(x_ref if own else dst, dst, sc.at[kind, zz], rc.at[kind, zz], (dp ^ 1, z))

    def arrived(ref, sem):
        remote(ref, ref, sem, sem, (dp ^ 1, z)).wait_recv()

    def places(distance):
        for sign in (0,) if distance == 0 else (-1, 1):
            yield sign, z + sign * distance

    def spread(distance):
        for sign, zz in places(distance):
            own = distance == 0

            @pl.when((zz >= 0) & (zz < nz))
            def _():
                if not own:
                    arrived(at(0, zz), rz.at[zz])
                if sign <= 0:

                    @pl.when(z < nz - 1)
                    def _():
                        z_copy(zz, 1, own).start()

                if sign >= 0:

                    @pl.when(z > 0)
                    def _():
                        z_copy(zz, -1, own).start()

                x_copy(zz, own).start()
                y_copy(zz, own).start()
                c_copy(0, zz, own).start()

    def relay(distance):
        for _, zz in places(distance):

            @pl.when((zz >= 0) & (zz < nz))
            def _():
                arrived(at(4, zz), ry.at[zz])
                a_copy(zz).start()
                c_copy(2, zz).start()
                arrived(at(2, zz), rx.at[zz])
                b_copy(zz).start()
                c_copy(1, zz).start()

    def corner(distance):
        for _, zz in places(distance):

            @pl.when((zz >= 0) & (zz < nz))
            def _():
                arrived(at(6, zz).at[pl.ds(0, half)], rda.at[zz])
                c_copy(3, zz).start()
                arrived(at(6, zz).at[pl.ds(half, half)], rdb.at[zz])
                c_copy(4, zz).start()

    keep = pltpu.make_async_copy(x_ref, at(0, z), local_sem)
    keep.start()
    for step in range(nz + 2):
        if step < nz:
            spread(step)
        if 0 <= step - 1 < nz:
            relay(step - 1)
        if 0 <= step - 2 < nz:
            corner(step - 2)
    keep.wait()
    for zz in range(nz):

        @pl.when((zz <= z) & (z < nz - 1))
        def _():
            z_copy(zz, 1, False).wait_send()

        @pl.when((zz >= z) & (z > 0))
        def _():
            z_copy(zz, -1, False).wait_send()

        x_copy(zz, False).wait_send()
        y_copy(zz, False).wait_send()
        a_copy(zz).wait_send()
        b_copy(zz).wait_send()
        for kind in range(5):
            c_copy(kind, zz).wait_send()
        for kind, flip in ((0, 1), (1, 3), (2, 5)):
            arrived(at(flip, zz), rc.at[kind, zz])
        for kind in (3, 4):
            arrived(at(7, zz).at[pl.ds((kind - 3) * half, half)], rc.at[kind, zz])


def gather_all(x, nz, collective_id):
    rows, width = x.shape
    dma = pltpu.SemaphoreType.DMA
    return pl.pallas_call(
        functools.partial(gather_kernel, nz),
        name="gather_all",
        out_shape=jax.ShapeDtypeStruct((8 * nz, rows, width), x.dtype),
        in_specs=[pl.BlockSpec(memory_space=pltpu.VMEM)],
        out_specs=pl.BlockSpec(memory_space=pl.ANY),
        scratch_shapes=[dma(())]
        + [dma((2, nz)), dma((nz,)), dma((nz,)), dma((nz,)), dma((nz,)), dma((5, nz))]
        + [dma((nz,)), dma((nz,)), dma((nz,)), dma((nz,)), dma((nz,)), dma((5, nz))],
        compiler_params=pltpu.CompilerParams(
            collective_id=collective_id, has_side_effects=True, vmem_limit_bytes=8 * 2**20
        ),
    )(x)


def z_order(nz):
    return [sorted(range(nz), key=lambda zz: (-abs(zz - z), zz if z >= nz // 2 else -zz)) for z in range(nz)]


CHUNK = 16


def scatter_kernel(nz, p_ref, out_ref, acc, rc, ra, rb, rx, ry, ru, rd, s_local, s_core, r_core, s_a, r_a, s_b, r_b, s_x, r_x, s_y, r_y, s_u, r_u, s_d, r_d):
    dp, z = lax.axis_index("dp"), lax.axis_index("tensor")
    rows = acc.shape[2]
    half = rows // 2
    order = z_order(nz)

    def place(i):
        zz = order[0][i]
        for zv in range(1, nz):
            zz = jnp.where(z == zv, order[zv][i], zz)
        return zz

    def remote(src, dst, send, recv, device):
        return pltpu.make_async_remote_copy(
            src_ref=src, dst_ref=dst, send_sem=send, recv_sem=recv, device_id=device, device_id_type=MESH
        )

    flips = (0, 2, 4, 6)

    def load(kind, zz):
        return pltpu.make_async_copy(
            p_ref.at[(dp ^ flips[kind]) * nz + zz], acc.at[kind, zz], s_local.at[kind, zz]
        )

    def core_copy(kind, zz):
        return remote(
            p_ref.at[(dp ^ flips[kind] ^ 1) * nz + zz], rc.at[kind, zz], s_core.at[kind, zz], r_core.at[kind, zz], (dp ^ 1, z)
        )

    def a_copy(zz):
        return remote(acc.at[3, zz, pl.ds(0, half)], ra.at[zz], s_a.at[zz], r_a.at[zz], (dp ^ 2, z))

    def b_copy(zz):
        return remote(acc.at[3, zz, pl.ds(half, half)], rb.at[zz], s_b.at[zz], r_b.at[zz], (dp ^ 4, z))

    def x_copy(zz):
        return remote(acc.at[1, zz], rx.at[zz], s_x.at[zz], r_x.at[zz], (dp ^ 2, z))

    def y_copy(zz):
        return remote(acc.at[2, zz], ry.at[zz], s_y.at[zz], r_y.at[zz], (dp ^ 4, z))

    def up_copy(zz):
        return remote(acc.at[0, zz], ru.at[zz], s_u.at[zz], r_u.at[zz], (dp, z + 1))

    def down_copy(zz):
        return remote(acc.at[0, zz], rd.at[zz], s_d.at[zz], r_d.at[zz], (dp, z - 1))

    def add(dst, *others, start=0, count=rows):
        def body(k, carry):
            at = pl.ds(start + k * CHUNK, CHUNK)
            total = dst[at, :].astype(jnp.float32)
            for ref, base in others:
                total = total + ref[pl.ds(base + k * CHUNK, CHUNK), :].astype(jnp.float32)
            dst[at, :] = total.astype(dst.dtype)
            return carry

        lax.fori_loop(0, count // CHUNK, body, 0)

    def wave(i):
        zz = place(i)
        for kind in (3, 1, 2, 0):
            core_copy(kind, zz).start()
            load(kind, zz).start()

    def paired(kind, zz):
        load(kind, zz).wait()
        core_copy(kind, zz).wait_recv()

    def stage_diagonal(i):
        zz = place(i)
        paired(3, zz)
        add(acc.at[3, zz], (rc.at[3, zz], 0))
        a_copy(zz).start()
        b_copy(zz).start()

    def stage_side(i):
        zz = place(i)
        paired(1, zz)
        paired(2, zz)
        a_copy(zz).wait_recv()
        add(acc.at[2, zz], (rc.at[2, zz], 0), (ra.at[zz], 0), start=0, count=half)
        add(acc.at[2, zz], (rc.at[2, zz], half), start=half, count=half)
        y_copy(zz).start()
        b_copy(zz).wait_recv()
        add(acc.at[1, zz], (rc.at[1, zz], half), (rb.at[zz], 0), start=half, count=half)
        add(acc.at[1, zz], (rc.at[1, zz], 0), start=0, count=half)
        x_copy(zz).start()

    def stage_column(i):
        zz = place(i)
        paired(0, zz)
        x_copy(zz).wait_recv()
        y_copy(zz).wait_recv()
        add(acc.at[0, zz], (rc.at[0, zz], 0), (rx.at[zz], 0), (ry.at[zz], 0))

        @pl.when((zz > z) & (z == 0))
        def _():
            up_copy(zz).start()

        @pl.when((zz < z) & (z == nz - 1))
        def _():
            down_copy(zz).start()

    def stage_line(i):
        zz = place(i)

        @pl.when((zz > z) & (z > 0))
        def _():
            up_copy(zz).wait_recv()
            add(acc.at[0, zz], (ru.at[zz], 0))
            up_copy(zz).start()

        @pl.when((zz < z) & (z < nz - 1))
        def _():
            down_copy(zz).wait_recv()
            add(acc.at[0, zz], (rd.at[zz], 0))
            down_copy(zz).start()

    greet(dp, z, nz)
    wave(0)
    for i in range(nz + 3):
        if i + 1 < nz:
            wave(i + 1)
        if i < nz:
            stage_diagonal(i)
        if 0 <= i - 1 < nz:
            stage_side(i - 1)
        if 0 <= i - 2 < nz:
            stage_column(i - 2)
        if 0 <= i - 3 < nz:
            stage_line(i - 3)

    @pl.when(z > 0)
    def _():
        up_copy(z).wait_recv()

    @pl.when(z < nz - 1)
    def _():
        down_copy(z).wait_recv()

    def finish(k, carry):
        at = pl.ds(k * CHUNK, CHUNK)
        total = acc[0, z, at, :].astype(jnp.float32)
        zero = jnp.zeros_like(total)
        total = total + jnp.where(z > 0, ru[z, at, :].astype(jnp.float32), zero)
        total = total + jnp.where(z < nz - 1, rd[z, at, :].astype(jnp.float32), zero)
        out_ref[at, :] = total
        return carry

    lax.fori_loop(0, rows // CHUNK, finish, 0)
    for zz in range(nz):
        for kind in range(4):
            core_copy(kind, zz).wait_send()
        a_copy(zz).wait_send()
        b_copy(zz).wait_send()
        x_copy(zz).wait_send()
        y_copy(zz).wait_send()

        @pl.when(zz > z)
        def _():
            up_copy(zz).wait_send()

        @pl.when(zz < z)
        def _():
            down_copy(zz).wait_send()


def scatter_all(p, nz, collective_id):
    _, rows, width = p.shape
    dma, vmem = pltpu.SemaphoreType.DMA, functools.partial(pltpu.VMEM, dtype=p.dtype)
    half = rows // 2
    return pl.pallas_call(
        functools.partial(scatter_kernel, nz),
        name="scatter_all",
        out_shape=jax.ShapeDtypeStruct((rows, width), jnp.float32),
        in_specs=[pl.BlockSpec(memory_space=pl.ANY)],
        out_specs=pl.BlockSpec(memory_space=pltpu.VMEM),
        scratch_shapes=[vmem((4, nz, rows, width)), vmem((4, nz, rows, width))]
        + [vmem((nz, half, width)) for _ in range(2)]
        + [vmem((nz, rows, width)) for _ in range(4)]
        + [dma((4, nz)), dma((4, nz)), dma((4, nz))]
        + [dma((nz,)) for _ in range(12)],
        compiler_params=pltpu.CompilerParams(
            collective_id=collective_id, has_side_effects=True, vmem_limit_bytes=VMEM_LIMIT
        ),
    )(p)


def experts_routed(
    hidden_after_attention,
    expert_ids,
    expert_norm_gain,
    w_router,
    w_gate,
    w_up,
    w_down,
    grad_output,
):
    tok_count, d_model = hidden_after_attention.shape
    n_tensor = lax.axis_size("tensor")
    n_dp = lax.axis_size("dp")
    devices = n_dp * n_tensor
    second_norm_scale = root_mean_square_scale(hidden_after_attention)
    second_unit_rows = hidden_after_attention * second_norm_scale
    second_normalized = (second_unit_rows * expert_norm_gain).astype(jnp.bfloat16)
    experts = w_router.shape[1]
    topk = expert_ids.shape[1]
    exp_dev = w_gate.shape[0]
    most = 2 * ((tok_count * topk * 9 + experts * 16 - 1) // (experts * 16))
    route_probs = jax.nn.softmax(
        jnp.dot(second_normalized, w_router, preferred_element_type=jnp.float32), axis=-1
    )
    chosen = expert_ids[:, :, None] == jnp.arange(experts, dtype=jnp.int32)[None, None, :]
    gate_values = jnp.sum(jnp.where(chosen, route_probs[:, None, :], 0.0), axis=-1)
    flat_ids, pair_rank = slot_positions(expert_ids, experts)
    pair_slot = (flat_ids % exp_dev * n_dp + flat_ids // exp_dev) * most + pair_rank
    pair_count = tok_count * topk
    slot_count = exp_dev * n_dp * most
    slot_owner = (
        jnp.full((slot_count,), pair_count, jnp.int32)
        .at[pair_slot]
        .set(jnp.arange(pair_count, dtype=jnp.int32))
    )
    padded = jnp.concatenate([second_normalized, jnp.zeros((1, d_model), jnp.bfloat16)], axis=0)
    outgoing = padded[slot_owner // topk].reshape(exp_dev, n_dp, most, d_model)
    copies = jnp.broadcast_to(
        outgoing[:, :, None], (exp_dev, n_dp, n_tensor, most, d_model)
    ).reshape(exp_dev, devices, most, d_model)
    arrived = lax.all_to_all(copies, ("dp", "tensor"), split_axis=1, concat_axis=1, tiled=True)
    expert_rows = arrived.reshape(exp_dev, devices * most, d_model)
    gate_pre = jnp.einsum("erd,edf->erf", expert_rows, w_gate, preferred_element_type=jnp.float32)
    up_pre = jnp.einsum("erd,edf->erf", expert_rows, w_up, preferred_element_type=jnp.float32)
    gate_sigmoid = jax.nn.sigmoid(gate_pre)
    silu_gate = gate_pre * gate_sigmoid
    hidden = (silu_gate * up_pre).astype(jnp.bfloat16)
    partial_value = (
        jnp.einsum("erf,efd->erd", hidden, w_down, preferred_element_type=jnp.float32)
        .astype(jnp.bfloat16)
        .reshape(exp_dev, devices, most, d_model)
    )
    returned = lax.all_to_all(
        partial_value, ("dp", "tensor"), split_axis=1, concat_axis=1, tiled=True
    )
    expert_out = jnp.sum(
        returned.reshape(exp_dev, n_dp, n_tensor, most, d_model).astype(jnp.float32), axis=2
    ).reshape(slot_count, d_model)
    pair_out = expert_out[pair_slot].reshape(tok_count, topk, d_model)
    result = (hidden_after_attention + jnp.sum(gate_values[:, :, None] * pair_out, axis=1)).astype(
        jnp.bfloat16
    )
    cotangent = grad_output.astype(jnp.float32)
    grad_gates = jnp.sum(pair_out * cotangent[:, None, :], axis=-1)
    grad_pairs = (
        (gate_values[:, :, None] * cotangent[:, None, :])
        .astype(jnp.bfloat16)
        .reshape(pair_count, d_model)
    )
    grad_slots = jnp.concatenate([grad_pairs, jnp.zeros((1, d_model), jnp.bfloat16)], axis=0)[
        slot_owner
    ].reshape(exp_dev, n_dp, most, d_model)
    grad_copies = jnp.broadcast_to(
        grad_slots[:, :, None], (exp_dev, n_dp, n_tensor, most, d_model)
    ).reshape(exp_dev, devices, most, d_model)
    grad_arrived = lax.all_to_all(
        grad_copies, ("dp", "tensor"), split_axis=1, concat_axis=1, tiled=True
    )
    grad_rows = grad_arrived.reshape(exp_dev, devices * most, d_model)
    grad_hidden = jnp.einsum("erd,efd->erf", grad_rows, w_down, preferred_element_type=jnp.float32)
    grad_down = jnp.einsum("erf,erd->efd", hidden, grad_rows, preferred_element_type=jnp.float32)
    grad_gate_pre = (
        grad_hidden * up_pre * gate_sigmoid * (1.0 + gate_pre * (1.0 - gate_sigmoid))
    ).astype(jnp.bfloat16)
    grad_up_pre = (grad_hidden * silu_gate).astype(jnp.bfloat16)
    grad_gate = jnp.einsum(
        "erd,erf->edf", expert_rows, grad_gate_pre, preferred_element_type=jnp.float32
    )
    grad_up = jnp.einsum(
        "erd,erf->edf", expert_rows, grad_up_pre, preferred_element_type=jnp.float32
    )
    grad_expert_in = jnp.einsum(
        "erf,edf->erd", grad_gate_pre, w_gate, preferred_element_type=jnp.float32
    )
    grad_expert_in = grad_expert_in + jnp.einsum(
        "erf,edf->erd", grad_up_pre, w_up, preferred_element_type=jnp.float32
    )
    grad_expert_in = grad_expert_in.astype(jnp.bfloat16).reshape(exp_dev, devices, most, d_model)
    grad_back = lax.all_to_all(
        grad_expert_in, ("dp", "tensor"), split_axis=1, concat_axis=1, tiled=True
    )
    grad_slot_in = jnp.sum(
        grad_back.reshape(exp_dev, n_dp, n_tensor, most, d_model).astype(jnp.float32), axis=2
    ).reshape(slot_count, d_model)
    grad_second_normalized = jnp.sum(
        grad_slot_in[pair_slot].reshape(tok_count, topk, d_model), axis=1
    )
    grad_route = jnp.sum(jnp.where(chosen, grad_gates[:, :, None], 0.0), axis=1)
    grad_logits = (
        route_probs * (grad_route - jnp.sum(route_probs * grad_route, axis=-1, keepdims=True))
    ).astype(jnp.bfloat16)
    grad_router_part = jnp.einsum(
        "td,te->de", second_normalized, grad_logits, preferred_element_type=jnp.float32
    )
    grad_second_normalized = grad_second_normalized + jnp.einsum(
        "te,de->td", grad_logits, w_router, preferred_element_type=jnp.float32
    )
    grad_expert_share = jnp.sum(grad_second_normalized * second_unit_rows, axis=0)
    grad_second_unit_rows = grad_second_normalized * expert_norm_gain
    grad_hidden_one = (
        second_norm_scale
        * (
            grad_second_unit_rows
            - second_unit_rows
            * jnp.mean(grad_second_unit_rows * second_unit_rows, axis=-1, keepdims=True)
        )
        + cotangent
    )
    return (
        result,
        grad_hidden_one,
        grad_expert_share,
        grad_router_part,
        grad_gate,
        grad_up,
        grad_down,
    )


def experts_dense(
    hidden_after_attention,
    expert_ids,
    expert_norm_gain,
    w_router,
    w_gate,
    w_up,
    w_down,
    grad_output,
):
    tok_count, d_model = hidden_after_attention.shape
    n_tensor = lax.axis_size("tensor")
    n_dp = lax.axis_size("dp")
    devices = n_dp * n_tensor
    everyone = ("dp", "tensor")
    second_norm_scale = root_mean_square_scale(hidden_after_attention)
    second_unit_rows = hidden_after_attention * second_norm_scale
    second_normalized = (second_unit_rows * expert_norm_gain).astype(jnp.bfloat16)
    experts = w_router.shape[1]
    exp_dev, _, width = w_gate.shape
    all_count = devices * tok_count
    expert_at = jnp.arange(experts, dtype=jnp.int32)
    local_at = lax.axis_index("dp") * exp_dev + jnp.arange(exp_dev, dtype=jnp.int32)

    all_rows = gather_all(second_normalized, n_tensor, 0).reshape(all_count, d_model)
    all_cotangents = lax.all_gather(grad_output, everyone, axis=0, tiled=True)
    all_ids = lax.all_gather(expert_ids, everyone, axis=0, tiled=True)

    def route(rows):
        return jax.nn.softmax(
            jnp.dot(rows, w_router, preferred_element_type=jnp.float32), axis=-1
        )

    down_rows = w_down.reshape(exp_dev * width, d_model)
    wide = jnp.concatenate([w_gate[e] for e in range(exp_dev)] + [w_up[e] for e in range(exp_dev)], axis=1)
    all_route = route(all_rows)
    named = jnp.any(all_ids[:, :, None] == local_at[None, None, :], axis=1)
    local_route = jnp.sum(
        jnp.where(local_at[None, :, None] == expert_at[None, None, :], all_route[:, None, :], 0.0), axis=-1
    )
    local_gate = jnp.where(named, local_route, 0.0)
    spread = jnp.repeat(local_gate, width, axis=1)
    both = exp_dev * width
    pre = jnp.dot(all_rows, wide, preferred_element_type=jnp.float32)
    gate_pre, up_pre = pre[:, :both], pre[:, both:]
    gate_sigmoid = jax.nn.sigmoid(gate_pre)
    silu_gate = gate_pre * gate_sigmoid
    hidden = silu_gate * up_pre
    gated_hidden = (spread * hidden).astype(jnp.bfloat16)
    out_part = jnp.dot(gated_hidden, down_rows, preferred_element_type=jnp.float32).astype(jnp.bfloat16)
    back = jnp.einsum("td,fd->tf", all_cotangents, down_rows, preferred_element_type=jnp.float32)
    gate_grads = jnp.sum((hidden * back).reshape(all_count, exp_dev, width), axis=-1)
    grad_hidden = spread * back
    grad_gate_pre = (
        grad_hidden * up_pre * gate_sigmoid * (1.0 + gate_pre * (1.0 - gate_sigmoid))
    ).astype(jnp.bfloat16)
    grad_up_pre = (grad_hidden * silu_gate).astype(jnp.bfloat16)
    grad_pre = jnp.concatenate([grad_gate_pre, grad_up_pre], axis=1)
    in_part = jnp.einsum("tf,df->td", grad_pre, wide, preferred_element_type=jnp.float32).astype(jnp.bfloat16)
    grad_in = scatter_all(in_part.reshape(devices, tok_count, d_model), n_tensor, 1)
    moe_out = scatter_all(out_part.reshape(devices, tok_count, d_model), n_tensor, 1)
    grad_down = jnp.einsum(
        "tf,td->fd", gated_hidden, all_cotangents, preferred_element_type=jnp.float32
    ).reshape(exp_dev, width, d_model)
    grad_wide = jnp.einsum("td,tf->df", all_rows, grad_pre, preferred_element_type=jnp.float32)
    grad_gate = jnp.stack([grad_wide[:, e * width : (e + 1) * width] for e in range(exp_dev)])
    grad_up = jnp.stack([grad_wide[:, both + e * width : both + (e + 1) * width] for e in range(exp_dev)])

    route_grads = jnp.sum(
        jnp.where(
            (named[:, :, None]) & (local_at[None, :, None] == expert_at[None, None, :]),
            gate_grads[:, :, None],
            0.0,
        ),
        axis=1,
    )
    grad_route = lax.psum_scatter(route_grads, everyone, scatter_dimension=0, tiled=True)
    cotangent = grad_output.astype(jnp.float32)
    result = (hidden_after_attention + moe_out).astype(jnp.bfloat16)
    route_probs = route(second_normalized)
    grad_logits = (
        route_probs * (grad_route - jnp.sum(route_probs * grad_route, axis=-1, keepdims=True))
    ).astype(jnp.bfloat16)
    grad_router_part = jnp.einsum(
        "td,te->de", second_normalized, grad_logits, preferred_element_type=jnp.float32
    )
    grad_second_normalized = grad_in + jnp.einsum(
        "te,de->td", grad_logits, w_router, preferred_element_type=jnp.float32
    )
    grad_expert_share = jnp.sum(grad_second_normalized * second_unit_rows, axis=0)
    grad_second_unit_rows = grad_second_normalized * expert_norm_gain
    grad_hidden_one = (
        second_norm_scale
        * (
            grad_second_unit_rows
            - second_unit_rows
            * jnp.mean(grad_second_unit_rows * second_unit_rows, axis=-1, keepdims=True)
        )
        + cotangent
    )
    return (
        result,
        grad_hidden_one,
        grad_expert_share,
        grad_router_part,
        grad_gate,
        grad_up,
        grad_down,
    )


def local(
    tokens,
    file_ids,
    expert_ids,
    attention_norm_gain,
    w_query,
    w_key,
    w_value,
    query_gain,
    key_gain,
    w_output,
    expert_norm_gain,
    w_router,
    w_gate,
    w_up,
    w_down,
    grad_output,
):
    tok_count, d_model = tokens.shape
    n_tensor = lax.axis_size("tensor")
    n_dp = lax.axis_size("dp")
    devices = n_dp * n_tensor
    local_dim = w_query.shape[1]
    head_dim = HEAD_DIM
    local_heads = local_dim // head_dim
    seq_len = tok_count * n_tensor
    block_rows = min(512, seq_len)
    score_scale = 1.0 / math.sqrt(head_dim)
    file_row = file_ids[0]
    cosine, sine_table = rope_tables(seq_len, head_dim)
    input_tensors = tokens.astype(jnp.float32)
    first_norm_scale = root_mean_square_scale(input_tensors)
    first_unit_rows = input_tensors * first_norm_scale
    first_normalized = (first_unit_rows * attention_norm_gain).astype(jnp.bfloat16)
    normed_all = lax.all_gather(first_normalized, "tensor", axis=0, tiled=True)
    query_raw = jnp.dot(normed_all, w_query, preferred_element_type=jnp.float32)
    key_raw = jnp.dot(normed_all, w_key, preferred_element_type=jnp.float32)
    value_rows = (
        jnp.dot(normed_all, w_value, preferred_element_type=jnp.float32)
        .astype(jnp.bfloat16)
        .reshape(seq_len, local_heads, head_dim)
    )
    query_total, key_total = lax.psum(
        (jnp.sum(query_raw * query_raw, axis=1), jnp.sum(key_raw * key_raw, axis=1)), "tensor"
    )
    query_scale = lax.rsqrt(query_total / d_model + EPSILON)[:, None]
    key_scale = lax.rsqrt(key_total / d_model + EPSILON)[:, None]
    query_hat = query_raw * query_scale
    key_hat = key_raw * key_scale
    queries = rotate(
        (query_hat * query_gain).reshape(seq_len, local_heads, head_dim), cosine, sine_table
    ).astype(jnp.bfloat16)
    key_rows = rotate(
        (key_hat * key_gain).reshape(seq_len, local_heads, head_dim), cosine, sine_table
    ).astype(jnp.bfloat16)
    block_start = 0
    scores = block_scores(queries, key_rows, file_row, block_start, score_scale)
    row_peak = jnp.max(scores, axis=-1, keepdims=True)
    log_total = row_peak + jnp.log(jnp.sum(jnp.exp(scores - row_peak), axis=-1, keepdims=True))
    attn_probs = jnp.exp(scores - log_total).astype(jnp.bfloat16)
    context_blocks = jnp.einsum(
        "hqk,khd->qhd", attn_probs, value_rows, preferred_element_type=jnp.float32
    )
    log_totals = [log_total]
    context = context_blocks.reshape(seq_len, local_dim).astype(jnp.bfloat16)
    attn_out = lax.psum_scatter(
        jnp.dot(context, w_output, preferred_element_type=jnp.float32).astype(jnp.bfloat16),
        "tensor",
        scatter_dimension=0,
        tiled=True,
    ).astype(jnp.float32)
    hidden_after_attention = input_tensors + attn_out
    dense = n_dp == 8 and n_dp <= expert_ids.shape[1]
    result, grad_hidden_one, grad_expert_share, grad_router_part, grad_gate, grad_up, grad_down = (
        experts_dense if dense else experts_routed
    )(
        hidden_after_attention,
        expert_ids,
        expert_norm_gain,
        w_router,
        w_gate,
        w_up,
        w_down,
        grad_output,
    )
    grad_attn = grad_hidden_one.astype(jnp.bfloat16)
    grad_attn_all = lax.all_gather(grad_attn, "tensor", axis=0, tiled=True)
    grad_output_part = jnp.einsum(
        "sd,se->de", context, grad_attn_all, preferred_element_type=jnp.float32
    )
    grad_context = (
        jnp.einsum("se,de->sd", grad_attn_all, w_output, preferred_element_type=jnp.float32)
        .astype(jnp.bfloat16)
        .reshape(seq_len, local_heads, head_dim)
    )
    grad_query_blocks = []
    grad_key_total = jnp.zeros((seq_len, local_heads, head_dim), jnp.float32)
    grad_value_total = jnp.zeros((seq_len, local_heads, head_dim), jnp.float32)
    for block_index, block_start in enumerate(range(0, seq_len, block_rows)):
        scores = block_scores(queries, key_rows, file_row, block_start, score_scale)
        probs_full = jnp.exp(scores - log_totals[block_index])
        probs_low = probs_full.astype(jnp.bfloat16)
        grad_value_total = jnp.einsum(
            "hqk,qhd->khd", probs_low, grad_context, preferred_element_type=jnp.float32
        )
        grad_probs = jnp.einsum(
            "qhd,khd->hqk", grad_context, value_rows, preferred_element_type=jnp.float32
        )
        row_shift = jnp.sum(probs_full * grad_probs, axis=-1, keepdims=True)
        grad_scores = (probs_full * (grad_probs - row_shift)).astype(jnp.bfloat16)
        grad_query_blocks.append(
            jnp.einsum("hqk,khd->qhd", grad_scores, key_rows, preferred_element_type=jnp.float32)
            * score_scale
        )
        grad_key_total = (
            jnp.einsum("hqk,qhd->khd", grad_scores, queries, preferred_element_type=jnp.float32)
            * score_scale
        )
    grad_query_normed = unrotate(grad_query_blocks[0], cosine, sine_table).reshape(
        seq_len, local_dim
    )
    grad_key_normed = unrotate(grad_key_total, cosine, sine_table).reshape(seq_len, local_dim)
    grad_qgain_part = jnp.sum(grad_query_normed * query_hat, axis=0)
    grad_kgain_part = jnp.sum(grad_key_normed * key_hat, axis=0)
    grad_query_hat = grad_query_normed * query_gain
    grad_key_hat = grad_key_normed * key_gain
    query_inner, key_inner = lax.psum(
        (jnp.sum(grad_query_hat * query_hat, axis=1), jnp.sum(grad_key_hat * key_hat, axis=1)),
        "tensor",
    )
    grad_query_raw = (
        query_scale * (grad_query_hat - query_hat * (query_inner / d_model)[:, None])
    ).astype(jnp.bfloat16)
    grad_key_raw = (key_scale * (grad_key_hat - key_hat * (key_inner / d_model)[:, None])).astype(
        jnp.bfloat16
    )
    grad_value_raw = grad_value_total.reshape(seq_len, local_dim).astype(jnp.bfloat16)
    grad_query_part = jnp.einsum(
        "sd,sf->df", normed_all, grad_query_raw, preferred_element_type=jnp.float32
    )
    grad_key_part = jnp.einsum(
        "sd,sf->df", normed_all, grad_key_raw, preferred_element_type=jnp.float32
    )
    grad_value_part = jnp.einsum(
        "sd,sf->df", normed_all, grad_value_raw, preferred_element_type=jnp.float32
    )
    summed = jnp.einsum("sf,df->sd", grad_query_raw, w_query, preferred_element_type=jnp.float32)
    summed = summed + jnp.einsum(
        "sf,df->sd", grad_key_raw, w_key, preferred_element_type=jnp.float32
    )
    grad_first_normalized = lax.psum_scatter(
        (
            summed
            + jnp.einsum("sf,df->sd", grad_value_raw, w_value, preferred_element_type=jnp.float32)
        ).astype(jnp.bfloat16),
        "tensor",
        scatter_dimension=0,
        tiled=True,
    ).astype(jnp.float32)
    grad_attention_share = jnp.sum(grad_first_normalized * first_unit_rows, axis=0)
    grad_first_unit_rows = grad_first_normalized * attention_norm_gain
    grad_tokens = (
        first_norm_scale
        * (
            grad_first_unit_rows
            - first_unit_rows
            * jnp.mean(grad_first_unit_rows * first_unit_rows, axis=-1, keepdims=True)
        )
        + grad_hidden_one
    ).astype(jnp.bfloat16)
    total_query, total_key, total_value, total_output, total_qgain, total_kgain = (
        lax.psum(grad_query_part.astype(jnp.bfloat16), "dp").astype(jnp.float32),
        lax.psum(grad_key_part.astype(jnp.bfloat16), "dp").astype(jnp.float32),
        lax.psum(grad_value_part.astype(jnp.bfloat16), "dp").astype(jnp.float32),
        lax.psum(grad_output_part.astype(jnp.bfloat16), "dp").astype(jnp.float32),
        lax.psum(grad_qgain_part.astype(jnp.bfloat16), "dp").astype(jnp.float32),
        lax.psum(grad_kgain_part.astype(jnp.bfloat16), "dp").astype(jnp.float32),
    )
    total_attn_gain, total_ffn_gain, total_router = lax.psum(
        (grad_attention_share, grad_expert_share, grad_router_part), ("dp", "tensor")
    )
    return (
        result,
        grad_tokens,
        total_query,
        total_key,
        total_value,
        total_output,
        total_qgain,
        total_kgain,
        total_attn_gain,
        total_ffn_gain,
        total_router,
        grad_gate,
        grad_up,
        grad_down,
    )


def solution(mesh):
    return jax.shard_map(
        local,
        mesh=mesh,
        in_specs=(
            P(("dp", "tensor"), None),
            P("dp", None),
            P(("dp", "tensor"), None),
            P(),
            P(None, "tensor"),
            P(None, "tensor"),
            P(None, "tensor"),
            P("tensor"),
            P("tensor"),
            P("tensor", None),
            P(),
            P(),
            P("dp", None, "tensor"),
            P("dp", None, "tensor"),
            P("dp", "tensor", None),
            P(("dp", "tensor"), None),
        ),
        out_specs=(
            P(("dp", "tensor"), None),
            P(("dp", "tensor"), None),
            P(None, "tensor"),
            P(None, "tensor"),
            P(None, "tensor"),
            P("tensor", None),
            P("tensor"),
            P("tensor"),
            P(),
            P(),
            P(),
            P("dp", None, "tensor"),
            P("dp", None, "tensor"),
            P("dp", "tensor", None),
        ),
        check_vma=False,
    )
```

```python
import functools
import math

import jax
import jax.numpy as jnp
from jax import lax
from jax.experimental import pallas as pl
from jax.experimental.pallas import tpu as pltpu
from jax.sharding import PartitionSpec as P

HEAD_DIM = 128


EPSILON = 1e-05
THETA = 10000.0
NEG_LARGE = -1e30


def root_mean_square_scale(values):
    return lax.rsqrt(jnp.mean(values * values, axis=-1, keepdims=True) + EPSILON)


def rope_tables(length, head_dim):
    half_dim = head_dim // 2
    freq_index = jnp.arange(half_dim, dtype=jnp.float32)
    frequency = THETA ** (-(2.0 * freq_index) / head_dim)
    angles = jnp.arange(length, dtype=jnp.float32)[:, None] * frequency[None, :]
    cosine = jnp.concatenate([jnp.cos(angles), jnp.cos(angles)], axis=1)
    sine_table = jnp.concatenate([jnp.sin(angles), jnp.sin(angles)], axis=1)
    return (cosine[:, None, :], sine_table[:, None, :])


def rotate(values, cosine, sine_table):
    half_dim = values.shape[-1] // 2
    turned = jnp.concatenate([-values[..., half_dim:], values[..., :half_dim]], axis=-1)
    return values * cosine + turned * sine_table


def unrotate(grad_rows, cosine, sine_table):
    half_dim = grad_rows.shape[-1] // 2
    scaled = grad_rows * sine_table
    turned = jnp.concatenate([scaled[..., half_dim:], -scaled[..., :half_dim]], axis=-1)
    return grad_rows * cosine + turned


def slot_positions(ids, experts):
    flat_ids = ids.reshape(-1)
    onehot = (flat_ids[:, None] == jnp.arange(experts, dtype=jnp.int32)[None, :]).astype(jnp.int32)
    running = jnp.cumsum(onehot, axis=0)
    return (flat_ids, jnp.sum(running * onehot, axis=1) - 1)


def block_scores(query_block, key_rows, file_row, block_start, score_scale):
    block_rows = query_block.shape[0]
    raw_scores = (
        jnp.einsum("qhd,khd->hqk", query_block, key_rows, preferred_element_type=jnp.float32)
        * score_scale
    )
    rows_at = block_start + jnp.arange(block_rows, dtype=jnp.int32)
    cols_at = jnp.arange(key_rows.shape[0], dtype=jnp.int32)
    allowed = (cols_at[None, :] <= rows_at[:, None]) & (file_row[None, :] == file_row[:, None])
    return jnp.where(allowed[None], raw_scores, NEG_LARGE)


MESH = pl.DeviceIdType.MESH
VMEM_LIMIT = 60 * 2**20


def greet(dp, z, nz):
    barrier = pltpu.get_barrier_semaphore()
    for flip in (1, 2, 4):
        pl.semaphore_signal(barrier, 1, device_id=(dp ^ flip, z), device_id_type=MESH)

    @pl.when(z > 0)
    def _():
        pl.semaphore_signal(barrier, 1, device_id=(dp, z - 1), device_id_type=MESH)

    @pl.when(z < nz - 1)
    def _():
        pl.semaphore_signal(barrier, 1, device_id=(dp, z + 1), device_id_type=MESH)

    ends = jnp.where(z > 0, 1, 0) + jnp.where(z < nz - 1, 1, 0)
    pl.semaphore_wait(barrier, 3 + ends)


def remote(src, dst, send, recv, device):
    return pltpu.make_async_remote_copy(
        src_ref=src, dst_ref=dst, send_sem=send, recv_sem=recv, device_id=device, device_id_type=MESH
    )


def gather_kernel(nz, x_ref, t_ref, out_ref, tags_ref, local_sem, sz, sx, sy, sda, sdb, sc, rz, rx, ry, rda, rdb, rc):
    dp, z = lax.axis_index("dp"), lax.axis_index("tensor")
    half = x_ref.shape[0] // 2
    greet(dp, z, nz)

    def rows_at(flip, zz):
        return out_ref.at[(dp ^ flip) * nz + zz]

    def tags_at(flip, zz):
        return tags_ref.at[(dp ^ flip) * nz + zz]

    def whole(flip, zz, own, send, recv, device):
        return (
            remote(x_ref if own else rows_at(flip, zz), rows_at(flip, zz), send(0), recv(0), device),
            remote(t_ref if own else tags_at(flip, zz), tags_at(flip, zz), send(1), recv(1), device),
        )

    def z_copy(zz, step, own):
        return whole(
            0, zz, own, lambda k: sz.at[k, (step + 1) // 2, zz], lambda k: rz.at[k, zz], (dp, z + step)
        )

    def x_copy(zz, own):
        return whole(0, zz, own, lambda k: sx.at[k, zz], lambda k: rx.at[k, zz], (dp ^ 2, z))

    def y_copy(zz, own):
        return whole(0, zz, own, lambda k: sy.at[k, zz], lambda k: ry.at[k, zz], (dp ^ 4, z))

    def a_copy(zz):
        ref = rows_at(4, zz).at[pl.ds(0, half)]
        return (
            remote(ref, ref, sda.at[0, zz], rda.at[0, zz], (dp ^ 2, z)),
            remote(tags_at(4, zz), tags_at(4, zz), sda.at[1, zz], rda.at[1, zz], (dp ^ 2, z)),
        )

    def b_copy(zz):
        ref = rows_at(2, zz).at[pl.ds(half, half)]
        return (remote(ref, ref, sdb.at[zz], rdb.at[zz], (dp ^ 4, z)),)

    def c_copy(kind, zz, own=False):
        send, recv = (lambda k: sc.at[k, kind, zz]), (lambda k: rc.at[k, kind, zz])
        if kind < 3:
            return whole((0, 2, 4)[kind], zz, own, send, recv, (dp ^ 1, z))
        ref = rows_at(6, zz).at[pl.ds((kind - 3) * half, half)]
        copies = (remote(ref, ref, send(0), recv(0), (dp ^ 1, z)),)
        if kind == 3:
            copies += (remote(tags_at(6, zz), tags_at(6, zz), send(1), recv(1), (dp ^ 1, z)),)
        return copies

    def start(copies):
        for copy in copies:
            copy.start()

    def arrived(ref, sem):
        remote(ref, ref, sem, sem, (dp ^ 1, z)).wait_recv()

    def both_arrived(flip, zz, recv):
        arrived(rows_at(flip, zz), recv(0))
        arrived(tags_at(flip, zz), recv(1))

    def places(distance):
        for sign in (0,) if distance == 0 else (-1, 1):
            yield sign, z + sign * distance

    def spread(distance):
        for sign, zz in places(distance):
            own = distance == 0

            @pl.when((zz >= 0) & (zz < nz))
            def _():
                if not own:
                    both_arrived(0, zz, lambda k: rz.at[k, zz])
                if sign <= 0:

                    @pl.when(z < nz - 1)
                    def _():
                        start(z_copy(zz, 1, own))

                if sign >= 0:

                    @pl.when(z > 0)
                    def _():
                        start(z_copy(zz, -1, own))

                start(x_copy(zz, own))
                start(y_copy(zz, own))
                start(c_copy(0, zz, own))

    def relay(distance):
        for _, zz in places(distance):

            @pl.when((zz >= 0) & (zz < nz))
            def _():
                both_arrived(4, zz, lambda k: ry.at[k, zz])
                start(a_copy(zz))
                start(c_copy(2, zz))
                both_arrived(2, zz, lambda k: rx.at[k, zz])
                start(b_copy(zz))
                start(c_copy(1, zz))

    def corner(distance):
        for _, zz in places(distance):

            @pl.when((zz >= 0) & (zz < nz))
            def _():
                arrived(rows_at(6, zz).at[pl.ds(0, half)], rda.at[0, zz])
                arrived(tags_at(6, zz), rda.at[1, zz])
                start(c_copy(3, zz))
                arrived(rows_at(6, zz).at[pl.ds(half, half)], rdb.at[zz])
                start(c_copy(4, zz))

    keep = pltpu.make_async_copy(x_ref, rows_at(0, z), local_sem.at[0])
    keep_tags = pltpu.make_async_copy(t_ref, tags_at(0, z), local_sem.at[1])
    keep.start()
    keep_tags.start()
    for step in range(nz + 2):
        if step < nz:
            spread(step)
        if 0 <= step - 1 < nz:
            relay(step - 1)
        if 0 <= step - 2 < nz:
            corner(step - 2)
    keep.wait()
    keep_tags.wait()

    def sent(copies):
        for copy in copies:
            copy.wait_send()

    for zz in range(nz):

        @pl.when((zz <= z) & (z < nz - 1))
        def _():
            sent(z_copy(zz, 1, False))

        @pl.when((zz >= z) & (z > 0))
        def _():
            sent(z_copy(zz, -1, False))

        sent(x_copy(zz, False))
        sent(y_copy(zz, False))
        sent(a_copy(zz))
        sent(b_copy(zz))
        for kind in range(5):
            sent(c_copy(kind, zz))
        for kind, flip in ((0, 1), (1, 3), (2, 5)):
            both_arrived(flip, zz, lambda k: rc.at[k, kind, zz])
        for kind in (3, 4):
            arrived(rows_at(7, zz).at[pl.ds((kind - 3) * half, half)], rc.at[0, kind, zz])
        arrived(tags_at(7, zz), rc.at[1, 3, zz])


def gather_all(x, tags, nz, collective_id):
    rows, width = x.shape
    dma = pltpu.SemaphoreType.DMA
    any_place, vmem = pl.BlockSpec(memory_space=pl.ANY), pl.BlockSpec(memory_space=pltpu.VMEM)
    return pl.pallas_call(
        functools.partial(gather_kernel, nz),
        name="gather_all",
        out_shape=(
            jax.ShapeDtypeStruct((8 * nz, rows, width), x.dtype),
            jax.ShapeDtypeStruct((8 * nz,) + tags.shape, tags.dtype),
        ),
        in_specs=[vmem, vmem],
        out_specs=(any_place, any_place),
        scratch_shapes=[dma((2,))]
        + [dma((2, 2, nz)), dma((2, nz)), dma((2, nz)), dma((2, nz)), dma((nz,)), dma((2, 5, nz))]
        + [dma((2, nz)), dma((2, nz)), dma((2, nz)), dma((2, nz)), dma((nz,)), dma((2, 5, nz))],
        compiler_params=pltpu.CompilerParams(
            collective_id=collective_id, has_side_effects=True, vmem_limit_bytes=8 * 2**20
        ),
    )(x, tags)


def greet_line(dp, z, nz):
    barrier = pltpu.get_barrier_semaphore()

    @pl.when(z > 0)
    def _():
        pl.semaphore_signal(barrier, 1, device_id=(dp, z - 1), device_id_type=MESH)

    @pl.when(z < nz - 1)
    def _():
        pl.semaphore_signal(barrier, 1, device_id=(dp, z + 1), device_id_type=MESH)

    pl.semaphore_wait(barrier, jnp.where(z > 0, 1, 0) + jnp.where(z < nz - 1, 1, 0))


PARTS = 2
PIECES = 2


def greet_total(dp, z, nz):
    barrier = pltpu.get_barrier_semaphore()
    for flip in (1, 2, 4):
        pl.semaphore_signal(barrier, 1, device_id=(dp ^ flip, z), device_id_type=MESH)
    for turn in range(1, nz):
        pl.semaphore_signal(barrier, 1, device_id=(dp, lax.rem(z + turn, nz)), device_id_type=MESH)
    pl.semaphore_wait(barrier, 2 + nz)


class Total:
    steps = 5

    def __init__(self, nz, dp, z, got, s_plane, r_plane, s_line, r_line):
        self.nz, self.z, self.got = nz, z, got
        self.plane = [
            remote(got.at[2 * k], got.at[2 * k + 1], s_plane.at[k], r_plane.at[k], (dp ^ flip, z))
            for k, flip in enumerate((1, 2, 4))
        ]
        self.line = [
            remote(got.at[6], got.at[6 + turn], s_line.at[turn - 1], r_line.at[turn - 1], (dp, lax.rem(z + turn, nz)))
            for turn in range(1, nz)
        ]

    def step(self, k, out_ref):
        got, nz = self.got, self.nz
        if 1 <= k <= 3:
            self.plane[k - 1].wait()
            got[2 * k] = got[2 * k - 2] + got[2 * k - 1]
        if k < 3:
            self.plane[k].start()
        elif k == 3:
            for copy in self.line:
                copy.start()
        else:
            for copy in self.line:
                copy.wait()
            total = got[6 + lax.rem(self.z, nz)]
            for zz in range(1, nz):
                total = total + got[6 + lax.rem(self.z - zz + nz, nz)]
            out_ref[...] = total


def total_scratch(nz, shape, dtype):
    dma = pltpu.SemaphoreType.DMA
    return [pltpu.VMEM((6 + nz,) + shape, dtype), dma((3,)), dma((3,)), dma((nz - 1,)), dma((nz - 1,))]


def line_gather_kernel(nz, *refs):
    dp, z = lax.axis_index("dp"), lax.axis_index("tensor")
    summed = len(refs) > 6
    if summed:
        x_ref, small_ref, out_ref, total_ref, local_sem, s_up, s_down, r_line = refs[:8]
        greet_total(dp, z, nz)
        total = Total(nz, dp, z, *refs[8:])
        total.got[0] = small_ref[...]
    else:
        x_ref, out_ref, local_sem, s_up, s_down, r_line = refs
        greet_line(dp, z, nz)
    part = x_ref.shape[0] // PARTS

    def copy(zz, k, step, own):
        at = pl.ds(k * part, part)
        dst = out_ref.at[zz, at]
        sems = s_up if step > 0 else s_down
        return remote(x_ref.at[at] if own else dst, dst, sems.at[zz, k], r_line.at[zz, k], (dp, z + step))

    keep = pltpu.make_async_copy(x_ref, out_ref.at[z], local_sem)
    for distance in range(nz):
        for k in range(PARTS):
            for sign in (0,) if distance == 0 else (-1, 1):
                zz, own = z + sign * distance, distance == 0

                @pl.when((zz >= 0) & (zz < nz))
                def _():
                    if not own:
                        copy(zz, k, 1, False).wait_recv()
                    if sign <= 0:

                        @pl.when(z < nz - 1)
                        def _():
                            copy(zz, k, 1, own).start()

                    if sign >= 0:

                        @pl.when(z > 0)
                        def _():
                            copy(zz, k, -1, own).start()

        if distance == 0:
            keep.start()
        if summed:
            total.step(distance, total_ref)
    if summed:
        for k in range(nz, Total.steps):
            total.step(k, total_ref)
    keep.wait()
    for zz in range(nz):
        for k in range(PARTS):

            @pl.when((zz <= z) & (z < nz - 1))
            def _():
                copy(zz, k, 1, False).wait_send()

            @pl.when((zz >= z) & (z > 0))
            def _():
                copy(zz, k, -1, False).wait_send()


def line_gather(x, nz, collective_id, small=None):
    dma, vmem = pltpu.SemaphoreType.DMA, pl.BlockSpec(memory_space=pltpu.VMEM)
    blocks = jax.ShapeDtypeStruct((nz,) + x.shape, x.dtype)
    scratch = [dma(())] + [dma((nz, PARTS)) for _ in range(3)]
    params = pltpu.CompilerParams(
        collective_id=collective_id, has_side_effects=True, vmem_limit_bytes=8 * 2**20
    )
    kernel = functools.partial(line_gather_kernel, nz)
    if small is None:
        return pl.pallas_call(
            kernel,
            name="line_gather",
            out_shape=blocks,
            in_specs=[vmem],
            out_specs=pl.BlockSpec(memory_space=pl.ANY),
            scratch_shapes=scratch,
            compiler_params=params,
        )(x)
    return pl.pallas_call(
        kernel,
        name="line_gather_total",
        out_shape=(blocks, jax.ShapeDtypeStruct(small.shape, small.dtype)),
        in_specs=[vmem, vmem],
        out_specs=(pl.BlockSpec(memory_space=pl.ANY), vmem),
        scratch_shapes=scratch + total_scratch(nz, small.shape, small.dtype),
        compiler_params=params,
    )(x, small)


CHUNK = 16


def add_rows(dst, *others, start=0, count):
    def body(k, carry):
        at = pl.ds(start + k * CHUNK, CHUNK)
        total = dst[at, :].astype(jnp.float32)
        for ref, base in others:
            total = total + ref[pl.ds(base + k * CHUNK, CHUNK), :].astype(jnp.float32)
        dst[at, :] = total.astype(dst.dtype)
        return carry

    lax.fori_loop(0, count // CHUNK, body, 0)


class Line:
    def __init__(self, nz, dp, z, acc, up, down, s_up, r_up, s_down, r_down):
        self.nz, self.dp, self.z, self.acc, self.up, self.down = nz, dp, z, acc, up, down
        self.sems = s_up, r_up, s_down, r_down
        self.part = acc.shape[1] // PARTS

    def copy(self, zz, k, step):
        at = pl.ds(k * self.part, self.part)
        s_up, r_up, s_down, r_down = self.sems
        if step > 0:
            return remote(self.acc.at[zz, at], self.up.at[zz, at], s_up.at[zz, k], r_up.at[zz, k], (self.dp, self.z + 1))
        return remote(self.acc.at[zz, at], self.down.at[zz, at], s_down.at[zz, k], r_down.at[zz, k], (self.dp, self.z - 1))

    def first(self):
        nz, z = self.nz, self.z

        @pl.when(z == 0)
        def _():
            for zz in range(nz - 1, 0, -1):
                for k in range(PARTS):
                    self.copy(zz, k, 1).start()

        @pl.when(z == nz - 1)
        def _():
            for zz in range(nz - 1):
                for k in range(PARTS):
                    self.copy(zz, k, -1).start()

    def step(self, distance):
        nz, z = self.nz, self.z
        for k in range(PARTS):
            for sign in (1, -1):
                far = nz - distance if sign > 0 else distance - 1
                through = (far > z) & (z > 0) if sign > 0 else (far < z) & (z < nz - 1)

                @pl.when(through)
                def _():
                    self.copy(far, k, sign).wait_recv()
                    source = self.up if sign > 0 else self.down
                    add_rows(self.acc.at[far], (source.at[far], k * self.part), start=k * self.part, count=self.part)
                    self.copy(far, k, sign).start()

    def finish(self, out_ref):
        nz, z = self.nz, self.z
        for k in range(PARTS):

            @pl.when(z > 0)
            def _():
                self.copy(z, k, 1).wait_recv()

            @pl.when(z < nz - 1)
            def _():
                self.copy(z, k, -1).wait_recv()

        def body(k, carry):
            at = pl.ds(k * CHUNK, CHUNK)
            total = self.acc[z, at, :].astype(jnp.float32)
            zero = jnp.zeros_like(total)
            total = total + jnp.where(z > 0, self.up[z, at, :].astype(jnp.float32), zero)
            total = total + jnp.where(z < nz - 1, self.down[z, at, :].astype(jnp.float32), zero)
            out_ref[at, :] = total
            return carry

        lax.fori_loop(0, out_ref.shape[0] // CHUNK, body, 0)

    def drain(self):
        nz, z = self.nz, self.z
        for zz in range(nz):
            for k in range(PARTS):

                @pl.when(zz > z)
                def _():
                    self.copy(zz, k, 1).wait_send()

                @pl.when(zz < z)
                def _():
                    self.copy(zz, k, -1).wait_send()


def line_scatter_kernel(nz, p_ref, out_ref, acc, up, down, local_sem, s_up, r_up, s_down, r_down):
    dp, z = lax.axis_index("dp"), lax.axis_index("tensor")
    loaded = pltpu.make_async_copy(p_ref, acc, local_sem)
    loaded.start()
    greet_line(dp, z, nz)
    loaded.wait()
    line = Line(nz, dp, z, acc, up, down, s_up, r_up, s_down, r_down)
    line.first()
    for distance in range(1, nz - 1):
        line.step(distance)
    line.finish(out_ref)
    line.drain()


def line_scatter(p, nz, collective_id):
    _, rows, width = p.shape
    dma, vmem = pltpu.SemaphoreType.DMA, functools.partial(pltpu.VMEM, dtype=p.dtype)
    return pl.pallas_call(
        functools.partial(line_scatter_kernel, nz),
        name="line_scatter",
        out_shape=jax.ShapeDtypeStruct((rows, width), jnp.float32),
        in_specs=[pl.BlockSpec(memory_space=pl.ANY)],
        out_specs=pl.BlockSpec(memory_space=pltpu.VMEM),
        scratch_shapes=[vmem((nz, rows, width)) for _ in range(3)]
        + [dma(())]
        + [dma((nz, PARTS)) for _ in range(4)],
        compiler_params=pltpu.CompilerParams(
            collective_id=collective_id, has_side_effects=True, vmem_limit_bytes=16 * 2**20
        ),
    )(p)


def z_order(nz):
    return [sorted(range(nz), key=lambda zz: (-abs(zz - z), zz if z >= nz // 2 else -zz)) for z in range(nz)]


def scatter_kernel(nz, p_ref, out_ref, acc, rc, ra, rb, rx, ry, ru, rd, s_local, s_core, r_core, s_a, r_a, s_b, r_b, s_x, r_x, s_y, r_y, s_u, r_u, s_d, r_d):
    dp, z = lax.axis_index("dp"), lax.axis_index("tensor")
    rows = acc.shape[2]
    half = rows // 2
    order = z_order(nz)

    def place(i):
        zz = order[0][i]
        for zv in range(1, nz):
            zz = jnp.where(z == zv, order[zv][i], zz)
        return zz

    flips = (0, 2, 4, 6)

    def load(kind, zz):
        return pltpu.make_async_copy(
            p_ref.at[(dp ^ flips[kind]) * nz + zz], acc.at[kind, zz], s_local.at[kind, zz]
        )

    def core_copy(kind, zz):
        return remote(
            p_ref.at[(dp ^ flips[kind] ^ 1) * nz + zz], rc.at[kind, zz], s_core.at[kind, zz], r_core.at[kind, zz], (dp ^ 1, z)
        )

    def a_copy(zz):
        return remote(acc.at[3, zz, pl.ds(0, half)], ra.at[zz], s_a.at[zz], r_a.at[zz], (dp ^ 2, z))

    def b_copy(zz):
        return remote(acc.at[3, zz, pl.ds(half, half)], rb.at[zz], s_b.at[zz], r_b.at[zz], (dp ^ 4, z))

    def x_copy(zz):
        return remote(acc.at[1, zz], rx.at[zz], s_x.at[zz], r_x.at[zz], (dp ^ 2, z))

    def y_copy(zz):
        return remote(acc.at[2, zz], ry.at[zz], s_y.at[zz], r_y.at[zz], (dp ^ 4, z))

    def up_copy(zz):
        return remote(acc.at[0, zz], ru.at[zz], s_u.at[zz], r_u.at[zz], (dp, z + 1))

    def down_copy(zz):
        return remote(acc.at[0, zz], rd.at[zz], s_d.at[zz], r_d.at[zz], (dp, z - 1))

    def add(dst, *others, start=0, count=rows):
        add_rows(dst, *others, start=start, count=count)

    def wave(i):
        zz = place(i)
        for kind in (3, 1, 2, 0):
            core_copy(kind, zz).start()
            load(kind, zz).start()

    def paired(kind, zz):
        load(kind, zz).wait()
        core_copy(kind, zz).wait_recv()

    def stage_diagonal(i):
        zz = place(i)
        paired(3, zz)
        add(acc.at[3, zz], (rc.at[3, zz], 0))
        a_copy(zz).start()
        b_copy(zz).start()

    def stage_side(i):
        zz = place(i)
        paired(1, zz)
        paired(2, zz)
        a_copy(zz).wait_recv()
        add(acc.at[2, zz], (rc.at[2, zz], 0), (ra.at[zz], 0), start=0, count=half)
        add(acc.at[2, zz], (rc.at[2, zz], half), start=half, count=half)
        y_copy(zz).start()
        b_copy(zz).wait_recv()
        add(acc.at[1, zz], (rc.at[1, zz], half), (rb.at[zz], 0), start=half, count=half)
        add(acc.at[1, zz], (rc.at[1, zz], 0), start=0, count=half)
        x_copy(zz).start()

    def stage_column(i):
        zz = place(i)
        paired(0, zz)
        x_copy(zz).wait_recv()
        y_copy(zz).wait_recv()
        add(acc.at[0, zz], (rc.at[0, zz], 0), (rx.at[zz], 0), (ry.at[zz], 0))

        @pl.when((zz > z) & (z == 0))
        def _():
            up_copy(zz).start()

        @pl.when((zz < z) & (z == nz - 1))
        def _():
            down_copy(zz).start()

    def stage_line(i):
        zz = place(i)

        @pl.when((zz > z) & (z > 0))
        def _():
            up_copy(zz).wait_recv()
            add(acc.at[0, zz], (ru.at[zz], 0))
            up_copy(zz).start()

        @pl.when((zz < z) & (z < nz - 1))
        def _():
            down_copy(zz).wait_recv()
            add(acc.at[0, zz], (rd.at[zz], 0))
            down_copy(zz).start()

    greet(dp, z, nz)
    wave(0)
    for i in range(nz + 3):
        if i + 1 < nz:
            wave(i + 1)
        if i < nz:
            stage_diagonal(i)
        if 0 <= i - 1 < nz:
            stage_side(i - 1)
        if 0 <= i - 2 < nz:
            stage_column(i - 2)
        if 0 <= i - 3 < nz:
            stage_line(i - 3)

    @pl.when(z > 0)
    def _():
        up_copy(z).wait_recv()

    @pl.when(z < nz - 1)
    def _():
        down_copy(z).wait_recv()

    def finish(k, carry):
        at = pl.ds(k * CHUNK, CHUNK)
        total = acc[0, z, at, :].astype(jnp.float32)
        zero = jnp.zeros_like(total)
        total = total + jnp.where(z > 0, ru[z, at, :].astype(jnp.float32), zero)
        total = total + jnp.where(z < nz - 1, rd[z, at, :].astype(jnp.float32), zero)
        out_ref[at, :] = total
        return carry

    lax.fori_loop(0, rows // CHUNK, finish, 0)
    for zz in range(nz):
        for kind in range(4):
            core_copy(kind, zz).wait_send()
        a_copy(zz).wait_send()
        b_copy(zz).wait_send()
        x_copy(zz).wait_send()
        y_copy(zz).wait_send()

        @pl.when(zz > z)
        def _():
            up_copy(zz).wait_send()

        @pl.when(zz < z)
        def _():
            down_copy(zz).wait_send()


def scatter_all(p, nz, collective_id):
    _, rows, width = p.shape
    dma, vmem = pltpu.SemaphoreType.DMA, functools.partial(pltpu.VMEM, dtype=p.dtype)
    half = rows // 2
    return pl.pallas_call(
        functools.partial(scatter_kernel, nz),
        name="scatter_all",
        out_shape=jax.ShapeDtypeStruct((rows, width), jnp.float32),
        in_specs=[pl.BlockSpec(memory_space=pl.ANY)],
        out_specs=pl.BlockSpec(memory_space=pltpu.VMEM),
        scratch_shapes=[vmem((4, nz, rows, width)), vmem((4, nz, rows, width))]
        + [vmem((nz, half, width)) for _ in range(2)]
        + [vmem((nz, rows, width)) for _ in range(4)]
        + [dma((4, nz)), dma((4, nz)), dma((4, nz))]
        + [dma((nz,)) for _ in range(12)],
        compiler_params=pltpu.CompilerParams(
            collective_id=collective_id, has_side_effects=True, vmem_limit_bytes=VMEM_LIMIT
        ),
    )(p)


def finish_kernel(nz, nc, g_ref, p_ref, unit_ref, small_ref, sum_q, sum_k, sum_v, out_ref, total_ref, buf, acc, rc, ra, rb, rx, ry, line_acc, up, down, *sems):
    (s_load, s_core, r_core, s_a, r_a, s_b, r_b, s_x, r_x, s_y, r_y) = sems[:11]
    (t_x, q_x, t_y, q_y, t_a, q_a, t_b, q_b, t_c, q_c) = sems[11:21]
    s_line, s_store, s_up, r_up, s_down, r_down = sems[21:27]
    total = Total(nz, lax.axis_index("dp"), lax.axis_index("tensor"), *sems[27:])
    dp, z = lax.axis_index("dp"), lax.axis_index("tensor")
    rows = acc.shape[2]
    half = rows // 2
    flips = (0, 2, 4, 6)

    def load(kind, c):
        return pltpu.make_async_copy(g_ref.at[(dp ^ flips[kind]) * nc + c], acc.at[kind, c], s_load.at[kind, c])

    def core_copy(kind, c):
        return remote(
            g_ref.at[(dp ^ flips[kind] ^ 1) * nc + c], rc.at[kind, c], s_core.at[kind, c], r_core.at[kind, c], (dp ^ 1, z)
        )

    def a_copy(c):
        return remote(acc.at[3, c, pl.ds(0, half)], ra.at[c], s_a.at[c], r_a.at[c], (dp ^ 2, z))

    def b_copy(c):
        return remote(acc.at[3, c, pl.ds(half, half)], rb.at[c], s_b.at[c], r_b.at[c], (dp ^ 4, z))

    def x_copy(c):
        return remote(acc.at[1, c], rx.at[c], s_x.at[c], r_x.at[c], (dp ^ 2, z))

    def y_copy(c):
        return remote(acc.at[2, c], ry.at[c], s_y.at[c], r_y.at[c], (dp ^ 4, z))

    def full(flip, c):
        return buf.at[(dp ^ flip) * nc + c]

    def back_x(c):
        return remote(full(0, c), full(0, c), t_x.at[c], q_x.at[c], (dp ^ 2, z))

    def back_y(c):
        return remote(full(0, c), full(0, c), t_y.at[c], q_y.at[c], (dp ^ 4, z))

    def back_a(c):
        ref = full(4, c).at[pl.ds(0, half)]
        return remote(ref, ref, t_a.at[c], q_a.at[c], (dp ^ 2, z))

    def back_b(c):
        ref = full(2, c).at[pl.ds(half, half)]
        return remote(ref, ref, t_b.at[c], q_b.at[c], (dp ^ 4, z))

    def back_core(kind, c):
        ref = full((0, 2, 4, 6, 6)[kind], c)
        if kind >= 3:
            ref = ref.at[pl.ds((kind - 3) * half, half)]
        return remote(ref, ref, t_c.at[kind, c], q_c.at[kind, c], (dp ^ 1, z))

    def arrived(ref, sem):
        remote(ref, ref, sem, sem, (dp ^ 1, z)).wait_recv()

    def paired(kind, c):
        load(kind, c).wait()
        core_copy(kind, c).wait_recv()

    def stage_diagonal(c):
        paired(3, c)
        add_rows(acc.at[3, c], (rc.at[3, c], 0), count=rows)
        a_copy(c).start()
        b_copy(c).start()

    def stage_side(c):
        paired(1, c)
        paired(2, c)
        a_copy(c).wait_recv()
        add_rows(acc.at[2, c], (rc.at[2, c], 0), (ra.at[c], 0), start=0, count=half)
        add_rows(acc.at[2, c], (rc.at[2, c], half), start=half, count=half)
        y_copy(c).start()
        b_copy(c).wait_recv()
        add_rows(acc.at[1, c], (rc.at[1, c], half), (rb.at[c], 0), start=half, count=half)
        add_rows(acc.at[1, c], (rc.at[1, c], 0), start=0, count=half)
        x_copy(c).start()

    def stage_own(c):
        paired(0, c)
        x_copy(c).wait_recv()
        y_copy(c).wait_recv()
        dst = full(0, c)

        def body(k, carry):
            at = pl.ds(k * CHUNK, CHUNK)
            total = acc[0, c, at, :].astype(jnp.float32) + rc[0, c, at, :].astype(jnp.float32)
            total = total + rx[c, at, :].astype(jnp.float32) + ry[c, at, :].astype(jnp.float32)
            dst[at, :] = total.astype(dst.dtype)
            return carry

        lax.fori_loop(0, rows // CHUNK, body, 0)
        back_x(c).start()
        back_y(c).start()
        back_core(0, c).start()

    def stage_relay(c):
        arrived(full(4, c), q_y.at[c])
        back_a(c).start()
        back_core(2, c).start()
        arrived(full(2, c), q_x.at[c])
        back_b(c).start()
        back_core(1, c).start()

    def stage_corner(c):
        arrived(full(6, c).at[pl.ds(0, half)], q_a.at[c])
        back_core(3, c).start()
        arrived(full(6, c).at[pl.ds(half, half)], q_b.at[c])
        back_core(4, c).start()

    line_load = pltpu.make_async_copy(p_ref, line_acc, s_line)
    line_load.start()
    for c in range(nc):
        for kind in (3, 1, 2, 0):
            load(kind, c).start()
    greet_total(dp, z, nz)
    for c in range(nc):
        for kind in (3, 1, 2, 0):
            core_copy(kind, c).start()
    line = Line(nz, dp, z, line_acc, up, down, s_up, r_up, s_down, r_down)
    line_load.wait()
    line.first()
    def line_end():
        line.finish(out_ref)
        line.drain()
        share = jnp.sum(out_ref[...] * unit_ref[...], axis=0, keepdims=True)
        total.got[0] = small_ref[...]
        wide = small_ref.shape[1]
        for k in range(out_ref.shape[1] // wide):
            total.got[0, k : k + 1, :] = share[:, k * wide : (k + 1) * wide]

    side = [functools.partial(line.step, distance) for distance in range(1, nz - 1)] + [line_end]
    side += [functools.partial(total.step, k, total_ref) for k in range(Total.steps)]
    stages = (stage_diagonal, stage_side, stage_own, stage_relay, stage_corner)
    for i in range(nc + len(stages) - 1):
        for lag, stage in enumerate(stages):
            if 0 <= i - lag < nc:
                stage(i - lag)
                if i >= 1 and side:
                    side.pop(0)()
    for one in side:
        one()
    for c in range(nc):
        for kind, flip in ((0, 1), (1, 3), (2, 5)):
            arrived(full(flip, c), q_c.at[kind, c])
        for kind in (3, 4):
            arrived(full(7, c).at[pl.ds((kind - 3) * half, half)], q_c.at[kind, c])
    wide = buf.shape[2] // 3
    stores = [
        pltpu.make_async_copy(buf.at[:, :, pl.ds(k * wide, wide)], ref, s_store.at[k])
        for k, ref in enumerate((sum_q, sum_k, sum_v))
    ]
    for store in stores:
        store.start()
    for c in range(nc):
        for kind in range(4):
            core_copy(kind, c).wait_send()
        for copy in (a_copy, b_copy, x_copy, y_copy, back_x, back_y, back_a, back_b):
            copy(c).wait_send()
        for kind in range(5):
            back_core(kind, c).wait_send()
    for store in stores:
        store.wait()


def finish_sums(g, p, unit, small, nz, nc, collective_id):
    _, rows, width = g.shape
    _, line_rows, line_width = p.shape
    half = rows // 2
    dma, vmem = pltpu.SemaphoreType.DMA, functools.partial(pltpu.VMEM, dtype=g.dtype)
    return pl.pallas_call(
        functools.partial(finish_kernel, nz, nc),
        name="finish_sums",
        out_shape=(
            *[jax.ShapeDtypeStruct(g.shape[:2] + (width // 3,), g.dtype)] * 3,
            jax.ShapeDtypeStruct((line_rows, line_width), jnp.float32),
            jax.ShapeDtypeStruct(small.shape, small.dtype),
        ),
        in_specs=[pl.BlockSpec(memory_space=pl.ANY)] * 2 + [pl.BlockSpec(memory_space=pltpu.VMEM)] * 2,
        out_specs=(
            *[pl.BlockSpec(memory_space=pl.ANY)] * 3,
            *[pl.BlockSpec(memory_space=pltpu.VMEM)] * 2,
        ),
        scratch_shapes=[vmem(g.shape), vmem((4, nc, rows, width)), vmem((4, nc, rows, width))]
        + [vmem((nc, half, width)) for _ in range(2)]
        + [vmem((nc, rows, width)) for _ in range(2)]
        + [vmem((nz, line_rows, line_width)) for _ in range(3)]
        + [dma((4, nc)) for _ in range(3)]
        + [dma((nc,)) for _ in range(16)]
        + [dma((5, nc)), dma((5, nc))]
        + [dma(()), dma((3,))]
        + [dma((nz, PARTS)) for _ in range(4)]
        + total_scratch(nz, small.shape, small.dtype),
        compiler_params=pltpu.CompilerParams(
            collective_id=collective_id, has_side_effects=True, vmem_limit_bytes=VMEM_LIMIT
        ),
    )(g, p, unit, small)


def experts_routed(
    hidden_after_attention,
    expert_ids,
    expert_norm_gain,
    w_router,
    w_gate,
    w_up,
    w_down,
    grad_output,
):
    tok_count, d_model = hidden_after_attention.shape
    n_tensor = lax.axis_size("tensor")
    n_dp = lax.axis_size("dp")
    devices = n_dp * n_tensor
    second_norm_scale = root_mean_square_scale(hidden_after_attention)
    second_unit_rows = hidden_after_attention * second_norm_scale
    second_normalized = (second_unit_rows * expert_norm_gain).astype(jnp.bfloat16)
    experts = w_router.shape[1]
    topk = expert_ids.shape[1]
    exp_dev = w_gate.shape[0]
    most = 2 * ((tok_count * topk * 9 + experts * 16 - 1) // (experts * 16))
    route_probs = jax.nn.softmax(
        jnp.dot(second_normalized, w_router, preferred_element_type=jnp.float32), axis=-1
    )
    chosen = expert_ids[:, :, None] == jnp.arange(experts, dtype=jnp.int32)[None, None, :]
    gate_values = jnp.sum(jnp.where(chosen, route_probs[:, None, :], 0.0), axis=-1)
    flat_ids, pair_rank = slot_positions(expert_ids, experts)
    pair_slot = (flat_ids % exp_dev * n_dp + flat_ids // exp_dev) * most + pair_rank
    pair_count = tok_count * topk
    slot_count = exp_dev * n_dp * most
    slot_owner = (
        jnp.full((slot_count,), pair_count, jnp.int32)
        .at[pair_slot]
        .set(jnp.arange(pair_count, dtype=jnp.int32))
    )
    padded = jnp.concatenate([second_normalized, jnp.zeros((1, d_model), jnp.bfloat16)], axis=0)
    outgoing = padded[slot_owner // topk].reshape(exp_dev, n_dp, most, d_model)
    copies = jnp.broadcast_to(
        outgoing[:, :, None], (exp_dev, n_dp, n_tensor, most, d_model)
    ).reshape(exp_dev, devices, most, d_model)
    arrived = lax.all_to_all(copies, ("dp", "tensor"), split_axis=1, concat_axis=1, tiled=True)
    expert_rows = arrived.reshape(exp_dev, devices * most, d_model)
    gate_pre = jnp.einsum("erd,edf->erf", expert_rows, w_gate, preferred_element_type=jnp.float32)
    up_pre = jnp.einsum("erd,edf->erf", expert_rows, w_up, preferred_element_type=jnp.float32)
    gate_sigmoid = jax.nn.sigmoid(gate_pre)
    silu_gate = gate_pre * gate_sigmoid
    hidden = (silu_gate * up_pre).astype(jnp.bfloat16)
    partial_value = (
        jnp.einsum("erf,efd->erd", hidden, w_down, preferred_element_type=jnp.float32)
        .astype(jnp.bfloat16)
        .reshape(exp_dev, devices, most, d_model)
    )
    returned = lax.all_to_all(
        partial_value, ("dp", "tensor"), split_axis=1, concat_axis=1, tiled=True
    )
    expert_out = jnp.sum(
        returned.reshape(exp_dev, n_dp, n_tensor, most, d_model).astype(jnp.float32), axis=2
    ).reshape(slot_count, d_model)
    pair_out = expert_out[pair_slot].reshape(tok_count, topk, d_model)
    result = (hidden_after_attention + jnp.sum(gate_values[:, :, None] * pair_out, axis=1)).astype(
        jnp.bfloat16
    )
    cotangent = grad_output.astype(jnp.float32)
    grad_gates = jnp.sum(pair_out * cotangent[:, None, :], axis=-1)
    grad_pairs = (
        (gate_values[:, :, None] * cotangent[:, None, :])
        .astype(jnp.bfloat16)
        .reshape(pair_count, d_model)
    )
    grad_slots = jnp.concatenate([grad_pairs, jnp.zeros((1, d_model), jnp.bfloat16)], axis=0)[
        slot_owner
    ].reshape(exp_dev, n_dp, most, d_model)
    grad_copies = jnp.broadcast_to(
        grad_slots[:, :, None], (exp_dev, n_dp, n_tensor, most, d_model)
    ).reshape(exp_dev, devices, most, d_model)
    grad_arrived = lax.all_to_all(
        grad_copies, ("dp", "tensor"), split_axis=1, concat_axis=1, tiled=True
    )
    grad_rows = grad_arrived.reshape(exp_dev, devices * most, d_model)
    grad_hidden = jnp.einsum("erd,efd->erf", grad_rows, w_down, preferred_element_type=jnp.float32)
    grad_down = jnp.einsum("erf,erd->efd", hidden, grad_rows, preferred_element_type=jnp.float32)
    grad_gate_pre = (
        grad_hidden * up_pre * gate_sigmoid * (1.0 + gate_pre * (1.0 - gate_sigmoid))
    ).astype(jnp.bfloat16)
    grad_up_pre = (grad_hidden * silu_gate).astype(jnp.bfloat16)
    grad_gate = jnp.einsum(
        "erd,erf->edf", expert_rows, grad_gate_pre, preferred_element_type=jnp.float32
    )
    grad_up = jnp.einsum(
        "erd,erf->edf", expert_rows, grad_up_pre, preferred_element_type=jnp.float32
    )
    grad_expert_in = jnp.einsum(
        "erf,edf->erd", grad_gate_pre, w_gate, preferred_element_type=jnp.float32
    )
    grad_expert_in = grad_expert_in + jnp.einsum(
        "erf,edf->erd", grad_up_pre, w_up, preferred_element_type=jnp.float32
    )
    grad_expert_in = grad_expert_in.astype(jnp.bfloat16).reshape(exp_dev, devices, most, d_model)
    grad_back = lax.all_to_all(
        grad_expert_in, ("dp", "tensor"), split_axis=1, concat_axis=1, tiled=True
    )
    grad_slot_in = jnp.sum(
        grad_back.reshape(exp_dev, n_dp, n_tensor, most, d_model).astype(jnp.float32), axis=2
    ).reshape(slot_count, d_model)
    grad_second_normalized = jnp.sum(
        grad_slot_in[pair_slot].reshape(tok_count, topk, d_model), axis=1
    )
    grad_route = jnp.sum(jnp.where(chosen, grad_gates[:, :, None], 0.0), axis=1)
    grad_logits = (
        route_probs * (grad_route - jnp.sum(route_probs * grad_route, axis=-1, keepdims=True))
    ).astype(jnp.bfloat16)
    grad_router_part = jnp.einsum(
        "td,te->de", second_normalized, grad_logits, preferred_element_type=jnp.float32
    )
    grad_second_normalized = grad_second_normalized + jnp.einsum(
        "te,de->td", grad_logits, w_router, preferred_element_type=jnp.float32
    )
    grad_expert_share = jnp.sum(grad_second_normalized * second_unit_rows, axis=0)
    grad_second_unit_rows = grad_second_normalized * expert_norm_gain
    grad_hidden_one = (
        second_norm_scale
        * (
            grad_second_unit_rows
            - second_unit_rows
            * jnp.mean(grad_second_unit_rows * second_unit_rows, axis=-1, keepdims=True)
        )
        + cotangent
    )
    return (
        result,
        grad_hidden_one,
        grad_expert_share,
        grad_router_part,
        grad_gate,
        grad_up,
        grad_down,
    )


def experts_dense(
    hidden_after_attention,
    expert_ids,
    expert_norm_gain,
    w_router,
    w_gate,
    w_up,
    w_down,
    grad_output,
    all_cotangents,
):
    tok_count, d_model = hidden_after_attention.shape
    n_tensor = lax.axis_size("tensor")
    n_dp = lax.axis_size("dp")
    devices = n_dp * n_tensor
    everyone = ("dp", "tensor")
    second_norm_scale = root_mean_square_scale(hidden_after_attention)
    second_unit_rows = hidden_after_attention * second_norm_scale
    second_normalized = (second_unit_rows * expert_norm_gain).astype(jnp.bfloat16)
    experts = w_router.shape[1]
    exp_dev, _, width = w_gate.shape
    all_count = devices * tok_count
    expert_at = jnp.arange(experts, dtype=jnp.int32)
    local_at = lax.axis_index("dp") * exp_dev + jnp.arange(exp_dev, dtype=jnp.int32)

    chosen = jnp.any(expert_ids[:, :, None] == expert_at[None, None, :], axis=1)
    route_probs = jax.nn.softmax(
        jnp.dot(second_normalized, w_router, preferred_element_type=jnp.float32), axis=-1
    )
    gates = jnp.where(chosen, route_probs, 0.0).T
    all_rows, all_gates = gather_all(second_normalized, gates, n_tensor, 0)
    all_rows = all_rows.reshape(all_count, d_model)

    down_rows = w_down.reshape(exp_dev * width, d_model)
    wide = jnp.concatenate([w_gate[e] for e in range(exp_dev)] + [w_up[e] for e in range(exp_dev)], axis=1)
    local_gate = lax.dynamic_slice_in_dim(all_gates, lax.axis_index("dp") * exp_dev, exp_dev, axis=1)
    local_gate = local_gate.transpose(0, 2, 1).reshape(all_count, exp_dev)
    spread = jnp.repeat(local_gate, width, axis=1)
    both = exp_dev * width
    pre = jnp.dot(all_rows, wide, preferred_element_type=jnp.float32)
    gate_pre, up_pre = pre[:, :both], pre[:, both:]
    gate_sigmoid = jax.nn.sigmoid(gate_pre)
    silu_gate = gate_pre * gate_sigmoid
    hidden = silu_gate * up_pre
    gated_hidden = (spread * hidden).astype(jnp.bfloat16)
    out_part = jnp.dot(gated_hidden, down_rows, preferred_element_type=jnp.float32).astype(jnp.bfloat16)
    back = jnp.einsum("td,fd->tf", all_cotangents, down_rows, preferred_element_type=jnp.float32)
    gate_grads = jnp.sum((hidden * back).reshape(all_count, exp_dev, width), axis=-1)
    grad_hidden = spread * back
    grad_gate_pre = (
        grad_hidden * up_pre * gate_sigmoid * (1.0 + gate_pre * (1.0 - gate_sigmoid))
    ).astype(jnp.bfloat16)
    grad_up_pre = (grad_hidden * silu_gate).astype(jnp.bfloat16)
    grad_pre = jnp.concatenate([grad_gate_pre, grad_up_pre], axis=1)
    in_part = jnp.einsum("tf,df->td", grad_pre, wide, preferred_element_type=jnp.float32).astype(jnp.bfloat16)
    grad_in = scatter_all(in_part.reshape(devices, tok_count, d_model), n_tensor, 1)
    moe_out = scatter_all(out_part.reshape(devices, tok_count, d_model), n_tensor, 1)
    grad_down = jnp.einsum(
        "tf,td->fd", gated_hidden, all_cotangents, preferred_element_type=jnp.float32
    ).reshape(exp_dev, width, d_model)
    grad_wide = jnp.einsum("td,tf->df", all_rows, grad_pre, preferred_element_type=jnp.float32)
    grad_gate = jnp.stack([grad_wide[:, e * width : (e + 1) * width] for e in range(exp_dev)])
    grad_up = jnp.stack([grad_wide[:, both + e * width : both + (e + 1) * width] for e in range(exp_dev)])

    route_grads = jnp.sum(
        jnp.where(
            local_at[None, :, None] == expert_at[None, None, :],
            gate_grads[:, :, None],
            0.0,
        ),
        axis=1,
    )
    grad_route = jnp.where(
        chosen, lax.psum_scatter(route_grads, everyone, scatter_dimension=0, tiled=True), 0.0
    )
    cotangent = grad_output.astype(jnp.float32)
    result = (hidden_after_attention + moe_out).astype(jnp.bfloat16)
    grad_logits = (
        route_probs * (grad_route - jnp.sum(route_probs * grad_route, axis=-1, keepdims=True))
    ).astype(jnp.bfloat16)
    grad_router_part = jnp.einsum(
        "td,te->de", second_normalized, grad_logits, preferred_element_type=jnp.float32
    )
    grad_second_normalized = grad_in + jnp.einsum(
        "te,de->td", grad_logits, w_router, preferred_element_type=jnp.float32
    )
    grad_expert_share = jnp.sum(grad_second_normalized * second_unit_rows, axis=0)
    grad_second_unit_rows = grad_second_normalized * expert_norm_gain
    grad_hidden_one = (
        second_norm_scale
        * (
            grad_second_unit_rows
            - second_unit_rows
            * jnp.mean(grad_second_unit_rows * second_unit_rows, axis=-1, keepdims=True)
        )
        + cotangent
    )
    return (
        result,
        grad_hidden_one,
        grad_expert_share,
        grad_router_part,
        grad_gate,
        grad_up,
        grad_down,
    )


def local_gathered(
    tokens,
    file_ids,
    expert_ids,
    attention_norm_gain,
    w_query,
    w_key,
    w_value,
    query_gain,
    key_gain,
    w_output,
    expert_norm_gain,
    w_router,
    w_gate,
    w_up,
    w_down,
    grad_output,
):
    tok_count, d_model = tokens.shape
    n_tensor = lax.axis_size("tensor")
    n_dp = lax.axis_size("dp")
    devices = n_dp * n_tensor
    local_dim = w_query.shape[1]
    head_dim = HEAD_DIM
    local_heads = local_dim // head_dim
    seq_len = tok_count * n_tensor
    block_rows = min(512, seq_len)
    score_scale = 1.0 / math.sqrt(head_dim)
    file_row = file_ids[0]
    cosine, sine_table = rope_tables(seq_len, head_dim)
    input_tensors = tokens.astype(jnp.float32)
    first_norm_scale = root_mean_square_scale(input_tensors)
    first_unit_rows = input_tensors * first_norm_scale
    first_normalized = (first_unit_rows * attention_norm_gain).astype(jnp.bfloat16)
    normed_all = line_gather(first_normalized, n_tensor, 2).reshape(seq_len, d_model)
    normed_all, later_cotangent = lax.optimization_barrier((normed_all, grad_output))
    all_cotangents = lax.all_gather(later_cotangent, ("dp", "tensor"), axis=0, tiled=True)
    query_raw = jnp.dot(normed_all, w_query, preferred_element_type=jnp.float32)
    key_raw = jnp.dot(normed_all, w_key, preferred_element_type=jnp.float32)
    value_rows = (
        jnp.dot(normed_all, w_value, preferred_element_type=jnp.float32)
        .astype(jnp.bfloat16)
        .reshape(seq_len, local_heads, head_dim)
    )
    query_total, key_total = lax.psum(
        (jnp.sum(query_raw * query_raw, axis=1), jnp.sum(key_raw * key_raw, axis=1)), "tensor"
    )
    query_scale = lax.rsqrt(query_total / d_model + EPSILON)[:, None]
    key_scale = lax.rsqrt(key_total / d_model + EPSILON)[:, None]
    query_hat = query_raw * query_scale
    key_hat = key_raw * key_scale
    queries = rotate(
        (query_hat * query_gain).reshape(seq_len, local_heads, head_dim), cosine, sine_table
    ).astype(jnp.bfloat16)
    key_rows = rotate(
        (key_hat * key_gain).reshape(seq_len, local_heads, head_dim), cosine, sine_table
    ).astype(jnp.bfloat16)
    block_start = 0
    scores = block_scores(queries, key_rows, file_row, block_start, score_scale)
    row_peak = jnp.max(scores, axis=-1, keepdims=True)
    log_total = row_peak + jnp.log(jnp.sum(jnp.exp(scores - row_peak), axis=-1, keepdims=True))
    attn_probs = jnp.exp(scores - log_total).astype(jnp.bfloat16)
    context_blocks = jnp.einsum(
        "hqk,khd->qhd", attn_probs, value_rows, preferred_element_type=jnp.float32
    )
    log_totals = [log_total]
    context = context_blocks.reshape(seq_len, local_dim).astype(jnp.bfloat16)
    attn_out = line_scatter(
        jnp.dot(context, w_output, preferred_element_type=jnp.float32)
        .astype(jnp.bfloat16)
        .reshape(n_tensor, tok_count, d_model),
        n_tensor,
        3,
    )
    hidden_after_attention = input_tensors + attn_out
    result, grad_hidden_one, grad_expert_share, grad_router_part, grad_gate, grad_up, grad_down = (
        experts_dense(
            hidden_after_attention,
            expert_ids,
            expert_norm_gain,
            w_router,
            w_gate,
            w_up,
            w_down,
            grad_output,
            all_cotangents,
        )
    )
    grad_attn = grad_hidden_one.astype(jnp.bfloat16)
    side_parts = jnp.concatenate([grad_router_part.T, grad_expert_share[None, :]])
    grad_attn_all, side_total = line_gather(grad_attn, n_tensor, 5, side_parts)
    grad_attn_all = grad_attn_all.reshape(seq_len, d_model)
    total_router, total_ffn_gain = side_total[:-1].T, side_total[-1]
    grad_output_part = jnp.einsum(
        "sd,se->de", context, grad_attn_all, preferred_element_type=jnp.float32
    )
    grad_context = (
        jnp.einsum("se,de->sd", grad_attn_all, w_output, preferred_element_type=jnp.float32)
        .astype(jnp.bfloat16)
        .reshape(seq_len, local_heads, head_dim)
    )
    grad_query_blocks = []
    grad_key_total = jnp.zeros((seq_len, local_heads, head_dim), jnp.float32)
    grad_value_total = jnp.zeros((seq_len, local_heads, head_dim), jnp.float32)
    for block_index, block_start in enumerate(range(0, seq_len, block_rows)):
        scores = block_scores(queries, key_rows, file_row, block_start, score_scale)
        probs_full = jnp.exp(scores - log_totals[block_index])
        probs_low = probs_full.astype(jnp.bfloat16)
        grad_value_total = jnp.einsum(
            "hqk,qhd->khd", probs_low, grad_context, preferred_element_type=jnp.float32
        )
        grad_probs = jnp.einsum(
            "qhd,khd->hqk", grad_context, value_rows, preferred_element_type=jnp.float32
        )
        row_shift = jnp.sum(probs_full * grad_probs, axis=-1, keepdims=True)
        grad_scores = (probs_full * (grad_probs - row_shift)).astype(jnp.bfloat16)
        grad_query_blocks.append(
            jnp.einsum("hqk,khd->qhd", grad_scores, key_rows, preferred_element_type=jnp.float32)
            * score_scale
        )
        grad_key_total = (
            jnp.einsum("hqk,qhd->khd", grad_scores, queries, preferred_element_type=jnp.float32)
            * score_scale
        )
    grad_query_normed = unrotate(grad_query_blocks[0], cosine, sine_table).reshape(
        seq_len, local_dim
    )
    grad_key_normed = unrotate(grad_key_total, cosine, sine_table).reshape(seq_len, local_dim)
    grad_qgain_part = jnp.sum(grad_query_normed * query_hat, axis=0)
    grad_kgain_part = jnp.sum(grad_key_normed * key_hat, axis=0)
    grad_query_hat = grad_query_normed * query_gain
    grad_key_hat = grad_key_normed * key_gain
    query_inner, key_inner = lax.psum(
        (jnp.sum(grad_query_hat * query_hat, axis=1), jnp.sum(grad_key_hat * key_hat, axis=1)),
        "tensor",
    )
    grad_query_raw = (
        query_scale * (grad_query_hat - query_hat * (query_inner / d_model)[:, None])
    ).astype(jnp.bfloat16)
    grad_key_raw = (key_scale * (grad_key_hat - key_hat * (key_inner / d_model)[:, None])).astype(
        jnp.bfloat16
    )
    grad_value_raw = grad_value_total.reshape(seq_len, local_dim).astype(jnp.bfloat16)
    grad_raw = jnp.concatenate([grad_query_raw, grad_key_raw, grad_value_raw], axis=1)
    w_raw = jnp.concatenate([w_query, w_key, w_value], axis=1)
    raw_part = jnp.einsum("sd,sf->df", normed_all, grad_raw, preferred_element_type=jnp.float32)
    row_part = jnp.einsum("sf,df->sd", grad_raw, w_raw, preferred_element_type=jnp.float32)
    mine = (jnp.arange(n_tensor) == lax.axis_index("tensor"))[:, None]
    gain_parts = jnp.stack(
        [
            jnp.zeros((d_model,), jnp.float32),
            jnp.where(mine, grad_qgain_part[None, :], 0.0).reshape(-1),
            jnp.where(mine, grad_kgain_part[None, :], 0.0).reshape(-1),
            jnp.zeros((d_model,), jnp.float32),
        ]
    )
    total_query, total_key, total_value, grad_first_normalized, gain_totals = finish_sums(
        raw_part.astype(jnp.bfloat16).reshape(n_dp * PIECES, -1, 3 * local_dim),
        row_part.astype(jnp.bfloat16).reshape(n_tensor, tok_count, d_model),
        first_unit_rows,
        gain_parts.reshape(8, -1),
        n_tensor,
        PIECES,
        4,
    )
    total_query, total_key, total_value = (
        total.reshape(d_model, local_dim).astype(jnp.float32)
        for total in (total_query, total_key, total_value)
    )
    grad_first_unit_rows = grad_first_normalized * attention_norm_gain
    grad_tokens = (
        first_norm_scale
        * (
            grad_first_unit_rows
            - first_unit_rows
            * jnp.mean(grad_first_unit_rows * first_unit_rows, axis=-1, keepdims=True)
        )
        + grad_hidden_one
    ).astype(jnp.bfloat16)
    total_output = lax.psum(grad_output_part.astype(jnp.bfloat16), "dp").astype(jnp.float32)
    gain_totals = gain_totals.reshape(4, d_model)
    total_attn_gain = gain_totals[0]
    own_gains = lax.dynamic_slice_in_dim(
        gain_totals, lax.axis_index("tensor") * local_dim, local_dim, axis=1
    )
    total_qgain, total_kgain = own_gains[1], own_gains[2]
    return (
        result,
        grad_tokens,
        total_query,
        total_key,
        total_value,
        total_output,
        total_qgain,
        total_kgain,
        total_attn_gain,
        total_ffn_gain,
        total_router,
        grad_gate,
        grad_up,
        grad_down,
    )


def local_routed(
    tokens,
    file_ids,
    expert_ids,
    attention_norm_gain,
    w_query,
    w_key,
    w_value,
    query_gain,
    key_gain,
    w_output,
    expert_norm_gain,
    w_router,
    w_gate,
    w_up,
    w_down,
    grad_output,
):
    tok_count, d_model = tokens.shape
    n_tensor = lax.axis_size("tensor")
    n_dp = lax.axis_size("dp")
    devices = n_dp * n_tensor
    local_dim = w_query.shape[1]
    head_dim = HEAD_DIM
    local_heads = local_dim // head_dim
    seq_len = tok_count * n_tensor
    block_rows = min(512, seq_len)
    score_scale = 1.0 / math.sqrt(head_dim)
    file_row = file_ids[0]
    cosine, sine_table = rope_tables(seq_len, head_dim)
    input_tensors = tokens.astype(jnp.float32)
    first_norm_scale = root_mean_square_scale(input_tensors)
    first_unit_rows = input_tensors * first_norm_scale
    first_normalized = (first_unit_rows * attention_norm_gain).astype(jnp.bfloat16)
    normed_all = lax.all_gather(first_normalized, "tensor", axis=0, tiled=True)
    query_raw = jnp.dot(normed_all, w_query, preferred_element_type=jnp.float32)
    key_raw = jnp.dot(normed_all, w_key, preferred_element_type=jnp.float32)
    value_rows = (
        jnp.dot(normed_all, w_value, preferred_element_type=jnp.float32)
        .astype(jnp.bfloat16)
        .reshape(seq_len, local_heads, head_dim)
    )
    query_total, key_total = lax.psum(
        (jnp.sum(query_raw * query_raw, axis=1), jnp.sum(key_raw * key_raw, axis=1)), "tensor"
    )
    query_scale = lax.rsqrt(query_total / d_model + EPSILON)[:, None]
    key_scale = lax.rsqrt(key_total / d_model + EPSILON)[:, None]
    query_hat = query_raw * query_scale
    key_hat = key_raw * key_scale
    queries = rotate(
        (query_hat * query_gain).reshape(seq_len, local_heads, head_dim), cosine, sine_table
    ).astype(jnp.bfloat16)
    key_rows = rotate(
        (key_hat * key_gain).reshape(seq_len, local_heads, head_dim), cosine, sine_table
    ).astype(jnp.bfloat16)
    block_start = 0
    scores = block_scores(queries, key_rows, file_row, block_start, score_scale)
    row_peak = jnp.max(scores, axis=-1, keepdims=True)
    log_total = row_peak + jnp.log(jnp.sum(jnp.exp(scores - row_peak), axis=-1, keepdims=True))
    attn_probs = jnp.exp(scores - log_total).astype(jnp.bfloat16)
    context_blocks = jnp.einsum(
        "hqk,khd->qhd", attn_probs, value_rows, preferred_element_type=jnp.float32
    )
    log_totals = [log_total]
    context = context_blocks.reshape(seq_len, local_dim).astype(jnp.bfloat16)
    attn_out = lax.psum_scatter(
        jnp.dot(context, w_output, preferred_element_type=jnp.float32).astype(jnp.bfloat16),
        "tensor",
        scatter_dimension=0,
        tiled=True,
    ).astype(jnp.float32)
    hidden_after_attention = input_tensors + attn_out
    result, grad_hidden_one, grad_expert_share, grad_router_part, grad_gate, grad_up, grad_down = (
        experts_routed(
            hidden_after_attention,
            expert_ids,
            expert_norm_gain,
            w_router,
            w_gate,
            w_up,
            w_down,
            grad_output,
        )
    )
    grad_attn = grad_hidden_one.astype(jnp.bfloat16)
    grad_attn_all = lax.all_gather(grad_attn, "tensor", axis=0, tiled=True)
    grad_output_part = jnp.einsum(
        "sd,se->de", context, grad_attn_all, preferred_element_type=jnp.float32
    )
    grad_context = (
        jnp.einsum("se,de->sd", grad_attn_all, w_output, preferred_element_type=jnp.float32)
        .astype(jnp.bfloat16)
        .reshape(seq_len, local_heads, head_dim)
    )
    grad_query_blocks = []
    grad_key_total = jnp.zeros((seq_len, local_heads, head_dim), jnp.float32)
    grad_value_total = jnp.zeros((seq_len, local_heads, head_dim), jnp.float32)
    for block_index, block_start in enumerate(range(0, seq_len, block_rows)):
        scores = block_scores(queries, key_rows, file_row, block_start, score_scale)
        probs_full = jnp.exp(scores - log_totals[block_index])
        probs_low = probs_full.astype(jnp.bfloat16)
        grad_value_total = jnp.einsum(
            "hqk,qhd->khd", probs_low, grad_context, preferred_element_type=jnp.float32
        )
        grad_probs = jnp.einsum(
            "qhd,khd->hqk", grad_context, value_rows, preferred_element_type=jnp.float32
        )
        row_shift = jnp.sum(probs_full * grad_probs, axis=-1, keepdims=True)
        grad_scores = (probs_full * (grad_probs - row_shift)).astype(jnp.bfloat16)
        grad_query_blocks.append(
            jnp.einsum("hqk,khd->qhd", grad_scores, key_rows, preferred_element_type=jnp.float32)
            * score_scale
        )
        grad_key_total = (
            jnp.einsum("hqk,qhd->khd", grad_scores, queries, preferred_element_type=jnp.float32)
            * score_scale
        )
    grad_query_normed = unrotate(grad_query_blocks[0], cosine, sine_table).reshape(
        seq_len, local_dim
    )
    grad_key_normed = unrotate(grad_key_total, cosine, sine_table).reshape(seq_len, local_dim)
    grad_qgain_part = jnp.sum(grad_query_normed * query_hat, axis=0)
    grad_kgain_part = jnp.sum(grad_key_normed * key_hat, axis=0)
    grad_query_hat = grad_query_normed * query_gain
    grad_key_hat = grad_key_normed * key_gain
    query_inner, key_inner = lax.psum(
        (jnp.sum(grad_query_hat * query_hat, axis=1), jnp.sum(grad_key_hat * key_hat, axis=1)),
        "tensor",
    )
    grad_query_raw = (
        query_scale * (grad_query_hat - query_hat * (query_inner / d_model)[:, None])
    ).astype(jnp.bfloat16)
    grad_key_raw = (key_scale * (grad_key_hat - key_hat * (key_inner / d_model)[:, None])).astype(
        jnp.bfloat16
    )
    grad_value_raw = grad_value_total.reshape(seq_len, local_dim).astype(jnp.bfloat16)
    grad_query_part = jnp.einsum(
        "sd,sf->df", normed_all, grad_query_raw, preferred_element_type=jnp.float32
    )
    grad_key_part = jnp.einsum(
        "sd,sf->df", normed_all, grad_key_raw, preferred_element_type=jnp.float32
    )
    grad_value_part = jnp.einsum(
        "sd,sf->df", normed_all, grad_value_raw, preferred_element_type=jnp.float32
    )
    summed = jnp.einsum("sf,df->sd", grad_query_raw, w_query, preferred_element_type=jnp.float32)
    summed = summed + jnp.einsum(
        "sf,df->sd", grad_key_raw, w_key, preferred_element_type=jnp.float32
    )
    grad_first_normalized = lax.psum_scatter(
        (
            summed
            + jnp.einsum("sf,df->sd", grad_value_raw, w_value, preferred_element_type=jnp.float32)
        ).astype(jnp.bfloat16),
        "tensor",
        scatter_dimension=0,
        tiled=True,
    ).astype(jnp.float32)
    grad_attention_share = jnp.sum(grad_first_normalized * first_unit_rows, axis=0)
    grad_first_unit_rows = grad_first_normalized * attention_norm_gain
    grad_tokens = (
        first_norm_scale
        * (
            grad_first_unit_rows
            - first_unit_rows
            * jnp.mean(grad_first_unit_rows * first_unit_rows, axis=-1, keepdims=True)
        )
        + grad_hidden_one
    ).astype(jnp.bfloat16)
    total_query, total_key, total_value, total_output, total_qgain, total_kgain = (
        lax.psum(grad_query_part.astype(jnp.bfloat16), "dp").astype(jnp.float32),
        lax.psum(grad_key_part.astype(jnp.bfloat16), "dp").astype(jnp.float32),
        lax.psum(grad_value_part.astype(jnp.bfloat16), "dp").astype(jnp.float32),
        lax.psum(grad_output_part.astype(jnp.bfloat16), "dp").astype(jnp.float32),
        lax.psum(grad_qgain_part.astype(jnp.bfloat16), "dp").astype(jnp.float32),
        lax.psum(grad_kgain_part.astype(jnp.bfloat16), "dp").astype(jnp.float32),
    )
    total_attn_gain, total_ffn_gain, total_router = lax.psum(
        (grad_attention_share, grad_expert_share, grad_router_part), ("dp", "tensor")
    )
    return (
        result,
        grad_tokens,
        total_query,
        total_key,
        total_value,
        total_output,
        total_qgain,
        total_kgain,
        total_attn_gain,
        total_ffn_gain,
        total_router,
        grad_gate,
        grad_up,
        grad_down,
    )


def solution(mesh):
    return jax.shard_map(
        local_gathered if mesh.shape["dp"] == 8 else local_routed,
        mesh=mesh,
        in_specs=(
            P(("dp", "tensor"), None),
            P("dp", None),
            P(("dp", "tensor"), None),
            P(),
            P(None, "tensor"),
            P(None, "tensor"),
            P(None, "tensor"),
            P("tensor"),
            P("tensor"),
            P("tensor", None),
            P(),
            P(),
            P("dp", None, "tensor"),
            P("dp", None, "tensor"),
            P("dp", "tensor", None),
            P(("dp", "tensor"), None),
        ),
        out_specs=(
            P(("dp", "tensor"), None),
            P(("dp", "tensor"), None),
            P(None, "tensor"),
            P(None, "tensor"),
            P(None, "tensor"),
            P("tensor", None),
            P("tensor"),
            P("tensor"),
            P(),
            P(),
            P(),
            P("dp", None, "tensor"),
            P("dp", None, "tensor"),
            P("dp", "tensor", None),
        ),
        check_vma=False,
    )
```

```python
import functools
import math

import jax
import jax.numpy as jnp
from jax import lax
from jax.experimental import pallas as pl
from jax.experimental.pallas import tpu as pltpu
from jax.sharding import PartitionSpec as P

HEAD_DIM = 128


EPSILON = 1e-05
THETA = 10000.0
NEG_LARGE = -1e30


def root_mean_square_scale(values):
    return lax.rsqrt(jnp.mean(values * values, axis=-1, keepdims=True) + EPSILON)


def rope_tables(length, head_dim):
    half_dim = head_dim // 2
    freq_index = jnp.arange(half_dim, dtype=jnp.float32)
    frequency = THETA ** (-(2.0 * freq_index) / head_dim)
    angles = jnp.arange(length, dtype=jnp.float32)[:, None] * frequency[None, :]
    cosine = jnp.concatenate([jnp.cos(angles), jnp.cos(angles)], axis=1)
    sine_table = jnp.concatenate([jnp.sin(angles), jnp.sin(angles)], axis=1)
    return (cosine[:, None, :], sine_table[:, None, :])


def rotate(values, cosine, sine_table):
    half_dim = values.shape[-1] // 2
    turned = jnp.concatenate([-values[..., half_dim:], values[..., :half_dim]], axis=-1)
    return values * cosine + turned * sine_table


def unrotate(grad_rows, cosine, sine_table):
    half_dim = grad_rows.shape[-1] // 2
    scaled = grad_rows * sine_table
    turned = jnp.concatenate([scaled[..., half_dim:], -scaled[..., :half_dim]], axis=-1)
    return grad_rows * cosine + turned


def slot_positions(ids, experts):
    flat_ids = ids.reshape(-1)
    onehot = (flat_ids[:, None] == jnp.arange(experts, dtype=jnp.int32)[None, :]).astype(jnp.int32)
    running = jnp.cumsum(onehot, axis=0)
    return (flat_ids, jnp.sum(running * onehot, axis=1) - 1)


def block_scores(query_block, key_rows, file_row, block_start, score_scale):
    block_rows = query_block.shape[0]
    raw_scores = (
        jnp.einsum("qhd,khd->hqk", query_block, key_rows, preferred_element_type=jnp.float32)
        * score_scale
    )
    rows_at = block_start + jnp.arange(block_rows, dtype=jnp.int32)
    cols_at = jnp.arange(key_rows.shape[0], dtype=jnp.int32)
    allowed = (cols_at[None, :] <= rows_at[:, None]) & (file_row[None, :] == file_row[:, None])
    return jnp.where(allowed[None], raw_scores, NEG_LARGE)


MESH = pl.DeviceIdType.MESH
VMEM_LIMIT = 60 * 2**20


def greet(dp, z, nz):
    barrier = pltpu.get_barrier_semaphore()
    for flip in (1, 2, 4):
        pl.semaphore_signal(barrier, 1, device_id=(dp ^ flip, z), device_id_type=MESH)

    @pl.when(z > 0)
    def _():
        pl.semaphore_signal(barrier, 1, device_id=(dp, z - 1), device_id_type=MESH)

    @pl.when(z < nz - 1)
    def _():
        pl.semaphore_signal(barrier, 1, device_id=(dp, z + 1), device_id_type=MESH)

    ends = jnp.where(z > 0, 1, 0) + jnp.where(z < nz - 1, 1, 0)
    pl.semaphore_wait(barrier, 3 + ends)


def remote(src, dst, send, recv, device):
    return pltpu.make_async_remote_copy(
        src_ref=src, dst_ref=dst, send_sem=send, recv_sem=recv, device_id=device, device_id_type=MESH
    )


def gather_kernel(nz, x_ref, t_ref, out_ref, tags_ref, local_sem, sz, sx, sy, sda, sdb, sc, rz, rx, ry, rda, rdb, rc):
    dp, z = lax.axis_index("dp"), lax.axis_index("tensor")
    half = x_ref.shape[0] // 2
    greet(dp, z, nz)

    def rows_at(flip, zz):
        return out_ref.at[(dp ^ flip) * nz + zz]

    def tags_at(flip, zz):
        return tags_ref.at[(dp ^ flip) * nz + zz]

    def whole(flip, zz, own, send, recv, device):
        return (
            remote(x_ref if own else rows_at(flip, zz), rows_at(flip, zz), send(0), recv(0), device),
            remote(t_ref if own else tags_at(flip, zz), tags_at(flip, zz), send(1), recv(1), device),
        )

    def z_copy(zz, step, own):
        return whole(
            0, zz, own, lambda k: sz.at[k, (step + 1) // 2, zz], lambda k: rz.at[k, zz], (dp, z + step)
        )

    def x_copy(zz, own):
        return whole(0, zz, own, lambda k: sx.at[k, zz], lambda k: rx.at[k, zz], (dp ^ 2, z))

    def y_copy(zz, own):
        return whole(0, zz, own, lambda k: sy.at[k, zz], lambda k: ry.at[k, zz], (dp ^ 4, z))

    def a_copy(zz):
        ref = rows_at(4, zz).at[pl.ds(0, half)]
        return (
            remote(ref, ref, sda.at[0, zz], rda.at[0, zz], (dp ^ 2, z)),
            remote(tags_at(4, zz), tags_at(4, zz), sda.at[1, zz], rda.at[1, zz], (dp ^ 2, z)),
        )

    def b_copy(zz):
        ref = rows_at(2, zz).at[pl.ds(half, half)]
        return (remote(ref, ref, sdb.at[zz], rdb.at[zz], (dp ^ 4, z)),)

    def c_copy(kind, zz, own=False):
        send, recv = (lambda k: sc.at[k, kind, zz]), (lambda k: rc.at[k, kind, zz])
        if kind < 3:
            return whole((0, 2, 4)[kind], zz, own, send, recv, (dp ^ 1, z))
        ref = rows_at(6, zz).at[pl.ds((kind - 3) * half, half)]
        copies = (remote(ref, ref, send(0), recv(0), (dp ^ 1, z)),)
        if kind == 3:
            copies += (remote(tags_at(6, zz), tags_at(6, zz), send(1), recv(1), (dp ^ 1, z)),)
        return copies

    def start(copies):
        for copy in copies:
            copy.start()

    def arrived(ref, sem):
        remote(ref, ref, sem, sem, (dp ^ 1, z)).wait_recv()

    def both_arrived(flip, zz, recv):
        arrived(rows_at(flip, zz), recv(0))
        arrived(tags_at(flip, zz), recv(1))

    def places(distance):
        for sign in (0,) if distance == 0 else (-1, 1):
            yield sign, z + sign * distance

    def spread(distance):
        for sign, zz in places(distance):
            own = distance == 0

            @pl.when((zz >= 0) & (zz < nz))
            def _():
                if not own:
                    both_arrived(0, zz, lambda k: rz.at[k, zz])
                if sign <= 0:

                    @pl.when(z < nz - 1)
                    def _():
                        start(z_copy(zz, 1, own))

                if sign >= 0:

                    @pl.when(z > 0)
                    def _():
                        start(z_copy(zz, -1, own))

                start(x_copy(zz, own))
                start(y_copy(zz, own))
                start(c_copy(0, zz, own))

    def relay(distance):
        for _, zz in places(distance):

            @pl.when((zz >= 0) & (zz < nz))
            def _():
                both_arrived(4, zz, lambda k: ry.at[k, zz])
                start(a_copy(zz))
                start(c_copy(2, zz))
                both_arrived(2, zz, lambda k: rx.at[k, zz])
                start(b_copy(zz))
                start(c_copy(1, zz))

    def corner(distance):
        for _, zz in places(distance):

            @pl.when((zz >= 0) & (zz < nz))
            def _():
                arrived(rows_at(6, zz).at[pl.ds(0, half)], rda.at[0, zz])
                arrived(tags_at(6, zz), rda.at[1, zz])
                start(c_copy(3, zz))
                arrived(rows_at(6, zz).at[pl.ds(half, half)], rdb.at[zz])
                start(c_copy(4, zz))

    keep = pltpu.make_async_copy(x_ref, rows_at(0, z), local_sem.at[0])
    keep_tags = pltpu.make_async_copy(t_ref, tags_at(0, z), local_sem.at[1])
    keep.start()
    keep_tags.start()
    for step in range(nz + 2):
        if step < nz:
            spread(step)
        if 0 <= step - 1 < nz:
            relay(step - 1)
        if 0 <= step - 2 < nz:
            corner(step - 2)
    keep.wait()
    keep_tags.wait()

    def sent(copies):
        for copy in copies:
            copy.wait_send()

    for zz in range(nz):

        @pl.when((zz <= z) & (z < nz - 1))
        def _():
            sent(z_copy(zz, 1, False))

        @pl.when((zz >= z) & (z > 0))
        def _():
            sent(z_copy(zz, -1, False))

        sent(x_copy(zz, False))
        sent(y_copy(zz, False))
        sent(a_copy(zz))
        sent(b_copy(zz))
        for kind in range(5):
            sent(c_copy(kind, zz))
        for kind, flip in ((0, 1), (1, 3), (2, 5)):
            both_arrived(flip, zz, lambda k: rc.at[k, kind, zz])
        for kind in (3, 4):
            arrived(rows_at(7, zz).at[pl.ds((kind - 3) * half, half)], rc.at[0, kind, zz])
        arrived(tags_at(7, zz), rc.at[1, 3, zz])


def gather_all(x, tags, nz, collective_id):
    rows, width = x.shape
    dma = pltpu.SemaphoreType.DMA
    any_place, vmem = pl.BlockSpec(memory_space=pl.ANY), pl.BlockSpec(memory_space=pltpu.VMEM)
    return pl.pallas_call(
        functools.partial(gather_kernel, nz),
        name="gather_all",
        out_shape=(
            jax.ShapeDtypeStruct((8 * nz, rows, width), x.dtype),
            jax.ShapeDtypeStruct((8 * nz,) + tags.shape, tags.dtype),
        ),
        in_specs=[vmem, vmem],
        out_specs=(any_place, any_place),
        scratch_shapes=[dma((2,))]
        + [dma((2, 2, nz)), dma((2, nz)), dma((2, nz)), dma((2, nz)), dma((nz,)), dma((2, 5, nz))]
        + [dma((2, nz)), dma((2, nz)), dma((2, nz)), dma((2, nz)), dma((nz,)), dma((2, 5, nz))],
        compiler_params=pltpu.CompilerParams(
            collective_id=collective_id, has_side_effects=True, vmem_limit_bytes=8 * 2**20
        ),
    )(x, tags)


def greet_line(dp, z, nz):
    barrier = pltpu.get_barrier_semaphore()

    @pl.when(z > 0)
    def _():
        pl.semaphore_signal(barrier, 1, device_id=(dp, z - 1), device_id_type=MESH)

    @pl.when(z < nz - 1)
    def _():
        pl.semaphore_signal(barrier, 1, device_id=(dp, z + 1), device_id_type=MESH)

    pl.semaphore_wait(barrier, jnp.where(z > 0, 1, 0) + jnp.where(z < nz - 1, 1, 0))


PARTS = 2
PIECES = 2


def greet_total(dp, z, nz):
    barrier = pltpu.get_barrier_semaphore()
    for flip in (1, 2, 4):
        pl.semaphore_signal(barrier, 1, device_id=(dp ^ flip, z), device_id_type=MESH)
    for turn in range(1, nz):
        pl.semaphore_signal(barrier, 1, device_id=(dp, lax.rem(z + turn, nz)), device_id_type=MESH)
    pl.semaphore_wait(barrier, 2 + nz)


class Total:
    steps = 5

    def __init__(self, nz, dp, z, got, s_plane, r_plane, s_line, r_line):
        self.nz, self.z, self.got = nz, z, got
        self.plane = [
            remote(got.at[2 * k], got.at[2 * k + 1], s_plane.at[k], r_plane.at[k], (dp ^ flip, z))
            for k, flip in enumerate((1, 2, 4))
        ]
        self.line = [
            remote(got.at[6], got.at[6 + turn], s_line.at[turn - 1], r_line.at[turn - 1], (dp, lax.rem(z + turn, nz)))
            for turn in range(1, nz)
        ]

    def step(self, k, out_ref):
        got, nz = self.got, self.nz
        if 1 <= k <= 3:
            self.plane[k - 1].wait()
            got[2 * k] = got[2 * k - 2] + got[2 * k - 1]
        if k < 3:
            self.plane[k].start()
        elif k == 3:
            for copy in self.line:
                copy.start()
        else:
            for copy in self.line:
                copy.wait()
            total = got[6 + lax.rem(self.z, nz)]
            for zz in range(1, nz):
                total = total + got[6 + lax.rem(self.z - zz + nz, nz)]
            out_ref[...] = total


def total_scratch(nz, shape, dtype):
    dma = pltpu.SemaphoreType.DMA
    return [pltpu.VMEM((6 + nz,) + shape, dtype), dma((3,)), dma((3,)), dma((nz - 1,)), dma((nz - 1,))]


def line_gather_kernel(nz, *refs):
    dp, z = lax.axis_index("dp"), lax.axis_index("tensor")
    summed = len(refs) > 6
    if summed:
        x_ref, small_ref, out_ref, total_ref, local_sem, s_up, s_down, r_line = refs[:8]
        greet_total(dp, z, nz)
        total = Total(nz, dp, z, *refs[8:])
        total.got[0] = small_ref[...]
    else:
        x_ref, out_ref, local_sem, s_up, s_down, r_line = refs
        greet_line(dp, z, nz)
    part = x_ref.shape[0] // PARTS

    def copy(zz, k, step, own):
        at = pl.ds(k * part, part)
        dst = out_ref.at[zz, at]
        sems = s_up if step > 0 else s_down
        return remote(x_ref.at[at] if own else dst, dst, sems.at[zz, k], r_line.at[zz, k], (dp, z + step))

    keep = pltpu.make_async_copy(x_ref, out_ref.at[z], local_sem)
    for distance in range(nz):
        for k in range(PARTS):
            for sign in (0,) if distance == 0 else (-1, 1):
                zz, own = z + sign * distance, distance == 0

                @pl.when((zz >= 0) & (zz < nz))
                def _():
                    if not own:
                        copy(zz, k, 1, False).wait_recv()
                    if sign <= 0:

                        @pl.when(z < nz - 1)
                        def _():
                            copy(zz, k, 1, own).start()

                    if sign >= 0:

                        @pl.when(z > 0)
                        def _():
                            copy(zz, k, -1, own).start()

        if distance == 0:
            keep.start()
        if summed:
            total.step(distance, total_ref)
    if summed:
        for k in range(nz, Total.steps):
            total.step(k, total_ref)
    keep.wait()
    for zz in range(nz):
        for k in range(PARTS):

            @pl.when((zz <= z) & (z < nz - 1))
            def _():
                copy(zz, k, 1, False).wait_send()

            @pl.when((zz >= z) & (z > 0))
            def _():
                copy(zz, k, -1, False).wait_send()


def line_gather(x, nz, collective_id, small=None):
    dma, vmem = pltpu.SemaphoreType.DMA, pl.BlockSpec(memory_space=pltpu.VMEM)
    blocks = jax.ShapeDtypeStruct((nz,) + x.shape, x.dtype)
    scratch = [dma(())] + [dma((nz, PARTS)) for _ in range(3)]
    params = pltpu.CompilerParams(
        collective_id=collective_id, has_side_effects=True, vmem_limit_bytes=8 * 2**20
    )
    kernel = functools.partial(line_gather_kernel, nz)
    if small is None:
        return pl.pallas_call(
            kernel,
            name="line_gather",
            out_shape=blocks,
            in_specs=[vmem],
            out_specs=pl.BlockSpec(memory_space=pl.ANY),
            scratch_shapes=scratch,
            compiler_params=params,
        )(x)
    return pl.pallas_call(
        kernel,
        name="line_gather_total",
        out_shape=(blocks, jax.ShapeDtypeStruct(small.shape, small.dtype)),
        in_specs=[vmem, vmem],
        out_specs=(pl.BlockSpec(memory_space=pl.ANY), vmem),
        scratch_shapes=scratch + total_scratch(nz, small.shape, small.dtype),
        compiler_params=params,
    )(x, small)


def line_total_kernel(nz, x_ref, out_ref, got, send, recv):
    dp, z = lax.axis_index("dp"), lax.axis_index("tensor")
    others = [lax.rem(z + turn, nz) for turn in range(1, nz)]
    barrier = pltpu.get_barrier_semaphore()
    for other in others:
        pl.semaphore_signal(barrier, 1, device_id=(dp, other), device_id_type=MESH)
    pl.semaphore_wait(barrier, nz - 1)
    copies = [
        remote(x_ref, got.at[turn], send.at[turn], recv.at[turn], (dp, other)) for turn, other in enumerate(others)
    ]
    for copy in copies:
        copy.start()
    for copy in copies:
        copy.wait()
    total = x_ref[...]
    for turn in range(nz - 1):
        total = total + got[turn]
    out_ref[...] = total


def line_total(x, nz, collective_id):
    dma, vmem = pltpu.SemaphoreType.DMA, pl.BlockSpec(memory_space=pltpu.VMEM)
    return pl.pallas_call(
        functools.partial(line_total_kernel, nz),
        name="line_total",
        out_shape=jax.ShapeDtypeStruct(x.shape, x.dtype),
        in_specs=[vmem],
        out_specs=vmem,
        scratch_shapes=[pltpu.VMEM((nz - 1,) + x.shape, x.dtype), dma((nz - 1,)), dma((nz - 1,))],
        compiler_params=pltpu.CompilerParams(
            collective_id=collective_id, has_side_effects=True, vmem_limit_bytes=4 * 2**20
        ),
    )(x)


CHUNK = 16


def add_rows(dst, *others, start=0, count):
    def body(k, carry):
        at = pl.ds(start + k * CHUNK, CHUNK)
        total = dst[at, :].astype(jnp.float32)
        for ref, base in others:
            total = total + ref[pl.ds(base + k * CHUNK, CHUNK), :].astype(jnp.float32)
        dst[at, :] = total.astype(dst.dtype)
        return carry

    lax.fori_loop(0, count // CHUNK, body, 0)


class Line:
    def __init__(self, nz, dp, z, acc, up, down, s_up, r_up, s_down, r_down):
        self.nz, self.dp, self.z, self.acc, self.up, self.down = nz, dp, z, acc, up, down
        self.sems = s_up, r_up, s_down, r_down
        self.part = acc.shape[1] // PARTS

    def copy(self, zz, k, step):
        at = pl.ds(k * self.part, self.part)
        s_up, r_up, s_down, r_down = self.sems
        if step > 0:
            return remote(self.acc.at[zz, at], self.up.at[zz, at], s_up.at[zz, k], r_up.at[zz, k], (self.dp, self.z + 1))
        return remote(self.acc.at[zz, at], self.down.at[zz, at], s_down.at[zz, k], r_down.at[zz, k], (self.dp, self.z - 1))

    def first(self):
        nz, z = self.nz, self.z

        @pl.when(z == 0)
        def _():
            for zz in range(nz - 1, 0, -1):
                for k in range(PARTS):
                    self.copy(zz, k, 1).start()

        @pl.when(z == nz - 1)
        def _():
            for zz in range(nz - 1):
                for k in range(PARTS):
                    self.copy(zz, k, -1).start()

    def step(self, distance):
        nz, z = self.nz, self.z
        for k in range(PARTS):
            for sign in (1, -1):
                far = nz - distance if sign > 0 else distance - 1
                through = (far > z) & (z > 0) if sign > 0 else (far < z) & (z < nz - 1)

                @pl.when(through)
                def _():
                    self.copy(far, k, sign).wait_recv()
                    source = self.up if sign > 0 else self.down
                    add_rows(self.acc.at[far], (source.at[far], k * self.part), start=k * self.part, count=self.part)
                    self.copy(far, k, sign).start()

    def finish(self, out_ref):
        nz, z = self.nz, self.z
        for k in range(PARTS):

            @pl.when(z > 0)
            def _():
                self.copy(z, k, 1).wait_recv()

            @pl.when(z < nz - 1)
            def _():
                self.copy(z, k, -1).wait_recv()

        def body(k, carry):
            at = pl.ds(k * CHUNK, CHUNK)
            total = self.acc[z, at, :].astype(jnp.float32)
            zero = jnp.zeros_like(total)
            total = total + jnp.where(z > 0, self.up[z, at, :].astype(jnp.float32), zero)
            total = total + jnp.where(z < nz - 1, self.down[z, at, :].astype(jnp.float32), zero)
            out_ref[at, :] = total
            return carry

        lax.fori_loop(0, out_ref.shape[0] // CHUNK, body, 0)

    def drain(self):
        nz, z = self.nz, self.z
        for zz in range(nz):
            for k in range(PARTS):

                @pl.when(zz > z)
                def _():
                    self.copy(zz, k, 1).wait_send()

                @pl.when(zz < z)
                def _():
                    self.copy(zz, k, -1).wait_send()


def line_scatter_kernel(nz, p_ref, out_ref, acc, up, down, local_sem, s_up, r_up, s_down, r_down):
    dp, z = lax.axis_index("dp"), lax.axis_index("tensor")
    loaded = pltpu.make_async_copy(p_ref, acc, local_sem)
    loaded.start()
    greet_line(dp, z, nz)
    loaded.wait()
    line = Line(nz, dp, z, acc, up, down, s_up, r_up, s_down, r_down)
    line.first()
    for distance in range(1, nz - 1):
        line.step(distance)
    line.finish(out_ref)
    line.drain()


def line_scatter(p, nz, collective_id):
    _, rows, width = p.shape
    dma, vmem = pltpu.SemaphoreType.DMA, functools.partial(pltpu.VMEM, dtype=p.dtype)
    return pl.pallas_call(
        functools.partial(line_scatter_kernel, nz),
        name="line_scatter",
        out_shape=jax.ShapeDtypeStruct((rows, width), jnp.float32),
        in_specs=[pl.BlockSpec(memory_space=pl.ANY)],
        out_specs=pl.BlockSpec(memory_space=pltpu.VMEM),
        scratch_shapes=[vmem((nz, rows, width)) for _ in range(3)]
        + [dma(())]
        + [dma((nz, PARTS)) for _ in range(4)],
        compiler_params=pltpu.CompilerParams(
            collective_id=collective_id, has_side_effects=True, vmem_limit_bytes=16 * 2**20
        ),
    )(p)


def z_order(nz):
    return [sorted(range(nz), key=lambda zz: (-abs(zz - z), zz if z >= nz // 2 else -zz)) for z in range(nz)]


def scatter_kernel(nz, p_ref, t_ref, out_ref, tiles_ref, acc, rc, ra, rb, rx, ry, ru, rd, s_tile, r_tile, s_keep, s_local, s_core, r_core, s_a, r_a, s_b, r_b, s_x, r_x, s_y, r_y, s_u, r_u, s_d, r_d):
    dp, z = lax.axis_index("dp"), lax.axis_index("tensor")
    rows = acc.shape[2]
    half = rows // 2
    order = z_order(nz)

    def place(i):
        zz = order[0][i]
        for zv in range(1, nz):
            zz = jnp.where(z == zv, order[zv][i], zz)
        return zz

    flips = (0, 2, 4, 6)

    def load(kind, zz):
        return pltpu.make_async_copy(
            p_ref.at[(dp ^ flips[kind]) * nz + zz], acc.at[kind, zz], s_local.at[kind, zz]
        )

    def core_copy(kind, zz):
        return remote(
            p_ref.at[(dp ^ flips[kind] ^ 1) * nz + zz], rc.at[kind, zz], s_core.at[kind, zz], r_core.at[kind, zz], (dp ^ 1, z)
        )

    def a_copy(zz):
        return remote(acc.at[3, zz, pl.ds(0, half)], ra.at[zz], s_a.at[zz], r_a.at[zz], (dp ^ 2, z))

    def b_copy(zz):
        return remote(acc.at[3, zz, pl.ds(half, half)], rb.at[zz], s_b.at[zz], r_b.at[zz], (dp ^ 4, z))

    def x_copy(zz):
        return remote(acc.at[1, zz], rx.at[zz], s_x.at[zz], r_x.at[zz], (dp ^ 2, z))

    def y_copy(zz):
        return remote(acc.at[2, zz], ry.at[zz], s_y.at[zz], r_y.at[zz], (dp ^ 4, z))

    def up_copy(zz):
        return remote(acc.at[0, zz], ru.at[zz], s_u.at[zz], r_u.at[zz], (dp, z + 1))

    def down_copy(zz):
        return remote(acc.at[0, zz], rd.at[zz], s_d.at[zz], r_d.at[zz], (dp, z - 1))

    def add(dst, *others, start=0, count=rows):
        add_rows(dst, *others, start=start, count=count)

    def wave(i):
        zz = place(i)
        for kind in (3, 1, 2, 0):
            core_copy(kind, zz).start()
            load(kind, zz).start()

    def paired(kind, zz):
        load(kind, zz).wait()
        core_copy(kind, zz).wait_recv()

    def stage_diagonal(i):
        zz = place(i)
        paired(3, zz)
        add(acc.at[3, zz], (rc.at[3, zz], 0))
        a_copy(zz).start()
        b_copy(zz).start()

    def stage_side(i):
        zz = place(i)
        paired(1, zz)
        paired(2, zz)
        a_copy(zz).wait_recv()
        add(acc.at[2, zz], (rc.at[2, zz], 0), (ra.at[zz], 0), start=0, count=half)
        add(acc.at[2, zz], (rc.at[2, zz], half), start=half, count=half)
        y_copy(zz).start()
        b_copy(zz).wait_recv()
        add(acc.at[1, zz], (rc.at[1, zz], half), (rb.at[zz], 0), start=half, count=half)
        add(acc.at[1, zz], (rc.at[1, zz], 0), start=0, count=half)
        x_copy(zz).start()

    def stage_column(i):
        zz = place(i)
        paired(0, zz)
        x_copy(zz).wait_recv()
        y_copy(zz).wait_recv()
        add(acc.at[0, zz], (rc.at[0, zz], 0), (rx.at[zz], 0), (ry.at[zz], 0))

        @pl.when((zz > z) & (z == 0))
        def _():
            up_copy(zz).start()

        @pl.when((zz < z) & (z == nz - 1))
        def _():
            down_copy(zz).start()

    def stage_line(i):
        zz = place(i)

        @pl.when((zz > z) & (z > 0))
        def _():
            up_copy(zz).wait_recv()
            add(acc.at[0, zz], (ru.at[zz], 0))
            up_copy(zz).start()

        @pl.when((zz < z) & (z < nz - 1))
        def _():
            down_copy(zz).wait_recv()
            add(acc.at[0, zz], (rd.at[zz], 0))
            down_copy(zz).start()

    def peers():
        for flip in range(8):
            for turn in range(nz):
                if flip or turn:
                    yield flip, turn, dp ^ flip, lax.rem(z + turn, nz)

    def tile_copy(flip, turn, peer, line):
        here = dp * nz + z
        return remote(
            t_ref.at[peer * nz + line], tiles_ref.at[here], s_tile.at[flip, turn], r_tile.at[flip, turn], (peer, line)
        )

    barrier = pltpu.get_barrier_semaphore()
    for _, _, peer, line in peers():
        pl.semaphore_signal(barrier, 1, device_id=(peer, line), device_id_type=MESH)
    pl.semaphore_wait(barrier, 8 * nz - 1)
    wave(0)
    keep = pltpu.make_async_copy(t_ref.at[dp * nz + z], tiles_ref.at[dp * nz + z], s_keep)
    keep.start()
    for peer in peers():
        tile_copy(*peer).start()
    for i in range(nz + 3):
        if i + 1 < nz:
            wave(i + 1)
        if i < nz:
            stage_diagonal(i)
        if 0 <= i - 1 < nz:
            stage_side(i - 1)
        if 0 <= i - 2 < nz:
            stage_column(i - 2)
        if 0 <= i - 3 < nz:
            stage_line(i - 3)

    keep.wait()
    for flip, turn, peer, line in peers():
        tile_copy(flip, turn, peer, line).wait_send()
        source = tiles_ref.at[peer * nz + lax.rem(z - turn + nz, nz)]
        remote(source, source, s_tile.at[flip, turn], r_tile.at[flip, turn], (dp ^ 1, z)).wait_recv()

    @pl.when(z > 0)
    def _():
        up_copy(z).wait_recv()

    @pl.when(z < nz - 1)
    def _():
        down_copy(z).wait_recv()

    def finish(k, carry):
        at = pl.ds(k * CHUNK, CHUNK)
        total = acc[0, z, at, :].astype(jnp.float32)
        zero = jnp.zeros_like(total)
        total = total + jnp.where(z > 0, ru[z, at, :].astype(jnp.float32), zero)
        total = total + jnp.where(z < nz - 1, rd[z, at, :].astype(jnp.float32), zero)
        out_ref[at, :] = total
        return carry

    lax.fori_loop(0, rows // CHUNK, finish, 0)
    for zz in range(nz):
        for kind in range(4):
            core_copy(kind, zz).wait_send()
        a_copy(zz).wait_send()
        b_copy(zz).wait_send()
        x_copy(zz).wait_send()
        y_copy(zz).wait_send()

        @pl.when(zz > z)
        def _():
            up_copy(zz).wait_send()

        @pl.when(zz < z)
        def _():
            down_copy(zz).wait_send()


def scatter_all(p, tiles, nz, collective_id):
    _, rows, width = p.shape
    dma, vmem = pltpu.SemaphoreType.DMA, functools.partial(pltpu.VMEM, dtype=p.dtype)
    half = rows // 2
    return pl.pallas_call(
        functools.partial(scatter_kernel, nz),
        name="scatter_all",
        out_shape=(
            jax.ShapeDtypeStruct((rows, width), jnp.float32),
            jax.ShapeDtypeStruct(tiles.shape, tiles.dtype),
        ),
        in_specs=[pl.BlockSpec(memory_space=pl.ANY), pl.BlockSpec(memory_space=pltpu.VMEM)],
        out_specs=(pl.BlockSpec(memory_space=pltpu.VMEM), pl.BlockSpec(memory_space=pltpu.VMEM)),
        scratch_shapes=[vmem((4, nz, rows, width)), vmem((4, nz, rows, width))]
        + [vmem((nz, half, width)) for _ in range(2)]
        + [vmem((nz, rows, width)) for _ in range(4)]
        + [dma((8, nz)), dma((8, nz)), dma(())]
        + [dma((4, nz)), dma((4, nz)), dma((4, nz))]
        + [dma((nz,)) for _ in range(12)],
        compiler_params=pltpu.CompilerParams(
            collective_id=collective_id, has_side_effects=True, vmem_limit_bytes=VMEM_LIMIT
        ),
    )(p, tiles)


def finish_kernel(nz, nc, g_ref, h_ref, p_ref, unit_ref, small_ref, sum_q, sum_k, sum_v, sum_o, out_ref, total_ref, buf, acc, rc, ra, rb, rx, ry, line_acc, up, down, *sems):
    (s_load, s_core, r_core, s_a, r_a, s_b, r_b, s_x, r_x, s_y, r_y) = sems[:11]
    (t_x, q_x, t_y, q_y, t_a, q_a, t_b, q_b, t_c, q_c) = sems[11:21]
    s_line, s_store, s_up, r_up, s_down, r_down = sems[21:27]
    total = Total(nz, lax.axis_index("dp"), lax.axis_index("tensor"), *sems[27:])
    dp, z = lax.axis_index("dp"), lax.axis_index("tensor")
    rows = acc.shape[2]
    half = rows // 2
    flips = (0, 2, 4, 6)

    parts = ((g_ref, 0, g_ref.shape[2]), (h_ref, g_ref.shape[2], h_ref.shape[2]))

    def loads(kind, c):
        return [
            pltpu.make_async_copy(
                ref.at[(dp ^ flips[kind]) * nc + c], acc.at[kind, c, :, pl.ds(at, size)], s_load.at[k, kind, c]
            )
            for k, (ref, at, size) in enumerate(parts)
        ]

    def core_copies(kind, c):
        return [
            remote(
                ref.at[(dp ^ flips[kind] ^ 1) * nc + c],
                rc.at[kind, c, :, pl.ds(at, size)],
                s_core.at[k, kind, c],
                r_core.at[k, kind, c],
                (dp ^ 1, z),
            )
            for k, (ref, at, size) in enumerate(parts)
        ]

    def a_copy(c):
        return remote(acc.at[3, c, pl.ds(0, half)], ra.at[c], s_a.at[c], r_a.at[c], (dp ^ 2, z))

    def b_copy(c):
        return remote(acc.at[3, c, pl.ds(half, half)], rb.at[c], s_b.at[c], r_b.at[c], (dp ^ 4, z))

    def x_copy(c):
        return remote(acc.at[1, c], rx.at[c], s_x.at[c], r_x.at[c], (dp ^ 2, z))

    def y_copy(c):
        return remote(acc.at[2, c], ry.at[c], s_y.at[c], r_y.at[c], (dp ^ 4, z))

    def full(flip, c):
        return buf.at[(dp ^ flip) * nc + c]

    def back_x(c):
        return remote(full(0, c), full(0, c), t_x.at[c], q_x.at[c], (dp ^ 2, z))

    def back_y(c):
        return remote(full(0, c), full(0, c), t_y.at[c], q_y.at[c], (dp ^ 4, z))

    def back_a(c):
        ref = full(4, c).at[pl.ds(0, half)]
        return remote(ref, ref, t_a.at[c], q_a.at[c], (dp ^ 2, z))

    def back_b(c):
        ref = full(2, c).at[pl.ds(half, half)]
        return remote(ref, ref, t_b.at[c], q_b.at[c], (dp ^ 4, z))

    def back_core(kind, c):
        ref = full((0, 2, 4, 6, 6)[kind], c)
        if kind >= 3:
            ref = ref.at[pl.ds((kind - 3) * half, half)]
        return remote(ref, ref, t_c.at[kind, c], q_c.at[kind, c], (dp ^ 1, z))

    def arrived(ref, sem):
        remote(ref, ref, sem, sem, (dp ^ 1, z)).wait_recv()

    def paired(kind, c):
        for copy in loads(kind, c):
            copy.wait()
        for copy in core_copies(kind, c):
            copy.wait_recv()

    def stage_diagonal(c):
        paired(3, c)
        add_rows(acc.at[3, c], (rc.at[3, c], 0), count=rows)
        a_copy(c).start()
        b_copy(c).start()

    def stage_side(c):
        paired(1, c)
        paired(2, c)
        a_copy(c).wait_recv()
        add_rows(acc.at[2, c], (rc.at[2, c], 0), (ra.at[c], 0), start=0, count=half)
        add_rows(acc.at[2, c], (rc.at[2, c], half), start=half, count=half)
        y_copy(c).start()
        b_copy(c).wait_recv()
        add_rows(acc.at[1, c], (rc.at[1, c], half), (rb.at[c], 0), start=half, count=half)
        add_rows(acc.at[1, c], (rc.at[1, c], 0), start=0, count=half)
        x_copy(c).start()

    def stage_own(c):
        paired(0, c)
        x_copy(c).wait_recv()
        y_copy(c).wait_recv()
        dst = full(0, c)

        def body(k, carry):
            at = pl.ds(k * CHUNK, CHUNK)
            total = acc[0, c, at, :].astype(jnp.float32) + rc[0, c, at, :].astype(jnp.float32)
            total = total + rx[c, at, :].astype(jnp.float32) + ry[c, at, :].astype(jnp.float32)
            dst[at, :] = total.astype(dst.dtype)
            return carry

        lax.fori_loop(0, rows // CHUNK, body, 0)
        back_x(c).start()
        back_y(c).start()
        back_core(0, c).start()

    def stage_relay(c):
        arrived(full(4, c), q_y.at[c])
        back_a(c).start()
        back_core(2, c).start()
        arrived(full(2, c), q_x.at[c])
        back_b(c).start()
        back_core(1, c).start()

    def stage_corner(c):
        arrived(full(6, c).at[pl.ds(0, half)], q_a.at[c])
        back_core(3, c).start()
        arrived(full(6, c).at[pl.ds(half, half)], q_b.at[c])
        back_core(4, c).start()

    line_load = pltpu.make_async_copy(p_ref, line_acc, s_line)
    line_load.start()
    for c in range(nc):
        for kind in (3, 1, 2, 0):
            for copy in loads(kind, c):
                copy.start()
    greet_total(dp, z, nz)
    for c in range(nc):
        for kind in (3, 1, 2, 0):
            for copy in core_copies(kind, c):
                copy.start()
    line = Line(nz, dp, z, line_acc, up, down, s_up, r_up, s_down, r_down)
    line_load.wait()
    line.first()
    def line_end():
        line.finish(out_ref)
        line.drain()
        share = jnp.sum(out_ref[...] * unit_ref[...], axis=0, keepdims=True)
        total.got[0] = small_ref[...]
        wide = small_ref.shape[1]
        for k in range(out_ref.shape[1] // wide):
            total.got[0, k : k + 1, :] = share[:, k * wide : (k + 1) * wide]

    side = [functools.partial(line.step, distance) for distance in range(1, nz - 1)] + [line_end]
    side += [functools.partial(total.step, k, total_ref) for k in range(Total.steps)]
    stages = (stage_diagonal, stage_side, stage_own, stage_relay, stage_corner)
    for i in range(nc + len(stages) - 1):
        for lag, stage in enumerate(stages):
            if 0 <= i - lag < nc:
                stage(i - lag)
                if i >= 1 and side:
                    side.pop(0)()
    for one in side:
        one()
    for c in range(nc):
        for kind, flip in ((0, 1), (1, 3), (2, 5)):
            arrived(full(flip, c), q_c.at[kind, c])
        for kind in (3, 4):
            arrived(full(7, c).at[pl.ds((kind - 3) * half, half)], q_c.at[kind, c])
    wide = buf.shape[2] // 4
    stores = [
        pltpu.make_async_copy(buf.at[:, :, pl.ds(k * wide, wide)], ref, s_store.at[k])
        for k, ref in enumerate((sum_q, sum_k, sum_v, sum_o))
    ]
    for store in stores:
        store.start()
    for c in range(nc):
        for kind in range(4):
            for copy in core_copies(kind, c):
                copy.wait_send()
        for copy in (a_copy, b_copy, x_copy, y_copy, back_x, back_y, back_a, back_b):
            copy(c).wait_send()
        for kind in range(5):
            back_core(kind, c).wait_send()
    for store in stores:
        store.wait()


def finish_sums(g, h, p, unit, small, nz, nc, collective_id):
    _, rows, width = g.shape
    width += h.shape[2]
    _, line_rows, line_width = p.shape
    half = rows // 2
    dma, vmem = pltpu.SemaphoreType.DMA, functools.partial(pltpu.VMEM, dtype=g.dtype)
    return pl.pallas_call(
        functools.partial(finish_kernel, nz, nc),
        name="finish_sums",
        out_shape=(
            *[jax.ShapeDtypeStruct(g.shape[:2] + (width // 4,), g.dtype)] * 4,
            jax.ShapeDtypeStruct((line_rows, line_width), jnp.float32),
            jax.ShapeDtypeStruct(small.shape, small.dtype),
        ),
        in_specs=[pl.BlockSpec(memory_space=pl.ANY)] * 3 + [pl.BlockSpec(memory_space=pltpu.VMEM)] * 2,
        out_specs=(
            *[pl.BlockSpec(memory_space=pl.ANY)] * 4,
            *[pl.BlockSpec(memory_space=pltpu.VMEM)] * 2,
        ),
        scratch_shapes=[vmem(g.shape[:2] + (width,)), vmem((4, nc, rows, width)), vmem((4, nc, rows, width))]
        + [vmem((nc, half, width)) for _ in range(2)]
        + [vmem((nc, rows, width)) for _ in range(2)]
        + [vmem((nz, line_rows, line_width)) for _ in range(3)]
        + [dma((2, 4, nc)) for _ in range(3)]
        + [dma((nc,)) for _ in range(16)]
        + [dma((5, nc)), dma((5, nc))]
        + [dma(()), dma((4,))]
        + [dma((nz, PARTS)) for _ in range(4)]
        + total_scratch(nz, small.shape, small.dtype),
        compiler_params=pltpu.CompilerParams(
            collective_id=collective_id, has_side_effects=True, vmem_limit_bytes=VMEM_LIMIT
        ),
    )(g, h, p, unit, small)


class Spread:
    def __init__(self, nz, row_shape):
        self.nz, self.row_shape = nz, row_shape

    @staticmethod
    def swap(value, flip):
        return lax.ppermute(value, "dp", [(i, i ^ flip) for i in range(8)])

    @staticmethod
    def plus(a, b):
        return (a.astype(jnp.float32) + b.astype(jnp.float32)).astype(a.dtype)

    def pair(self, mine, partners):
        self.mine = mine
        return self.swap(partners, 1)

    def sides(self, theirs):
        nz, plus = self.nz, self.plus
        self.low, self.high = slice(0, nz // 2), slice(nz // 2, nz)
        mine = self.mine.reshape((4, nz) + self.row_shape)
        self.whole = whole = plus(mine, theirs.reshape(mine.shape))
        to_x = jnp.stack([whole[1, self.low], whole[3, self.low]])
        to_y = jnp.stack([whole[2, self.high], whole[3, self.high]])
        return to_x, to_y

    def side(self, sides):
        return self.swap(sides[0], 2), self.swap(sides[1], 4)

    def last_side(self, sides):
        by_x, by_y = sides
        whole, low, high, plus = self.whole, self.low, self.high, self.plus
        self.low_own, low_y = plus(whole[0, low], by_x[0]), plus(whole[2, low], by_x[1])
        self.high_own, high_x = plus(whole[0, high], by_y[0]), plus(whole[1, high], by_y[1])
        return self.swap(low_y, 4), self.swap(high_x, 2)

    def column(self, sides):
        return jnp.concatenate([self.plus(self.low_own, sides[0]), self.plus(self.high_own, sides[1])])

    def blocks(self, column):
        z = lax.axis_index("tensor")
        return tuple(
            lax.dynamic_index_in_dim(column, (z + turn) % self.nz, axis=0, keepdims=False)
            for turn in range(self.nz)
        )

    def line(self, blocks):
        nz = self.nz
        self.own = blocks[0]
        return tuple(
            lax.ppermute(blocks[turn], "tensor", [(i, (i + turn) % nz) for i in range(nz)])
            for turn in range(1, nz)
        )

    def total(self, terms):
        total = self.own.astype(jnp.float32)
        for term in terms:
            total = total + term.astype(jnp.float32)
        return total


def hold(first, second):
    return lax.optimization_barrier((first, second))


def experts_routed(
    hidden_after_attention,
    expert_ids,
    expert_norm_gain,
    w_router,
    w_gate,
    w_up,
    w_down,
    grad_output,
):
    tok_count, d_model = hidden_after_attention.shape
    n_tensor = lax.axis_size("tensor")
    n_dp = lax.axis_size("dp")
    devices = n_dp * n_tensor
    second_norm_scale = root_mean_square_scale(hidden_after_attention)
    second_unit_rows = hidden_after_attention * second_norm_scale
    second_normalized = (second_unit_rows * expert_norm_gain).astype(jnp.bfloat16)
    experts = w_router.shape[1]
    topk = expert_ids.shape[1]
    exp_dev = w_gate.shape[0]
    most = 2 * ((tok_count * topk * 9 + experts * 16 - 1) // (experts * 16))
    route_probs = jax.nn.softmax(
        jnp.dot(second_normalized, w_router, preferred_element_type=jnp.float32), axis=-1
    )
    chosen = expert_ids[:, :, None] == jnp.arange(experts, dtype=jnp.int32)[None, None, :]
    gate_values = jnp.sum(jnp.where(chosen, route_probs[:, None, :], 0.0), axis=-1)
    flat_ids, pair_rank = slot_positions(expert_ids, experts)
    pair_slot = (flat_ids % exp_dev * n_dp + flat_ids // exp_dev) * most + pair_rank
    pair_count = tok_count * topk
    slot_count = exp_dev * n_dp * most
    slot_owner = (
        jnp.full((slot_count,), pair_count, jnp.int32)
        .at[pair_slot]
        .set(jnp.arange(pair_count, dtype=jnp.int32))
    )
    padded = jnp.concatenate([second_normalized, jnp.zeros((1, d_model), jnp.bfloat16)], axis=0)
    outgoing = padded[slot_owner // topk].reshape(exp_dev, n_dp, most, d_model)
    copies = jnp.broadcast_to(
        outgoing[:, :, None], (exp_dev, n_dp, n_tensor, most, d_model)
    ).reshape(exp_dev, devices, most, d_model)
    arrived = lax.all_to_all(copies, ("dp", "tensor"), split_axis=1, concat_axis=1, tiled=True)
    expert_rows = arrived.reshape(exp_dev, devices * most, d_model)
    gate_pre = jnp.einsum("erd,edf->erf", expert_rows, w_gate, preferred_element_type=jnp.float32)
    up_pre = jnp.einsum("erd,edf->erf", expert_rows, w_up, preferred_element_type=jnp.float32)
    gate_sigmoid = jax.nn.sigmoid(gate_pre)
    silu_gate = gate_pre * gate_sigmoid
    hidden = (silu_gate * up_pre).astype(jnp.bfloat16)
    partial_value = (
        jnp.einsum("erf,efd->erd", hidden, w_down, preferred_element_type=jnp.float32)
        .astype(jnp.bfloat16)
        .reshape(exp_dev, devices, most, d_model)
    )
    returned = lax.all_to_all(
        partial_value, ("dp", "tensor"), split_axis=1, concat_axis=1, tiled=True
    )
    expert_out = jnp.sum(
        returned.reshape(exp_dev, n_dp, n_tensor, most, d_model).astype(jnp.float32), axis=2
    ).reshape(slot_count, d_model)
    pair_out = expert_out[pair_slot].reshape(tok_count, topk, d_model)
    result = (hidden_after_attention + jnp.sum(gate_values[:, :, None] * pair_out, axis=1)).astype(
        jnp.bfloat16
    )
    cotangent = grad_output.astype(jnp.float32)
    grad_gates = jnp.sum(pair_out * cotangent[:, None, :], axis=-1)
    grad_pairs = (
        (gate_values[:, :, None] * cotangent[:, None, :])
        .astype(jnp.bfloat16)
        .reshape(pair_count, d_model)
    )
    grad_slots = jnp.concatenate([grad_pairs, jnp.zeros((1, d_model), jnp.bfloat16)], axis=0)[
        slot_owner
    ].reshape(exp_dev, n_dp, most, d_model)
    grad_copies = jnp.broadcast_to(
        grad_slots[:, :, None], (exp_dev, n_dp, n_tensor, most, d_model)
    ).reshape(exp_dev, devices, most, d_model)
    grad_arrived = lax.all_to_all(
        grad_copies, ("dp", "tensor"), split_axis=1, concat_axis=1, tiled=True
    )
    grad_rows = grad_arrived.reshape(exp_dev, devices * most, d_model)
    grad_hidden = jnp.einsum("erd,efd->erf", grad_rows, w_down, preferred_element_type=jnp.float32)
    grad_down = jnp.einsum("erf,erd->efd", hidden, grad_rows, preferred_element_type=jnp.float32)
    grad_gate_pre = (
        grad_hidden * up_pre * gate_sigmoid * (1.0 + gate_pre * (1.0 - gate_sigmoid))
    ).astype(jnp.bfloat16)
    grad_up_pre = (grad_hidden * silu_gate).astype(jnp.bfloat16)
    grad_gate = jnp.einsum(
        "erd,erf->edf", expert_rows, grad_gate_pre, preferred_element_type=jnp.float32
    )
    grad_up = jnp.einsum(
        "erd,erf->edf", expert_rows, grad_up_pre, preferred_element_type=jnp.float32
    )
    grad_expert_in = jnp.einsum(
        "erf,edf->erd", grad_gate_pre, w_gate, preferred_element_type=jnp.float32
    )
    grad_expert_in = grad_expert_in + jnp.einsum(
        "erf,edf->erd", grad_up_pre, w_up, preferred_element_type=jnp.float32
    )
    grad_expert_in = grad_expert_in.astype(jnp.bfloat16).reshape(exp_dev, devices, most, d_model)
    grad_back = lax.all_to_all(
        grad_expert_in, ("dp", "tensor"), split_axis=1, concat_axis=1, tiled=True
    )
    grad_slot_in = jnp.sum(
        grad_back.reshape(exp_dev, n_dp, n_tensor, most, d_model).astype(jnp.float32), axis=2
    ).reshape(slot_count, d_model)
    grad_second_normalized = jnp.sum(
        grad_slot_in[pair_slot].reshape(tok_count, topk, d_model), axis=1
    )
    grad_route = jnp.sum(jnp.where(chosen, grad_gates[:, :, None], 0.0), axis=1)
    grad_logits = (
        route_probs * (grad_route - jnp.sum(route_probs * grad_route, axis=-1, keepdims=True))
    ).astype(jnp.bfloat16)
    grad_router_part = jnp.einsum(
        "td,te->de", second_normalized, grad_logits, preferred_element_type=jnp.float32
    )
    grad_second_normalized = grad_second_normalized + jnp.einsum(
        "te,de->td", grad_logits, w_router, preferred_element_type=jnp.float32
    )
    grad_expert_share = jnp.sum(grad_second_normalized * second_unit_rows, axis=0)
    grad_second_unit_rows = grad_second_normalized * expert_norm_gain
    grad_hidden_one = (
        second_norm_scale
        * (
            grad_second_unit_rows
            - second_unit_rows
            * jnp.mean(grad_second_unit_rows * second_unit_rows, axis=-1, keepdims=True)
        )
        + cotangent
    )
    return (
        result,
        grad_hidden_one,
        grad_expert_share,
        grad_router_part,
        grad_gate,
        grad_up,
        grad_down,
    )


def experts_dense(
    hidden_after_attention,
    expert_ids,
    expert_norm_gain,
    w_router,
    w_gate,
    w_up,
    w_down,
    grad_output,
    all_cotangents,
):
    tok_count, d_model = hidden_after_attention.shape
    n_tensor = lax.axis_size("tensor")
    n_dp = lax.axis_size("dp")
    devices = n_dp * n_tensor
    everyone = ("dp", "tensor")
    second_norm_scale = root_mean_square_scale(hidden_after_attention)
    second_unit_rows = hidden_after_attention * second_norm_scale
    second_normalized = (second_unit_rows * expert_norm_gain).astype(jnp.bfloat16)
    experts = w_router.shape[1]
    exp_dev, _, width = w_gate.shape
    all_count = devices * tok_count
    expert_at = jnp.arange(experts, dtype=jnp.int32)

    chosen = jnp.any(expert_ids[:, :, None] == expert_at[None, None, :], axis=1)
    route_probs = jax.nn.softmax(
        jnp.dot(second_normalized, w_router, preferred_element_type=jnp.float32), axis=-1
    )
    gates = jnp.where(chosen, route_probs, 0.0).T
    all_rows, all_gates = gather_all(second_normalized, gates, n_tensor, 0)
    all_rows = all_rows.reshape(all_count, d_model)

    down_rows = w_down.reshape(exp_dev * width, d_model)
    wide = jnp.concatenate([w_gate[e] for e in range(exp_dev)] + [w_up[e] for e in range(exp_dev)], axis=1)
    local_gate = lax.dynamic_slice_in_dim(all_gates, lax.axis_index("dp") * exp_dev, exp_dev, axis=1)
    local_gate = local_gate.transpose(0, 2, 1).reshape(all_count, exp_dev)
    spread = jnp.repeat(local_gate, width, axis=1)
    both = exp_dev * width
    pre = jnp.dot(all_rows, wide, preferred_element_type=jnp.float32)
    gate_pre, up_pre = pre[:, :both], pre[:, both:]
    gate_sigmoid = jax.nn.sigmoid(gate_pre)
    silu_gate = gate_pre * gate_sigmoid
    hidden = silu_gate * up_pre
    gated_hidden = (spread * hidden).astype(jnp.bfloat16)
    lines = gated_hidden.reshape(n_dp, n_tensor * tok_count, both)

    def out_rows(places):
        picked = [
            lax.dynamic_index_in_dim(lines, lax.axis_index("dp") ^ k, axis=0, keepdims=False)
            for k in places
        ]
        return jnp.dot(
            jnp.concatenate(picked), down_rows, preferred_element_type=jnp.float32
        ).astype(jnp.bfloat16)

    back = jnp.einsum("td,fd->tf", all_cotangents, down_rows, preferred_element_type=jnp.float32)
    gate_grads = jnp.sum((hidden * back).reshape(all_count, exp_dev, width), axis=-1)
    grad_hidden = spread * back
    grad_gate_pre = (
        grad_hidden * up_pre * gate_sigmoid * (1.0 + gate_pre * (1.0 - gate_sigmoid))
    ).astype(jnp.bfloat16)
    grad_up_pre = (grad_hidden * silu_gate).astype(jnp.bfloat16)
    grad_pre = jnp.concatenate([grad_gate_pre, grad_up_pre], axis=1)
    in_part = jnp.einsum("tf,df->td", grad_pre, wide, preferred_element_type=jnp.float32).astype(jnp.bfloat16)
    spread = Spread(n_tensor, (tok_count, d_model))
    partner_rows = out_rows((1, 3, 5, 7))
    in_part, partner_rows = hold(in_part, partner_rows)
    theirs = spread.pair(out_rows((0, 2, 4, 6)), partner_rows)
    tiles = gate_grads.reshape(devices, tok_count, exp_dev).transpose(0, 2, 1)
    tiles = jnp.pad(tiles, ((0, 0), (0, 8 - exp_dev), (0, 0)))
    grad_in, gate_tiles = scatter_all(
        in_part.reshape(devices, tok_count, d_model), tiles, n_tensor, 1
    )
    grad_in, theirs = hold(grad_in, theirs)
    sides = spread.side(spread.sides(theirs))
    grad_down = jnp.einsum(
        "tf,td->fd", gated_hidden, all_cotangents, preferred_element_type=jnp.float32
    ).reshape(exp_dev, width, d_model)
    grad_wide = jnp.einsum("td,tf->df", all_rows, grad_pre, preferred_element_type=jnp.float32)
    grad_gate = jnp.stack([grad_wide[:, e * width : (e + 1) * width] for e in range(exp_dev)])
    grad_up = jnp.stack([grad_wide[:, both + e * width : both + (e + 1) * width] for e in range(exp_dev)])

    grad_route = jnp.sum(gate_tiles[:, :exp_dev].reshape(n_dp, n_tensor, exp_dev, tok_count), axis=1)
    grad_route = jnp.where(chosen, grad_route.reshape(experts, tok_count).T, 0.0)
    cotangent = grad_output.astype(jnp.float32)
    grad_logits = (
        route_probs * (grad_route - jnp.sum(route_probs * grad_route, axis=-1, keepdims=True))
    ).astype(jnp.bfloat16)
    grad_router_part = jnp.einsum(
        "td,te->de", second_normalized, grad_logits, preferred_element_type=jnp.float32
    )
    grad_second_normalized = grad_in + jnp.einsum(
        "te,de->td", grad_logits, w_router, preferred_element_type=jnp.float32
    )
    grad_expert_share = jnp.sum(grad_second_normalized * second_unit_rows, axis=0)
    grad_second_unit_rows = grad_second_normalized * expert_norm_gain
    grad_hidden_one = (
        second_norm_scale
        * (
            grad_second_unit_rows
            - second_unit_rows
            * jnp.mean(grad_second_unit_rows * second_unit_rows, axis=-1, keepdims=True)
        )
        + cotangent
    )
    return (
        spread,
        sides,
        grad_hidden_one,
        grad_expert_share,
        grad_router_part,
        grad_gate,
        grad_up,
        grad_down,
    )


def local_gathered(
    tokens,
    file_ids,
    expert_ids,
    attention_norm_gain,
    w_query,
    w_key,
    w_value,
    query_gain,
    key_gain,
    w_output,
    expert_norm_gain,
    w_router,
    w_gate,
    w_up,
    w_down,
    grad_output,
):
    tok_count, d_model = tokens.shape
    n_tensor = lax.axis_size("tensor")
    n_dp = lax.axis_size("dp")
    devices = n_dp * n_tensor
    local_dim = w_query.shape[1]
    head_dim = HEAD_DIM
    local_heads = local_dim // head_dim
    seq_len = tok_count * n_tensor
    block_rows = min(512, seq_len)
    score_scale = 1.0 / math.sqrt(head_dim)
    file_row = file_ids[0]
    cosine, sine_table = rope_tables(seq_len, head_dim)
    input_tensors = tokens.astype(jnp.float32)
    first_norm_scale = root_mean_square_scale(input_tensors)
    first_unit_rows = input_tensors * first_norm_scale
    first_normalized = (first_unit_rows * attention_norm_gain).astype(jnp.bfloat16)
    normed_all = line_gather(first_normalized, n_tensor, 2).reshape(seq_len, d_model)
    normed_all, later_cotangent = lax.optimization_barrier((normed_all, grad_output))
    all_cotangents = lax.all_gather(later_cotangent, ("dp", "tensor"), axis=0, tiled=True)
    query_raw = jnp.dot(normed_all, w_query, preferred_element_type=jnp.float32)
    key_raw = jnp.dot(normed_all, w_key, preferred_element_type=jnp.float32)
    value_rows = (
        jnp.dot(normed_all, w_value, preferred_element_type=jnp.float32)
        .astype(jnp.bfloat16)
        .reshape(seq_len, local_heads, head_dim)
    )
    query_total, key_total = line_total(
        jnp.stack([jnp.sum(query_raw * query_raw, axis=1), jnp.sum(key_raw * key_raw, axis=1)]), n_tensor, 6
    )
    query_scale = lax.rsqrt(query_total / d_model + EPSILON)[:, None]
    key_scale = lax.rsqrt(key_total / d_model + EPSILON)[:, None]
    query_hat = query_raw * query_scale
    key_hat = key_raw * key_scale
    queries = rotate(
        (query_hat * query_gain).reshape(seq_len, local_heads, head_dim), cosine, sine_table
    ).astype(jnp.bfloat16)
    key_rows = rotate(
        (key_hat * key_gain).reshape(seq_len, local_heads, head_dim), cosine, sine_table
    ).astype(jnp.bfloat16)
    block_start = 0
    scores = block_scores(queries, key_rows, file_row, block_start, score_scale)
    row_peak = jnp.max(scores, axis=-1, keepdims=True)
    log_total = row_peak + jnp.log(jnp.sum(jnp.exp(scores - row_peak), axis=-1, keepdims=True))
    attn_probs = jnp.exp(scores - log_total).astype(jnp.bfloat16)
    context_blocks = jnp.einsum(
        "hqk,khd->qhd", attn_probs, value_rows, preferred_element_type=jnp.float32
    )
    log_totals = [log_total]
    context = context_blocks.reshape(seq_len, local_dim).astype(jnp.bfloat16)
    attn_out = line_scatter(
        jnp.dot(context, w_output, preferred_element_type=jnp.float32)
        .astype(jnp.bfloat16)
        .reshape(n_tensor, tok_count, d_model),
        n_tensor,
        3,
    )
    hidden_after_attention = input_tensors + attn_out
    spread, sides, grad_hidden_one, grad_expert_share, grad_router_part, grad_gate, grad_up, grad_down = (
        experts_dense(
            hidden_after_attention,
            expert_ids,
            expert_norm_gain,
            w_router,
            w_gate,
            w_up,
            w_down,
            grad_output,
            all_cotangents,
        )
    )
    grad_attn = grad_hidden_one.astype(jnp.bfloat16)
    side_parts = jnp.concatenate([grad_router_part.T, grad_expert_share[None, :]])
    side_total = lax.psum(side_parts, ("dp", "tensor"))
    grad_attn_all = line_gather(grad_attn, n_tensor, 2)
    grad_attn_all, sides = hold(grad_attn_all, sides)
    sides = spread.last_side(sides)
    grad_attn_all = grad_attn_all.reshape(seq_len, d_model)
    grad_output_part = jnp.einsum(
        "sd,se->ed", context, grad_attn_all, preferred_element_type=jnp.float32
    )
    grad_context = (
        jnp.einsum("se,de->sd", grad_attn_all, w_output, preferred_element_type=jnp.float32)
        .astype(jnp.bfloat16)
        .reshape(seq_len, local_heads, head_dim)
    )
    grad_query_blocks = []
    grad_key_total = jnp.zeros((seq_len, local_heads, head_dim), jnp.float32)
    grad_value_total = jnp.zeros((seq_len, local_heads, head_dim), jnp.float32)
    for block_index, block_start in enumerate(range(0, seq_len, block_rows)):
        scores = block_scores(queries, key_rows, file_row, block_start, score_scale)
        probs_full = jnp.exp(scores - log_totals[block_index])
        probs_low = probs_full.astype(jnp.bfloat16)
        grad_value_total = jnp.einsum(
            "hqk,qhd->khd", probs_low, grad_context, preferred_element_type=jnp.float32
        )
        grad_probs = jnp.einsum(
            "qhd,khd->hqk", grad_context, value_rows, preferred_element_type=jnp.float32
        )
        row_shift = jnp.sum(probs_full * grad_probs, axis=-1, keepdims=True)
        grad_scores = (probs_full * (grad_probs - row_shift)).astype(jnp.bfloat16)
        grad_query_blocks.append(
            jnp.einsum("hqk,khd->qhd", grad_scores, key_rows, preferred_element_type=jnp.float32)
            * score_scale
        )
        grad_key_total = (
            jnp.einsum("hqk,qhd->khd", grad_scores, queries, preferred_element_type=jnp.float32)
            * score_scale
        )
    grad_query_normed = unrotate(grad_query_blocks[0], cosine, sine_table).reshape(
        seq_len, local_dim
    )
    grad_key_normed = unrotate(grad_key_total, cosine, sine_table).reshape(seq_len, local_dim)
    grad_qgain_part = jnp.sum(grad_query_normed * query_hat, axis=0)
    grad_kgain_part = jnp.sum(grad_key_normed * key_hat, axis=0)
    grad_query_hat = grad_query_normed * query_gain
    grad_key_hat = grad_key_normed * key_gain
    query_inner, key_inner = line_total(
        jnp.stack(
            [jnp.sum(grad_query_hat * query_hat, axis=1), jnp.sum(grad_key_hat * key_hat, axis=1)]
        ),
        n_tensor,
        6,
    )
    grad_query_raw = (
        query_scale * (grad_query_hat - query_hat * (query_inner / d_model)[:, None])
    ).astype(jnp.bfloat16)
    grad_key_raw = (key_scale * (grad_key_hat - key_hat * (key_inner / d_model)[:, None])).astype(
        jnp.bfloat16
    )
    grad_value_raw = grad_value_total.reshape(seq_len, local_dim).astype(jnp.bfloat16)
    grad_raw = jnp.concatenate([grad_query_raw, grad_key_raw, grad_value_raw], axis=1)
    grad_raw, sides = hold(grad_raw, sides)
    column = spread.column(sides)
    w_raw = jnp.concatenate([w_query, w_key, w_value], axis=1)
    raw_part = jnp.einsum("sd,sf->df", normed_all, grad_raw, preferred_element_type=jnp.float32)
    row_part = jnp.einsum("sf,df->sd", grad_raw, w_raw, preferred_element_type=jnp.float32)
    mine = (jnp.arange(n_tensor) == lax.axis_index("tensor"))[:, None]
    gain_parts = jnp.stack(
        [
            jnp.zeros((d_model,), jnp.float32),
            jnp.where(mine, grad_qgain_part[None, :], 0.0).reshape(-1),
            jnp.where(mine, grad_kgain_part[None, :], 0.0).reshape(-1),
            jnp.zeros((d_model,), jnp.float32),
        ]
    )
    gain_parts, column = hold(gain_parts, column)
    terms = spread.line(spread.blocks(column))
    finished = finish_sums(
        raw_part.astype(jnp.bfloat16).reshape(n_dp * PIECES, -1, 3 * local_dim),
        grad_output_part.astype(jnp.bfloat16).reshape(n_dp * PIECES, -1, local_dim),
        row_part.astype(jnp.bfloat16).reshape(n_tensor, tok_count, d_model),
        first_unit_rows,
        gain_parts.reshape(8, -1),
        n_tensor,
        PIECES,
        4,
    )
    finished, (terms, side_total) = hold(finished, (terms, side_total))
    total_query, total_key, total_value, total_output, grad_first_normalized, gain_totals = finished
    total_router, total_ffn_gain = side_total[:-1].T, side_total[-1]
    total_query, total_key, total_value, total_output = (
        total.reshape(d_model, local_dim).astype(jnp.float32)
        for total in (total_query, total_key, total_value, total_output)
    )
    total_output = total_output.T
    grad_first_unit_rows = grad_first_normalized * attention_norm_gain
    grad_tokens = (
        first_norm_scale
        * (
            grad_first_unit_rows
            - first_unit_rows
            * jnp.mean(grad_first_unit_rows * first_unit_rows, axis=-1, keepdims=True)
        )
        + grad_hidden_one
    ).astype(jnp.bfloat16)
    result = (hidden_after_attention + spread.total(terms)).astype(jnp.bfloat16)
    gain_totals = gain_totals.reshape(4, d_model)
    total_attn_gain = gain_totals[0]
    own_gains = lax.dynamic_slice_in_dim(
        gain_totals, lax.axis_index("tensor") * local_dim, local_dim, axis=1
    )
    total_qgain, total_kgain = own_gains[1], own_gains[2]
    return (
        result,
        grad_tokens,
        total_query,
        total_key,
        total_value,
        total_output,
        total_qgain,
        total_kgain,
        total_attn_gain,
        total_ffn_gain,
        total_router,
        grad_gate,
        grad_up,
        grad_down,
    )


def local_routed(
    tokens,
    file_ids,
    expert_ids,
    attention_norm_gain,
    w_query,
    w_key,
    w_value,
    query_gain,
    key_gain,
    w_output,
    expert_norm_gain,
    w_router,
    w_gate,
    w_up,
    w_down,
    grad_output,
):
    tok_count, d_model = tokens.shape
    n_tensor = lax.axis_size("tensor")
    n_dp = lax.axis_size("dp")
    devices = n_dp * n_tensor
    local_dim = w_query.shape[1]
    head_dim = HEAD_DIM
    local_heads = local_dim // head_dim
    seq_len = tok_count * n_tensor
    block_rows = min(512, seq_len)
    score_scale = 1.0 / math.sqrt(head_dim)
    file_row = file_ids[0]
    cosine, sine_table = rope_tables(seq_len, head_dim)
    input_tensors = tokens.astype(jnp.float32)
    first_norm_scale = root_mean_square_scale(input_tensors)
    first_unit_rows = input_tensors * first_norm_scale
    first_normalized = (first_unit_rows * attention_norm_gain).astype(jnp.bfloat16)
    normed_all = lax.all_gather(first_normalized, "tensor", axis=0, tiled=True)
    query_raw = jnp.dot(normed_all, w_query, preferred_element_type=jnp.float32)
    key_raw = jnp.dot(normed_all, w_key, preferred_element_type=jnp.float32)
    value_rows = (
        jnp.dot(normed_all, w_value, preferred_element_type=jnp.float32)
        .astype(jnp.bfloat16)
        .reshape(seq_len, local_heads, head_dim)
    )
    query_total, key_total = lax.psum(
        (jnp.sum(query_raw * query_raw, axis=1), jnp.sum(key_raw * key_raw, axis=1)), "tensor"
    )
    query_scale = lax.rsqrt(query_total / d_model + EPSILON)[:, None]
    key_scale = lax.rsqrt(key_total / d_model + EPSILON)[:, None]
    query_hat = query_raw * query_scale
    key_hat = key_raw * key_scale
    queries = rotate(
        (query_hat * query_gain).reshape(seq_len, local_heads, head_dim), cosine, sine_table
    ).astype(jnp.bfloat16)
    key_rows = rotate(
        (key_hat * key_gain).reshape(seq_len, local_heads, head_dim), cosine, sine_table
    ).astype(jnp.bfloat16)
    block_start = 0
    scores = block_scores(queries, key_rows, file_row, block_start, score_scale)
    row_peak = jnp.max(scores, axis=-1, keepdims=True)
    log_total = row_peak + jnp.log(jnp.sum(jnp.exp(scores - row_peak), axis=-1, keepdims=True))
    attn_probs = jnp.exp(scores - log_total).astype(jnp.bfloat16)
    context_blocks = jnp.einsum(
        "hqk,khd->qhd", attn_probs, value_rows, preferred_element_type=jnp.float32
    )
    log_totals = [log_total]
    context = context_blocks.reshape(seq_len, local_dim).astype(jnp.bfloat16)
    attn_out = lax.psum_scatter(
        jnp.dot(context, w_output, preferred_element_type=jnp.float32).astype(jnp.bfloat16),
        "tensor",
        scatter_dimension=0,
        tiled=True,
    ).astype(jnp.float32)
    hidden_after_attention = input_tensors + attn_out
    result, grad_hidden_one, grad_expert_share, grad_router_part, grad_gate, grad_up, grad_down = (
        experts_routed(
            hidden_after_attention,
            expert_ids,
            expert_norm_gain,
            w_router,
            w_gate,
            w_up,
            w_down,
            grad_output,
        )
    )
    grad_attn = grad_hidden_one.astype(jnp.bfloat16)
    grad_attn_all = lax.all_gather(grad_attn, "tensor", axis=0, tiled=True)
    grad_output_part = jnp.einsum(
        "sd,se->de", context, grad_attn_all, preferred_element_type=jnp.float32
    )
    grad_context = (
        jnp.einsum("se,de->sd", grad_attn_all, w_output, preferred_element_type=jnp.float32)
        .astype(jnp.bfloat16)
        .reshape(seq_len, local_heads, head_dim)
    )
    grad_query_blocks = []
    grad_key_total = jnp.zeros((seq_len, local_heads, head_dim), jnp.float32)
    grad_value_total = jnp.zeros((seq_len, local_heads, head_dim), jnp.float32)
    for block_index, block_start in enumerate(range(0, seq_len, block_rows)):
        scores = block_scores(queries, key_rows, file_row, block_start, score_scale)
        probs_full = jnp.exp(scores - log_totals[block_index])
        probs_low = probs_full.astype(jnp.bfloat16)
        grad_value_total = jnp.einsum(
            "hqk,qhd->khd", probs_low, grad_context, preferred_element_type=jnp.float32
        )
        grad_probs = jnp.einsum(
            "qhd,khd->hqk", grad_context, value_rows, preferred_element_type=jnp.float32
        )
        row_shift = jnp.sum(probs_full * grad_probs, axis=-1, keepdims=True)
        grad_scores = (probs_full * (grad_probs - row_shift)).astype(jnp.bfloat16)
        grad_query_blocks.append(
            jnp.einsum("hqk,khd->qhd", grad_scores, key_rows, preferred_element_type=jnp.float32)
            * score_scale
        )
        grad_key_total = (
            jnp.einsum("hqk,qhd->khd", grad_scores, queries, preferred_element_type=jnp.float32)
            * score_scale
        )
    grad_query_normed = unrotate(grad_query_blocks[0], cosine, sine_table).reshape(
        seq_len, local_dim
    )
    grad_key_normed = unrotate(grad_key_total, cosine, sine_table).reshape(seq_len, local_dim)
    grad_qgain_part = jnp.sum(grad_query_normed * query_hat, axis=0)
    grad_kgain_part = jnp.sum(grad_key_normed * key_hat, axis=0)
    grad_query_hat = grad_query_normed * query_gain
    grad_key_hat = grad_key_normed * key_gain
    query_inner, key_inner = lax.psum(
        (jnp.sum(grad_query_hat * query_hat, axis=1), jnp.sum(grad_key_hat * key_hat, axis=1)),
        "tensor",
    )
    grad_query_raw = (
        query_scale * (grad_query_hat - query_hat * (query_inner / d_model)[:, None])
    ).astype(jnp.bfloat16)
    grad_key_raw = (key_scale * (grad_key_hat - key_hat * (key_inner / d_model)[:, None])).astype(
        jnp.bfloat16
    )
    grad_value_raw = grad_value_total.reshape(seq_len, local_dim).astype(jnp.bfloat16)
    grad_query_part = jnp.einsum(
        "sd,sf->df", normed_all, grad_query_raw, preferred_element_type=jnp.float32
    )
    grad_key_part = jnp.einsum(
        "sd,sf->df", normed_all, grad_key_raw, preferred_element_type=jnp.float32
    )
    grad_value_part = jnp.einsum(
        "sd,sf->df", normed_all, grad_value_raw, preferred_element_type=jnp.float32
    )
    summed = jnp.einsum("sf,df->sd", grad_query_raw, w_query, preferred_element_type=jnp.float32)
    summed = summed + jnp.einsum(
        "sf,df->sd", grad_key_raw, w_key, preferred_element_type=jnp.float32
    )
    grad_first_normalized = lax.psum_scatter(
        (
            summed
            + jnp.einsum("sf,df->sd", grad_value_raw, w_value, preferred_element_type=jnp.float32)
        ).astype(jnp.bfloat16),
        "tensor",
        scatter_dimension=0,
        tiled=True,
    ).astype(jnp.float32)
    grad_attention_share = jnp.sum(grad_first_normalized * first_unit_rows, axis=0)
    grad_first_unit_rows = grad_first_normalized * attention_norm_gain
    grad_tokens = (
        first_norm_scale
        * (
            grad_first_unit_rows
            - first_unit_rows
            * jnp.mean(grad_first_unit_rows * first_unit_rows, axis=-1, keepdims=True)
        )
        + grad_hidden_one
    ).astype(jnp.bfloat16)
    total_query, total_key, total_value, total_output, total_qgain, total_kgain = (
        lax.psum(grad_query_part.astype(jnp.bfloat16), "dp").astype(jnp.float32),
        lax.psum(grad_key_part.astype(jnp.bfloat16), "dp").astype(jnp.float32),
        lax.psum(grad_value_part.astype(jnp.bfloat16), "dp").astype(jnp.float32),
        lax.psum(grad_output_part.astype(jnp.bfloat16), "dp").astype(jnp.float32),
        lax.psum(grad_qgain_part.astype(jnp.bfloat16), "dp").astype(jnp.float32),
        lax.psum(grad_kgain_part.astype(jnp.bfloat16), "dp").astype(jnp.float32),
    )
    total_attn_gain, total_ffn_gain, total_router = lax.psum(
        (grad_attention_share, grad_expert_share, grad_router_part), ("dp", "tensor")
    )
    return (
        result,
        grad_tokens,
        total_query,
        total_key,
        total_value,
        total_output,
        total_qgain,
        total_kgain,
        total_attn_gain,
        total_ffn_gain,
        total_router,
        grad_gate,
        grad_up,
        grad_down,
    )


def solution(mesh):
    return jax.shard_map(
        local_gathered if mesh.shape["dp"] == 8 else local_routed,
        mesh=mesh,
        in_specs=(
            P(("dp", "tensor"), None),
            P("dp", None),
            P(("dp", "tensor"), None),
            P(),
            P(None, "tensor"),
            P(None, "tensor"),
            P(None, "tensor"),
            P("tensor"),
            P("tensor"),
            P("tensor", None),
            P(),
            P(),
            P("dp", None, "tensor"),
            P("dp", None, "tensor"),
            P("dp", "tensor", None),
            P(("dp", "tensor"), None),
        ),
        out_specs=(
            P(("dp", "tensor"), None),
            P(("dp", "tensor"), None),
            P(None, "tensor"),
            P(None, "tensor"),
            P(None, "tensor"),
            P("tensor", None),
            P("tensor"),
            P("tensor"),
            P(),
            P(),
            P(),
            P("dp", None, "tensor"),
            P("dp", None, "tensor"),
            P("dp", "tensor", None),
        ),
        check_vma=False,
    )
```

```python
import functools
import math

import jax
import jax.numpy as jnp
from jax import lax
from jax.experimental import pallas as pl
from jax.experimental.pallas import tpu as pltpu
from jax.sharding import PartitionSpec as P

HEAD_DIM = 128


EPSILON = 1e-05
THETA = 10000.0
NEG_LARGE = -1e30


def root_mean_square_scale(values):
    return lax.rsqrt(jnp.mean(values * values, axis=-1, keepdims=True) + EPSILON)


def rope_tables(length, head_dim):
    half_dim = head_dim // 2
    freq_index = jnp.arange(half_dim, dtype=jnp.float32)
    frequency = THETA ** (-(2.0 * freq_index) / head_dim)
    angles = jnp.arange(length, dtype=jnp.float32)[:, None] * frequency[None, :]
    cosine = jnp.concatenate([jnp.cos(angles), jnp.cos(angles)], axis=1)
    sine_table = jnp.concatenate([jnp.sin(angles), jnp.sin(angles)], axis=1)
    return (cosine[:, None, :], sine_table[:, None, :])


def rotate(values, cosine, sine_table):
    half_dim = values.shape[-1] // 2
    turned = jnp.concatenate([-values[..., half_dim:], values[..., :half_dim]], axis=-1)
    return values * cosine + turned * sine_table


def unrotate(grad_rows, cosine, sine_table):
    half_dim = grad_rows.shape[-1] // 2
    scaled = grad_rows * sine_table
    turned = jnp.concatenate([scaled[..., half_dim:], -scaled[..., :half_dim]], axis=-1)
    return grad_rows * cosine + turned


def slot_positions(ids, experts):
    flat_ids = ids.reshape(-1)
    onehot = (flat_ids[:, None] == jnp.arange(experts, dtype=jnp.int32)[None, :]).astype(jnp.int32)
    running = jnp.cumsum(onehot, axis=0)
    return (flat_ids, jnp.sum(running * onehot, axis=1) - 1)


def block_scores(query_block, key_rows, file_row, block_start, score_scale):
    block_rows = query_block.shape[0]
    raw_scores = (
        jnp.einsum("qhd,khd->hqk", query_block, key_rows, preferred_element_type=jnp.float32)
        * score_scale
    )
    rows_at = block_start + jnp.arange(block_rows, dtype=jnp.int32)
    cols_at = jnp.arange(key_rows.shape[0], dtype=jnp.int32)
    allowed = (cols_at[None, :] <= rows_at[:, None]) & (file_row[None, :] == file_row[:, None])
    return jnp.where(allowed[None], raw_scores, NEG_LARGE)


MESH = pl.DeviceIdType.MESH
VMEM_LIMIT = 60 * 2**20


def greet(dp, z, nz):
    barrier = pltpu.get_barrier_semaphore()
    for flip in (1, 2, 4):
        pl.semaphore_signal(barrier, 1, device_id=(dp ^ flip, z), device_id_type=MESH)

    @pl.when(z > 0)
    def _():
        pl.semaphore_signal(barrier, 1, device_id=(dp, z - 1), device_id_type=MESH)

    @pl.when(z < nz - 1)
    def _():
        pl.semaphore_signal(barrier, 1, device_id=(dp, z + 1), device_id_type=MESH)

    ends = jnp.where(z > 0, 1, 0) + jnp.where(z < nz - 1, 1, 0)
    pl.semaphore_wait(barrier, 3 + ends)


def remote(src, dst, send, recv, device):
    return pltpu.make_async_remote_copy(
        src_ref=src, dst_ref=dst, send_sem=send, recv_sem=recv, device_id=device, device_id_type=MESH
    )


def experts_kernel(nz, x_ref, t_ref, g_ref, wide_ref, down_ref, rows_ref, slopes_ref, gated_ref, tiles_ref, land, tags, g_buf, pre, back, gate_at, grad_at, local_sem, s_rows, s_g, sz, sx, sy, sda, sdb, sc, rz, rx, ry, rda, rdb, rc):
    dp, z = lax.axis_index("dp"), lax.axis_index("tensor")
    count, width = x_ref.shape
    half = count // 2
    both = back.shape[1]
    each = both // gate_at.shape[0]
    other = (dp ^ 1, z)

    def rows_at(flip, zz):
        place = dp ^ flip
        return land.at[place // 2, zz, pl.ds(pl.multiple_of((place % 2) * count, count), count)]

    def half_at(flip, zz, k):
        place = dp ^ flip
        return land.at[place // 2, zz, pl.ds(pl.multiple_of((place % 2) * count + k * half, half), half)]

    def tags_at(flip, zz):
        return tags.at[(dp ^ flip) * nz + zz]

    def whole(flip, zz, send, recv, device):
        return (
            remote(rows_at(flip, zz), rows_at(flip, zz), send(0), recv(0), device),
            remote(tags_at(flip, zz), tags_at(flip, zz), send(1), recv(1), device),
        )

    def z_copy(zz, step):
        return whole(0, zz, lambda k: sz.at[k, (step + 1) // 2, zz], lambda k: rz.at[k, zz], (dp, z + step))

    def x_copy(zz):
        return whole(0, zz, lambda k: sx.at[k, zz], lambda k: rx.at[k, zz], (dp ^ 2, z))

    def y_copy(zz):
        return whole(0, zz, lambda k: sy.at[k, zz], lambda k: ry.at[k, zz], (dp ^ 4, z))

    def a_copy(zz):
        return (
            remote(half_at(4, zz, 0), half_at(4, zz, 0), sda.at[0, zz], rda.at[0, zz], (dp ^ 2, z)),
            remote(tags_at(4, zz), tags_at(4, zz), sda.at[1, zz], rda.at[1, zz], (dp ^ 2, z)),
        )

    def b_copy(zz):
        return (remote(half_at(2, zz, 1), half_at(2, zz, 1), sdb.at[zz], rdb.at[zz], (dp ^ 4, z)),)

    def c_copy(kind, zz):
        send, recv = (lambda k: sc.at[k, kind, zz]), (lambda k: rc.at[k, kind, zz])
        if kind < 3:
            return whole((0, 2, 4)[kind], zz, send, recv, other)
        ref = half_at(6, zz, kind - 3)
        copies = (remote(ref, ref, send(0), recv(0), other),)
        if kind == 3:
            copies += (remote(tags_at(6, zz), tags_at(6, zz), send(1), recv(1), other),)
        return copies

    def start(copies):
        for copy in copies:
            copy.start()

    def arrived(ref, sem):
        remote(ref, ref, sem, sem, other).wait_recv()

    def both_arrived(flip, zz, recv):
        arrived(rows_at(flip, zz), recv(0))
        arrived(tags_at(flip, zz), recv(1))

    def held(distance, zz, sign):
        inside = (distance >= 0) & (distance < nz) & (zz >= 0) & (zz < nz)
        return inside & ((distance > 0) | (sign > 0))

    def spread(distance):
        for sign in (1, -1):
            zz = z + sign * distance

            @pl.when(held(distance, zz, sign))
            def _():
                @pl.when(distance > 0)
                def _():
                    both_arrived(0, zz, lambda k: rz.at[k, zz])

                @pl.when((zz <= z) & (z < nz - 1))
                def _():
                    start(z_copy(zz, 1))

                @pl.when((zz >= z) & (z > 0))
                def _():
                    start(z_copy(zz, -1))

                start(x_copy(zz))
                start(y_copy(zz))
                start(c_copy(0, zz))

    def relay(distance):
        for sign in (1, -1):
            zz = z + sign * distance

            @pl.when(held(distance, zz, sign))
            def _():
                both_arrived(4, zz, lambda k: ry.at[k, zz])
                start(a_copy(zz))
                start(c_copy(2, zz))
                both_arrived(2, zz, lambda k: rx.at[k, zz])
                start(b_copy(zz))
                start(c_copy(1, zz))

    def corner(distance):
        for sign in (1, -1):
            zz = z + sign * distance

            @pl.when(held(distance, zz, sign))
            def _():
                arrived(half_at(6, zz, 0), rda.at[0, zz])
                arrived(tags_at(6, zz), rda.at[1, zz])
                start(c_copy(3, zz))
                arrived(half_at(6, zz, 1), rdb.at[zz])
                start(c_copy(4, zz))

    def store_rows(chip, zz):
        return pltpu.make_async_copy(land.at[chip, zz], rows_ref.at[chip, zz], s_rows.at[chip, zz])

    def load_g(chip, zz, c):
        return pltpu.make_async_copy(
            g_ref.at[(2 * chip + c) * nz + zz], g_buf.at[pl.ds(c * count, count)], s_g.at[c]
        )

    diagonal = (
        lax.broadcasted_iota(jnp.int32, (count, count), 0) == lax.broadcasted_iota(jnp.int32, (count, count), 1)
    ).astype(jnp.float32)

    def experts(chip, zz):
        store_rows(chip, zz).start()
        for c in range(2):
            load_g(chip, zz, c).start()
        x = land.at[chip, zz]

        def product(k, carry):
            at = pl.ds(pl.multiple_of(k * 256, 256), 256)
            pre[:, at] = jnp.dot(x[...], wide_ref[:, at], preferred_element_type=jnp.float32)
            return carry

        lax.fori_loop(0, 2 * both // 256, product, 0, unroll=True)
        for j in range(gate_at.shape[0]):
            for c in range(2):
                row = tags[(2 * chip + c) * nz + zz, pl.ds(dp * gate_at.shape[0] + j, 1), :]
                column = jnp.sum(diagonal * row, axis=1, keepdims=True)
                gate_at[j, pl.ds(c * count, count), :] = jnp.broadcast_to(column, (count, 128))
        for c in range(2):
            load_g(chip, zz, c).wait()

        def back_product(k, carry):
            at = pl.ds(pl.multiple_of(k * 256, 256), 256)
            back[:, at] = jnp.dot(g_buf[...], down_ref[:, at], preferred_element_type=jnp.float32)
            return carry

        lax.fori_loop(0, both // 256, back_product, 0, unroll=True)

        def elementwise(k, carry):
            at = pl.ds(pl.multiple_of(k * 64, 64), 64)
            for j in range(gate_at.shape[0]):
                cols, up_cols = pl.ds(j * each, each), pl.ds(both + j * each, each)
                gate = jnp.concatenate([gate_at[j, at, :]] * (each // 128), axis=1)
                gate_pre, up_pre, grad = pre[at, cols], pre[at, up_cols], back[at, cols]
                sigmoid = 1.0 / (1.0 + jnp.exp(-gate_pre))
                silu = gate_pre * sigmoid
                hidden = silu * up_pre
                gated_ref[chip, zz, at, cols] = (gate * hidden).astype(gated_ref.dtype)
                share = jnp.sum(hidden * grad, axis=1, keepdims=True)
                grad_at[j, at, :] = jnp.broadcast_to(share, (64, 128))
                slope = gate * grad
                slopes_ref[chip, zz, at, cols] = (
                    slope * up_pre * sigmoid * (1.0 + gate_pre * (1.0 - sigmoid))
                ).astype(slopes_ref.dtype)
                slopes_ref[chip, zz, at, up_cols] = (slope * silu).astype(slopes_ref.dtype)
            return carry

        lax.fori_loop(0, 2 * count // 64, elementwise, 0)
        for c in range(2):
            shares = [
                jnp.sum(diagonal * grad_at[j, pl.ds(c * count, count), :], axis=0, keepdims=True)
                for j in range(gate_at.shape[0])
            ]
            shares.append(jnp.zeros((8 - len(shares), count), jnp.float32))
            tiles_ref[(2 * chip + c) * nz + zz] = jnp.concatenate(shares, axis=0)

    def job(step, k):
        kind, sign = k // 2, 1 - 2 * (k % 2)
        distance = step - 1 - (kind + 1) // 2
        zz = z + sign * distance
        flip = 2 * kind

        @pl.when(held(distance, zz, sign))
        def _():
            @pl.when(kind < 3)
            def _():
                both_arrived(flip + 1, zz, lambda m: rc.at[m, kind, zz])

            @pl.when(kind == 3)
            def _():
                arrived(half_at(7, zz, 0), rc.at[0, 3, zz])
                arrived(tags_at(7, zz), rc.at[1, 3, zz])
                arrived(half_at(7, zz, 1), rc.at[0, 4, zz])

            experts((dp ^ flip) // 2, zz)

    keep = pltpu.make_async_copy(x_ref, rows_at(0, z), local_sem.at[0])
    keep_tags = pltpu.make_async_copy(t_ref, tags_at(0, z), local_sem.at[1])
    keep.start()
    keep_tags.start()
    greet(dp, z, nz)
    keep.wait()
    keep_tags.wait()

    def step_body(step, carry):
        spread(step)
        relay(step - 1)
        corner(step - 2)

        def inner(k, inner_carry):
            job(step, k)
            return inner_carry

        lax.fori_loop(0, 8, inner, 0)
        return carry

    lax.fori_loop(0, nz + 3, step_body, 0)

    def sent(copies):
        for copy in copies:
            copy.wait_send()

    for zz in range(nz):

        @pl.when((zz <= z) & (z < nz - 1))
        def _():
            sent(z_copy(zz, 1))

        @pl.when((zz >= z) & (z > 0))
        def _():
            sent(z_copy(zz, -1))

        sent(x_copy(zz))
        sent(y_copy(zz))
        sent(a_copy(zz))
        sent(b_copy(zz))
        for kind in range(5):
            sent(c_copy(kind, zz))
        for chip in range(4):
            store_rows(chip, zz).wait()


def gather_experts(x, gates, cotangents, wide, down, experts_here, nz, collective_id):
    rows, width = x.shape
    both = down.shape[1]
    dma, vmem = pltpu.SemaphoreType.DMA, pl.BlockSpec(memory_space=pltpu.VMEM)
    any_place = pl.BlockSpec(memory_space=pl.ANY)
    group = (4, nz, 2 * rows)
    flops = 2 * 8 * nz * rows * width * 3 * both
    return pl.pallas_call(
        functools.partial(experts_kernel, nz),
        name="gather_experts",
        out_shape=(
            jax.ShapeDtypeStruct(group + (width,), x.dtype),
            jax.ShapeDtypeStruct(group + (2 * both,), x.dtype),
            jax.ShapeDtypeStruct(group + (both,), x.dtype),
            jax.ShapeDtypeStruct((8 * nz, 8, rows), jnp.float32),
        ),
        in_specs=[vmem, vmem, any_place, vmem, vmem],
        out_specs=(any_place, vmem, vmem, vmem),
        scratch_shapes=[
            pltpu.VMEM(group + (width,), x.dtype),
            pltpu.VMEM((8 * nz,) + gates.shape, gates.dtype),
            pltpu.VMEM((2 * rows, width), x.dtype),
            pltpu.VMEM((2 * rows, 2 * both), jnp.float32),
            pltpu.VMEM((2 * rows, both), jnp.float32),
            pltpu.VMEM((experts_here, 2 * rows, 128), jnp.float32),
            pltpu.VMEM((experts_here, 2 * rows, 128), jnp.float32),
            dma((2,)),
            dma((4, nz)),
            dma((2,)),
        ]
        + [dma((2, 2, nz)), dma((2, nz)), dma((2, nz)), dma((2, nz)), dma((nz,)), dma((2, 5, nz))]
        + [dma((2, nz)), dma((2, nz)), dma((2, nz)), dma((2, nz)), dma((nz,)), dma((2, 5, nz))],
        compiler_params=pltpu.CompilerParams(
            collective_id=collective_id, has_side_effects=True, vmem_limit_bytes=VMEM_LIMIT
        ),
        cost_estimate=pl.CostEstimate(flops=flops, bytes_accessed=64 * 2**20, transcendentals=0),
    )(x, gates, cotangents, wide, down)


def greet_line(dp, z, nz):
    barrier = pltpu.get_barrier_semaphore()

    @pl.when(z > 0)
    def _():
        pl.semaphore_signal(barrier, 1, device_id=(dp, z - 1), device_id_type=MESH)

    @pl.when(z < nz - 1)
    def _():
        pl.semaphore_signal(barrier, 1, device_id=(dp, z + 1), device_id_type=MESH)

    pl.semaphore_wait(barrier, jnp.where(z > 0, 1, 0) + jnp.where(z < nz - 1, 1, 0))


PARTS = 2
PIECES = 2


def greet_total(dp, z, nz):
    barrier = pltpu.get_barrier_semaphore()
    for flip in (1, 2, 4):
        pl.semaphore_signal(barrier, 1, device_id=(dp ^ flip, z), device_id_type=MESH)
    for turn in range(1, nz):
        pl.semaphore_signal(barrier, 1, device_id=(dp, lax.rem(z + turn, nz)), device_id_type=MESH)
    pl.semaphore_wait(barrier, 2 + nz)


class Total:
    steps = 5

    def __init__(self, nz, dp, z, got, s_plane, r_plane, s_line, r_line):
        self.nz, self.z, self.got = nz, z, got
        self.plane = [
            remote(got.at[2 * k], got.at[2 * k + 1], s_plane.at[k], r_plane.at[k], (dp ^ flip, z))
            for k, flip in enumerate((1, 2, 4))
        ]
        self.line = [
            remote(got.at[6], got.at[6 + turn], s_line.at[turn - 1], r_line.at[turn - 1], (dp, lax.rem(z + turn, nz)))
            for turn in range(1, nz)
        ]

    def step(self, k, out_ref):
        got, nz = self.got, self.nz
        if 1 <= k <= 3:
            self.plane[k - 1].wait()
            got[2 * k] = got[2 * k - 2] + got[2 * k - 1]
        if k < 3:
            self.plane[k].start()
        elif k == 3:
            for copy in self.line:
                copy.start()
        else:
            for copy in self.line:
                copy.wait()
            total = got[6 + lax.rem(self.z, nz)]
            for zz in range(1, nz):
                total = total + got[6 + lax.rem(self.z - zz + nz, nz)]
            out_ref[...] = total


def total_scratch(nz, shape, dtype):
    dma = pltpu.SemaphoreType.DMA
    return [pltpu.VMEM((6 + nz,) + shape, dtype), dma((3,)), dma((3,)), dma((nz - 1,)), dma((nz - 1,))]


def line_gather_kernel(nz, *refs):
    dp, z = lax.axis_index("dp"), lax.axis_index("tensor")
    summed = len(refs) > 6
    if summed:
        x_ref, small_ref, out_ref, total_ref, local_sem, s_up, s_down, r_line = refs[:8]
        greet_total(dp, z, nz)
        total = Total(nz, dp, z, *refs[8:])
        total.got[0] = small_ref[...]
    else:
        x_ref, out_ref, local_sem, s_up, s_down, r_line = refs
        greet_line(dp, z, nz)
    part = x_ref.shape[0] // PARTS

    def copy(zz, k, step, own):
        at = pl.ds(k * part, part)
        dst = out_ref.at[zz, at]
        sems = s_up if step > 0 else s_down
        return remote(x_ref.at[at] if own else dst, dst, sems.at[zz, k], r_line.at[zz, k], (dp, z + step))

    keep = pltpu.make_async_copy(x_ref, out_ref.at[z], local_sem)
    for distance in range(nz):
        for k in range(PARTS):
            for sign in (0,) if distance == 0 else (-1, 1):
                zz, own = z + sign * distance, distance == 0

                @pl.when((zz >= 0) & (zz < nz))
                def _():
                    if not own:
                        copy(zz, k, 1, False).wait_recv()
                    if sign <= 0:

                        @pl.when(z < nz - 1)
                        def _():
                            copy(zz, k, 1, own).start()

                    if sign >= 0:

                        @pl.when(z > 0)
                        def _():
                            copy(zz, k, -1, own).start()

        if distance == 0:
            keep.start()
        if summed:
            total.step(distance, total_ref)
    if summed:
        for k in range(nz, Total.steps):
            total.step(k, total_ref)
    keep.wait()
    for zz in range(nz):
        for k in range(PARTS):

            @pl.when((zz <= z) & (z < nz - 1))
            def _():
                copy(zz, k, 1, False).wait_send()

            @pl.when((zz >= z) & (z > 0))
            def _():
                copy(zz, k, -1, False).wait_send()


def line_gather(x, nz, collective_id, small=None):
    dma, vmem = pltpu.SemaphoreType.DMA, pl.BlockSpec(memory_space=pltpu.VMEM)
    blocks = jax.ShapeDtypeStruct((nz,) + x.shape, x.dtype)
    scratch = [dma(())] + [dma((nz, PARTS)) for _ in range(3)]
    params = pltpu.CompilerParams(
        collective_id=collective_id, has_side_effects=True, vmem_limit_bytes=8 * 2**20
    )
    kernel = functools.partial(line_gather_kernel, nz)
    if small is None:
        return pl.pallas_call(
            kernel,
            name="line_gather",
            out_shape=blocks,
            in_specs=[vmem],
            out_specs=pl.BlockSpec(memory_space=pl.ANY),
            scratch_shapes=scratch,
            compiler_params=params,
        )(x)
    return pl.pallas_call(
        kernel,
        name="line_gather_total",
        out_shape=(blocks, jax.ShapeDtypeStruct(small.shape, small.dtype)),
        in_specs=[vmem, vmem],
        out_specs=(pl.BlockSpec(memory_space=pl.ANY), vmem),
        scratch_shapes=scratch + total_scratch(nz, small.shape, small.dtype),
        compiler_params=params,
    )(x, small)


def line_total_kernel(nz, x_ref, out_ref, got, send, recv):
    dp, z = lax.axis_index("dp"), lax.axis_index("tensor")
    others = [lax.rem(z + turn, nz) for turn in range(1, nz)]
    barrier = pltpu.get_barrier_semaphore()
    for other in others:
        pl.semaphore_signal(barrier, 1, device_id=(dp, other), device_id_type=MESH)
    pl.semaphore_wait(barrier, nz - 1)
    copies = [
        remote(x_ref, got.at[turn], send.at[turn], recv.at[turn], (dp, other)) for turn, other in enumerate(others)
    ]
    for copy in copies:
        copy.start()
    for copy in copies:
        copy.wait()
    total = x_ref[...]
    for turn in range(nz - 1):
        total = total + got[turn]
    out_ref[...] = total


def line_total(x, nz, collective_id):
    dma, vmem = pltpu.SemaphoreType.DMA, pl.BlockSpec(memory_space=pltpu.VMEM)
    return pl.pallas_call(
        functools.partial(line_total_kernel, nz),
        name="line_total",
        out_shape=jax.ShapeDtypeStruct(x.shape, x.dtype),
        in_specs=[vmem],
        out_specs=vmem,
        scratch_shapes=[pltpu.VMEM((nz - 1,) + x.shape, x.dtype), dma((nz - 1,)), dma((nz - 1,))],
        compiler_params=pltpu.CompilerParams(
            collective_id=collective_id, has_side_effects=True, vmem_limit_bytes=4 * 2**20
        ),
    )(x)


CHUNK = 16


def add_rows(dst, *others, start=0, count):
    def body(k, carry):
        at = pl.ds(start + k * CHUNK, CHUNK)
        total = dst[at, :].astype(jnp.float32)
        for ref, base in others:
            total = total + ref[pl.ds(base + k * CHUNK, CHUNK), :].astype(jnp.float32)
        dst[at, :] = total.astype(dst.dtype)
        return carry

    lax.fori_loop(0, count // CHUNK, body, 0)


class Line:
    def __init__(self, nz, dp, z, acc, up, down, s_up, r_up, s_down, r_down):
        self.nz, self.dp, self.z, self.acc, self.up, self.down = nz, dp, z, acc, up, down
        self.sems = s_up, r_up, s_down, r_down
        self.part = acc.shape[1] // PARTS

    def copy(self, zz, k, step):
        at = pl.ds(k * self.part, self.part)
        s_up, r_up, s_down, r_down = self.sems
        if step > 0:
            return remote(self.acc.at[zz, at], self.up.at[zz, at], s_up.at[zz, k], r_up.at[zz, k], (self.dp, self.z + 1))
        return remote(self.acc.at[zz, at], self.down.at[zz, at], s_down.at[zz, k], r_down.at[zz, k], (self.dp, self.z - 1))

    def first(self):
        nz, z = self.nz, self.z

        @pl.when(z == 0)
        def _():
            for zz in range(nz - 1, 0, -1):
                for k in range(PARTS):
                    self.copy(zz, k, 1).start()

        @pl.when(z == nz - 1)
        def _():
            for zz in range(nz - 1):
                for k in range(PARTS):
                    self.copy(zz, k, -1).start()

    def step(self, distance):
        nz, z = self.nz, self.z
        for k in range(PARTS):
            for sign in (1, -1):
                far = nz - distance if sign > 0 else distance - 1
                through = (far > z) & (z > 0) if sign > 0 else (far < z) & (z < nz - 1)

                @pl.when(through)
                def _():
                    self.copy(far, k, sign).wait_recv()
                    source = self.up if sign > 0 else self.down
                    add_rows(self.acc.at[far], (source.at[far], k * self.part), start=k * self.part, count=self.part)
                    self.copy(far, k, sign).start()

    def finish(self, out_ref):
        nz, z = self.nz, self.z
        for k in range(PARTS):

            @pl.when(z > 0)
            def _():
                self.copy(z, k, 1).wait_recv()

            @pl.when(z < nz - 1)
            def _():
                self.copy(z, k, -1).wait_recv()

        def body(k, carry):
            at = pl.ds(k * CHUNK, CHUNK)
            total = self.acc[z, at, :].astype(jnp.float32)
            zero = jnp.zeros_like(total)
            total = total + jnp.where(z > 0, self.up[z, at, :].astype(jnp.float32), zero)
            total = total + jnp.where(z < nz - 1, self.down[z, at, :].astype(jnp.float32), zero)
            out_ref[at, :] = total
            return carry

        lax.fori_loop(0, out_ref.shape[0] // CHUNK, body, 0)

    def drain(self):
        nz, z = self.nz, self.z
        for zz in range(nz):
            for k in range(PARTS):

                @pl.when(zz > z)
                def _():
                    self.copy(zz, k, 1).wait_send()

                @pl.when(zz < z)
                def _():
                    self.copy(zz, k, -1).wait_send()


def line_scatter_kernel(nz, p_ref, out_ref, acc, up, down, local_sem, s_up, r_up, s_down, r_down):
    dp, z = lax.axis_index("dp"), lax.axis_index("tensor")
    loaded = pltpu.make_async_copy(p_ref, acc, local_sem)
    loaded.start()
    greet_line(dp, z, nz)
    loaded.wait()
    line = Line(nz, dp, z, acc, up, down, s_up, r_up, s_down, r_down)
    line.first()
    for distance in range(1, nz - 1):
        line.step(distance)
    line.finish(out_ref)
    line.drain()


def line_scatter(p, nz, collective_id):
    _, rows, width = p.shape
    dma, vmem = pltpu.SemaphoreType.DMA, functools.partial(pltpu.VMEM, dtype=p.dtype)
    return pl.pallas_call(
        functools.partial(line_scatter_kernel, nz),
        name="line_scatter",
        out_shape=jax.ShapeDtypeStruct((rows, width), jnp.float32),
        in_specs=[pl.BlockSpec(memory_space=pl.ANY)],
        out_specs=pl.BlockSpec(memory_space=pltpu.VMEM),
        scratch_shapes=[vmem((nz, rows, width)) for _ in range(3)]
        + [dma(())]
        + [dma((nz, PARTS)) for _ in range(4)],
        compiler_params=pltpu.CompilerParams(
            collective_id=collective_id, has_side_effects=True, vmem_limit_bytes=16 * 2**20
        ),
    )(p)


def z_order(nz):
    return [sorted(range(nz), key=lambda zz: (-abs(zz - z), zz if z >= nz // 2 else -zz)) for z in range(nz)]


def scatter_kernel(nz, p_ref, t_ref, out_ref, tiles_ref, acc, rc, ra, rb, rx, ry, ru, rd, s_tile, r_tile, s_keep, s_local, s_core, r_core, s_a, r_a, s_b, r_b, s_x, r_x, s_y, r_y, s_u, r_u, s_d, r_d):
    dp, z = lax.axis_index("dp"), lax.axis_index("tensor")
    rows = acc.shape[2]
    half = rows // 2
    order = z_order(nz)

    def place(i):
        zz = order[0][i]
        for zv in range(1, nz):
            zz = jnp.where(z == zv, order[zv][i], zz)
        return zz

    def block_of(place, zz):
        return p_ref.at[(place // 2 * nz + zz) * 2 + place % 2]

    flips = (0, 2, 4, 6)

    def load(kind, zz):
        return pltpu.make_async_copy(
            block_of(dp ^ flips[kind], zz), acc.at[kind, zz], s_local.at[kind, zz]
        )

    def core_copy(kind, zz):
        return remote(
            block_of(dp ^ flips[kind] ^ 1, zz), rc.at[kind, zz], s_core.at[kind, zz], r_core.at[kind, zz], (dp ^ 1, z)
        )

    def a_copy(zz):
        return remote(acc.at[3, zz, pl.ds(0, half)], ra.at[zz], s_a.at[zz], r_a.at[zz], (dp ^ 2, z))

    def b_copy(zz):
        return remote(acc.at[3, zz, pl.ds(half, half)], rb.at[zz], s_b.at[zz], r_b.at[zz], (dp ^ 4, z))

    def x_copy(zz):
        return remote(acc.at[1, zz], rx.at[zz], s_x.at[zz], r_x.at[zz], (dp ^ 2, z))

    def y_copy(zz):
        return remote(acc.at[2, zz], ry.at[zz], s_y.at[zz], r_y.at[zz], (dp ^ 4, z))

    def up_copy(zz):
        return remote(acc.at[0, zz], ru.at[zz], s_u.at[zz], r_u.at[zz], (dp, z + 1))

    def down_copy(zz):
        return remote(acc.at[0, zz], rd.at[zz], s_d.at[zz], r_d.at[zz], (dp, z - 1))

    def add(dst, *others, start=0, count=rows):
        add_rows(dst, *others, start=start, count=count)

    def wave(i):
        zz = place(i)
        for kind in (3, 1, 2, 0):
            core_copy(kind, zz).start()
            load(kind, zz).start()

    def paired(kind, zz):
        load(kind, zz).wait()
        core_copy(kind, zz).wait_recv()

    def stage_diagonal(i):
        zz = place(i)
        paired(3, zz)
        add(acc.at[3, zz], (rc.at[3, zz], 0))
        a_copy(zz).start()
        b_copy(zz).start()

    def stage_side(i):
        zz = place(i)
        paired(1, zz)
        paired(2, zz)
        a_copy(zz).wait_recv()
        add(acc.at[2, zz], (rc.at[2, zz], 0), (ra.at[zz], 0), start=0, count=half)
        add(acc.at[2, zz], (rc.at[2, zz], half), start=half, count=half)
        y_copy(zz).start()
        b_copy(zz).wait_recv()
        add(acc.at[1, zz], (rc.at[1, zz], half), (rb.at[zz], 0), start=half, count=half)
        add(acc.at[1, zz], (rc.at[1, zz], 0), start=0, count=half)
        x_copy(zz).start()

    def stage_column(i):
        zz = place(i)
        paired(0, zz)
        x_copy(zz).wait_recv()
        y_copy(zz).wait_recv()
        add(acc.at[0, zz], (rc.at[0, zz], 0), (rx.at[zz], 0), (ry.at[zz], 0))

        @pl.when((zz > z) & (z == 0))
        def _():
            up_copy(zz).start()

        @pl.when((zz < z) & (z == nz - 1))
        def _():
            down_copy(zz).start()

    def stage_line(i):
        zz = place(i)

        @pl.when((zz > z) & (z > 0))
        def _():
            up_copy(zz).wait_recv()
            add(acc.at[0, zz], (ru.at[zz], 0))
            up_copy(zz).start()

        @pl.when((zz < z) & (z < nz - 1))
        def _():
            down_copy(zz).wait_recv()
            add(acc.at[0, zz], (rd.at[zz], 0))
            down_copy(zz).start()

    def peers():
        for flip in range(8):
            for turn in range(nz):
                if flip or turn:
                    yield flip, turn, dp ^ flip, lax.rem(z + turn, nz)

    def tile_copy(flip, turn, peer, line):
        here = dp * nz + z
        return remote(
            t_ref.at[peer * nz + line], tiles_ref.at[here], s_tile.at[flip, turn], r_tile.at[flip, turn], (peer, line)
        )

    barrier = pltpu.get_barrier_semaphore()
    for _, _, peer, line in peers():
        pl.semaphore_signal(barrier, 1, device_id=(peer, line), device_id_type=MESH)
    pl.semaphore_wait(barrier, 8 * nz - 1)
    wave(0)
    keep = pltpu.make_async_copy(t_ref.at[dp * nz + z], tiles_ref.at[dp * nz + z], s_keep)
    keep.start()
    for peer in peers():
        tile_copy(*peer).start()
    for i in range(nz + 3):
        if i + 1 < nz:
            wave(i + 1)
        if i < nz:
            stage_diagonal(i)
        if 0 <= i - 1 < nz:
            stage_side(i - 1)
        if 0 <= i - 2 < nz:
            stage_column(i - 2)
        if 0 <= i - 3 < nz:
            stage_line(i - 3)

    keep.wait()
    for flip, turn, peer, line in peers():
        tile_copy(flip, turn, peer, line).wait_send()
        source = tiles_ref.at[peer * nz + lax.rem(z - turn + nz, nz)]
        remote(source, source, s_tile.at[flip, turn], r_tile.at[flip, turn], (dp ^ 1, z)).wait_recv()

    @pl.when(z > 0)
    def _():
        up_copy(z).wait_recv()

    @pl.when(z < nz - 1)
    def _():
        down_copy(z).wait_recv()

    def finish(k, carry):
        at = pl.ds(k * CHUNK, CHUNK)
        total = acc[0, z, at, :].astype(jnp.float32)
        zero = jnp.zeros_like(total)
        total = total + jnp.where(z > 0, ru[z, at, :].astype(jnp.float32), zero)
        total = total + jnp.where(z < nz - 1, rd[z, at, :].astype(jnp.float32), zero)
        out_ref[at, :] = total
        return carry

    lax.fori_loop(0, rows // CHUNK, finish, 0)
    for zz in range(nz):
        for kind in range(4):
            core_copy(kind, zz).wait_send()
        a_copy(zz).wait_send()
        b_copy(zz).wait_send()
        x_copy(zz).wait_send()
        y_copy(zz).wait_send()

        @pl.when(zz > z)
        def _():
            up_copy(zz).wait_send()

        @pl.when(zz < z)
        def _():
            down_copy(zz).wait_send()


def scatter_all(p, tiles, nz, collective_id):
    _, rows, width = p.shape
    dma, vmem = pltpu.SemaphoreType.DMA, functools.partial(pltpu.VMEM, dtype=p.dtype)
    half = rows // 2
    return pl.pallas_call(
        functools.partial(scatter_kernel, nz),
        name="scatter_all",
        out_shape=(
            jax.ShapeDtypeStruct((rows, width), jnp.float32),
            jax.ShapeDtypeStruct(tiles.shape, tiles.dtype),
        ),
        in_specs=[pl.BlockSpec(memory_space=pl.ANY), pl.BlockSpec(memory_space=pltpu.VMEM)],
        out_specs=(pl.BlockSpec(memory_space=pltpu.VMEM), pl.BlockSpec(memory_space=pltpu.VMEM)),
        scratch_shapes=[vmem((4, nz, rows, width)), vmem((4, nz, rows, width))]
        + [vmem((nz, half, width)) for _ in range(2)]
        + [vmem((nz, rows, width)) for _ in range(4)]
        + [dma((8, nz)), dma((8, nz)), dma(())]
        + [dma((4, nz)), dma((4, nz)), dma((4, nz))]
        + [dma((nz,)) for _ in range(12)],
        compiler_params=pltpu.CompilerParams(
            collective_id=collective_id, has_side_effects=True, vmem_limit_bytes=VMEM_LIMIT
        ),
    )(p, tiles)


def finish_kernel(nz, nc, g_ref, h_ref, p_ref, e_ref, unit_ref, small_ref, sum_q, sum_k, sum_v, sum_o, out_ref, routed_ref, total_ref, buf, acc, rc, ra, rb, rx, ry, line_acc, up, down, more_acc, more_got, *sems):
    (s_load, s_core, r_core, s_a, r_a, s_b, r_b, s_x, r_x, s_y, r_y) = sems[:11]
    (t_x, q_x, t_y, q_y, t_a, q_a, t_b, q_b, t_c, q_c) = sems[11:21]
    s_line, s_store, s_up, r_up, s_down, r_down = sems[21:27]
    (s_load_more, s_more, r_more), sems = sems[27:30], sems[:27] + sems[30:]
    total = Total(nz, lax.axis_index("dp"), lax.axis_index("tensor"), *sems[27:])
    dp, z = lax.axis_index("dp"), lax.axis_index("tensor")
    rows = acc.shape[2]
    half = rows // 2
    flips = (0, 2, 4, 6)

    parts = ((g_ref, 0, g_ref.shape[2]), (h_ref, g_ref.shape[2], h_ref.shape[2]))

    def loads(kind, c):
        return [
            pltpu.make_async_copy(
                ref.at[(dp ^ flips[kind]) * nc + c], acc.at[kind, c, :, pl.ds(at, size)], s_load.at[k, kind, c]
            )
            for k, (ref, at, size) in enumerate(parts)
        ]

    def core_copies(kind, c):
        return [
            remote(
                ref.at[(dp ^ flips[kind] ^ 1) * nc + c],
                rc.at[kind, c, :, pl.ds(at, size)],
                s_core.at[k, kind, c],
                r_core.at[k, kind, c],
                (dp ^ 1, z),
            )
            for k, (ref, at, size) in enumerate(parts)
        ]

    def a_copy(c):
        return remote(acc.at[3, c, pl.ds(0, half)], ra.at[c], s_a.at[c], r_a.at[c], (dp ^ 2, z))

    def b_copy(c):
        return remote(acc.at[3, c, pl.ds(half, half)], rb.at[c], s_b.at[c], r_b.at[c], (dp ^ 4, z))

    def x_copy(c):
        return remote(acc.at[1, c], rx.at[c], s_x.at[c], r_x.at[c], (dp ^ 2, z))

    def y_copy(c):
        return remote(acc.at[2, c], ry.at[c], s_y.at[c], r_y.at[c], (dp ^ 4, z))

    def full(flip, c):
        return buf.at[(dp ^ flip) * nc + c]

    def back_x(c):
        return remote(full(0, c), full(0, c), t_x.at[c], q_x.at[c], (dp ^ 2, z))

    def back_y(c):
        return remote(full(0, c), full(0, c), t_y.at[c], q_y.at[c], (dp ^ 4, z))

    def back_a(c):
        ref = full(4, c).at[pl.ds(0, half)]
        return remote(ref, ref, t_a.at[c], q_a.at[c], (dp ^ 2, z))

    def back_b(c):
        ref = full(2, c).at[pl.ds(half, half)]
        return remote(ref, ref, t_b.at[c], q_b.at[c], (dp ^ 4, z))

    def back_core(kind, c):
        ref = full((0, 2, 4, 6, 6)[kind], c)
        if kind >= 3:
            ref = ref.at[pl.ds((kind - 3) * half, half)]
        return remote(ref, ref, t_c.at[kind, c], q_c.at[kind, c], (dp ^ 1, z))

    def arrived(ref, sem):
        remote(ref, ref, sem, sem, (dp ^ 1, z)).wait_recv()

    def paired(kind, c):
        for copy in loads(kind, c):
            copy.wait()
        for copy in core_copies(kind, c):
            copy.wait_recv()

    def stage_diagonal(c):
        paired(3, c)
        add_rows(acc.at[3, c], (rc.at[3, c], 0), count=rows)
        a_copy(c).start()
        b_copy(c).start()

    def stage_side(c):
        paired(1, c)
        paired(2, c)
        a_copy(c).wait_recv()
        add_rows(acc.at[2, c], (rc.at[2, c], 0), (ra.at[c], 0), start=0, count=half)
        add_rows(acc.at[2, c], (rc.at[2, c], half), start=half, count=half)
        y_copy(c).start()
        b_copy(c).wait_recv()
        add_rows(acc.at[1, c], (rc.at[1, c], half), (rb.at[c], 0), start=half, count=half)
        add_rows(acc.at[1, c], (rc.at[1, c], 0), start=0, count=half)
        x_copy(c).start()

    def stage_own(c):
        paired(0, c)
        x_copy(c).wait_recv()
        y_copy(c).wait_recv()
        dst = full(0, c)

        def body(k, carry):
            at = pl.ds(k * CHUNK, CHUNK)
            total = acc[0, c, at, :].astype(jnp.float32) + rc[0, c, at, :].astype(jnp.float32)
            total = total + rx[c, at, :].astype(jnp.float32) + ry[c, at, :].astype(jnp.float32)
            dst[at, :] = total.astype(dst.dtype)
            return carry

        lax.fori_loop(0, rows // CHUNK, body, 0)
        back_x(c).start()
        back_y(c).start()
        back_core(0, c).start()

    def stage_relay(c):
        arrived(full(4, c), q_y.at[c])
        back_a(c).start()
        back_core(2, c).start()
        arrived(full(2, c), q_x.at[c])
        back_b(c).start()
        back_core(1, c).start()

    def stage_corner(c):
        arrived(full(6, c).at[pl.ds(0, half)], q_a.at[c])
        back_core(3, c).start()
        arrived(full(6, c).at[pl.ds(half, half)], q_b.at[c])
        back_core(4, c).start()

    line_load = pltpu.make_async_copy(p_ref, line_acc, s_line)
    line_load.start()
    more_load = pltpu.make_async_copy(e_ref, more_acc, s_load_more)
    more_load.start()
    for c in range(nc):
        for kind in (3, 1, 2, 0):
            for copy in loads(kind, c):
                copy.start()
    greet_total(dp, z, nz)
    for c in range(nc):
        for kind in (3, 1, 2, 0):
            for copy in core_copies(kind, c):
                copy.start()
    line = Line(nz, dp, z, line_acc, up, down, s_up, r_up, s_down, r_down)
    line_load.wait()
    line.first()

    def line_end():
        line.finish(out_ref)
        line.drain()
        share = jnp.sum(out_ref[...] * unit_ref[...], axis=0, keepdims=True)
        total.got[0] = small_ref[...]
        wide = small_ref.shape[1]
        for k in range(out_ref.shape[1] // wide):
            total.got[0, k : k + 1, :] = share[:, k * wide : (k + 1) * wide]

    others = [lax.rem(z + turn, nz) for turn in range(1, nz)]
    more = [
        remote(more_acc.at[place], more_got.at[turn], s_more.at[turn], r_more.at[turn], (dp, place))
        for turn, place in enumerate(others)
    ]

    def more_start():
        more_load.wait()
        for copy in more:
            copy.start()

    def more_end():
        for copy in more:
            copy.wait()

        def body(k, carry):
            at = pl.ds(k * CHUNK, CHUNK)
            part = more_acc[z, at, :].astype(jnp.float32)
            for turn in range(nz - 1):
                part = part + more_got[turn, at, :].astype(jnp.float32)
            routed_ref[at, :] = part
            return carry

        lax.fori_loop(0, routed_ref.shape[0] // CHUNK, body, 0)

    side = [functools.partial(line.step, distance) for distance in range(1, nz - 1)] + [line_end, more_start]
    late = [functools.partial(total.step, k, total_ref) for k in range(3)] + [more_end]
    late += [functools.partial(total.step, k, total_ref) for k in range(3, Total.steps)]
    stages = (stage_diagonal, stage_side, stage_own, stage_relay, stage_corner)
    for i in range(nc + len(stages) - 1):
        for lag, stage in enumerate(stages):
            if 0 <= i - lag < nc:
                stage(i - lag)
                if i >= 1 and side:
                    side.pop(0)()
    for one in side + late:
        one()
    for c in range(nc):
        for kind, flip in ((0, 1), (1, 3), (2, 5)):
            arrived(full(flip, c), q_c.at[kind, c])
        for kind in (3, 4):
            arrived(full(7, c).at[pl.ds((kind - 3) * half, half)], q_c.at[kind, c])
    wide = buf.shape[2] // 4
    stores = [
        pltpu.make_async_copy(buf.at[:, :, pl.ds(k * wide, wide)], ref, s_store.at[k])
        for k, ref in enumerate((sum_q, sum_k, sum_v, sum_o))
    ]
    for store in stores:
        store.start()
    for c in range(nc):
        for kind in range(4):
            for copy in core_copies(kind, c):
                copy.wait_send()
        for copy in (a_copy, b_copy, x_copy, y_copy, back_x, back_y, back_a, back_b):
            copy(c).wait_send()
        for kind in range(5):
            back_core(kind, c).wait_send()
    for store in stores:
        store.wait()


def finish_sums(g, h, p, e, unit, small, nz, nc, collective_id):
    _, rows, width = g.shape
    width += h.shape[2]
    _, line_rows, line_width = p.shape
    half = rows // 2
    dma, vmem = pltpu.SemaphoreType.DMA, functools.partial(pltpu.VMEM, dtype=g.dtype)
    return pl.pallas_call(
        functools.partial(finish_kernel, nz, nc),
        name="finish_sums",
        out_shape=(
            *[jax.ShapeDtypeStruct(g.shape[:2] + (width // 4,), g.dtype)] * 4,
            *[jax.ShapeDtypeStruct((line_rows, line_width), jnp.float32)] * 2,
            jax.ShapeDtypeStruct(small.shape, small.dtype),
        ),
        in_specs=[pl.BlockSpec(memory_space=pl.ANY)] * 4 + [pl.BlockSpec(memory_space=pltpu.VMEM)] * 2,
        out_specs=(
            *[pl.BlockSpec(memory_space=pl.ANY)] * 4,
            *[pl.BlockSpec(memory_space=pltpu.VMEM)] * 3,
        ),
        scratch_shapes=[vmem(g.shape[:2] + (width,)), vmem((4, nc, rows, width)), vmem((4, nc, rows, width))]
        + [vmem((nc, half, width)) for _ in range(2)]
        + [vmem((nc, rows, width)) for _ in range(2)]
        + [vmem((nz, line_rows, line_width)) for _ in range(4)]
        + [vmem((nz - 1, line_rows, line_width))]
        + [dma((2, 4, nc)) for _ in range(3)]
        + [dma((nc,)) for _ in range(16)]
        + [dma((5, nc)), dma((5, nc))]
        + [dma(()), dma((4,))]
        + [dma((nz, PARTS)) for _ in range(4)]
        + [dma(()), dma((nz - 1,)), dma((nz - 1,))]
        + total_scratch(nz, small.shape, small.dtype),
        compiler_params=pltpu.CompilerParams(
            collective_id=collective_id, has_side_effects=True, vmem_limit_bytes=VMEM_LIMIT
        ),
    )(g, h, p, e, unit, small)


class Spread:
    def __init__(self, nz, row_shape):
        self.nz, self.row_shape = nz, row_shape

    @staticmethod
    def swap(value, flip):
        return lax.ppermute(value, "dp", [(i, i ^ flip) for i in range(8)])

    @staticmethod
    def plus(a, b):
        return (a.astype(jnp.float32) + b.astype(jnp.float32)).astype(a.dtype)

    def pair(self, mine, partners):
        self.mine = mine
        return self.swap(partners, 1)

    def sides(self, theirs):
        nz, plus = self.nz, self.plus
        self.low, self.high = slice(0, nz // 2), slice(nz // 2, nz)
        mine = self.mine.reshape((4, nz) + self.row_shape)
        self.whole = whole = plus(mine, theirs.reshape(mine.shape))
        to_x = jnp.stack([whole[1, self.low], whole[3, self.low]])
        to_y = jnp.stack([whole[2, self.high], whole[3, self.high]])
        return to_x, to_y

    def side(self, sides):
        return self.swap(sides[0], 2), self.swap(sides[1], 4)

    def last_side(self, sides):
        by_x, by_y = sides
        whole, low, high, plus = self.whole, self.low, self.high, self.plus
        self.low_own, low_y = plus(whole[0, low], by_x[0]), plus(whole[2, low], by_x[1])
        self.high_own, high_x = plus(whole[0, high], by_y[0]), plus(whole[1, high], by_y[1])
        return self.swap(low_y, 4), self.swap(high_x, 2)

    def column(self, sides):
        return jnp.concatenate([self.plus(self.low_own, sides[0]), self.plus(self.high_own, sides[1])])


def hold(first, second):
    return lax.optimization_barrier((first, second))


def experts_routed(
    hidden_after_attention,
    expert_ids,
    expert_norm_gain,
    w_router,
    w_gate,
    w_up,
    w_down,
    grad_output,
):
    tok_count, d_model = hidden_after_attention.shape
    n_tensor = lax.axis_size("tensor")
    n_dp = lax.axis_size("dp")
    devices = n_dp * n_tensor
    second_norm_scale = root_mean_square_scale(hidden_after_attention)
    second_unit_rows = hidden_after_attention * second_norm_scale
    second_normalized = (second_unit_rows * expert_norm_gain).astype(jnp.bfloat16)
    experts = w_router.shape[1]
    topk = expert_ids.shape[1]
    exp_dev = w_gate.shape[0]
    most = 2 * ((tok_count * topk * 9 + experts * 16 - 1) // (experts * 16))
    route_probs = jax.nn.softmax(
        jnp.dot(second_normalized, w_router, preferred_element_type=jnp.float32), axis=-1
    )
    chosen = expert_ids[:, :, None] == jnp.arange(experts, dtype=jnp.int32)[None, None, :]
    gate_values = jnp.sum(jnp.where(chosen, route_probs[:, None, :], 0.0), axis=-1)
    flat_ids, pair_rank = slot_positions(expert_ids, experts)
    pair_slot = (flat_ids % exp_dev * n_dp + flat_ids // exp_dev) * most + pair_rank
    pair_count = tok_count * topk
    slot_count = exp_dev * n_dp * most
    slot_owner = (
        jnp.full((slot_count,), pair_count, jnp.int32)
        .at[pair_slot]
        .set(jnp.arange(pair_count, dtype=jnp.int32))
    )
    padded = jnp.concatenate([second_normalized, jnp.zeros((1, d_model), jnp.bfloat16)], axis=0)
    outgoing = padded[slot_owner // topk].reshape(exp_dev, n_dp, most, d_model)
    copies = jnp.broadcast_to(
        outgoing[:, :, None], (exp_dev, n_dp, n_tensor, most, d_model)
    ).reshape(exp_dev, devices, most, d_model)
    arrived = lax.all_to_all(copies, ("dp", "tensor"), split_axis=1, concat_axis=1, tiled=True)
    expert_rows = arrived.reshape(exp_dev, devices * most, d_model)
    gate_pre = jnp.einsum("erd,edf->erf", expert_rows, w_gate, preferred_element_type=jnp.float32)
    up_pre = jnp.einsum("erd,edf->erf", expert_rows, w_up, preferred_element_type=jnp.float32)
    gate_sigmoid = jax.nn.sigmoid(gate_pre)
    silu_gate = gate_pre * gate_sigmoid
    hidden = (silu_gate * up_pre).astype(jnp.bfloat16)
    partial_value = (
        jnp.einsum("erf,efd->erd", hidden, w_down, preferred_element_type=jnp.float32)
        .astype(jnp.bfloat16)
        .reshape(exp_dev, devices, most, d_model)
    )
    returned = lax.all_to_all(
        partial_value, ("dp", "tensor"), split_axis=1, concat_axis=1, tiled=True
    )
    expert_out = jnp.sum(
        returned.reshape(exp_dev, n_dp, n_tensor, most, d_model).astype(jnp.float32), axis=2
    ).reshape(slot_count, d_model)
    pair_out = expert_out[pair_slot].reshape(tok_count, topk, d_model)
    result = (hidden_after_attention + jnp.sum(gate_values[:, :, None] * pair_out, axis=1)).astype(
        jnp.bfloat16
    )
    cotangent = grad_output.astype(jnp.float32)
    grad_gates = jnp.sum(pair_out * cotangent[:, None, :], axis=-1)
    grad_pairs = (
        (gate_values[:, :, None] * cotangent[:, None, :])
        .astype(jnp.bfloat16)
        .reshape(pair_count, d_model)
    )
    grad_slots = jnp.concatenate([grad_pairs, jnp.zeros((1, d_model), jnp.bfloat16)], axis=0)[
        slot_owner
    ].reshape(exp_dev, n_dp, most, d_model)
    grad_copies = jnp.broadcast_to(
        grad_slots[:, :, None], (exp_dev, n_dp, n_tensor, most, d_model)
    ).reshape(exp_dev, devices, most, d_model)
    grad_arrived = lax.all_to_all(
        grad_copies, ("dp", "tensor"), split_axis=1, concat_axis=1, tiled=True
    )
    grad_rows = grad_arrived.reshape(exp_dev, devices * most, d_model)
    grad_hidden = jnp.einsum("erd,efd->erf", grad_rows, w_down, preferred_element_type=jnp.float32)
    grad_down = jnp.einsum("erf,erd->efd", hidden, grad_rows, preferred_element_type=jnp.float32)
    grad_gate_pre = (
        grad_hidden * up_pre * gate_sigmoid * (1.0 + gate_pre * (1.0 - gate_sigmoid))
    ).astype(jnp.bfloat16)
    grad_up_pre = (grad_hidden * silu_gate).astype(jnp.bfloat16)
    grad_gate = jnp.einsum(
        "erd,erf->edf", expert_rows, grad_gate_pre, preferred_element_type=jnp.float32
    )
    grad_up = jnp.einsum(
        "erd,erf->edf", expert_rows, grad_up_pre, preferred_element_type=jnp.float32
    )
    grad_expert_in = jnp.einsum(
        "erf,edf->erd", grad_gate_pre, w_gate, preferred_element_type=jnp.float32
    )
    grad_expert_in = grad_expert_in + jnp.einsum(
        "erf,edf->erd", grad_up_pre, w_up, preferred_element_type=jnp.float32
    )
    grad_expert_in = grad_expert_in.astype(jnp.bfloat16).reshape(exp_dev, devices, most, d_model)
    grad_back = lax.all_to_all(
        grad_expert_in, ("dp", "tensor"), split_axis=1, concat_axis=1, tiled=True
    )
    grad_slot_in = jnp.sum(
        grad_back.reshape(exp_dev, n_dp, n_tensor, most, d_model).astype(jnp.float32), axis=2
    ).reshape(slot_count, d_model)
    grad_second_normalized = jnp.sum(
        grad_slot_in[pair_slot].reshape(tok_count, topk, d_model), axis=1
    )
    grad_route = jnp.sum(jnp.where(chosen, grad_gates[:, :, None], 0.0), axis=1)
    grad_logits = (
        route_probs * (grad_route - jnp.sum(route_probs * grad_route, axis=-1, keepdims=True))
    ).astype(jnp.bfloat16)
    grad_router_part = jnp.einsum(
        "td,te->de", second_normalized, grad_logits, preferred_element_type=jnp.float32
    )
    grad_second_normalized = grad_second_normalized + jnp.einsum(
        "te,de->td", grad_logits, w_router, preferred_element_type=jnp.float32
    )
    grad_expert_share = jnp.sum(grad_second_normalized * second_unit_rows, axis=0)
    grad_second_unit_rows = grad_second_normalized * expert_norm_gain
    grad_hidden_one = (
        second_norm_scale
        * (
            grad_second_unit_rows
            - second_unit_rows
            * jnp.mean(grad_second_unit_rows * second_unit_rows, axis=-1, keepdims=True)
        )
        + cotangent
    )
    return (
        result,
        grad_hidden_one,
        grad_expert_share,
        grad_router_part,
        grad_gate,
        grad_up,
        grad_down,
    )


def experts_dense(
    hidden_after_attention,
    expert_ids,
    expert_norm_gain,
    w_router,
    w_gate,
    w_up,
    w_down,
    grad_output,
    all_cotangents,
):
    tok_count, d_model = hidden_after_attention.shape
    n_tensor = lax.axis_size("tensor")
    n_dp = lax.axis_size("dp")
    devices = n_dp * n_tensor
    everyone = ("dp", "tensor")
    second_norm_scale = root_mean_square_scale(hidden_after_attention)
    second_unit_rows = hidden_after_attention * second_norm_scale
    second_normalized = (second_unit_rows * expert_norm_gain).astype(jnp.bfloat16)
    experts = w_router.shape[1]
    exp_dev, _, width = w_gate.shape
    all_count = devices * tok_count
    expert_at = jnp.arange(experts, dtype=jnp.int32)

    chosen = jnp.any(expert_ids[:, :, None] == expert_at[None, None, :], axis=1)
    route_probs = jax.nn.softmax(
        jnp.dot(second_normalized, w_router, preferred_element_type=jnp.float32), axis=-1
    )
    gates = jnp.where(chosen, route_probs, 0.0).T

    down_rows = w_down.reshape(exp_dev * width, d_model)
    wide = jnp.concatenate([w_gate[e] for e in range(exp_dev)] + [w_up[e] for e in range(exp_dev)], axis=1)
    both = exp_dev * width
    all_rows, grad_pre, gated, tiles = gather_experts(
        second_normalized,
        gates,
        all_cotangents.reshape(devices, tok_count, d_model),
        wide,
        down_rows.T,
        exp_dev,
        n_tensor,
        0,
    )
    all_rows, grad_pre = all_rows.reshape(all_count, d_model), grad_pre.reshape(all_count, 2 * both)
    lines = gated.reshape(n_dp // 2, n_tensor, 2, tok_count, both).transpose(0, 2, 1, 3, 4)
    gated_hidden = lines.reshape(all_count, both)
    lines = lines.reshape(n_dp, n_tensor * tok_count, both)

    def out_rows(places):
        picked = [
            lax.dynamic_index_in_dim(lines, lax.axis_index("dp") ^ k, axis=0, keepdims=False)
            for k in places
        ]
        return jnp.dot(
            jnp.concatenate(picked), down_rows, preferred_element_type=jnp.float32
        ).astype(jnp.bfloat16)

    in_part = jnp.einsum("tf,df->td", grad_pre, wide, preferred_element_type=jnp.float32).astype(jnp.bfloat16)
    spread = Spread(n_tensor, (tok_count, d_model))
    partner_rows = out_rows((1, 3, 5, 7))
    in_part, partner_rows = hold(in_part, partner_rows)
    grad_in, gate_tiles = scatter_all(
        in_part.reshape(devices, tok_count, d_model), tiles, n_tensor, 1
    )
    grad_in, partner_rows = hold(grad_in, partner_rows)
    theirs = spread.pair(out_rows((0, 2, 4, 6)), partner_rows)
    sides = spread.sides(theirs)
    grad_down = jnp.einsum(
        "tf,td->fd", gated_hidden, all_cotangents, preferred_element_type=jnp.float32
    ).reshape(exp_dev, width, d_model)
    grad_wide = jnp.einsum("td,tf->df", all_rows, grad_pre, preferred_element_type=jnp.float32)
    grad_gate = jnp.stack([grad_wide[:, e * width : (e + 1) * width] for e in range(exp_dev)])
    grad_up = jnp.stack([grad_wide[:, both + e * width : both + (e + 1) * width] for e in range(exp_dev)])

    grad_route = jnp.sum(gate_tiles[:, :exp_dev].reshape(n_dp, n_tensor, exp_dev, tok_count), axis=1)
    grad_route = jnp.where(chosen, grad_route.reshape(experts, tok_count).T, 0.0)
    cotangent = grad_output.astype(jnp.float32)
    grad_logits = (
        route_probs * (grad_route - jnp.sum(route_probs * grad_route, axis=-1, keepdims=True))
    ).astype(jnp.bfloat16)
    grad_router_part = jnp.einsum(
        "td,te->de", second_normalized, grad_logits, preferred_element_type=jnp.float32
    )
    grad_second_normalized = grad_in + jnp.einsum(
        "te,de->td", grad_logits, w_router, preferred_element_type=jnp.float32
    )
    grad_expert_share = jnp.sum(grad_second_normalized * second_unit_rows, axis=0)
    grad_second_unit_rows = grad_second_normalized * expert_norm_gain
    grad_hidden_one = (
        second_norm_scale
        * (
            grad_second_unit_rows
            - second_unit_rows
            * jnp.mean(grad_second_unit_rows * second_unit_rows, axis=-1, keepdims=True)
        )
        + cotangent
    )
    return (
        spread,
        sides,
        grad_hidden_one,
        grad_expert_share,
        grad_router_part,
        grad_gate,
        grad_up,
        grad_down,
    )


def local_gathered(
    tokens,
    file_ids,
    expert_ids,
    attention_norm_gain,
    w_query,
    w_key,
    w_value,
    query_gain,
    key_gain,
    w_output,
    expert_norm_gain,
    w_router,
    w_gate,
    w_up,
    w_down,
    grad_output,
):
    tok_count, d_model = tokens.shape
    n_tensor = lax.axis_size("tensor")
    n_dp = lax.axis_size("dp")
    devices = n_dp * n_tensor
    local_dim = w_query.shape[1]
    head_dim = HEAD_DIM
    local_heads = local_dim // head_dim
    seq_len = tok_count * n_tensor
    block_rows = min(512, seq_len)
    score_scale = 1.0 / math.sqrt(head_dim)
    file_row = file_ids[0]
    cosine, sine_table = rope_tables(seq_len, head_dim)
    input_tensors = tokens.astype(jnp.float32)
    first_norm_scale = root_mean_square_scale(input_tensors)
    first_unit_rows = input_tensors * first_norm_scale
    first_normalized = (first_unit_rows * attention_norm_gain).astype(jnp.bfloat16)
    normed_all = line_gather(first_normalized, n_tensor, 2).reshape(seq_len, d_model)
    all_cotangents = lax.all_gather(grad_output, ("dp", "tensor"), axis=0, tiled=True)
    query_raw = jnp.dot(normed_all, w_query, preferred_element_type=jnp.float32)
    key_raw = jnp.dot(normed_all, w_key, preferred_element_type=jnp.float32)
    value_rows = (
        jnp.dot(normed_all, w_value, preferred_element_type=jnp.float32)
        .astype(jnp.bfloat16)
        .reshape(seq_len, local_heads, head_dim)
    )
    query_total, key_total = line_total(
        jnp.stack([jnp.sum(query_raw * query_raw, axis=1), jnp.sum(key_raw * key_raw, axis=1)]), n_tensor, 6
    )
    query_scale = lax.rsqrt(query_total / d_model + EPSILON)[:, None]
    key_scale = lax.rsqrt(key_total / d_model + EPSILON)[:, None]
    query_hat = query_raw * query_scale
    key_hat = key_raw * key_scale
    queries = rotate(
        (query_hat * query_gain).reshape(seq_len, local_heads, head_dim), cosine, sine_table
    ).astype(jnp.bfloat16)
    key_rows = rotate(
        (key_hat * key_gain).reshape(seq_len, local_heads, head_dim), cosine, sine_table
    ).astype(jnp.bfloat16)
    block_start = 0
    scores = block_scores(queries, key_rows, file_row, block_start, score_scale)
    row_peak = jnp.max(scores, axis=-1, keepdims=True)
    log_total = row_peak + jnp.log(jnp.sum(jnp.exp(scores - row_peak), axis=-1, keepdims=True))
    attn_probs = jnp.exp(scores - log_total).astype(jnp.bfloat16)
    context_blocks = jnp.einsum(
        "hqk,khd->qhd", attn_probs, value_rows, preferred_element_type=jnp.float32
    )
    log_totals = [log_total]
    context = context_blocks.reshape(seq_len, local_dim).astype(jnp.bfloat16)
    attn_out = line_scatter(
        jnp.dot(context, w_output, preferred_element_type=jnp.float32)
        .astype(jnp.bfloat16)
        .reshape(n_tensor, tok_count, d_model),
        n_tensor,
        3,
    )
    hidden_after_attention = input_tensors + attn_out
    spread, sides, grad_hidden_one, grad_expert_share, grad_router_part, grad_gate, grad_up, grad_down = (
        experts_dense(
            hidden_after_attention,
            expert_ids,
            expert_norm_gain,
            w_router,
            w_gate,
            w_up,
            w_down,
            grad_output,
            all_cotangents,
        )
    )
    grad_attn = grad_hidden_one.astype(jnp.bfloat16)
    side_parts = jnp.concatenate([grad_router_part.T, grad_expert_share[None, :]])
    side_total = lax.psum(side_parts, ("dp", "tensor"))
    grad_attn, sides = hold(grad_attn, sides)
    sides = spread.side(sides)
    grad_attn_all = line_gather(grad_attn, n_tensor, 2)
    grad_attn_all, sides = hold(grad_attn_all, sides)
    sides = spread.last_side(sides)
    grad_attn_all = grad_attn_all.reshape(seq_len, d_model)
    grad_output_part = jnp.einsum(
        "sd,se->ed", context, grad_attn_all, preferred_element_type=jnp.float32
    )
    grad_context = (
        jnp.einsum("se,de->sd", grad_attn_all, w_output, preferred_element_type=jnp.float32)
        .astype(jnp.bfloat16)
        .reshape(seq_len, local_heads, head_dim)
    )
    grad_query_blocks = []
    grad_key_total = jnp.zeros((seq_len, local_heads, head_dim), jnp.float32)
    grad_value_total = jnp.zeros((seq_len, local_heads, head_dim), jnp.float32)
    for block_index, block_start in enumerate(range(0, seq_len, block_rows)):
        scores = block_scores(queries, key_rows, file_row, block_start, score_scale)
        probs_full = jnp.exp(scores - log_totals[block_index])
        probs_low = probs_full.astype(jnp.bfloat16)
        grad_value_total = jnp.einsum(
            "hqk,qhd->khd", probs_low, grad_context, preferred_element_type=jnp.float32
        )
        grad_probs = jnp.einsum(
            "qhd,khd->hqk", grad_context, value_rows, preferred_element_type=jnp.float32
        )
        row_shift = jnp.sum(probs_full * grad_probs, axis=-1, keepdims=True)
        grad_scores = (probs_full * (grad_probs - row_shift)).astype(jnp.bfloat16)
        grad_query_blocks.append(
            jnp.einsum("hqk,khd->qhd", grad_scores, key_rows, preferred_element_type=jnp.float32)
            * score_scale
        )
        grad_key_total = (
            jnp.einsum("hqk,qhd->khd", grad_scores, queries, preferred_element_type=jnp.float32)
            * score_scale
        )
    grad_query_normed = unrotate(grad_query_blocks[0], cosine, sine_table).reshape(
        seq_len, local_dim
    )
    grad_key_normed = unrotate(grad_key_total, cosine, sine_table).reshape(seq_len, local_dim)
    grad_qgain_part = jnp.sum(grad_query_normed * query_hat, axis=0)
    grad_kgain_part = jnp.sum(grad_key_normed * key_hat, axis=0)
    grad_query_hat = grad_query_normed * query_gain
    grad_key_hat = grad_key_normed * key_gain
    query_inner, key_inner = line_total(
        jnp.stack(
            [jnp.sum(grad_query_hat * query_hat, axis=1), jnp.sum(grad_key_hat * key_hat, axis=1)]
        ),
        n_tensor,
        6,
    )
    grad_query_raw = (
        query_scale * (grad_query_hat - query_hat * (query_inner / d_model)[:, None])
    ).astype(jnp.bfloat16)
    grad_key_raw = (key_scale * (grad_key_hat - key_hat * (key_inner / d_model)[:, None])).astype(
        jnp.bfloat16
    )
    grad_value_raw = grad_value_total.reshape(seq_len, local_dim).astype(jnp.bfloat16)
    grad_raw = jnp.concatenate([grad_query_raw, grad_key_raw, grad_value_raw], axis=1)
    w_raw = jnp.concatenate([w_query, w_key, w_value], axis=1)
    raw_part = jnp.einsum("sd,sf->df", normed_all, grad_raw, preferred_element_type=jnp.float32)
    row_part = jnp.einsum("sf,df->sd", grad_raw, w_raw, preferred_element_type=jnp.float32)
    column = spread.column(sides)
    mine = (jnp.arange(n_tensor) == lax.axis_index("tensor"))[:, None]
    gain_parts = jnp.stack(
        [
            jnp.zeros((d_model,), jnp.float32),
            jnp.where(mine, grad_qgain_part[None, :], 0.0).reshape(-1),
            jnp.where(mine, grad_kgain_part[None, :], 0.0).reshape(-1),
            jnp.zeros((d_model,), jnp.float32),
        ]
    )
    finished = finish_sums(
        raw_part.astype(jnp.bfloat16).reshape(n_dp * PIECES, -1, 3 * local_dim),
        grad_output_part.astype(jnp.bfloat16).reshape(n_dp * PIECES, -1, local_dim),
        row_part.astype(jnp.bfloat16).reshape(n_tensor, tok_count, d_model),
        column,
        first_unit_rows,
        gain_parts.reshape(8, -1),
        n_tensor,
        PIECES,
        4,
    )
    finished, side_total = hold(finished, side_total)
    total_query, total_key, total_value, total_output, grad_first_normalized, routed, gain_totals = finished
    total_router, total_ffn_gain = side_total[:-1].T, side_total[-1]
    total_query, total_key, total_value, total_output = (
        total.reshape(d_model, local_dim).astype(jnp.float32)
        for total in (total_query, total_key, total_value, total_output)
    )
    total_output = total_output.T
    grad_first_unit_rows = grad_first_normalized * attention_norm_gain
    grad_tokens = (
        first_norm_scale
        * (
            grad_first_unit_rows
            - first_unit_rows
            * jnp.mean(grad_first_unit_rows * first_unit_rows, axis=-1, keepdims=True)
        )
        + grad_hidden_one
    ).astype(jnp.bfloat16)
    result = (hidden_after_attention + routed).astype(jnp.bfloat16)
    gain_totals = gain_totals.reshape(4, d_model)
    total_attn_gain = gain_totals[0]
    own_gains = lax.dynamic_slice_in_dim(
        gain_totals, lax.axis_index("tensor") * local_dim, local_dim, axis=1
    )
    total_qgain, total_kgain = own_gains[1], own_gains[2]
    return (
        result,
        grad_tokens,
        total_query,
        total_key,
        total_value,
        total_output,
        total_qgain,
        total_kgain,
        total_attn_gain,
        total_ffn_gain,
        total_router,
        grad_gate,
        grad_up,
        grad_down,
    )


def local_routed(
    tokens,
    file_ids,
    expert_ids,
    attention_norm_gain,
    w_query,
    w_key,
    w_value,
    query_gain,
    key_gain,
    w_output,
    expert_norm_gain,
    w_router,
    w_gate,
    w_up,
    w_down,
    grad_output,
):
    tok_count, d_model = tokens.shape
    n_tensor = lax.axis_size("tensor")
    n_dp = lax.axis_size("dp")
    devices = n_dp * n_tensor
    local_dim = w_query.shape[1]
    head_dim = HEAD_DIM
    local_heads = local_dim // head_dim
    seq_len = tok_count * n_tensor
    block_rows = min(512, seq_len)
    score_scale = 1.0 / math.sqrt(head_dim)
    file_row = file_ids[0]
    cosine, sine_table = rope_tables(seq_len, head_dim)
    input_tensors = tokens.astype(jnp.float32)
    first_norm_scale = root_mean_square_scale(input_tensors)
    first_unit_rows = input_tensors * first_norm_scale
    first_normalized = (first_unit_rows * attention_norm_gain).astype(jnp.bfloat16)
    normed_all = lax.all_gather(first_normalized, "tensor", axis=0, tiled=True)
    query_raw = jnp.dot(normed_all, w_query, preferred_element_type=jnp.float32)
    key_raw = jnp.dot(normed_all, w_key, preferred_element_type=jnp.float32)
    value_rows = (
        jnp.dot(normed_all, w_value, preferred_element_type=jnp.float32)
        .astype(jnp.bfloat16)
        .reshape(seq_len, local_heads, head_dim)
    )
    query_total, key_total = lax.psum(
        (jnp.sum(query_raw * query_raw, axis=1), jnp.sum(key_raw * key_raw, axis=1)), "tensor"
    )
    query_scale = lax.rsqrt(query_total / d_model + EPSILON)[:, None]
    key_scale = lax.rsqrt(key_total / d_model + EPSILON)[:, None]
    query_hat = query_raw * query_scale
    key_hat = key_raw * key_scale
    queries = rotate(
        (query_hat * query_gain).reshape(seq_len, local_heads, head_dim), cosine, sine_table
    ).astype(jnp.bfloat16)
    key_rows = rotate(
        (key_hat * key_gain).reshape(seq_len, local_heads, head_dim), cosine, sine_table
    ).astype(jnp.bfloat16)
    block_start = 0
    scores = block_scores(queries, key_rows, file_row, block_start, score_scale)
    row_peak = jnp.max(scores, axis=-1, keepdims=True)
    log_total = row_peak + jnp.log(jnp.sum(jnp.exp(scores - row_peak), axis=-1, keepdims=True))
    attn_probs = jnp.exp(scores - log_total).astype(jnp.bfloat16)
    context_blocks = jnp.einsum(
        "hqk,khd->qhd", attn_probs, value_rows, preferred_element_type=jnp.float32
    )
    log_totals = [log_total]
    context = context_blocks.reshape(seq_len, local_dim).astype(jnp.bfloat16)
    attn_out = lax.psum_scatter(
        jnp.dot(context, w_output, preferred_element_type=jnp.float32).astype(jnp.bfloat16),
        "tensor",
        scatter_dimension=0,
        tiled=True,
    ).astype(jnp.float32)
    hidden_after_attention = input_tensors + attn_out
    result, grad_hidden_one, grad_expert_share, grad_router_part, grad_gate, grad_up, grad_down = (
        experts_routed(
            hidden_after_attention,
            expert_ids,
            expert_norm_gain,
            w_router,
            w_gate,
            w_up,
            w_down,
            grad_output,
        )
    )
    grad_attn = grad_hidden_one.astype(jnp.bfloat16)
    grad_attn_all = lax.all_gather(grad_attn, "tensor", axis=0, tiled=True)
    grad_output_part = jnp.einsum(
        "sd,se->de", context, grad_attn_all, preferred_element_type=jnp.float32
    )
    grad_context = (
        jnp.einsum("se,de->sd", grad_attn_all, w_output, preferred_element_type=jnp.float32)
        .astype(jnp.bfloat16)
        .reshape(seq_len, local_heads, head_dim)
    )
    grad_query_blocks = []
    grad_key_total = jnp.zeros((seq_len, local_heads, head_dim), jnp.float32)
    grad_value_total = jnp.zeros((seq_len, local_heads, head_dim), jnp.float32)
    for block_index, block_start in enumerate(range(0, seq_len, block_rows)):
        scores = block_scores(queries, key_rows, file_row, block_start, score_scale)
        probs_full = jnp.exp(scores - log_totals[block_index])
        probs_low = probs_full.astype(jnp.bfloat16)
        grad_value_total = jnp.einsum(
            "hqk,qhd->khd", probs_low, grad_context, preferred_element_type=jnp.float32
        )
        grad_probs = jnp.einsum(
            "qhd,khd->hqk", grad_context, value_rows, preferred_element_type=jnp.float32
        )
        row_shift = jnp.sum(probs_full * grad_probs, axis=-1, keepdims=True)
        grad_scores = (probs_full * (grad_probs - row_shift)).astype(jnp.bfloat16)
        grad_query_blocks.append(
            jnp.einsum("hqk,khd->qhd", grad_scores, key_rows, preferred_element_type=jnp.float32)
            * score_scale
        )
        grad_key_total = (
            jnp.einsum("hqk,qhd->khd", grad_scores, queries, preferred_element_type=jnp.float32)
            * score_scale
        )
    grad_query_normed = unrotate(grad_query_blocks[0], cosine, sine_table).reshape(
        seq_len, local_dim
    )
    grad_key_normed = unrotate(grad_key_total, cosine, sine_table).reshape(seq_len, local_dim)
    grad_qgain_part = jnp.sum(grad_query_normed * query_hat, axis=0)
    grad_kgain_part = jnp.sum(grad_key_normed * key_hat, axis=0)
    grad_query_hat = grad_query_normed * query_gain
    grad_key_hat = grad_key_normed * key_gain
    query_inner, key_inner = lax.psum(
        (jnp.sum(grad_query_hat * query_hat, axis=1), jnp.sum(grad_key_hat * key_hat, axis=1)),
        "tensor",
    )
    grad_query_raw = (
        query_scale * (grad_query_hat - query_hat * (query_inner / d_model)[:, None])
    ).astype(jnp.bfloat16)
    grad_key_raw = (key_scale * (grad_key_hat - key_hat * (key_inner / d_model)[:, None])).astype(
        jnp.bfloat16
    )
    grad_value_raw = grad_value_total.reshape(seq_len, local_dim).astype(jnp.bfloat16)
    grad_query_part = jnp.einsum(
        "sd,sf->df", normed_all, grad_query_raw, preferred_element_type=jnp.float32
    )
    grad_key_part = jnp.einsum(
        "sd,sf->df", normed_all, grad_key_raw, preferred_element_type=jnp.float32
    )
    grad_value_part = jnp.einsum(
        "sd,sf->df", normed_all, grad_value_raw, preferred_element_type=jnp.float32
    )
    summed = jnp.einsum("sf,df->sd", grad_query_raw, w_query, preferred_element_type=jnp.float32)
    summed = summed + jnp.einsum(
        "sf,df->sd", grad_key_raw, w_key, preferred_element_type=jnp.float32
    )
    grad_first_normalized = lax.psum_scatter(
        (
            summed
            + jnp.einsum("sf,df->sd", grad_value_raw, w_value, preferred_element_type=jnp.float32)
        ).astype(jnp.bfloat16),
        "tensor",
        scatter_dimension=0,
        tiled=True,
    ).astype(jnp.float32)
    grad_attention_share = jnp.sum(grad_first_normalized * first_unit_rows, axis=0)
    grad_first_unit_rows = grad_first_normalized * attention_norm_gain
    grad_tokens = (
        first_norm_scale
        * (
            grad_first_unit_rows
            - first_unit_rows
            * jnp.mean(grad_first_unit_rows * first_unit_rows, axis=-1, keepdims=True)
        )
        + grad_hidden_one
    ).astype(jnp.bfloat16)
    total_query, total_key, total_value, total_output, total_qgain, total_kgain = (
        lax.psum(grad_query_part.astype(jnp.bfloat16), "dp").astype(jnp.float32),
        lax.psum(grad_key_part.astype(jnp.bfloat16), "dp").astype(jnp.float32),
        lax.psum(grad_value_part.astype(jnp.bfloat16), "dp").astype(jnp.float32),
        lax.psum(grad_output_part.astype(jnp.bfloat16), "dp").astype(jnp.float32),
        lax.psum(grad_qgain_part.astype(jnp.bfloat16), "dp").astype(jnp.float32),
        lax.psum(grad_kgain_part.astype(jnp.bfloat16), "dp").astype(jnp.float32),
    )
    total_attn_gain, total_ffn_gain, total_router = lax.psum(
        (grad_attention_share, grad_expert_share, grad_router_part), ("dp", "tensor")
    )
    return (
        result,
        grad_tokens,
        total_query,
        total_key,
        total_value,
        total_output,
        total_qgain,
        total_kgain,
        total_attn_gain,
        total_ffn_gain,
        total_router,
        grad_gate,
        grad_up,
        grad_down,
    )


def solution(mesh):
    return jax.shard_map(
        local_gathered if mesh.shape["dp"] == 8 else local_routed,
        mesh=mesh,
        in_specs=(
            P(("dp", "tensor"), None),
            P("dp", None),
            P(("dp", "tensor"), None),
            P(),
            P(None, "tensor"),
            P(None, "tensor"),
            P(None, "tensor"),
            P("tensor"),
            P("tensor"),
            P("tensor", None),
            P(),
            P(),
            P("dp", None, "tensor"),
            P("dp", None, "tensor"),
            P("dp", "tensor", None),
            P(("dp", "tensor"), None),
        ),
        out_specs=(
            P(("dp", "tensor"), None),
            P(("dp", "tensor"), None),
            P(None, "tensor"),
            P(None, "tensor"),
            P(None, "tensor"),
            P("tensor", None),
            P("tensor"),
            P("tensor"),
            P(),
            P(),
            P(),
            P("dp", None, "tensor"),
            P("dp", None, "tensor"),
            P("dp", "tensor", None),
        ),
        check_vma=False,
    )
```

```python
import functools
import math

import jax
import jax.numpy as jnp
from jax import lax
from jax.experimental import pallas as pl
from jax.experimental.pallas import tpu as pltpu
from jax.sharding import PartitionSpec as P

HEAD_DIM = 128


EPSILON = 1e-05
THETA = 10000.0
NEG_LARGE = -1e30


def root_mean_square_scale(values):
    return lax.rsqrt(jnp.mean(values * values, axis=-1, keepdims=True) + EPSILON)


def rope_tables(length, head_dim):
    half_dim = head_dim // 2
    freq_index = jnp.arange(half_dim, dtype=jnp.float32)
    frequency = THETA ** (-(2.0 * freq_index) / head_dim)
    angles = jnp.arange(length, dtype=jnp.float32)[:, None] * frequency[None, :]
    cosine = jnp.concatenate([jnp.cos(angles), jnp.cos(angles)], axis=1)
    sine_table = jnp.concatenate([jnp.sin(angles), jnp.sin(angles)], axis=1)
    return (cosine[:, None, :], sine_table[:, None, :])


def rotate(values, cosine, sine_table):
    half_dim = values.shape[-1] // 2
    turned = jnp.concatenate([-values[..., half_dim:], values[..., :half_dim]], axis=-1)
    return values * cosine + turned * sine_table


def unrotate(grad_rows, cosine, sine_table):
    half_dim = grad_rows.shape[-1] // 2
    scaled = grad_rows * sine_table
    turned = jnp.concatenate([scaled[..., half_dim:], -scaled[..., :half_dim]], axis=-1)
    return grad_rows * cosine + turned


def slot_positions(ids, experts):
    flat_ids = ids.reshape(-1)
    onehot = (flat_ids[:, None] == jnp.arange(experts, dtype=jnp.int32)[None, :]).astype(jnp.int32)
    running = jnp.cumsum(onehot, axis=0)
    return (flat_ids, jnp.sum(running * onehot, axis=1) - 1)


def block_scores(query_block, key_rows, file_row, block_start, score_scale):
    block_rows = query_block.shape[0]
    raw_scores = (
        jnp.einsum("qhd,khd->hqk", query_block, key_rows, preferred_element_type=jnp.float32)
        * score_scale
    )
    rows_at = block_start + jnp.arange(block_rows, dtype=jnp.int32)
    cols_at = jnp.arange(key_rows.shape[0], dtype=jnp.int32)
    allowed = (cols_at[None, :] <= rows_at[:, None]) & (file_row[None, :] == file_row[:, None])
    return jnp.where(allowed[None], raw_scores, NEG_LARGE)


MESH = pl.DeviceIdType.MESH
VMEM_LIMIT = 60 * 2**20


def greet(dp, z, nz):
    barrier = pltpu.get_barrier_semaphore()
    for flip in (1, 2, 4):
        pl.semaphore_signal(barrier, 1, device_id=(dp ^ flip, z), device_id_type=MESH)

    @pl.when(z > 0)
    def _():
        pl.semaphore_signal(barrier, 1, device_id=(dp, z - 1), device_id_type=MESH)

    @pl.when(z < nz - 1)
    def _():
        pl.semaphore_signal(barrier, 1, device_id=(dp, z + 1), device_id_type=MESH)

    ends = jnp.where(z > 0, 1, 0) + jnp.where(z < nz - 1, 1, 0)
    pl.semaphore_wait(barrier, 3 + ends)


def remote(src, dst, send, recv, device):
    return pltpu.make_async_remote_copy(
        src_ref=src, dst_ref=dst, send_sem=send, recv_sem=recv, device_id=device, device_id_type=MESH
    )


def experts_kernel(nz, x_ref, t_ref, g_ref, gate_ref, up_ref, down_ref, rows_ref, slopes_ref, gated_ref, tiles_ref, land, tags, g_buf, pre, back, gate_at, grad_at, local_sem, s_rows, s_g, sz, sx, sy, sda, sdb, sc, rz, rx, ry, rda, rdb, rc):
    dp, z = lax.axis_index("dp"), lax.axis_index("tensor")
    count, width = x_ref.shape
    half = count // 2
    both = back.shape[1]
    each = both // gate_at.shape[0]
    other = (dp ^ 1, z)

    def rows_at(flip, zz):
        place = dp ^ flip
        return land.at[place // 2, zz, pl.ds(pl.multiple_of((place % 2) * count, count), count)]

    def half_at(flip, zz, k):
        place = dp ^ flip
        return land.at[place // 2, zz, pl.ds(pl.multiple_of((place % 2) * count + k * half, half), half)]

    def tags_at(flip, zz):
        return tags.at[(dp ^ flip) * nz + zz]

    def whole(flip, zz, send, recv, device):
        return (
            remote(rows_at(flip, zz), rows_at(flip, zz), send(0), recv(0), device),
            remote(tags_at(flip, zz), tags_at(flip, zz), send(1), recv(1), device),
        )

    def z_copy(zz, step):
        return whole(0, zz, lambda k: sz.at[k, (step + 1) // 2, zz], lambda k: rz.at[k, zz], (dp, z + step))

    def x_copy(zz):
        return whole(0, zz, lambda k: sx.at[k, zz], lambda k: rx.at[k, zz], (dp ^ 2, z))

    def y_copy(zz):
        return whole(0, zz, lambda k: sy.at[k, zz], lambda k: ry.at[k, zz], (dp ^ 4, z))

    def a_copy(zz):
        return (
            remote(half_at(4, zz, 0), half_at(4, zz, 0), sda.at[0, zz], rda.at[0, zz], (dp ^ 2, z)),
            remote(tags_at(4, zz), tags_at(4, zz), sda.at[1, zz], rda.at[1, zz], (dp ^ 2, z)),
        )

    def b_copy(zz):
        return (remote(half_at(2, zz, 1), half_at(2, zz, 1), sdb.at[zz], rdb.at[zz], (dp ^ 4, z)),)

    def c_copy(kind, zz):
        send, recv = (lambda k: sc.at[k, kind, zz]), (lambda k: rc.at[k, kind, zz])
        if kind < 3:
            return whole((0, 2, 4)[kind], zz, send, recv, other)
        ref = half_at(6, zz, kind - 3)
        copies = (remote(ref, ref, send(0), recv(0), other),)
        if kind == 3:
            copies += (remote(tags_at(6, zz), tags_at(6, zz), send(1), recv(1), other),)
        return copies

    def start(copies):
        for copy in copies:
            copy.start()

    def arrived(ref, sem):
        remote(ref, ref, sem, sem, other).wait_recv()

    def both_arrived(flip, zz, recv):
        arrived(rows_at(flip, zz), recv(0))
        arrived(tags_at(flip, zz), recv(1))

    def held(distance, zz, sign):
        inside = (distance >= 0) & (distance < nz) & (zz >= 0) & (zz < nz)
        return inside & ((distance > 0) | (sign > 0))

    def spread(distance):
        for sign in (1, -1):
            zz = z + sign * distance

            @pl.when(held(distance, zz, sign))
            def _():
                @pl.when(distance > 0)
                def _():
                    both_arrived(0, zz, lambda k: rz.at[k, zz])

                @pl.when((zz <= z) & (z < nz - 1))
                def _():
                    start(z_copy(zz, 1))

                @pl.when((zz >= z) & (z > 0))
                def _():
                    start(z_copy(zz, -1))

                start(x_copy(zz))
                start(y_copy(zz))
                start(c_copy(0, zz))

    def relay(distance):
        for sign in (1, -1):
            zz = z + sign * distance

            @pl.when(held(distance, zz, sign))
            def _():
                both_arrived(4, zz, lambda k: ry.at[k, zz])
                start(a_copy(zz))
                start(c_copy(2, zz))
                both_arrived(2, zz, lambda k: rx.at[k, zz])
                start(b_copy(zz))
                start(c_copy(1, zz))

    def corner(distance):
        for sign in (1, -1):
            zz = z + sign * distance

            @pl.when(held(distance, zz, sign))
            def _():
                arrived(half_at(6, zz, 0), rda.at[0, zz])
                arrived(tags_at(6, zz), rda.at[1, zz])
                start(c_copy(3, zz))
                arrived(half_at(6, zz, 1), rdb.at[zz])
                start(c_copy(4, zz))

    def store_rows(chip, zz):
        return pltpu.make_async_copy(land.at[chip, zz], rows_ref.at[chip, zz], s_rows.at[chip, zz])

    def load_g(chip, zz, c):
        return pltpu.make_async_copy(
            g_ref.at[(2 * chip + c) * nz + zz], g_buf.at[pl.ds(c * count, count)], s_g.at[c]
        )

    diagonal = (
        lax.broadcasted_iota(jnp.int32, (count, count), 0) == lax.broadcasted_iota(jnp.int32, (count, count), 1)
    ).astype(jnp.float32)

    def experts(chip, zz):
        store_rows(chip, zz).start()
        for c in range(2):
            load_g(chip, zz, c).start()
        x = land.at[chip, zz]

        for k, ref in enumerate((gate_ref, up_ref)):
            for j in range(gate_at.shape[0]):
                pre[:, pl.ds(k * both + j * each, each)] = jnp.dot(
                    x[...], ref[j], preferred_element_type=jnp.float32
                )
        for j in range(gate_at.shape[0]):
            for c in range(2):
                row = tags[(2 * chip + c) * nz + zz, pl.ds(dp * gate_at.shape[0] + j, 1), :]
                column = jnp.sum(diagonal * row, axis=1, keepdims=True)
                gate_at[j, pl.ds(c * count, count), :] = jnp.broadcast_to(column, (count, 128))
        for c in range(2):
            load_g(chip, zz, c).wait()

        for j in range(gate_at.shape[0]):
            back[:, pl.ds(j * each, each)] = lax.dot_general(
                g_buf[...], down_ref[j], (((1,), (1,)), ((), ())), preferred_element_type=jnp.float32
            )

        def elementwise(k, carry):
            at = pl.ds(pl.multiple_of(k * 64, 64), 64)
            place, inner = 2 * chip + k // (count // 64), pl.ds(pl.multiple_of(k % (count // 64) * 64, 64), 64)
            for j in range(gate_at.shape[0]):
                cols, up_cols = pl.ds(j * each, each), pl.ds(both + j * each, each)
                gate = jnp.concatenate([gate_at[j, at, :]] * (each // 128), axis=1)
                gate_pre, up_pre, grad = pre[at, cols], pre[at, up_cols], back[at, cols]
                sigmoid = 1.0 / (1.0 + jnp.exp(-gate_pre))
                silu = gate_pre * sigmoid
                hidden = silu * up_pre
                gated_ref[place, zz, inner, cols] = (gate * hidden).astype(gated_ref.dtype)
                share = jnp.sum(hidden * grad, axis=1, keepdims=True)
                grad_at[j, at, :] = jnp.broadcast_to(share, (64, 128))
                slope = gate * grad
                slopes_ref[chip, zz, at, cols] = (
                    slope * up_pre * sigmoid * (1.0 + gate_pre * (1.0 - sigmoid))
                ).astype(slopes_ref.dtype)
                slopes_ref[chip, zz, at, up_cols] = (slope * silu).astype(slopes_ref.dtype)
            return carry

        lax.fori_loop(0, 2 * count // 64, elementwise, 0)
        for c in range(2):
            shares = [
                jnp.sum(diagonal * grad_at[j, pl.ds(c * count, count), :], axis=0, keepdims=True)
                for j in range(gate_at.shape[0])
            ]
            shares.append(jnp.zeros((8 - len(shares), count), jnp.float32))
            tiles_ref[(2 * chip + c) * nz + zz] = jnp.concatenate(shares, axis=0)

    def job(step, k):
        kind, sign = k // 2, 1 - 2 * (k % 2)
        distance = step - 1 - (kind + 1) // 2
        zz = z + sign * distance
        flip = 2 * kind

        @pl.when(held(distance, zz, sign))
        def _():
            @pl.when(kind < 3)
            def _():
                both_arrived(flip + 1, zz, lambda m: rc.at[m, kind, zz])

            @pl.when(kind == 3)
            def _():
                arrived(half_at(7, zz, 0), rc.at[0, 3, zz])
                arrived(tags_at(7, zz), rc.at[1, 3, zz])
                arrived(half_at(7, zz, 1), rc.at[0, 4, zz])

            experts((dp ^ flip) // 2, zz)

    keep = pltpu.make_async_copy(x_ref, rows_at(0, z), local_sem.at[0])
    keep_tags = pltpu.make_async_copy(t_ref, tags_at(0, z), local_sem.at[1])
    keep.start()
    keep_tags.start()
    greet(dp, z, nz)
    keep.wait()
    keep_tags.wait()

    def step_body(step, carry):
        spread(step)
        relay(step - 1)
        corner(step - 2)

        def inner(k, inner_carry):
            job(step, k)
            return inner_carry

        lax.fori_loop(0, 8, inner, 0)
        return carry

    lax.fori_loop(0, nz + 3, step_body, 0)

    def sent(copies):
        for copy in copies:
            copy.wait_send()

    for zz in range(nz):

        @pl.when((zz <= z) & (z < nz - 1))
        def _():
            sent(z_copy(zz, 1))

        @pl.when((zz >= z) & (z > 0))
        def _():
            sent(z_copy(zz, -1))

        sent(x_copy(zz))
        sent(y_copy(zz))
        sent(a_copy(zz))
        sent(b_copy(zz))
        for kind in range(5):
            sent(c_copy(kind, zz))
        for chip in range(4):
            store_rows(chip, zz).wait()


def gather_experts(x, gates, cotangents, w_gate, w_up, w_down, nz, collective_id):
    rows, width = x.shape
    experts_here, each, _ = w_down.shape
    both = experts_here * each
    dma, vmem = pltpu.SemaphoreType.DMA, pl.BlockSpec(memory_space=pltpu.VMEM)
    any_place = pl.BlockSpec(memory_space=pl.ANY)
    group = (4, nz, 2 * rows)
    flops = 2 * 8 * nz * rows * width * 3 * both
    return pl.pallas_call(
        functools.partial(experts_kernel, nz),
        name="gather_experts",
        out_shape=(
            jax.ShapeDtypeStruct(group + (width,), x.dtype),
            jax.ShapeDtypeStruct(group + (2 * both,), x.dtype),
            jax.ShapeDtypeStruct((8, nz, rows, both), x.dtype),
            jax.ShapeDtypeStruct((8 * nz, 8, rows), jnp.float32),
        ),
        in_specs=[vmem, vmem, any_place, vmem, vmem, vmem],
        out_specs=(any_place, vmem, vmem, vmem),
        scratch_shapes=[
            pltpu.VMEM(group + (width,), x.dtype),
            pltpu.VMEM((8 * nz,) + gates.shape, gates.dtype),
            pltpu.VMEM((2 * rows, width), x.dtype),
            pltpu.VMEM((2 * rows, 2 * both), jnp.float32),
            pltpu.VMEM((2 * rows, both), jnp.float32),
            pltpu.VMEM((experts_here, 2 * rows, 128), jnp.float32),
            pltpu.VMEM((experts_here, 2 * rows, 128), jnp.float32),
            dma((2,)),
            dma((4, nz)),
            dma((2,)),
        ]
        + [dma((2, 2, nz)), dma((2, nz)), dma((2, nz)), dma((2, nz)), dma((nz,)), dma((2, 5, nz))]
        + [dma((2, nz)), dma((2, nz)), dma((2, nz)), dma((2, nz)), dma((nz,)), dma((2, 5, nz))],
        compiler_params=pltpu.CompilerParams(
            collective_id=collective_id, has_side_effects=True, vmem_limit_bytes=VMEM_LIMIT
        ),
        cost_estimate=pl.CostEstimate(flops=flops, bytes_accessed=64 * 2**20, transcendentals=0),
    )(x, gates, cotangents, w_gate, w_up, w_down)


def greet_line(dp, z, nz):
    barrier = pltpu.get_barrier_semaphore()

    @pl.when(z > 0)
    def _():
        pl.semaphore_signal(barrier, 1, device_id=(dp, z - 1), device_id_type=MESH)

    @pl.when(z < nz - 1)
    def _():
        pl.semaphore_signal(barrier, 1, device_id=(dp, z + 1), device_id_type=MESH)

    pl.semaphore_wait(barrier, jnp.where(z > 0, 1, 0) + jnp.where(z < nz - 1, 1, 0))


PARTS = 2
PIECES = 2


def greet_total(dp, z, nz):
    barrier = pltpu.get_barrier_semaphore()
    for flip in (1, 2, 4):
        pl.semaphore_signal(barrier, 1, device_id=(dp ^ flip, z), device_id_type=MESH)
    for turn in range(1, nz):
        pl.semaphore_signal(barrier, 1, device_id=(dp, lax.rem(z + turn, nz)), device_id_type=MESH)
    pl.semaphore_wait(barrier, 2 + nz)


class Total:
    steps = 5

    def __init__(self, nz, dp, z, got, s_plane, r_plane, s_line, r_line):
        self.nz, self.z, self.got = nz, z, got
        self.plane = [
            remote(got.at[2 * k], got.at[2 * k + 1], s_plane.at[k], r_plane.at[k], (dp ^ flip, z))
            for k, flip in enumerate((1, 2, 4))
        ]
        self.line = [
            remote(got.at[6], got.at[6 + turn], s_line.at[turn - 1], r_line.at[turn - 1], (dp, lax.rem(z + turn, nz)))
            for turn in range(1, nz)
        ]

    def step(self, k, out_ref):
        got, nz = self.got, self.nz
        if 1 <= k <= 3:
            self.plane[k - 1].wait()
            got[2 * k] = got[2 * k - 2] + got[2 * k - 1]
        if k < 3:
            self.plane[k].start()
        elif k == 3:
            for copy in self.line:
                copy.start()
        else:
            for copy in self.line:
                copy.wait()
            total = got[6 + lax.rem(self.z, nz)]
            for zz in range(1, nz):
                total = total + got[6 + lax.rem(self.z - zz + nz, nz)]
            out_ref[...] = total


def total_scratch(nz, shape, dtype):
    dma = pltpu.SemaphoreType.DMA
    return [pltpu.VMEM((6 + nz,) + shape, dtype), dma((3,)), dma((3,)), dma((nz - 1,)), dma((nz - 1,))]


def line_gather_kernel(nz, *refs):
    dp, z = lax.axis_index("dp"), lax.axis_index("tensor")
    summed = len(refs) > 6
    if summed:
        x_ref, small_ref, out_ref, total_ref, local_sem, s_up, s_down, r_line = refs[:8]
        greet_total(dp, z, nz)
        total = Total(nz, dp, z, *refs[8:])
        total.got[0] = small_ref[...]
    else:
        x_ref, out_ref, local_sem, s_up, s_down, r_line = refs
        greet_line(dp, z, nz)
    part = x_ref.shape[0] // PARTS

    def copy(zz, k, step, own):
        at = pl.ds(k * part, part)
        dst = out_ref.at[zz, at]
        sems = s_up if step > 0 else s_down
        return remote(x_ref.at[at] if own else dst, dst, sems.at[zz, k], r_line.at[zz, k], (dp, z + step))

    keep = pltpu.make_async_copy(x_ref, out_ref.at[z], local_sem)
    for distance in range(nz):
        for k in range(PARTS):
            for sign in (0,) if distance == 0 else (-1, 1):
                zz, own = z + sign * distance, distance == 0

                @pl.when((zz >= 0) & (zz < nz))
                def _():
                    if not own:
                        copy(zz, k, 1, False).wait_recv()
                    if sign <= 0:

                        @pl.when(z < nz - 1)
                        def _():
                            copy(zz, k, 1, own).start()

                    if sign >= 0:

                        @pl.when(z > 0)
                        def _():
                            copy(zz, k, -1, own).start()

        if distance == 0:
            keep.start()
        if summed:
            total.step(distance, total_ref)
    if summed:
        for k in range(nz, Total.steps):
            total.step(k, total_ref)
    keep.wait()
    for zz in range(nz):
        for k in range(PARTS):

            @pl.when((zz <= z) & (z < nz - 1))
            def _():
                copy(zz, k, 1, False).wait_send()

            @pl.when((zz >= z) & (z > 0))
            def _():
                copy(zz, k, -1, False).wait_send()


def line_gather(x, nz, collective_id, small=None):
    dma, vmem = pltpu.SemaphoreType.DMA, pl.BlockSpec(memory_space=pltpu.VMEM)
    blocks = jax.ShapeDtypeStruct((nz,) + x.shape, x.dtype)
    scratch = [dma(())] + [dma((nz, PARTS)) for _ in range(3)]
    params = pltpu.CompilerParams(
        collective_id=collective_id, has_side_effects=True, vmem_limit_bytes=8 * 2**20
    )
    kernel = functools.partial(line_gather_kernel, nz)
    if small is None:
        return pl.pallas_call(
            kernel,
            name="line_gather",
            out_shape=blocks,
            in_specs=[vmem],
            out_specs=pl.BlockSpec(memory_space=pl.ANY),
            scratch_shapes=scratch,
            compiler_params=params,
        )(x)
    return pl.pallas_call(
        kernel,
        name="line_gather_total",
        out_shape=(blocks, jax.ShapeDtypeStruct(small.shape, small.dtype)),
        in_specs=[vmem, vmem],
        out_specs=(pl.BlockSpec(memory_space=pl.ANY), vmem),
        scratch_shapes=scratch + total_scratch(nz, small.shape, small.dtype),
        compiler_params=params,
    )(x, small)


def line_total_kernel(nz, x_ref, out_ref, got, send, recv):
    dp, z = lax.axis_index("dp"), lax.axis_index("tensor")
    others = [lax.rem(z + turn, nz) for turn in range(1, nz)]
    barrier = pltpu.get_barrier_semaphore()
    for other in others:
        pl.semaphore_signal(barrier, 1, device_id=(dp, other), device_id_type=MESH)
    pl.semaphore_wait(barrier, nz - 1)
    copies = [
        remote(x_ref, got.at[turn], send.at[turn], recv.at[turn], (dp, other)) for turn, other in enumerate(others)
    ]
    for copy in copies:
        copy.start()
    for copy in copies:
        copy.wait()
    total = x_ref[...]
    for turn in range(nz - 1):
        total = total + got[turn]
    out_ref[...] = total


def line_total(x, nz, collective_id):
    dma, vmem = pltpu.SemaphoreType.DMA, pl.BlockSpec(memory_space=pltpu.VMEM)
    return pl.pallas_call(
        functools.partial(line_total_kernel, nz),
        name="line_total",
        out_shape=jax.ShapeDtypeStruct(x.shape, x.dtype),
        in_specs=[vmem],
        out_specs=vmem,
        scratch_shapes=[pltpu.VMEM((nz - 1,) + x.shape, x.dtype), dma((nz - 1,)), dma((nz - 1,))],
        compiler_params=pltpu.CompilerParams(
            collective_id=collective_id, has_side_effects=True, vmem_limit_bytes=4 * 2**20
        ),
    )(x)


CHUNK = 16


def add_rows(dst, *others, start=0, count):
    def body(k, carry):
        at = pl.ds(start + k * CHUNK, CHUNK)
        total = dst[at, :].astype(jnp.float32)
        for ref, base in others:
            total = total + ref[pl.ds(base + k * CHUNK, CHUNK), :].astype(jnp.float32)
        dst[at, :] = total.astype(dst.dtype)
        return carry

    lax.fori_loop(0, count // CHUNK, body, 0)


class Line:
    def __init__(self, nz, dp, z, acc, up, down, s_up, r_up, s_down, r_down):
        self.nz, self.dp, self.z, self.acc, self.up, self.down = nz, dp, z, acc, up, down
        self.sems = s_up, r_up, s_down, r_down
        self.part = acc.shape[1] // PARTS

    def copy(self, zz, k, step):
        at = pl.ds(k * self.part, self.part)
        s_up, r_up, s_down, r_down = self.sems
        if step > 0:
            return remote(self.acc.at[zz, at], self.up.at[zz, at], s_up.at[zz, k], r_up.at[zz, k], (self.dp, self.z + 1))
        return remote(self.acc.at[zz, at], self.down.at[zz, at], s_down.at[zz, k], r_down.at[zz, k], (self.dp, self.z - 1))

    def first(self):
        nz, z = self.nz, self.z

        @pl.when(z == 0)
        def _():
            for zz in range(nz - 1, 0, -1):
                for k in range(PARTS):
                    self.copy(zz, k, 1).start()

        @pl.when(z == nz - 1)
        def _():
            for zz in range(nz - 1):
                for k in range(PARTS):
                    self.copy(zz, k, -1).start()

    def step(self, distance):
        nz, z = self.nz, self.z
        for k in range(PARTS):
            for sign in (1, -1):
                far = nz - distance if sign > 0 else distance - 1
                through = (far > z) & (z > 0) if sign > 0 else (far < z) & (z < nz - 1)

                @pl.when(through)
                def _():
                    self.copy(far, k, sign).wait_recv()
                    source = self.up if sign > 0 else self.down
                    add_rows(self.acc.at[far], (source.at[far], k * self.part), start=k * self.part, count=self.part)
                    self.copy(far, k, sign).start()

    def finish(self, out_ref):
        nz, z = self.nz, self.z
        for k in range(PARTS):

            @pl.when(z > 0)
            def _():
                self.copy(z, k, 1).wait_recv()

            @pl.when(z < nz - 1)
            def _():
                self.copy(z, k, -1).wait_recv()

        def body(k, carry):
            at = pl.ds(k * CHUNK, CHUNK)
            total = self.acc[z, at, :].astype(jnp.float32)
            zero = jnp.zeros_like(total)
            total = total + jnp.where(z > 0, self.up[z, at, :].astype(jnp.float32), zero)
            total = total + jnp.where(z < nz - 1, self.down[z, at, :].astype(jnp.float32), zero)
            out_ref[at, :] = total
            return carry

        lax.fori_loop(0, out_ref.shape[0] // CHUNK, body, 0)

    def drain(self):
        nz, z = self.nz, self.z
        for zz in range(nz):
            for k in range(PARTS):

                @pl.when(zz > z)
                def _():
                    self.copy(zz, k, 1).wait_send()

                @pl.when(zz < z)
                def _():
                    self.copy(zz, k, -1).wait_send()


def line_scatter_kernel(nz, p_ref, out_ref, acc, up, down, local_sem, s_up, r_up, s_down, r_down):
    dp, z = lax.axis_index("dp"), lax.axis_index("tensor")
    loaded = pltpu.make_async_copy(p_ref, acc, local_sem)
    loaded.start()
    greet_line(dp, z, nz)
    loaded.wait()
    line = Line(nz, dp, z, acc, up, down, s_up, r_up, s_down, r_down)
    line.first()
    for distance in range(1, nz - 1):
        line.step(distance)
    line.finish(out_ref)
    line.drain()


def line_scatter(p, nz, collective_id):
    _, rows, width = p.shape
    dma, vmem = pltpu.SemaphoreType.DMA, functools.partial(pltpu.VMEM, dtype=p.dtype)
    return pl.pallas_call(
        functools.partial(line_scatter_kernel, nz),
        name="line_scatter",
        out_shape=jax.ShapeDtypeStruct((rows, width), jnp.float32),
        in_specs=[pl.BlockSpec(memory_space=pl.ANY)],
        out_specs=pl.BlockSpec(memory_space=pltpu.VMEM),
        scratch_shapes=[vmem((nz, rows, width)) for _ in range(3)]
        + [dma(())]
        + [dma((nz, PARTS)) for _ in range(4)],
        compiler_params=pltpu.CompilerParams(
            collective_id=collective_id, has_side_effects=True, vmem_limit_bytes=16 * 2**20
        ),
    )(p)


def z_order(nz):
    return [sorted(range(nz), key=lambda zz: (-abs(zz - z), zz if z >= nz // 2 else -zz)) for z in range(nz)]


def scatter_kernel(nz, p_ref, gate_ref, up_ref, t_ref, out_ref, tiles_ref, parts, weights, rc, ra, rb, rx, ry, ru, rd, s_weight, s_tile, r_tile, s_keep, s_core, r_core, s_a, r_a, s_b, r_b, s_x, r_x, s_y, r_y, s_u, r_u, s_d, r_d):
    dp, z = lax.axis_index("dp"), lax.axis_index("tensor")
    rows = parts.shape[3]
    half = rows // 2
    core = dp % 2

    def acc(kind, zz):
        return parts.at[kind, zz, core]

    order = z_order(nz)

    def place(i):
        zz = order[0][i]
        for zv in range(1, nz):
            zz = jnp.where(z == zv, order[zv][i], zz)
        return zz

    flips = (0, 2, 4, 6)

    def core_copy(kind, zz):
        return remote(
            parts.at[kind, zz, 1 - core], rc.at[kind, zz], s_core.at[kind, zz], r_core.at[kind, zz], (dp ^ 1, z)
        )

    def product(kind, zz):
        slopes = p_ref.at[(dp ^ (2 * kind)) // 2, zz]

        def tile(n, carry):
            at = pl.ds(pl.multiple_of(n * 256, 256), 256)
            total = lax.dot_general(
                slopes[...], weights[at, :], (((1,), (1,)), ((), ())), preferred_element_type=jnp.float32
            ).astype(parts.dtype)
            parts[kind, zz, 0, :, at] = total[:rows]
            parts[kind, zz, 1, :, at] = total[rows:]
            return carry

        lax.fori_loop(0, parts.shape[4] // 256, tile, 0, unroll=2)

    def a_copy(zz):
        return remote(acc(3, zz).at[pl.ds(0, half)], ra.at[zz], s_a.at[zz], r_a.at[zz], (dp ^ 2, z))

    def b_copy(zz):
        return remote(acc(3, zz).at[pl.ds(half, half)], rb.at[zz], s_b.at[zz], r_b.at[zz], (dp ^ 4, z))

    def x_copy(zz):
        return remote(acc(1, zz), rx.at[zz], s_x.at[zz], r_x.at[zz], (dp ^ 2, z))

    def y_copy(zz):
        return remote(acc(2, zz), ry.at[zz], s_y.at[zz], r_y.at[zz], (dp ^ 4, z))

    def up_copy(zz):
        return remote(acc(0, zz), ru.at[zz], s_u.at[zz], r_u.at[zz], (dp, z + 1))

    def down_copy(zz):
        return remote(acc(0, zz), rd.at[zz], s_d.at[zz], r_d.at[zz], (dp, z - 1))

    def add(dst, *others, start=0, count=rows):
        add_rows(dst, *others, start=start, count=count)

    def wave(i):
        zz = place(i)

        def one(k, carry):
            kind = 3 - k
            product(kind, zz)
            core_copy(kind, zz).start()
            return carry

        lax.fori_loop(0, 4, one, 0)

    def paired(kind, zz):
        core_copy(kind, zz).wait_recv()

    def stage_diagonal(i):
        zz = place(i)
        paired(3, zz)
        add(acc(3, zz), (rc.at[3, zz], 0))
        a_copy(zz).start()
        b_copy(zz).start()

    def stage_side(i):
        zz = place(i)
        paired(1, zz)
        paired(2, zz)
        a_copy(zz).wait_recv()
        add(acc(2, zz), (rc.at[2, zz], 0), (ra.at[zz], 0), start=0, count=half)
        add(acc(2, zz), (rc.at[2, zz], half), start=half, count=half)
        y_copy(zz).start()
        b_copy(zz).wait_recv()
        add(acc(1, zz), (rc.at[1, zz], half), (rb.at[zz], 0), start=half, count=half)
        add(acc(1, zz), (rc.at[1, zz], 0), start=0, count=half)
        x_copy(zz).start()

    def stage_column(i):
        zz = place(i)
        paired(0, zz)
        x_copy(zz).wait_recv()
        y_copy(zz).wait_recv()
        add(acc(0, zz), (rc.at[0, zz], 0), (rx.at[zz], 0), (ry.at[zz], 0))

        @pl.when((zz > z) & (z == 0))
        def _():
            up_copy(zz).start()

        @pl.when((zz < z) & (z == nz - 1))
        def _():
            down_copy(zz).start()

    def stage_line(i):
        zz = place(i)

        @pl.when((zz > z) & (z > 0))
        def _():
            up_copy(zz).wait_recv()
            add(acc(0, zz), (ru.at[zz], 0))
            up_copy(zz).start()

        @pl.when((zz < z) & (z < nz - 1))
        def _():
            down_copy(zz).wait_recv()
            add(acc(0, zz), (rd.at[zz], 0))
            down_copy(zz).start()

    def peers():
        for flip in range(8):
            for turn in range(nz):
                if flip or turn:
                    yield flip, turn, dp ^ flip, lax.rem(z + turn, nz)

    def tile_copy(flip, turn, peer, line):
        here = dp * nz + z
        return remote(
            t_ref.at[peer * nz + line], tiles_ref.at[here], s_tile.at[flip, turn], r_tile.at[flip, turn], (peer, line)
        )

    each = gate_ref.shape[2]
    here = gate_ref.shape[0]
    fetch = [
        pltpu.make_async_copy(
            ref.at[j], weights.at[:, pl.ds((k * here + j) * each, each)], s_weight.at[k, j]
        )
        for k, ref in enumerate((gate_ref, up_ref))
        for j in range(here)
    ]
    for copy in fetch:
        copy.start()
    barrier = pltpu.get_barrier_semaphore()
    for _, _, peer, line in peers():
        pl.semaphore_signal(barrier, 1, device_id=(peer, line), device_id_type=MESH)
    pl.semaphore_wait(barrier, 8 * nz - 1)
    for copy in fetch:
        copy.wait()
    wave(0)
    keep = pltpu.make_async_copy(t_ref.at[dp * nz + z], tiles_ref.at[dp * nz + z], s_keep)
    keep.start()
    for peer in peers():
        tile_copy(*peer).start()
    for i in range(nz + 3):
        if i < nz:
            stage_diagonal(i)
        if i + 1 < nz:
            wave(i + 1)
        if 0 <= i - 1 < nz:
            stage_side(i - 1)
        if 0 <= i - 2 < nz:
            stage_column(i - 2)
        if 0 <= i - 3 < nz:
            stage_line(i - 3)

    keep.wait()
    for flip, turn, peer, line in peers():
        tile_copy(flip, turn, peer, line).wait_send()
        source = tiles_ref.at[peer * nz + lax.rem(z - turn + nz, nz)]
        remote(source, source, s_tile.at[flip, turn], r_tile.at[flip, turn], (dp ^ 1, z)).wait_recv()

    @pl.when(z > 0)
    def _():
        up_copy(z).wait_recv()

    @pl.when(z < nz - 1)
    def _():
        down_copy(z).wait_recv()

    def finish(k, carry):
        at = pl.ds(k * CHUNK, CHUNK)
        total = parts[0, z, core, at, :].astype(jnp.float32)
        zero = jnp.zeros_like(total)
        total = total + jnp.where(z > 0, ru[z, at, :].astype(jnp.float32), zero)
        total = total + jnp.where(z < nz - 1, rd[z, at, :].astype(jnp.float32), zero)
        out_ref[at, :] = total
        return carry

    lax.fori_loop(0, rows // CHUNK, finish, 0)
    for zz in range(nz):
        for kind in range(4):
            core_copy(kind, zz).wait_send()
        a_copy(zz).wait_send()
        b_copy(zz).wait_send()
        x_copy(zz).wait_send()
        y_copy(zz).wait_send()

        @pl.when(zz > z)
        def _():
            up_copy(zz).wait_send()

        @pl.when(zz < z)
        def _():
            down_copy(zz).wait_send()


def scatter_all(p, w_gate, w_up, tiles, nz, collective_id):
    rows, width = p.shape[2] // 2, w_gate.shape[1]
    dma, vmem = pltpu.SemaphoreType.DMA, functools.partial(pltpu.VMEM, dtype=p.dtype)
    half = rows // 2
    return pl.pallas_call(
        functools.partial(scatter_kernel, nz),
        name="scatter_all",
        out_shape=(
            jax.ShapeDtypeStruct((rows, width), jnp.float32),
            jax.ShapeDtypeStruct(tiles.shape, tiles.dtype),
        ),
        in_specs=[
            pl.BlockSpec(memory_space=pltpu.VMEM),
            *[pl.BlockSpec(memory_space=pl.ANY)] * 2,
            pl.BlockSpec(memory_space=pltpu.VMEM),
        ],
        out_specs=(pl.BlockSpec(memory_space=pltpu.VMEM), pl.BlockSpec(memory_space=pltpu.VMEM)),
        scratch_shapes=[vmem((4, nz, 2, rows, width)), vmem((width, p.shape[3])), vmem((4, nz, rows, width))]
        + [vmem((nz, half, width)) for _ in range(2)]
        + [vmem((nz, rows, width)) for _ in range(4)]
        + [dma((2, w_gate.shape[0])), dma((8, nz)), dma((8, nz)), dma(())]
        + [dma((4, nz)), dma((4, nz))]
        + [dma((nz,)) for _ in range(12)],
        compiler_params=pltpu.CompilerParams(
            collective_id=collective_id, has_side_effects=True, vmem_limit_bytes=VMEM_LIMIT
        ),
    )(p, w_gate, w_up, tiles)


def finish_kernel(nz, nc, g_ref, h_ref, p_ref, e_ref, unit_ref, small_ref, sum_q, sum_k, sum_v, sum_o, out_ref, routed_ref, total_ref, buf, acc, rc, ra, rb, rx, ry, line_acc, up, down, more_acc, more_got, *sems):
    (s_load, s_core, r_core, s_a, r_a, s_b, r_b, s_x, r_x, s_y, r_y) = sems[:11]
    (t_x, q_x, t_y, q_y, t_a, q_a, t_b, q_b, t_c, q_c) = sems[11:21]
    s_line, s_store, s_up, r_up, s_down, r_down = sems[21:27]
    (s_load_more, s_more, r_more), sems = sems[27:30], sems[:27] + sems[30:]
    total = Total(nz, lax.axis_index("dp"), lax.axis_index("tensor"), *sems[27:])
    dp, z = lax.axis_index("dp"), lax.axis_index("tensor")
    rows = acc.shape[2]
    half = rows // 2
    flips = (0, 2, 4, 6)

    parts = ((g_ref, 0, g_ref.shape[2]), (h_ref, g_ref.shape[2], h_ref.shape[2]))

    def loads(kind, c):
        return [
            pltpu.make_async_copy(
                ref.at[(dp ^ flips[kind]) * nc + c], acc.at[kind, c, :, pl.ds(at, size)], s_load.at[k, kind, c]
            )
            for k, (ref, at, size) in enumerate(parts)
        ]

    def core_copies(kind, c):
        return [
            remote(
                ref.at[(dp ^ flips[kind] ^ 1) * nc + c],
                rc.at[kind, c, :, pl.ds(at, size)],
                s_core.at[k, kind, c],
                r_core.at[k, kind, c],
                (dp ^ 1, z),
            )
            for k, (ref, at, size) in enumerate(parts)
        ]

    def a_copy(c):
        return remote(acc.at[3, c, pl.ds(0, half)], ra.at[c], s_a.at[c], r_a.at[c], (dp ^ 2, z))

    def b_copy(c):
        return remote(acc.at[3, c, pl.ds(half, half)], rb.at[c], s_b.at[c], r_b.at[c], (dp ^ 4, z))

    def x_copy(c):
        return remote(acc.at[1, c], rx.at[c], s_x.at[c], r_x.at[c], (dp ^ 2, z))

    def y_copy(c):
        return remote(acc.at[2, c], ry.at[c], s_y.at[c], r_y.at[c], (dp ^ 4, z))

    def full(flip, c):
        return buf.at[(dp ^ flip) * nc + c]

    def back_x(c):
        return remote(full(0, c), full(0, c), t_x.at[c], q_x.at[c], (dp ^ 2, z))

    def back_y(c):
        return remote(full(0, c), full(0, c), t_y.at[c], q_y.at[c], (dp ^ 4, z))

    def back_a(c):
        ref = full(4, c).at[pl.ds(0, half)]
        return remote(ref, ref, t_a.at[c], q_a.at[c], (dp ^ 2, z))

    def back_b(c):
        ref = full(2, c).at[pl.ds(half, half)]
        return remote(ref, ref, t_b.at[c], q_b.at[c], (dp ^ 4, z))

    def back_core(kind, c):
        ref = full((0, 2, 4, 6, 6)[kind], c)
        if kind >= 3:
            ref = ref.at[pl.ds((kind - 3) * half, half)]
        return remote(ref, ref, t_c.at[kind, c], q_c.at[kind, c], (dp ^ 1, z))

    def arrived(ref, sem):
        remote(ref, ref, sem, sem, (dp ^ 1, z)).wait_recv()

    def paired(kind, c):
        for copy in loads(kind, c):
            copy.wait()
        for copy in core_copies(kind, c):
            copy.wait_recv()

    def stage_diagonal(c):
        paired(3, c)
        add_rows(acc.at[3, c], (rc.at[3, c], 0), count=rows)
        a_copy(c).start()
        b_copy(c).start()

    def stage_side(c):
        paired(1, c)
        paired(2, c)
        a_copy(c).wait_recv()
        add_rows(acc.at[2, c], (rc.at[2, c], 0), (ra.at[c], 0), start=0, count=half)
        add_rows(acc.at[2, c], (rc.at[2, c], half), start=half, count=half)
        y_copy(c).start()
        b_copy(c).wait_recv()
        add_rows(acc.at[1, c], (rc.at[1, c], half), (rb.at[c], 0), start=half, count=half)
        add_rows(acc.at[1, c], (rc.at[1, c], 0), start=0, count=half)
        x_copy(c).start()

    def stage_own(c):
        paired(0, c)
        x_copy(c).wait_recv()
        y_copy(c).wait_recv()
        dst = full(0, c)

        def body(k, carry):
            at = pl.ds(k * CHUNK, CHUNK)
            total = acc[0, c, at, :].astype(jnp.float32) + rc[0, c, at, :].astype(jnp.float32)
            total = total + rx[c, at, :].astype(jnp.float32) + ry[c, at, :].astype(jnp.float32)
            dst[at, :] = total.astype(dst.dtype)
            return carry

        lax.fori_loop(0, rows // CHUNK, body, 0)
        back_x(c).start()
        back_y(c).start()
        back_core(0, c).start()

    def stage_relay(c):
        arrived(full(4, c), q_y.at[c])
        back_a(c).start()
        back_core(2, c).start()
        arrived(full(2, c), q_x.at[c])
        back_b(c).start()
        back_core(1, c).start()

    def stage_corner(c):
        arrived(full(6, c).at[pl.ds(0, half)], q_a.at[c])
        back_core(3, c).start()
        arrived(full(6, c).at[pl.ds(half, half)], q_b.at[c])
        back_core(4, c).start()

    line_load = pltpu.make_async_copy(p_ref, line_acc, s_line)
    line_load.start()
    more_load = pltpu.make_async_copy(e_ref, more_acc, s_load_more)
    more_load.start()
    for c in range(nc):
        for kind in (3, 1, 2, 0):
            for copy in loads(kind, c):
                copy.start()
    greet_total(dp, z, nz)
    for c in range(nc):
        for kind in (3, 1, 2, 0):
            for copy in core_copies(kind, c):
                copy.start()
    line = Line(nz, dp, z, line_acc, up, down, s_up, r_up, s_down, r_down)
    line_load.wait()
    line.first()

    def line_end():
        line.finish(out_ref)
        line.drain()
        share = jnp.sum(out_ref[...] * unit_ref[...], axis=0, keepdims=True)
        total.got[0] = small_ref[...]
        wide = small_ref.shape[1]
        for k in range(out_ref.shape[1] // wide):
            total.got[0, k : k + 1, :] = share[:, k * wide : (k + 1) * wide]

    others = [lax.rem(z + turn, nz) for turn in range(1, nz)]
    more = [
        remote(more_acc.at[place], more_got.at[turn], s_more.at[turn], r_more.at[turn], (dp, place))
        for turn, place in enumerate(others)
    ]

    def more_start():
        more_load.wait()
        for copy in more:
            copy.start()

    def more_end():
        for copy in more:
            copy.wait()

        def body(k, carry):
            at = pl.ds(k * CHUNK, CHUNK)
            part = more_acc[z, at, :].astype(jnp.float32)
            for turn in range(nz - 1):
                part = part + more_got[turn, at, :].astype(jnp.float32)
            routed_ref[at, :] = part
            return carry

        lax.fori_loop(0, routed_ref.shape[0] // CHUNK, body, 0)

    side = [functools.partial(line.step, distance) for distance in range(1, nz - 1)] + [line_end, more_start]
    late = [functools.partial(total.step, k, total_ref) for k in range(3)] + [more_end]
    late += [functools.partial(total.step, k, total_ref) for k in range(3, Total.steps)]
    stages = (stage_diagonal, stage_side, stage_own, stage_relay, stage_corner)
    for i in range(nc + len(stages) - 1):
        for lag, stage in enumerate(stages):
            if 0 <= i - lag < nc:
                stage(i - lag)
                if i >= 1 and side:
                    side.pop(0)()
    for one in side + late:
        one()
    for c in range(nc):
        for kind, flip in ((0, 1), (1, 3), (2, 5)):
            arrived(full(flip, c), q_c.at[kind, c])
        for kind in (3, 4):
            arrived(full(7, c).at[pl.ds((kind - 3) * half, half)], q_c.at[kind, c])
    wide = buf.shape[2] // 4
    stores = [
        pltpu.make_async_copy(buf.at[:, :, pl.ds(k * wide, wide)], ref, s_store.at[k])
        for k, ref in enumerate((sum_q, sum_k, sum_v, sum_o))
    ]
    for store in stores:
        store.start()
    for c in range(nc):
        for kind in range(4):
            for copy in core_copies(kind, c):
                copy.wait_send()
        for copy in (a_copy, b_copy, x_copy, y_copy, back_x, back_y, back_a, back_b):
            copy(c).wait_send()
        for kind in range(5):
            back_core(kind, c).wait_send()
    for store in stores:
        store.wait()


def finish_sums(g, h, p, e, unit, small, nz, nc, collective_id):
    _, rows, width = g.shape
    width += h.shape[2]
    _, line_rows, line_width = p.shape
    half = rows // 2
    dma, vmem = pltpu.SemaphoreType.DMA, functools.partial(pltpu.VMEM, dtype=g.dtype)
    return pl.pallas_call(
        functools.partial(finish_kernel, nz, nc),
        name="finish_sums",
        out_shape=(
            *[jax.ShapeDtypeStruct(g.shape[:2] + (width // 4,), g.dtype)] * 4,
            *[jax.ShapeDtypeStruct((line_rows, line_width), jnp.float32)] * 2,
            jax.ShapeDtypeStruct(small.shape, small.dtype),
        ),
        in_specs=[pl.BlockSpec(memory_space=pl.ANY)] * 4 + [pl.BlockSpec(memory_space=pltpu.VMEM)] * 2,
        out_specs=(
            *[pl.BlockSpec(memory_space=pl.ANY)] * 4,
            *[pl.BlockSpec(memory_space=pltpu.VMEM)] * 3,
        ),
        scratch_shapes=[vmem(g.shape[:2] + (width,)), vmem((4, nc, rows, width)), vmem((4, nc, rows, width))]
        + [vmem((nc, half, width)) for _ in range(2)]
        + [vmem((nc, rows, width)) for _ in range(2)]
        + [vmem((nz, line_rows, line_width)) for _ in range(4)]
        + [vmem((nz - 1, line_rows, line_width))]
        + [dma((2, 4, nc)) for _ in range(3)]
        + [dma((nc,)) for _ in range(16)]
        + [dma((5, nc)), dma((5, nc))]
        + [dma(()), dma((4,))]
        + [dma((nz, PARTS)) for _ in range(4)]
        + [dma(()), dma((nz - 1,)), dma((nz - 1,))]
        + total_scratch(nz, small.shape, small.dtype),
        compiler_params=pltpu.CompilerParams(
            collective_id=collective_id, has_side_effects=True, vmem_limit_bytes=VMEM_LIMIT
        ),
    )(g, h, p, e, unit, small)


class Spread:
    def __init__(self, nz, row_shape):
        self.nz, self.row_shape = nz, row_shape

    @staticmethod
    def swap(value, flip):
        return lax.ppermute(value, "dp", [(i, i ^ flip) for i in range(8)])

    @staticmethod
    def plus(a, b):
        return (a.astype(jnp.float32) + b.astype(jnp.float32)).astype(a.dtype)

    def pair(self, mine, partners):
        self.mine = mine
        return self.swap(partners, 1)

    def sides(self, theirs):
        nz, plus = self.nz, self.plus
        self.low, self.high = slice(0, nz // 2), slice(nz // 2, nz)
        mine = self.mine.reshape((4, nz) + self.row_shape)
        self.whole = whole = plus(mine, theirs.reshape(mine.shape))
        to_x = jnp.stack([whole[1, self.low], whole[3, self.low]])
        to_y = jnp.stack([whole[2, self.high], whole[3, self.high]])
        return to_x, to_y

    def side(self, sides):
        return self.swap(sides[0], 2), self.swap(sides[1], 4)

    def last_side(self, sides):
        by_x, by_y = sides
        whole, low, high, plus = self.whole, self.low, self.high, self.plus
        self.low_own, low_y = plus(whole[0, low], by_x[0]), plus(whole[2, low], by_x[1])
        self.high_own, high_x = plus(whole[0, high], by_y[0]), plus(whole[1, high], by_y[1])
        return self.swap(low_y, 4), self.swap(high_x, 2)

    def column(self, sides):
        return jnp.concatenate([self.plus(self.low_own, sides[0]), self.plus(self.high_own, sides[1])])


def hold(first, second):
    return lax.optimization_barrier((first, second))


def experts_routed(
    hidden_after_attention,
    expert_ids,
    expert_norm_gain,
    w_router,
    w_gate,
    w_up,
    w_down,
    grad_output,
):
    tok_count, d_model = hidden_after_attention.shape
    n_tensor = lax.axis_size("tensor")
    n_dp = lax.axis_size("dp")
    devices = n_dp * n_tensor
    second_norm_scale = root_mean_square_scale(hidden_after_attention)
    second_unit_rows = hidden_after_attention * second_norm_scale
    second_normalized = (second_unit_rows * expert_norm_gain).astype(jnp.bfloat16)
    experts = w_router.shape[1]
    topk = expert_ids.shape[1]
    exp_dev = w_gate.shape[0]
    most = 2 * ((tok_count * topk * 9 + experts * 16 - 1) // (experts * 16))
    route_probs = jax.nn.softmax(
        jnp.dot(second_normalized, w_router, preferred_element_type=jnp.float32), axis=-1
    )
    chosen = expert_ids[:, :, None] == jnp.arange(experts, dtype=jnp.int32)[None, None, :]
    gate_values = jnp.sum(jnp.where(chosen, route_probs[:, None, :], 0.0), axis=-1)
    flat_ids, pair_rank = slot_positions(expert_ids, experts)
    pair_slot = (flat_ids % exp_dev * n_dp + flat_ids // exp_dev) * most + pair_rank
    pair_count = tok_count * topk
    slot_count = exp_dev * n_dp * most
    slot_owner = (
        jnp.full((slot_count,), pair_count, jnp.int32)
        .at[pair_slot]
        .set(jnp.arange(pair_count, dtype=jnp.int32))
    )
    padded = jnp.concatenate([second_normalized, jnp.zeros((1, d_model), jnp.bfloat16)], axis=0)
    outgoing = padded[slot_owner // topk].reshape(exp_dev, n_dp, most, d_model)
    copies = jnp.broadcast_to(
        outgoing[:, :, None], (exp_dev, n_dp, n_tensor, most, d_model)
    ).reshape(exp_dev, devices, most, d_model)
    arrived = lax.all_to_all(copies, ("dp", "tensor"), split_axis=1, concat_axis=1, tiled=True)
    expert_rows = arrived.reshape(exp_dev, devices * most, d_model)
    gate_pre = jnp.einsum("erd,edf->erf", expert_rows, w_gate, preferred_element_type=jnp.float32)
    up_pre = jnp.einsum("erd,edf->erf", expert_rows, w_up, preferred_element_type=jnp.float32)
    gate_sigmoid = jax.nn.sigmoid(gate_pre)
    silu_gate = gate_pre * gate_sigmoid
    hidden = (silu_gate * up_pre).astype(jnp.bfloat16)
    partial_value = (
        jnp.einsum("erf,efd->erd", hidden, w_down, preferred_element_type=jnp.float32)
        .astype(jnp.bfloat16)
        .reshape(exp_dev, devices, most, d_model)
    )
    returned = lax.all_to_all(
        partial_value, ("dp", "tensor"), split_axis=1, concat_axis=1, tiled=True
    )
    expert_out = jnp.sum(
        returned.reshape(exp_dev, n_dp, n_tensor, most, d_model).astype(jnp.float32), axis=2
    ).reshape(slot_count, d_model)
    pair_out = expert_out[pair_slot].reshape(tok_count, topk, d_model)
    result = (hidden_after_attention + jnp.sum(gate_values[:, :, None] * pair_out, axis=1)).astype(
        jnp.bfloat16
    )
    cotangent = grad_output.astype(jnp.float32)
    grad_gates = jnp.sum(pair_out * cotangent[:, None, :], axis=-1)
    grad_pairs = (
        (gate_values[:, :, None] * cotangent[:, None, :])
        .astype(jnp.bfloat16)
        .reshape(pair_count, d_model)
    )
    grad_slots = jnp.concatenate([grad_pairs, jnp.zeros((1, d_model), jnp.bfloat16)], axis=0)[
        slot_owner
    ].reshape(exp_dev, n_dp, most, d_model)
    grad_copies = jnp.broadcast_to(
        grad_slots[:, :, None], (exp_dev, n_dp, n_tensor, most, d_model)
    ).reshape(exp_dev, devices, most, d_model)
    grad_arrived = lax.all_to_all(
        grad_copies, ("dp", "tensor"), split_axis=1, concat_axis=1, tiled=True
    )
    grad_rows = grad_arrived.reshape(exp_dev, devices * most, d_model)
    grad_hidden = jnp.einsum("erd,efd->erf", grad_rows, w_down, preferred_element_type=jnp.float32)
    grad_down = jnp.einsum("erf,erd->efd", hidden, grad_rows, preferred_element_type=jnp.float32)
    grad_gate_pre = (
        grad_hidden * up_pre * gate_sigmoid * (1.0 + gate_pre * (1.0 - gate_sigmoid))
    ).astype(jnp.bfloat16)
    grad_up_pre = (grad_hidden * silu_gate).astype(jnp.bfloat16)
    grad_gate = jnp.einsum(
        "erd,erf->edf", expert_rows, grad_gate_pre, preferred_element_type=jnp.float32
    )
    grad_up = jnp.einsum(
        "erd,erf->edf", expert_rows, grad_up_pre, preferred_element_type=jnp.float32
    )
    grad_expert_in = jnp.einsum(
        "erf,edf->erd", grad_gate_pre, w_gate, preferred_element_type=jnp.float32
    )
    grad_expert_in = grad_expert_in + jnp.einsum(
        "erf,edf->erd", grad_up_pre, w_up, preferred_element_type=jnp.float32
    )
    grad_expert_in = grad_expert_in.astype(jnp.bfloat16).reshape(exp_dev, devices, most, d_model)
    grad_back = lax.all_to_all(
        grad_expert_in, ("dp", "tensor"), split_axis=1, concat_axis=1, tiled=True
    )
    grad_slot_in = jnp.sum(
        grad_back.reshape(exp_dev, n_dp, n_tensor, most, d_model).astype(jnp.float32), axis=2
    ).reshape(slot_count, d_model)
    grad_second_normalized = jnp.sum(
        grad_slot_in[pair_slot].reshape(tok_count, topk, d_model), axis=1
    )
    grad_route = jnp.sum(jnp.where(chosen, grad_gates[:, :, None], 0.0), axis=1)
    grad_logits = (
        route_probs * (grad_route - jnp.sum(route_probs * grad_route, axis=-1, keepdims=True))
    ).astype(jnp.bfloat16)
    grad_router_part = jnp.einsum(
        "td,te->de", second_normalized, grad_logits, preferred_element_type=jnp.float32
    )
    grad_second_normalized = grad_second_normalized + jnp.einsum(
        "te,de->td", grad_logits, w_router, preferred_element_type=jnp.float32
    )
    grad_expert_share = jnp.sum(grad_second_normalized * second_unit_rows, axis=0)
    grad_second_unit_rows = grad_second_normalized * expert_norm_gain
    grad_hidden_one = (
        second_norm_scale
        * (
            grad_second_unit_rows
            - second_unit_rows
            * jnp.mean(grad_second_unit_rows * second_unit_rows, axis=-1, keepdims=True)
        )
        + cotangent
    )
    return (
        result,
        grad_hidden_one,
        grad_expert_share,
        grad_router_part,
        grad_gate,
        grad_up,
        grad_down,
    )


def experts_dense(
    hidden_after_attention,
    expert_ids,
    expert_norm_gain,
    w_router,
    w_gate,
    w_up,
    w_down,
    grad_output,
    all_cotangents,
):
    tok_count, d_model = hidden_after_attention.shape
    n_tensor = lax.axis_size("tensor")
    n_dp = lax.axis_size("dp")
    devices = n_dp * n_tensor
    everyone = ("dp", "tensor")
    second_norm_scale = root_mean_square_scale(hidden_after_attention)
    second_unit_rows = hidden_after_attention * second_norm_scale
    second_normalized = (second_unit_rows * expert_norm_gain).astype(jnp.bfloat16)
    experts = w_router.shape[1]
    exp_dev, _, width = w_gate.shape
    all_count = devices * tok_count
    expert_at = jnp.arange(experts, dtype=jnp.int32)

    chosen = jnp.any(expert_ids[:, :, None] == expert_at[None, None, :], axis=1)
    route_probs = jax.nn.softmax(
        jnp.dot(second_normalized, w_router, preferred_element_type=jnp.float32), axis=-1
    )
    gates = jnp.where(chosen, route_probs, 0.0).T

    down_rows = w_down.reshape(exp_dev * width, d_model)
    both = exp_dev * width
    all_rows, slopes, gated, tiles = gather_experts(
        second_normalized,
        gates,
        all_cotangents.reshape(devices, tok_count, d_model),
        w_gate,
        w_up,
        w_down,
        n_tensor,
        0,
    )
    all_rows, grad_pre = all_rows.reshape(all_count, d_model), slopes.reshape(all_count, 2 * both)
    gated_hidden = gated.reshape(all_count, both)
    lines = gated.reshape(n_dp, n_tensor * tok_count, both)

    def out_rows(places):
        picked = [
            lax.dynamic_index_in_dim(lines, lax.axis_index("dp") ^ k, axis=0, keepdims=False)
            for k in places
        ]
        return jnp.dot(
            jnp.concatenate(picked), down_rows, preferred_element_type=jnp.float32
        ).astype(jnp.bfloat16)

    spread = Spread(n_tensor, (tok_count, d_model))
    partner_rows = out_rows((1, 3, 5, 7))
    grad_in, gate_tiles = scatter_all(slopes, w_gate, w_up, tiles, n_tensor, 1)
    grad_in, partner_rows = hold(grad_in, partner_rows)
    theirs = spread.pair(out_rows((0, 2, 4, 6)), partner_rows)
    sides = spread.sides(theirs)
    grad_down = jnp.einsum(
        "tf,td->fd", gated_hidden, all_cotangents, preferred_element_type=jnp.float32
    ).reshape(exp_dev, width, d_model)
    grad_wide = jnp.einsum("td,tf->df", all_rows, grad_pre, preferred_element_type=jnp.float32)
    grad_gate = jnp.stack([grad_wide[:, e * width : (e + 1) * width] for e in range(exp_dev)])
    grad_up = jnp.stack([grad_wide[:, both + e * width : both + (e + 1) * width] for e in range(exp_dev)])

    grad_route = jnp.sum(gate_tiles[:, :exp_dev].reshape(n_dp, n_tensor, exp_dev, tok_count), axis=1)
    grad_route = jnp.where(chosen, grad_route.reshape(experts, tok_count).T, 0.0)
    cotangent = grad_output.astype(jnp.float32)
    grad_logits = (
        route_probs * (grad_route - jnp.sum(route_probs * grad_route, axis=-1, keepdims=True))
    ).astype(jnp.bfloat16)
    grad_router_part = jnp.einsum(
        "td,te->de", second_normalized, grad_logits, preferred_element_type=jnp.float32
    )
    grad_second_normalized = grad_in + jnp.einsum(
        "te,de->td", grad_logits, w_router, preferred_element_type=jnp.float32
    )
    grad_expert_share = jnp.sum(grad_second_normalized * second_unit_rows, axis=0)
    grad_second_unit_rows = grad_second_normalized * expert_norm_gain
    grad_hidden_one = (
        second_norm_scale
        * (
            grad_second_unit_rows
            - second_unit_rows
            * jnp.mean(grad_second_unit_rows * second_unit_rows, axis=-1, keepdims=True)
        )
        + cotangent
    )
    return (
        spread,
        sides,
        grad_hidden_one,
        grad_expert_share,
        grad_router_part,
        grad_gate,
        grad_up,
        grad_down,
    )


def local_gathered(
    tokens,
    file_ids,
    expert_ids,
    attention_norm_gain,
    w_query,
    w_key,
    w_value,
    query_gain,
    key_gain,
    w_output,
    expert_norm_gain,
    w_router,
    w_gate,
    w_up,
    w_down,
    grad_output,
):
    tok_count, d_model = tokens.shape
    n_tensor = lax.axis_size("tensor")
    n_dp = lax.axis_size("dp")
    devices = n_dp * n_tensor
    local_dim = w_query.shape[1]
    head_dim = HEAD_DIM
    local_heads = local_dim // head_dim
    seq_len = tok_count * n_tensor
    block_rows = min(512, seq_len)
    score_scale = 1.0 / math.sqrt(head_dim)
    file_row = file_ids[0]
    cosine, sine_table = rope_tables(seq_len, head_dim)
    input_tensors = tokens.astype(jnp.float32)
    first_norm_scale = root_mean_square_scale(input_tensors)
    first_unit_rows = input_tensors * first_norm_scale
    first_normalized = (first_unit_rows * attention_norm_gain).astype(jnp.bfloat16)
    normed_all = line_gather(first_normalized, n_tensor, 2).reshape(seq_len, d_model)
    all_cotangents = lax.all_gather(grad_output, ("dp", "tensor"), axis=0, tiled=True)
    query_raw = jnp.dot(normed_all, w_query, preferred_element_type=jnp.float32)
    key_raw = jnp.dot(normed_all, w_key, preferred_element_type=jnp.float32)
    value_rows = (
        jnp.dot(normed_all, w_value, preferred_element_type=jnp.float32)
        .astype(jnp.bfloat16)
        .reshape(seq_len, local_heads, head_dim)
    )
    query_total, key_total = line_total(
        jnp.stack([jnp.sum(query_raw * query_raw, axis=1), jnp.sum(key_raw * key_raw, axis=1)]), n_tensor, 6
    )
    query_scale = lax.rsqrt(query_total / d_model + EPSILON)[:, None]
    key_scale = lax.rsqrt(key_total / d_model + EPSILON)[:, None]
    query_hat = query_raw * query_scale
    key_hat = key_raw * key_scale
    queries = rotate(
        (query_hat * query_gain).reshape(seq_len, local_heads, head_dim), cosine, sine_table
    ).astype(jnp.bfloat16)
    key_rows = rotate(
        (key_hat * key_gain).reshape(seq_len, local_heads, head_dim), cosine, sine_table
    ).astype(jnp.bfloat16)
    block_start = 0
    scores = block_scores(queries, key_rows, file_row, block_start, score_scale)
    row_peak = jnp.max(scores, axis=-1, keepdims=True)
    log_total = row_peak + jnp.log(jnp.sum(jnp.exp(scores - row_peak), axis=-1, keepdims=True))
    attn_probs = jnp.exp(scores - log_total).astype(jnp.bfloat16)
    context_blocks = jnp.einsum(
        "hqk,khd->qhd", attn_probs, value_rows, preferred_element_type=jnp.float32
    )
    log_totals = [log_total]
    context = context_blocks.reshape(seq_len, local_dim).astype(jnp.bfloat16)
    attn_out = line_scatter(
        jnp.dot(context, w_output, preferred_element_type=jnp.float32)
        .astype(jnp.bfloat16)
        .reshape(n_tensor, tok_count, d_model),
        n_tensor,
        3,
    )
    hidden_after_attention = input_tensors + attn_out
    spread, sides, grad_hidden_one, grad_expert_share, grad_router_part, grad_gate, grad_up, grad_down = (
        experts_dense(
            hidden_after_attention,
            expert_ids,
            expert_norm_gain,
            w_router,
            w_gate,
            w_up,
            w_down,
            grad_output,
            all_cotangents,
        )
    )
    grad_attn = grad_hidden_one.astype(jnp.bfloat16)
    side_parts = jnp.concatenate([grad_router_part.T, grad_expert_share[None, :]])
    side_total = lax.psum(side_parts, ("dp", "tensor"))
    grad_attn, sides = hold(grad_attn, sides)
    sides = spread.side(sides)
    grad_attn_all = line_gather(grad_attn, n_tensor, 2)
    grad_attn_all, sides = hold(grad_attn_all, sides)
    sides = spread.last_side(sides)
    grad_attn_all = grad_attn_all.reshape(seq_len, d_model)
    grad_output_part = jnp.einsum(
        "sd,se->ed", context, grad_attn_all, preferred_element_type=jnp.float32
    )
    grad_context = (
        jnp.einsum("se,de->sd", grad_attn_all, w_output, preferred_element_type=jnp.float32)
        .astype(jnp.bfloat16)
        .reshape(seq_len, local_heads, head_dim)
    )
    grad_query_blocks = []
    grad_key_total = jnp.zeros((seq_len, local_heads, head_dim), jnp.float32)
    grad_value_total = jnp.zeros((seq_len, local_heads, head_dim), jnp.float32)
    for block_index, block_start in enumerate(range(0, seq_len, block_rows)):
        scores = block_scores(queries, key_rows, file_row, block_start, score_scale)
        probs_full = jnp.exp(scores - log_totals[block_index])
        probs_low = probs_full.astype(jnp.bfloat16)
        grad_value_total = jnp.einsum(
            "hqk,qhd->khd", probs_low, grad_context, preferred_element_type=jnp.float32
        )
        grad_probs = jnp.einsum(
            "qhd,khd->hqk", grad_context, value_rows, preferred_element_type=jnp.float32
        )
        row_shift = jnp.sum(probs_full * grad_probs, axis=-1, keepdims=True)
        grad_scores = (probs_full * (grad_probs - row_shift)).astype(jnp.bfloat16)
        grad_query_blocks.append(
            jnp.einsum("hqk,khd->qhd", grad_scores, key_rows, preferred_element_type=jnp.float32)
            * score_scale
        )
        grad_key_total = (
            jnp.einsum("hqk,qhd->khd", grad_scores, queries, preferred_element_type=jnp.float32)
            * score_scale
        )
    grad_query_normed = unrotate(grad_query_blocks[0], cosine, sine_table).reshape(
        seq_len, local_dim
    )
    grad_key_normed = unrotate(grad_key_total, cosine, sine_table).reshape(seq_len, local_dim)
    grad_qgain_part = jnp.sum(grad_query_normed * query_hat, axis=0)
    grad_kgain_part = jnp.sum(grad_key_normed * key_hat, axis=0)
    grad_query_hat = grad_query_normed * query_gain
    grad_key_hat = grad_key_normed * key_gain
    query_inner, key_inner = line_total(
        jnp.stack(
            [jnp.sum(grad_query_hat * query_hat, axis=1), jnp.sum(grad_key_hat * key_hat, axis=1)]
        ),
        n_tensor,
        6,
    )
    grad_query_raw = (
        query_scale * (grad_query_hat - query_hat * (query_inner / d_model)[:, None])
    ).astype(jnp.bfloat16)
    grad_key_raw = (key_scale * (grad_key_hat - key_hat * (key_inner / d_model)[:, None])).astype(
        jnp.bfloat16
    )
    grad_value_raw = grad_value_total.reshape(seq_len, local_dim).astype(jnp.bfloat16)
    grad_raw = jnp.concatenate([grad_query_raw, grad_key_raw, grad_value_raw], axis=1)
    w_raw = jnp.concatenate([w_query, w_key, w_value], axis=1)
    raw_part = jnp.einsum("sd,sf->df", normed_all, grad_raw, preferred_element_type=jnp.float32)
    row_part = jnp.einsum("sf,df->sd", grad_raw, w_raw, preferred_element_type=jnp.float32)
    column = spread.column(sides)
    mine = (jnp.arange(n_tensor) == lax.axis_index("tensor"))[:, None]
    gain_parts = jnp.stack(
        [
            jnp.zeros((d_model,), jnp.float32),
            jnp.where(mine, grad_qgain_part[None, :], 0.0).reshape(-1),
            jnp.where(mine, grad_kgain_part[None, :], 0.0).reshape(-1),
            jnp.zeros((d_model,), jnp.float32),
        ]
    )
    finished = finish_sums(
        raw_part.astype(jnp.bfloat16).reshape(n_dp * PIECES, -1, 3 * local_dim),
        grad_output_part.astype(jnp.bfloat16).reshape(n_dp * PIECES, -1, local_dim),
        row_part.astype(jnp.bfloat16).reshape(n_tensor, tok_count, d_model),
        column,
        first_unit_rows,
        gain_parts.reshape(8, -1),
        n_tensor,
        PIECES,
        4,
    )
    finished, side_total = hold(finished, side_total)
    total_query, total_key, total_value, total_output, grad_first_normalized, routed, gain_totals = finished
    total_router, total_ffn_gain = side_total[:-1].T, side_total[-1]
    total_query, total_key, total_value, total_output = (
        total.reshape(d_model, local_dim).astype(jnp.float32)
        for total in (total_query, total_key, total_value, total_output)
    )
    total_output = total_output.T
    grad_first_unit_rows = grad_first_normalized * attention_norm_gain
    grad_tokens = (
        first_norm_scale
        * (
            grad_first_unit_rows
            - first_unit_rows
            * jnp.mean(grad_first_unit_rows * first_unit_rows, axis=-1, keepdims=True)
        )
        + grad_hidden_one
    ).astype(jnp.bfloat16)
    result = (hidden_after_attention + routed).astype(jnp.bfloat16)
    gain_totals = gain_totals.reshape(4, d_model)
    total_attn_gain = gain_totals[0]
    own_gains = lax.dynamic_slice_in_dim(
        gain_totals, lax.axis_index("tensor") * local_dim, local_dim, axis=1
    )
    total_qgain, total_kgain = own_gains[1], own_gains[2]
    return (
        result,
        grad_tokens,
        total_query,
        total_key,
        total_value,
        total_output,
        total_qgain,
        total_kgain,
        total_attn_gain,
        total_ffn_gain,
        total_router,
        grad_gate,
        grad_up,
        grad_down,
    )


def local_routed(
    tokens,
    file_ids,
    expert_ids,
    attention_norm_gain,
    w_query,
    w_key,
    w_value,
    query_gain,
    key_gain,
    w_output,
    expert_norm_gain,
    w_router,
    w_gate,
    w_up,
    w_down,
    grad_output,
):
    tok_count, d_model = tokens.shape
    n_tensor = lax.axis_size("tensor")
    n_dp = lax.axis_size("dp")
    devices = n_dp * n_tensor
    local_dim = w_query.shape[1]
    head_dim = HEAD_DIM
    local_heads = local_dim // head_dim
    seq_len = tok_count * n_tensor
    block_rows = min(512, seq_len)
    score_scale = 1.0 / math.sqrt(head_dim)
    file_row = file_ids[0]
    cosine, sine_table = rope_tables(seq_len, head_dim)
    input_tensors = tokens.astype(jnp.float32)
    first_norm_scale = root_mean_square_scale(input_tensors)
    first_unit_rows = input_tensors * first_norm_scale
    first_normalized = (first_unit_rows * attention_norm_gain).astype(jnp.bfloat16)
    normed_all = lax.all_gather(first_normalized, "tensor", axis=0, tiled=True)
    query_raw = jnp.dot(normed_all, w_query, preferred_element_type=jnp.float32)
    key_raw = jnp.dot(normed_all, w_key, preferred_element_type=jnp.float32)
    value_rows = (
        jnp.dot(normed_all, w_value, preferred_element_type=jnp.float32)
        .astype(jnp.bfloat16)
        .reshape(seq_len, local_heads, head_dim)
    )
    query_total, key_total = lax.psum(
        (jnp.sum(query_raw * query_raw, axis=1), jnp.sum(key_raw * key_raw, axis=1)), "tensor"
    )
    query_scale = lax.rsqrt(query_total / d_model + EPSILON)[:, None]
    key_scale = lax.rsqrt(key_total / d_model + EPSILON)[:, None]
    query_hat = query_raw * query_scale
    key_hat = key_raw * key_scale
    queries = rotate(
        (query_hat * query_gain).reshape(seq_len, local_heads, head_dim), cosine, sine_table
    ).astype(jnp.bfloat16)
    key_rows = rotate(
        (key_hat * key_gain).reshape(seq_len, local_heads, head_dim), cosine, sine_table
    ).astype(jnp.bfloat16)
    block_start = 0
    scores = block_scores(queries, key_rows, file_row, block_start, score_scale)
    row_peak = jnp.max(scores, axis=-1, keepdims=True)
    log_total = row_peak + jnp.log(jnp.sum(jnp.exp(scores - row_peak), axis=-1, keepdims=True))
    attn_probs = jnp.exp(scores - log_total).astype(jnp.bfloat16)
    context_blocks = jnp.einsum(
        "hqk,khd->qhd", attn_probs, value_rows, preferred_element_type=jnp.float32
    )
    log_totals = [log_total]
    context = context_blocks.reshape(seq_len, local_dim).astype(jnp.bfloat16)
    attn_out = lax.psum_scatter(
        jnp.dot(context, w_output, preferred_element_type=jnp.float32).astype(jnp.bfloat16),
        "tensor",
        scatter_dimension=0,
        tiled=True,
    ).astype(jnp.float32)
    hidden_after_attention = input_tensors + attn_out
    result, grad_hidden_one, grad_expert_share, grad_router_part, grad_gate, grad_up, grad_down = (
        experts_routed(
            hidden_after_attention,
            expert_ids,
            expert_norm_gain,
            w_router,
            w_gate,
            w_up,
            w_down,
            grad_output,
        )
    )
    grad_attn = grad_hidden_one.astype(jnp.bfloat16)
    grad_attn_all = lax.all_gather(grad_attn, "tensor", axis=0, tiled=True)
    grad_output_part = jnp.einsum(
        "sd,se->de", context, grad_attn_all, preferred_element_type=jnp.float32
    )
    grad_context = (
        jnp.einsum("se,de->sd", grad_attn_all, w_output, preferred_element_type=jnp.float32)
        .astype(jnp.bfloat16)
        .reshape(seq_len, local_heads, head_dim)
    )
    grad_query_blocks = []
    grad_key_total = jnp.zeros((seq_len, local_heads, head_dim), jnp.float32)
    grad_value_total = jnp.zeros((seq_len, local_heads, head_dim), jnp.float32)
    for block_index, block_start in enumerate(range(0, seq_len, block_rows)):
        scores = block_scores(queries, key_rows, file_row, block_start, score_scale)
        probs_full = jnp.exp(scores - log_totals[block_index])
        probs_low = probs_full.astype(jnp.bfloat16)
        grad_value_total = jnp.einsum(
            "hqk,qhd->khd", probs_low, grad_context, preferred_element_type=jnp.float32
        )
        grad_probs = jnp.einsum(
            "qhd,khd->hqk", grad_context, value_rows, preferred_element_type=jnp.float32
        )
        row_shift = jnp.sum(probs_full * grad_probs, axis=-1, keepdims=True)
        grad_scores = (probs_full * (grad_probs - row_shift)).astype(jnp.bfloat16)
        grad_query_blocks.append(
            jnp.einsum("hqk,khd->qhd", grad_scores, key_rows, preferred_element_type=jnp.float32)
            * score_scale
        )
        grad_key_total = (
            jnp.einsum("hqk,qhd->khd", grad_scores, queries, preferred_element_type=jnp.float32)
            * score_scale
        )
    grad_query_normed = unrotate(grad_query_blocks[0], cosine, sine_table).reshape(
        seq_len, local_dim
    )
    grad_key_normed = unrotate(grad_key_total, cosine, sine_table).reshape(seq_len, local_dim)
    grad_qgain_part = jnp.sum(grad_query_normed * query_hat, axis=0)
    grad_kgain_part = jnp.sum(grad_key_normed * key_hat, axis=0)
    grad_query_hat = grad_query_normed * query_gain
    grad_key_hat = grad_key_normed * key_gain
    query_inner, key_inner = lax.psum(
        (jnp.sum(grad_query_hat * query_hat, axis=1), jnp.sum(grad_key_hat * key_hat, axis=1)),
        "tensor",
    )
    grad_query_raw = (
        query_scale * (grad_query_hat - query_hat * (query_inner / d_model)[:, None])
    ).astype(jnp.bfloat16)
    grad_key_raw = (key_scale * (grad_key_hat - key_hat * (key_inner / d_model)[:, None])).astype(
        jnp.bfloat16
    )
    grad_value_raw = grad_value_total.reshape(seq_len, local_dim).astype(jnp.bfloat16)
    grad_query_part = jnp.einsum(
        "sd,sf->df", normed_all, grad_query_raw, preferred_element_type=jnp.float32
    )
    grad_key_part = jnp.einsum(
        "sd,sf->df", normed_all, grad_key_raw, preferred_element_type=jnp.float32
    )
    grad_value_part = jnp.einsum(
        "sd,sf->df", normed_all, grad_value_raw, preferred_element_type=jnp.float32
    )
    summed = jnp.einsum("sf,df->sd", grad_query_raw, w_query, preferred_element_type=jnp.float32)
    summed = summed + jnp.einsum(
        "sf,df->sd", grad_key_raw, w_key, preferred_element_type=jnp.float32
    )
    grad_first_normalized = lax.psum_scatter(
        (
            summed
            + jnp.einsum("sf,df->sd", grad_value_raw, w_value, preferred_element_type=jnp.float32)
        ).astype(jnp.bfloat16),
        "tensor",
        scatter_dimension=0,
        tiled=True,
    ).astype(jnp.float32)
    grad_attention_share = jnp.sum(grad_first_normalized * first_unit_rows, axis=0)
    grad_first_unit_rows = grad_first_normalized * attention_norm_gain
    grad_tokens = (
        first_norm_scale
        * (
            grad_first_unit_rows
            - first_unit_rows
            * jnp.mean(grad_first_unit_rows * first_unit_rows, axis=-1, keepdims=True)
        )
        + grad_hidden_one
    ).astype(jnp.bfloat16)
    total_query, total_key, total_value, total_output, total_qgain, total_kgain = (
        lax.psum(grad_query_part.astype(jnp.bfloat16), "dp").astype(jnp.float32),
        lax.psum(grad_key_part.astype(jnp.bfloat16), "dp").astype(jnp.float32),
        lax.psum(grad_value_part.astype(jnp.bfloat16), "dp").astype(jnp.float32),
        lax.psum(grad_output_part.astype(jnp.bfloat16), "dp").astype(jnp.float32),
        lax.psum(grad_qgain_part.astype(jnp.bfloat16), "dp").astype(jnp.float32),
        lax.psum(grad_kgain_part.astype(jnp.bfloat16), "dp").astype(jnp.float32),
    )
    total_attn_gain, total_ffn_gain, total_router = lax.psum(
        (grad_attention_share, grad_expert_share, grad_router_part), ("dp", "tensor")
    )
    return (
        result,
        grad_tokens,
        total_query,
        total_key,
        total_value,
        total_output,
        total_qgain,
        total_kgain,
        total_attn_gain,
        total_ffn_gain,
        total_router,
        grad_gate,
        grad_up,
        grad_down,
    )


def solution(mesh):
    return jax.shard_map(
        local_gathered if mesh.shape["dp"] == 8 else local_routed,
        mesh=mesh,
        in_specs=(
            P(("dp", "tensor"), None),
            P("dp", None),
            P(("dp", "tensor"), None),
            P(),
            P(None, "tensor"),
            P(None, "tensor"),
            P(None, "tensor"),
            P("tensor"),
            P("tensor"),
            P("tensor", None),
            P(),
            P(),
            P("dp", None, "tensor"),
            P("dp", None, "tensor"),
            P("dp", "tensor", None),
            P(("dp", "tensor"), None),
        ),
        out_specs=(
            P(("dp", "tensor"), None),
            P(("dp", "tensor"), None),
            P(None, "tensor"),
            P(None, "tensor"),
            P(None, "tensor"),
            P("tensor", None),
            P("tensor"),
            P("tensor"),
            P(),
            P(),
            P(),
            P("dp", None, "tensor"),
            P("dp", None, "tensor"),
            P("dp", "tensor", None),
        ),
        check_vma=False,
    )
```

```python
import functools
import math

import jax
import jax.numpy as jnp
from jax import lax
from jax.experimental import pallas as pl
from jax.experimental.pallas import tpu as pltpu
from jax.sharding import PartitionSpec as P

HEAD_DIM = 128


EPSILON = 1e-05
THETA = 10000.0
NEG_LARGE = -1e30


def root_mean_square_scale(values):
    return lax.rsqrt(jnp.mean(values * values, axis=-1, keepdims=True) + EPSILON)


def rope_tables(length, head_dim):
    half_dim = head_dim // 2
    freq_index = jnp.arange(half_dim, dtype=jnp.float32)
    frequency = THETA ** (-(2.0 * freq_index) / head_dim)
    angles = jnp.arange(length, dtype=jnp.float32)[:, None] * frequency[None, :]
    cosine = jnp.concatenate([jnp.cos(angles), jnp.cos(angles)], axis=1)
    sine_table = jnp.concatenate([jnp.sin(angles), jnp.sin(angles)], axis=1)
    return (cosine[:, None, :], sine_table[:, None, :])


def rotate(values, cosine, sine_table):
    half_dim = values.shape[-1] // 2
    turned = jnp.concatenate([-values[..., half_dim:], values[..., :half_dim]], axis=-1)
    return values * cosine + turned * sine_table


def unrotate(grad_rows, cosine, sine_table):
    half_dim = grad_rows.shape[-1] // 2
    scaled = grad_rows * sine_table
    turned = jnp.concatenate([scaled[..., half_dim:], -scaled[..., :half_dim]], axis=-1)
    return grad_rows * cosine + turned


def slot_positions(ids, experts):
    flat_ids = ids.reshape(-1)
    onehot = (flat_ids[:, None] == jnp.arange(experts, dtype=jnp.int32)[None, :]).astype(jnp.int32)
    running = jnp.cumsum(onehot, axis=0)
    return (flat_ids, jnp.sum(running * onehot, axis=1) - 1)


def block_scores(query_block, key_rows, file_row, block_start, score_scale):
    block_rows = query_block.shape[0]
    raw_scores = (
        jnp.einsum("qhd,khd->hqk", query_block, key_rows, preferred_element_type=jnp.float32)
        * score_scale
    )
    rows_at = block_start + jnp.arange(block_rows, dtype=jnp.int32)
    cols_at = jnp.arange(key_rows.shape[0], dtype=jnp.int32)
    allowed = (cols_at[None, :] <= rows_at[:, None]) & (file_row[None, :] == file_row[:, None])
    return jnp.where(allowed[None], raw_scores, NEG_LARGE)


MESH = pl.DeviceIdType.MESH
VMEM_LIMIT = 60 * 2**20


def greet(dp, z, nz):
    barrier = pltpu.get_barrier_semaphore()
    for flip in (1, 2, 4):
        pl.semaphore_signal(barrier, 1, device_id=(dp ^ flip, z), device_id_type=MESH)

    @pl.when(z > 0)
    def _():
        pl.semaphore_signal(barrier, 1, device_id=(dp, z - 1), device_id_type=MESH)

    @pl.when(z < nz - 1)
    def _():
        pl.semaphore_signal(barrier, 1, device_id=(dp, z + 1), device_id_type=MESH)

    ends = jnp.where(z > 0, 1, 0) + jnp.where(z < nz - 1, 1, 0)
    pl.semaphore_wait(barrier, 3 + ends)


def remote(src, dst, send, recv, device):
    return pltpu.make_async_remote_copy(
        src_ref=src, dst_ref=dst, send_sem=send, recv_sem=recv, device_id=device, device_id_type=MESH
    )


def experts_kernel(nz, x_ref, t_ref, g_ref, gate_ref, up_ref, down_ref, rows_ref, slopes_ref, gated_ref, tiles_ref, land, tags, g_buf, pre, back, gate_at, grad_at, local_sem, s_rows, s_g, sz, sx, sy, sda, sdb, sc, rz, rx, ry, rda, rdb, rc):
    dp, z = lax.axis_index("dp"), lax.axis_index("tensor")
    count, width = x_ref.shape
    half = count // 2
    both = back.shape[1]
    each = both // gate_at.shape[0]
    other = (dp ^ 1, z)

    def rows_at(flip, zz):
        place = dp ^ flip
        return land.at[place // 2, zz, pl.ds(pl.multiple_of((place % 2) * count, count), count)]

    def half_at(flip, zz, k):
        place = dp ^ flip
        return land.at[place // 2, zz, pl.ds(pl.multiple_of((place % 2) * count + k * half, half), half)]

    def tags_at(flip, zz):
        return tags.at[(dp ^ flip) * nz + zz]

    def whole(flip, zz, send, recv, device):
        return (
            remote(rows_at(flip, zz), rows_at(flip, zz), send(0), recv(0), device),
            remote(tags_at(flip, zz), tags_at(flip, zz), send(1), recv(1), device),
        )

    def z_copy(zz, step):
        return whole(0, zz, lambda k: sz.at[k, (step + 1) // 2, zz], lambda k: rz.at[k, zz], (dp, z + step))

    def x_copy(zz):
        return whole(0, zz, lambda k: sx.at[k, zz], lambda k: rx.at[k, zz], (dp ^ 2, z))

    def y_copy(zz):
        return whole(0, zz, lambda k: sy.at[k, zz], lambda k: ry.at[k, zz], (dp ^ 4, z))

    def a_copy(zz):
        return (
            remote(half_at(4, zz, 0), half_at(4, zz, 0), sda.at[0, zz], rda.at[0, zz], (dp ^ 2, z)),
            remote(tags_at(4, zz), tags_at(4, zz), sda.at[1, zz], rda.at[1, zz], (dp ^ 2, z)),
        )

    def b_copy(zz):
        return (remote(half_at(2, zz, 1), half_at(2, zz, 1), sdb.at[zz], rdb.at[zz], (dp ^ 4, z)),)

    def c_copy(kind, zz):
        send, recv = (lambda k: sc.at[k, kind, zz]), (lambda k: rc.at[k, kind, zz])
        if kind < 3:
            return whole((0, 2, 4)[kind], zz, send, recv, other)
        ref = half_at(6, zz, kind - 3)
        copies = (remote(ref, ref, send(0), recv(0), other),)
        if kind == 3:
            copies += (remote(tags_at(6, zz), tags_at(6, zz), send(1), recv(1), other),)
        return copies

    def start(copies):
        for copy in copies:
            copy.start()

    def arrived(ref, sem):
        remote(ref, ref, sem, sem, other).wait_recv()

    def both_arrived(flip, zz, recv):
        arrived(rows_at(flip, zz), recv(0))
        arrived(tags_at(flip, zz), recv(1))

    def held(distance, zz, sign):
        inside = (distance >= 0) & (distance < nz) & (zz >= 0) & (zz < nz)
        return inside & ((distance > 0) | (sign > 0))

    def spread(distance):
        for sign in (1, -1):
            zz = z + sign * distance

            @pl.when(held(distance, zz, sign))
            def _():
                @pl.when(distance > 0)
                def _():
                    both_arrived(0, zz, lambda k: rz.at[k, zz])

                @pl.when((zz <= z) & (z < nz - 1))
                def _():
                    start(z_copy(zz, 1))

                @pl.when((zz >= z) & (z > 0))
                def _():
                    start(z_copy(zz, -1))

                start(x_copy(zz))
                start(y_copy(zz))
                start(c_copy(0, zz))

    def relay(distance):
        for sign in (1, -1):
            zz = z + sign * distance

            @pl.when(held(distance, zz, sign))
            def _():
                both_arrived(4, zz, lambda k: ry.at[k, zz])
                start(a_copy(zz))
                start(c_copy(2, zz))
                both_arrived(2, zz, lambda k: rx.at[k, zz])
                start(b_copy(zz))
                start(c_copy(1, zz))

    def corner(distance):
        for sign in (1, -1):
            zz = z + sign * distance

            @pl.when(held(distance, zz, sign))
            def _():
                arrived(half_at(6, zz, 0), rda.at[0, zz])
                arrived(tags_at(6, zz), rda.at[1, zz])
                start(c_copy(3, zz))
                arrived(half_at(6, zz, 1), rdb.at[zz])
                start(c_copy(4, zz))

    def store_rows(chip, zz):
        return pltpu.make_async_copy(land.at[chip, zz], rows_ref.at[chip, zz], s_rows.at[chip, zz])

    def load_g(chip, zz, c):
        return pltpu.make_async_copy(
            g_ref.at[(2 * chip + c) * nz + zz], g_buf.at[pl.ds(c * count, count)], s_g.at[c]
        )

    diagonal = (
        lax.broadcasted_iota(jnp.int32, (count, count), 0) == lax.broadcasted_iota(jnp.int32, (count, count), 1)
    ).astype(jnp.float32)

    def experts(chip, zz):
        store_rows(chip, zz).start()
        for c in range(2):
            load_g(chip, zz, c).start()
        x = land.at[chip, zz]

        for k, ref in enumerate((gate_ref, up_ref)):
            for j in range(gate_at.shape[0]):
                pre[:, pl.ds(k * both + j * each, each)] = jnp.dot(
                    x[...], ref[j], preferred_element_type=jnp.float32
                )
        for j in range(gate_at.shape[0]):
            for c in range(2):
                row = tags[(2 * chip + c) * nz + zz, pl.ds(dp * gate_at.shape[0] + j, 1), :]
                column = jnp.sum(diagonal * row, axis=1, keepdims=True)
                gate_at[j, pl.ds(c * count, count), :] = jnp.broadcast_to(column, (count, 128))
        for c in range(2):
            load_g(chip, zz, c).wait()

        for j in range(gate_at.shape[0]):
            back[:, pl.ds(j * each, each)] = lax.dot_general(
                g_buf[...], down_ref[j], (((1,), (1,)), ((), ())), preferred_element_type=jnp.float32
            )

        def elementwise(k, carry):
            at = pl.ds(pl.multiple_of(k * 64, 64), 64)
            place, inner = 2 * chip + k // (count // 64), pl.ds(pl.multiple_of(k % (count // 64) * 64, 64), 64)
            for j in range(gate_at.shape[0]):
                cols, up_cols = pl.ds(j * each, each), pl.ds(both + j * each, each)
                gate = jnp.concatenate([gate_at[j, at, :]] * (each // 128), axis=1)
                gate_pre, up_pre, grad = pre[at, cols], pre[at, up_cols], back[at, cols]
                sigmoid = 0.5 + 0.5 * jnp.tanh(0.5 * gate_pre)
                silu = gate_pre * sigmoid
                hidden = silu * up_pre
                gated_ref[place, zz, inner, cols] = (gate * hidden).astype(gated_ref.dtype)
                share = jnp.sum(hidden * grad, axis=1, keepdims=True)
                grad_at[j, at, :] = jnp.broadcast_to(share, (64, 128))
                slope = gate * grad
                slopes_ref[chip, zz, at, cols] = (
                    slope * up_pre * sigmoid * (1.0 + gate_pre * (1.0 - sigmoid))
                ).astype(slopes_ref.dtype)
                slopes_ref[chip, zz, at, up_cols] = (slope * silu).astype(slopes_ref.dtype)
            return carry

        lax.fori_loop(0, 2 * count // 64, elementwise, 0)
        for c in range(2):
            shares = [
                jnp.sum(diagonal * grad_at[j, pl.ds(c * count, count), :], axis=0, keepdims=True)
                for j in range(gate_at.shape[0])
            ]
            shares.append(jnp.zeros((8 - len(shares), count), jnp.float32))
            tiles_ref[(2 * chip + c) * nz + zz] = jnp.concatenate(shares, axis=0)

    def job(step, k):
        kind, sign = k // 2, 1 - 2 * (k % 2)
        distance = step - 1 - jnp.where(kind == 0, 0, 1)
        zz = z + sign * distance
        flip = 2 * kind

        @pl.when(held(distance, zz, sign))
        def _():
            @pl.when(kind < 3)
            def _():
                both_arrived(flip + 1, zz, lambda m: rc.at[m, kind, zz])

            @pl.when(kind == 3)
            def _():
                arrived(half_at(7, zz, 0), rc.at[0, 3, zz])
                arrived(tags_at(7, zz), rc.at[1, 3, zz])
                arrived(half_at(7, zz, 1), rc.at[0, 4, zz])

            experts((dp ^ flip) // 2, zz)

    keep = pltpu.make_async_copy(x_ref, rows_at(0, z), local_sem.at[0])
    keep_tags = pltpu.make_async_copy(t_ref, tags_at(0, z), local_sem.at[1])
    keep.start()
    keep_tags.start()
    greet(dp, z, nz)
    keep.wait()
    keep_tags.wait()

    def step_body(step, carry):
        spread(step)
        relay(step - 1)
        corner(step - 2)

        def inner(k, inner_carry):
            job(step, k)
            return inner_carry

        lax.fori_loop(0, 8, inner, 0)
        return carry

    lax.fori_loop(0, nz + 2, step_body, 0)

    def sent(copies):
        for copy in copies:
            copy.wait_send()

    for zz in range(nz):

        @pl.when((zz <= z) & (z < nz - 1))
        def _():
            sent(z_copy(zz, 1))

        @pl.when((zz >= z) & (z > 0))
        def _():
            sent(z_copy(zz, -1))

        sent(x_copy(zz))
        sent(y_copy(zz))
        sent(a_copy(zz))
        sent(b_copy(zz))
        for kind in range(5):
            sent(c_copy(kind, zz))
        for chip in range(4):
            store_rows(chip, zz).wait()


def gather_experts(x, gates, cotangents, w_gate, w_up, w_down, nz, collective_id):
    rows, width = x.shape
    experts_here, each, _ = w_down.shape
    both = experts_here * each
    dma, vmem = pltpu.SemaphoreType.DMA, pl.BlockSpec(memory_space=pltpu.VMEM)
    any_place = pl.BlockSpec(memory_space=pl.ANY)
    group = (4, nz, 2 * rows)
    flops = 2 * 8 * nz * rows * width * 3 * both
    return pl.pallas_call(
        functools.partial(experts_kernel, nz),
        name="gather_experts",
        out_shape=(
            jax.ShapeDtypeStruct(group + (width,), x.dtype),
            jax.ShapeDtypeStruct(group + (2 * both,), x.dtype),
            jax.ShapeDtypeStruct((8, nz, rows, both), x.dtype),
            jax.ShapeDtypeStruct((8 * nz, 8, rows), jnp.float32),
        ),
        in_specs=[vmem, vmem, any_place, vmem, vmem, vmem],
        out_specs=(any_place, vmem, vmem, vmem),
        scratch_shapes=[
            pltpu.VMEM(group + (width,), x.dtype),
            pltpu.VMEM((8 * nz,) + gates.shape, gates.dtype),
            pltpu.VMEM((2 * rows, width), x.dtype),
            pltpu.VMEM((2 * rows, 2 * both), jnp.float32),
            pltpu.VMEM((2 * rows, both), jnp.float32),
            pltpu.VMEM((experts_here, 2 * rows, 128), jnp.float32),
            pltpu.VMEM((experts_here, 2 * rows, 128), jnp.float32),
            dma((2,)),
            dma((4, nz)),
            dma((2,)),
        ]
        + [dma((2, 2, nz)), dma((2, nz)), dma((2, nz)), dma((2, nz)), dma((nz,)), dma((2, 5, nz))]
        + [dma((2, nz)), dma((2, nz)), dma((2, nz)), dma((2, nz)), dma((nz,)), dma((2, 5, nz))],
        compiler_params=pltpu.CompilerParams(
            collective_id=collective_id, has_side_effects=True, vmem_limit_bytes=VMEM_LIMIT
        ),
        cost_estimate=pl.CostEstimate(flops=flops, bytes_accessed=64 * 2**20, transcendentals=0),
    )(x, gates, cotangents, w_gate, w_up, w_down)


def greet_line(dp, z, nz):
    barrier = pltpu.get_barrier_semaphore()

    @pl.when(z > 0)
    def _():
        pl.semaphore_signal(barrier, 1, device_id=(dp, z - 1), device_id_type=MESH)

    @pl.when(z < nz - 1)
    def _():
        pl.semaphore_signal(barrier, 1, device_id=(dp, z + 1), device_id_type=MESH)

    pl.semaphore_wait(barrier, jnp.where(z > 0, 1, 0) + jnp.where(z < nz - 1, 1, 0))


PARTS = 2
PIECES = 2


def greet_total(dp, z, nz):
    barrier = pltpu.get_barrier_semaphore()
    for flip in (1, 2, 4):
        pl.semaphore_signal(barrier, 1, device_id=(dp ^ flip, z), device_id_type=MESH)
    for turn in range(1, nz):
        pl.semaphore_signal(barrier, 1, device_id=(dp, lax.rem(z + turn, nz)), device_id_type=MESH)
    pl.semaphore_wait(barrier, 2 + nz)


class Total:
    steps = 5

    def __init__(self, nz, dp, z, got, s_plane, r_plane, s_line, r_line):
        self.nz, self.z, self.got = nz, z, got
        self.plane = [
            remote(got.at[2 * k], got.at[2 * k + 1], s_plane.at[k], r_plane.at[k], (dp ^ flip, z))
            for k, flip in enumerate((1, 2, 4))
        ]
        self.line = [
            remote(got.at[6], got.at[6 + turn], s_line.at[turn - 1], r_line.at[turn - 1], (dp, lax.rem(z + turn, nz)))
            for turn in range(1, nz)
        ]

    def step(self, k, out_ref):
        got, nz = self.got, self.nz
        if 1 <= k <= 3:
            self.plane[k - 1].wait()
            got[2 * k] = got[2 * k - 2] + got[2 * k - 1]
        if k < 3:
            self.plane[k].start()
        elif k == 3:
            for copy in self.line:
                copy.start()
        else:
            for copy in self.line:
                copy.wait()
            total = got[6 + lax.rem(self.z, nz)]
            for zz in range(1, nz):
                total = total + got[6 + lax.rem(self.z - zz + nz, nz)]
            out_ref[...] = total


def total_scratch(nz, shape, dtype):
    dma = pltpu.SemaphoreType.DMA
    return [pltpu.VMEM((6 + nz,) + shape, dtype), dma((3,)), dma((3,)), dma((nz - 1,)), dma((nz - 1,))]


def line_gather_kernel(nz, *refs):
    dp, z = lax.axis_index("dp"), lax.axis_index("tensor")
    summed = len(refs) > 6
    if summed:
        x_ref, small_ref, out_ref, total_ref, local_sem, s_up, s_down, r_line = refs[:8]
        greet_total(dp, z, nz)
        total = Total(nz, dp, z, *refs[8:])
        total.got[0] = small_ref[...]
    else:
        x_ref, out_ref, local_sem, s_up, s_down, r_line = refs
        greet_line(dp, z, nz)
    part = x_ref.shape[0] // PARTS

    def copy(zz, k, step, own):
        at = pl.ds(k * part, part)
        dst = out_ref.at[zz, at]
        sems = s_up if step > 0 else s_down
        return remote(x_ref.at[at] if own else dst, dst, sems.at[zz, k], r_line.at[zz, k], (dp, z + step))

    keep = pltpu.make_async_copy(x_ref, out_ref.at[z], local_sem)
    for distance in range(nz):
        for k in range(PARTS):
            for sign in (0,) if distance == 0 else (-1, 1):
                zz, own = z + sign * distance, distance == 0

                @pl.when((zz >= 0) & (zz < nz))
                def _():
                    if not own:
                        copy(zz, k, 1, False).wait_recv()
                    if sign <= 0:

                        @pl.when(z < nz - 1)
                        def _():
                            copy(zz, k, 1, own).start()

                    if sign >= 0:

                        @pl.when(z > 0)
                        def _():
                            copy(zz, k, -1, own).start()

        if distance == 0:
            keep.start()
        if summed:
            total.step(distance, total_ref)
    if summed:
        for k in range(nz, Total.steps):
            total.step(k, total_ref)
    keep.wait()
    for zz in range(nz):
        for k in range(PARTS):

            @pl.when((zz <= z) & (z < nz - 1))
            def _():
                copy(zz, k, 1, False).wait_send()

            @pl.when((zz >= z) & (z > 0))
            def _():
                copy(zz, k, -1, False).wait_send()


def line_gather(x, nz, collective_id, small=None):
    dma, vmem = pltpu.SemaphoreType.DMA, pl.BlockSpec(memory_space=pltpu.VMEM)
    blocks = jax.ShapeDtypeStruct((nz,) + x.shape, x.dtype)
    scratch = [dma(())] + [dma((nz, PARTS)) for _ in range(3)]
    params = pltpu.CompilerParams(
        collective_id=collective_id, has_side_effects=True, vmem_limit_bytes=8 * 2**20
    )
    kernel = functools.partial(line_gather_kernel, nz)
    if small is None:
        return pl.pallas_call(
            kernel,
            name="line_gather",
            out_shape=blocks,
            in_specs=[vmem],
            out_specs=pl.BlockSpec(memory_space=pl.ANY),
            scratch_shapes=scratch,
            compiler_params=params,
        )(x)
    return pl.pallas_call(
        kernel,
        name="line_gather_total",
        out_shape=(blocks, jax.ShapeDtypeStruct(small.shape, small.dtype)),
        in_specs=[vmem, vmem],
        out_specs=(pl.BlockSpec(memory_space=pl.ANY), vmem),
        scratch_shapes=scratch + total_scratch(nz, small.shape, small.dtype),
        compiler_params=params,
    )(x, small)


def line_total_kernel(nz, x_ref, out_ref, got, send, recv):
    dp, z = lax.axis_index("dp"), lax.axis_index("tensor")
    others = [lax.rem(z + turn, nz) for turn in range(1, nz)]
    barrier = pltpu.get_barrier_semaphore()
    for other in others:
        pl.semaphore_signal(barrier, 1, device_id=(dp, other), device_id_type=MESH)
    pl.semaphore_wait(barrier, nz - 1)
    copies = [
        remote(x_ref, got.at[turn], send.at[turn], recv.at[turn], (dp, other)) for turn, other in enumerate(others)
    ]
    for copy in copies:
        copy.start()
    for copy in copies:
        copy.wait()
    total = x_ref[...]
    for turn in range(nz - 1):
        total = total + got[turn]
    out_ref[...] = total


def line_total(x, nz, collective_id):
    dma, vmem = pltpu.SemaphoreType.DMA, pl.BlockSpec(memory_space=pltpu.VMEM)
    return pl.pallas_call(
        functools.partial(line_total_kernel, nz),
        name="line_total",
        out_shape=jax.ShapeDtypeStruct(x.shape, x.dtype),
        in_specs=[vmem],
        out_specs=vmem,
        scratch_shapes=[pltpu.VMEM((nz - 1,) + x.shape, x.dtype), dma((nz - 1,)), dma((nz - 1,))],
        compiler_params=pltpu.CompilerParams(
            collective_id=collective_id, has_side_effects=True, vmem_limit_bytes=4 * 2**20
        ),
    )(x)


CHUNK = 32


def add_rows(dst, *others, start=0, count):
    def body(k, carry):
        at = pl.ds(start + k * CHUNK, CHUNK)
        if len(others) == 1:
            ref, base = others[0]
            dst[at, :] = dst[at, :] + ref[pl.ds(base + k * CHUNK, CHUNK), :]
            return carry
        total = dst[at, :].astype(jnp.float32)
        for ref, base in others:
            total = total + ref[pl.ds(base + k * CHUNK, CHUNK), :].astype(jnp.float32)
        dst[at, :] = total.astype(dst.dtype)
        return carry

    lax.fori_loop(0, count // CHUNK, body, 0)


class Line:
    def __init__(self, nz, dp, z, acc, up, down, s_up, r_up, s_down, r_down):
        self.nz, self.dp, self.z, self.acc, self.up, self.down = nz, dp, z, acc, up, down
        self.sems = s_up, r_up, s_down, r_down
        self.part = acc.shape[1] // PARTS

    def copy(self, zz, k, step):
        at = pl.ds(k * self.part, self.part)
        s_up, r_up, s_down, r_down = self.sems
        if step > 0:
            return remote(self.acc.at[zz, at], self.up.at[zz, at], s_up.at[zz, k], r_up.at[zz, k], (self.dp, self.z + 1))
        return remote(self.acc.at[zz, at], self.down.at[zz, at], s_down.at[zz, k], r_down.at[zz, k], (self.dp, self.z - 1))

    def first(self):
        nz, z = self.nz, self.z

        @pl.when(z == 0)
        def _():
            for zz in range(nz - 1, 0, -1):
                for k in range(PARTS):
                    self.copy(zz, k, 1).start()

        @pl.when(z == nz - 1)
        def _():
            for zz in range(nz - 1):
                for k in range(PARTS):
                    self.copy(zz, k, -1).start()

    def step(self, distance):
        nz, z = self.nz, self.z
        for k in range(PARTS):
            for sign in (1, -1):
                far = nz - distance if sign > 0 else distance - 1
                through = (far > z) & (z > 0) if sign > 0 else (far < z) & (z < nz - 1)

                @pl.when(through)
                def _():
                    self.copy(far, k, sign).wait_recv()
                    source = self.up if sign > 0 else self.down
                    add_rows(self.acc.at[far], (source.at[far], k * self.part), start=k * self.part, count=self.part)
                    self.copy(far, k, sign).start()

    def finish(self, out_ref):
        nz, z = self.nz, self.z
        for k in range(PARTS):

            @pl.when(z > 0)
            def _():
                self.copy(z, k, 1).wait_recv()

            @pl.when(z < nz - 1)
            def _():
                self.copy(z, k, -1).wait_recv()

        def body(k, carry):
            at = pl.ds(k * CHUNK, CHUNK)
            total = self.acc[z, at, :].astype(jnp.float32)
            zero = jnp.zeros_like(total)
            total = total + jnp.where(z > 0, self.up[z, at, :].astype(jnp.float32), zero)
            total = total + jnp.where(z < nz - 1, self.down[z, at, :].astype(jnp.float32), zero)
            out_ref[at, :] = total
            return carry

        lax.fori_loop(0, out_ref.shape[0] // CHUNK, body, 0)

    def drain(self):
        nz, z = self.nz, self.z
        for zz in range(nz):
            for k in range(PARTS):

                @pl.when(zz > z)
                def _():
                    self.copy(zz, k, 1).wait_send()

                @pl.when(zz < z)
                def _():
                    self.copy(zz, k, -1).wait_send()


def line_scatter_kernel(nz, p_ref, out_ref, acc, up, down, local_sem, s_up, r_up, s_down, r_down):
    dp, z = lax.axis_index("dp"), lax.axis_index("tensor")
    loaded = pltpu.make_async_copy(p_ref, acc, local_sem)
    loaded.start()
    greet_line(dp, z, nz)
    loaded.wait()
    line = Line(nz, dp, z, acc, up, down, s_up, r_up, s_down, r_down)
    line.first()
    for distance in range(1, nz - 1):
        line.step(distance)
    line.finish(out_ref)
    line.drain()


def line_scatter(p, nz, collective_id):
    _, rows, width = p.shape
    dma, vmem = pltpu.SemaphoreType.DMA, functools.partial(pltpu.VMEM, dtype=p.dtype)
    return pl.pallas_call(
        functools.partial(line_scatter_kernel, nz),
        name="line_scatter",
        out_shape=jax.ShapeDtypeStruct((rows, width), jnp.float32),
        in_specs=[pl.BlockSpec(memory_space=pl.ANY)],
        out_specs=pl.BlockSpec(memory_space=pltpu.VMEM),
        scratch_shapes=[vmem((nz, rows, width)) for _ in range(3)]
        + [dma(())]
        + [dma((nz, PARTS)) for _ in range(4)],
        compiler_params=pltpu.CompilerParams(
            collective_id=collective_id, has_side_effects=True, vmem_limit_bytes=16 * 2**20
        ),
    )(p)


def z_order(nz):
    return [sorted(range(nz), key=lambda zz: (-abs(zz - z), zz if z >= nz // 2 else -zz)) for z in range(nz)]


def scatter_kernel(nz, p_ref, gate_ref, up_ref, t_ref, out_ref, tiles_ref, parts, weights, rc, ra, rb, rx, ry, ru, rd, s_weight, s_tile, r_tile, s_keep, s_core, r_core, s_a, r_a, s_b, r_b, s_x, r_x, s_y, r_y, s_u, r_u, s_d, r_d):
    dp, z = lax.axis_index("dp"), lax.axis_index("tensor")
    rows = parts.shape[3]
    half = rows // 2
    core = dp % 2

    def acc(kind, zz):
        return parts.at[kind, zz, core]

    order = z_order(nz)

    def place(i):
        zz = order[0][i]
        for zv in range(1, nz):
            zz = jnp.where(z == zv, order[zv][i], zz)
        return zz

    flips = (0, 2, 4, 6)

    def core_copy(kind, zz):
        return remote(
            parts.at[kind, zz, 1 - core], rc.at[kind, zz], s_core.at[kind, zz], r_core.at[kind, zz], (dp ^ 1, z)
        )

    def product(kind, zz):
        slopes = p_ref.at[(dp ^ (2 * kind)) // 2, zz]

        def tile(n, carry):
            at = pl.ds(pl.multiple_of(n * 256, 256), 256)
            total = lax.dot_general(
                slopes[...], weights[at, :], (((1,), (1,)), ((), ())), preferred_element_type=jnp.float32
            ).astype(parts.dtype)
            parts[kind, zz, 0, :, at] = total[:rows]
            parts[kind, zz, 1, :, at] = total[rows:]
            return carry

        lax.fori_loop(0, parts.shape[4] // 256, tile, 0, unroll=2)

    def a_copy(zz):
        return remote(acc(3, zz).at[pl.ds(0, half)], ra.at[zz], s_a.at[zz], r_a.at[zz], (dp ^ 2, z))

    def b_copy(zz):
        return remote(acc(3, zz).at[pl.ds(half, half)], rb.at[zz], s_b.at[zz], r_b.at[zz], (dp ^ 4, z))

    def x_copy(zz):
        return remote(acc(1, zz), rx.at[zz], s_x.at[zz], r_x.at[zz], (dp ^ 2, z))

    def y_copy(zz):
        return remote(acc(2, zz), ry.at[zz], s_y.at[zz], r_y.at[zz], (dp ^ 4, z))

    def up_copy(zz):
        return remote(acc(0, zz), ru.at[zz], s_u.at[zz], r_u.at[zz], (dp, z + 1))

    def down_copy(zz):
        return remote(acc(0, zz), rd.at[zz], s_d.at[zz], r_d.at[zz], (dp, z - 1))

    def add(dst, *others, start=0, count=rows):
        add_rows(dst, *others, start=start, count=count)

    def wave(i):
        zz = place(i)

        def one(k, carry):
            kind = 3 - k
            product(kind, zz)
            core_copy(kind, zz).start()
            return carry

        lax.fori_loop(0, 4, one, 0)

    def paired(kind, zz):
        core_copy(kind, zz).wait_recv()

    def stage_diagonal(i):
        zz = place(i)
        paired(3, zz)
        add(acc(3, zz), (rc.at[3, zz], 0))
        a_copy(zz).start()
        b_copy(zz).start()

    def stage_side(i):
        zz = place(i)
        paired(1, zz)
        paired(2, zz)
        a_copy(zz).wait_recv()
        add(acc(2, zz), (rc.at[2, zz], 0), (ra.at[zz], 0), start=0, count=half)
        add(acc(2, zz), (rc.at[2, zz], half), start=half, count=half)
        y_copy(zz).start()
        b_copy(zz).wait_recv()
        add(acc(1, zz), (rc.at[1, zz], half), (rb.at[zz], 0), start=half, count=half)
        add(acc(1, zz), (rc.at[1, zz], 0), start=0, count=half)
        x_copy(zz).start()

    def stage_column(i):
        zz = place(i)
        paired(0, zz)
        x_copy(zz).wait_recv()
        y_copy(zz).wait_recv()
        add(acc(0, zz), (rc.at[0, zz], 0), (rx.at[zz], 0), (ry.at[zz], 0))

        @pl.when((zz > z) & (z == 0))
        def _():
            up_copy(zz).start()

        @pl.when((zz < z) & (z == nz - 1))
        def _():
            down_copy(zz).start()

    def stage_line(i):
        zz = place(i)

        @pl.when((zz > z) & (z > 0))
        def _():
            up_copy(zz).wait_recv()
            add(acc(0, zz), (ru.at[zz], 0))
            up_copy(zz).start()

        @pl.when((zz < z) & (z < nz - 1))
        def _():
            down_copy(zz).wait_recv()
            add(acc(0, zz), (rd.at[zz], 0))
            down_copy(zz).start()

    def peers():
        for flip in range(8):
            for turn in range(nz):
                if flip or turn:
                    yield flip, turn, dp ^ flip, lax.rem(z + turn, nz)

    def tile_copy(flip, turn, peer, line):
        here = dp * nz + z
        return remote(
            t_ref.at[peer * nz + line], tiles_ref.at[here], s_tile.at[flip, turn], r_tile.at[flip, turn], (peer, line)
        )

    each = gate_ref.shape[2]
    here = gate_ref.shape[0]
    fetch = [
        pltpu.make_async_copy(
            ref.at[j], weights.at[:, pl.ds((k * here + j) * each, each)], s_weight.at[k, j]
        )
        for k, ref in enumerate((gate_ref, up_ref))
        for j in range(here)
    ]
    for copy in fetch:
        copy.start()
    barrier = pltpu.get_barrier_semaphore()
    for _, _, peer, line in peers():
        pl.semaphore_signal(barrier, 1, device_id=(peer, line), device_id_type=MESH)
    pl.semaphore_wait(barrier, 8 * nz - 1)
    for copy in fetch:
        copy.wait()
    wave(0)
    keep = pltpu.make_async_copy(t_ref.at[dp * nz + z], tiles_ref.at[dp * nz + z], s_keep)
    keep.start()
    for peer in peers():
        tile_copy(*peer).start()
    for i in range(nz + 3):
        if i < nz:
            stage_diagonal(i)
        if i + 1 < nz:
            wave(i + 1)
        if 0 <= i - 1 < nz:
            stage_side(i - 1)
        if 0 <= i - 2 < nz:
            stage_column(i - 2)
        if 0 <= i - 3 < nz:
            stage_line(i - 3)

    keep.wait()
    for flip, turn, peer, line in peers():
        tile_copy(flip, turn, peer, line).wait_send()
        source = tiles_ref.at[peer * nz + lax.rem(z - turn + nz, nz)]
        remote(source, source, s_tile.at[flip, turn], r_tile.at[flip, turn], (dp ^ 1, z)).wait_recv()

    @pl.when(z > 0)
    def _():
        up_copy(z).wait_recv()

    @pl.when(z < nz - 1)
    def _():
        down_copy(z).wait_recv()

    def finish(k, carry):
        at = pl.ds(k * CHUNK, CHUNK)
        total = parts[0, z, core, at, :].astype(jnp.float32)
        zero = jnp.zeros_like(total)
        total = total + jnp.where(z > 0, ru[z, at, :].astype(jnp.float32), zero)
        total = total + jnp.where(z < nz - 1, rd[z, at, :].astype(jnp.float32), zero)
        out_ref[at, :] = total
        return carry

    lax.fori_loop(0, rows // CHUNK, finish, 0)
    for zz in range(nz):
        for kind in range(4):
            core_copy(kind, zz).wait_send()
        a_copy(zz).wait_send()
        b_copy(zz).wait_send()
        x_copy(zz).wait_send()
        y_copy(zz).wait_send()

        @pl.when(zz > z)
        def _():
            up_copy(zz).wait_send()

        @pl.when(zz < z)
        def _():
            down_copy(zz).wait_send()


def scatter_all(p, w_gate, w_up, tiles, nz, collective_id):
    rows, width = p.shape[2] // 2, w_gate.shape[1]
    dma, vmem = pltpu.SemaphoreType.DMA, functools.partial(pltpu.VMEM, dtype=p.dtype)
    half = rows // 2
    return pl.pallas_call(
        functools.partial(scatter_kernel, nz),
        name="scatter_all",
        out_shape=(
            jax.ShapeDtypeStruct((rows, width), jnp.float32),
            jax.ShapeDtypeStruct(tiles.shape, tiles.dtype),
        ),
        in_specs=[
            pl.BlockSpec(memory_space=pltpu.VMEM),
            *[pl.BlockSpec(memory_space=pl.ANY)] * 2,
            pl.BlockSpec(memory_space=pltpu.VMEM),
        ],
        out_specs=(pl.BlockSpec(memory_space=pltpu.VMEM), pl.BlockSpec(memory_space=pltpu.VMEM)),
        scratch_shapes=[vmem((4, nz, 2, rows, width)), vmem((width, p.shape[3])), vmem((4, nz, rows, width))]
        + [vmem((nz, half, width)) for _ in range(2)]
        + [vmem((nz, rows, width)) for _ in range(4)]
        + [dma((2, w_gate.shape[0])), dma((8, nz)), dma((8, nz)), dma(())]
        + [dma((4, nz)), dma((4, nz))]
        + [dma((nz,)) for _ in range(12)],
        compiler_params=pltpu.CompilerParams(
            collective_id=collective_id, has_side_effects=True, vmem_limit_bytes=VMEM_LIMIT
        ),
    )(p, w_gate, w_up, tiles)


def finish_kernel(nz, nc, g_ref, h_ref, p_ref, e_ref, unit_ref, small_ref, sum_q, sum_k, sum_v, sum_o, out_ref, routed_ref, total_ref, buf, acc, rc, ra, rb, rx, ry, line_acc, up, down, more_acc, more_got, *sems):
    (s_load, s_core, r_core, s_a, r_a, s_b, r_b, s_x, r_x, s_y, r_y) = sems[:11]
    (t_x, q_x, t_y, q_y, t_a, q_a, t_b, q_b, t_c, q_c) = sems[11:21]
    s_line, s_store, s_up, r_up, s_down, r_down = sems[21:27]
    (s_load_more, s_more, r_more), sems = sems[27:30], sems[:27] + sems[30:]
    total = Total(nz, lax.axis_index("dp"), lax.axis_index("tensor"), *sems[27:])
    dp, z = lax.axis_index("dp"), lax.axis_index("tensor")
    rows = acc.shape[2]
    half = rows // 2
    flips = (0, 2, 4, 6)

    parts = ((g_ref, 0, g_ref.shape[2]), (h_ref, g_ref.shape[2], h_ref.shape[2]))

    def loads(kind, c):
        return [
            pltpu.make_async_copy(
                ref.at[(dp ^ flips[kind]) * nc + c], acc.at[kind, c, :, pl.ds(at, size)], s_load.at[k, kind, c]
            )
            for k, (ref, at, size) in enumerate(parts)
        ]

    def core_copies(kind, c):
        return [
            remote(
                ref.at[(dp ^ flips[kind] ^ 1) * nc + c],
                rc.at[kind, c, :, pl.ds(at, size)],
                s_core.at[k, kind, c],
                r_core.at[k, kind, c],
                (dp ^ 1, z),
            )
            for k, (ref, at, size) in enumerate(parts)
        ]

    def a_copy(c):
        return remote(acc.at[3, c, pl.ds(0, half)], ra.at[c], s_a.at[c], r_a.at[c], (dp ^ 2, z))

    def b_copy(c):
        return remote(acc.at[3, c, pl.ds(half, half)], rb.at[c], s_b.at[c], r_b.at[c], (dp ^ 4, z))

    def x_copy(c):
        return remote(acc.at[1, c], rx.at[c], s_x.at[c], r_x.at[c], (dp ^ 2, z))

    def y_copy(c):
        return remote(acc.at[2, c], ry.at[c], s_y.at[c], r_y.at[c], (dp ^ 4, z))

    def full(flip, c):
        return buf.at[(dp ^ flip) * nc + c]

    def back_x(c):
        return remote(full(0, c), full(0, c), t_x.at[c], q_x.at[c], (dp ^ 2, z))

    def back_y(c):
        return remote(full(0, c), full(0, c), t_y.at[c], q_y.at[c], (dp ^ 4, z))

    def back_a(c):
        ref = full(4, c).at[pl.ds(0, half)]
        return remote(ref, ref, t_a.at[c], q_a.at[c], (dp ^ 2, z))

    def back_b(c):
        ref = full(2, c).at[pl.ds(half, half)]
        return remote(ref, ref, t_b.at[c], q_b.at[c], (dp ^ 4, z))

    def back_core(kind, c):
        ref = full((0, 2, 4, 6, 6)[kind], c)
        if kind >= 3:
            ref = ref.at[pl.ds((kind - 3) * half, half)]
        return remote(ref, ref, t_c.at[kind, c], q_c.at[kind, c], (dp ^ 1, z))

    def arrived(ref, sem):
        remote(ref, ref, sem, sem, (dp ^ 1, z)).wait_recv()

    def paired(kind, c):
        for copy in loads(kind, c):
            copy.wait()
        for copy in core_copies(kind, c):
            copy.wait_recv()

    def stage_diagonal(c):
        paired(3, c)
        add_rows(acc.at[3, c], (rc.at[3, c], 0), count=rows)
        a_copy(c).start()
        b_copy(c).start()

    def stage_side(c):
        paired(1, c)
        paired(2, c)
        a_copy(c).wait_recv()
        add_rows(acc.at[2, c], (rc.at[2, c], 0), (ra.at[c], 0), start=0, count=half)
        add_rows(acc.at[2, c], (rc.at[2, c], half), start=half, count=half)
        y_copy(c).start()
        b_copy(c).wait_recv()
        add_rows(acc.at[1, c], (rc.at[1, c], half), (rb.at[c], 0), start=half, count=half)
        add_rows(acc.at[1, c], (rc.at[1, c], 0), start=0, count=half)
        x_copy(c).start()

    def stage_own(c):
        paired(0, c)
        x_copy(c).wait_recv()
        y_copy(c).wait_recv()
        dst = full(0, c)

        def body(k, carry):
            at = pl.ds(k * CHUNK, CHUNK)
            total = acc[0, c, at, :].astype(jnp.float32) + rc[0, c, at, :].astype(jnp.float32)
            total = total + rx[c, at, :].astype(jnp.float32) + ry[c, at, :].astype(jnp.float32)
            dst[at, :] = total.astype(dst.dtype)
            return carry

        lax.fori_loop(0, rows // CHUNK, body, 0)
        back_x(c).start()
        back_y(c).start()
        back_core(0, c).start()

    def stage_relay(c):
        arrived(full(4, c), q_y.at[c])
        back_a(c).start()
        back_core(2, c).start()
        arrived(full(2, c), q_x.at[c])
        back_b(c).start()
        back_core(1, c).start()

    def stage_corner(c):
        arrived(full(6, c).at[pl.ds(0, half)], q_a.at[c])
        back_core(3, c).start()
        arrived(full(6, c).at[pl.ds(half, half)], q_b.at[c])
        back_core(4, c).start()

    line_load = pltpu.make_async_copy(p_ref, line_acc, s_line)
    line_load.start()
    more_load = pltpu.make_async_copy(e_ref, more_acc, s_load_more)
    more_load.start()
    for c in range(nc):
        for kind in (3, 1, 2, 0):
            for copy in loads(kind, c):
                copy.start()
    greet_total(dp, z, nz)
    for c in range(nc):
        for kind in (3, 1, 2, 0):
            for copy in core_copies(kind, c):
                copy.start()
    line = Line(nz, dp, z, line_acc, up, down, s_up, r_up, s_down, r_down)
    line_load.wait()
    line.first()

    def line_end():
        line.finish(out_ref)
        line.drain()
        share = jnp.sum(out_ref[...] * unit_ref[...], axis=0, keepdims=True)
        total.got[0] = small_ref[...]
        wide = small_ref.shape[1]
        for k in range(out_ref.shape[1] // wide):
            total.got[0, k : k + 1, :] = share[:, k * wide : (k + 1) * wide]

    others = [lax.rem(z + turn, nz) for turn in range(1, nz)]
    more = [
        remote(more_acc.at[place], more_got.at[turn], s_more.at[turn], r_more.at[turn], (dp, place))
        for turn, place in enumerate(others)
    ]

    def more_start():
        more_load.wait()
        for copy in more:
            copy.start()

    def more_end():
        for copy in more:
            copy.wait()

        def body(k, carry):
            at = pl.ds(k * CHUNK, CHUNK)
            part = more_acc[z, at, :].astype(jnp.float32)
            for turn in range(nz - 1):
                part = part + more_got[turn, at, :].astype(jnp.float32)
            routed_ref[at, :] = part
            return carry

        lax.fori_loop(0, routed_ref.shape[0] // CHUNK, body, 0)

    side = [functools.partial(line.step, distance) for distance in range(1, nz - 1)] + [line_end, more_start]
    side += [functools.partial(total.step, 0, total_ref)]
    late = [functools.partial(total.step, k, total_ref) for k in range(1, 3)] + [more_end]
    late += [functools.partial(total.step, k, total_ref) for k in range(3, Total.steps)]
    stages = (stage_diagonal, stage_side, stage_own, stage_relay, stage_corner)
    for i in range(nc + len(stages) - 1):
        for lag, stage in enumerate(stages):
            if 0 <= i - lag < nc:
                stage(i - lag)
                if i >= 1 and side:
                    side.pop(0)()
    for one in side + late:
        one()
    for c in range(nc):
        for kind, flip in ((0, 1), (1, 3), (2, 5)):
            arrived(full(flip, c), q_c.at[kind, c])
        for kind in (3, 4):
            arrived(full(7, c).at[pl.ds((kind - 3) * half, half)], q_c.at[kind, c])
    wide = buf.shape[2] // 4
    stores = [
        pltpu.make_async_copy(buf.at[:, :, pl.ds(k * wide, wide)], ref, s_store.at[k])
        for k, ref in enumerate((sum_q, sum_k, sum_v, sum_o))
    ]
    for store in stores:
        store.start()
    for c in range(nc):
        for kind in range(4):
            for copy in core_copies(kind, c):
                copy.wait_send()
        for copy in (a_copy, b_copy, x_copy, y_copy, back_x, back_y, back_a, back_b):
            copy(c).wait_send()
        for kind in range(5):
            back_core(kind, c).wait_send()
    for store in stores:
        store.wait()


def finish_sums(g, h, p, e, unit, small, nz, nc, collective_id):
    _, rows, width = g.shape
    width += h.shape[2]
    _, line_rows, line_width = p.shape
    half = rows // 2
    dma, vmem = pltpu.SemaphoreType.DMA, functools.partial(pltpu.VMEM, dtype=g.dtype)
    return pl.pallas_call(
        functools.partial(finish_kernel, nz, nc),
        name="finish_sums",
        out_shape=(
            *[jax.ShapeDtypeStruct(g.shape[:2] + (width // 4,), g.dtype)] * 4,
            *[jax.ShapeDtypeStruct((line_rows, line_width), jnp.float32)] * 2,
            jax.ShapeDtypeStruct(small.shape, small.dtype),
        ),
        in_specs=[pl.BlockSpec(memory_space=pl.ANY)] * 4 + [pl.BlockSpec(memory_space=pltpu.VMEM)] * 2,
        out_specs=(
            *[pl.BlockSpec(memory_space=pl.ANY)] * 4,
            *[pl.BlockSpec(memory_space=pltpu.VMEM)] * 3,
        ),
        scratch_shapes=[vmem(g.shape[:2] + (width,)), vmem((4, nc, rows, width)), vmem((4, nc, rows, width))]
        + [vmem((nc, half, width)) for _ in range(2)]
        + [vmem((nc, rows, width)) for _ in range(2)]
        + [vmem((nz, line_rows, line_width)) for _ in range(4)]
        + [vmem((nz - 1, line_rows, line_width))]
        + [dma((2, 4, nc)) for _ in range(3)]
        + [dma((nc,)) for _ in range(16)]
        + [dma((5, nc)), dma((5, nc))]
        + [dma(()), dma((4,))]
        + [dma((nz, PARTS)) for _ in range(4)]
        + [dma(()), dma((nz - 1,)), dma((nz - 1,))]
        + total_scratch(nz, small.shape, small.dtype),
        compiler_params=pltpu.CompilerParams(
            collective_id=collective_id, has_side_effects=True, vmem_limit_bytes=VMEM_LIMIT
        ),
    )(g, h, p, e, unit, small)


class Spread:
    def __init__(self, nz, row_shape):
        self.nz, self.row_shape = nz, row_shape

    @staticmethod
    def swap(value, flip):
        return lax.ppermute(value, "dp", [(i, i ^ flip) for i in range(8)])

    @staticmethod
    def plus(a, b):
        return (a.astype(jnp.float32) + b.astype(jnp.float32)).astype(a.dtype)

    def pair(self, mine, partners):
        self.mine = mine
        return self.swap(partners, 1)

    def sides(self, theirs):
        nz, plus = self.nz, self.plus
        self.low, self.high = slice(0, nz // 2), slice(nz // 2, nz)
        mine = self.mine.reshape((4, nz) + self.row_shape)
        self.whole = whole = plus(mine, theirs.reshape(mine.shape))
        to_x = jnp.stack([whole[1, self.low], whole[3, self.low]])
        to_y = jnp.stack([whole[2, self.high], whole[3, self.high]])
        return to_x, to_y

    def side(self, sides):
        return self.swap(sides[0], 2), self.swap(sides[1], 4)

    def last_side(self, sides):
        by_x, by_y = sides
        whole, low, high, plus = self.whole, self.low, self.high, self.plus
        self.low_own, low_y = plus(whole[0, low], by_x[0]), plus(whole[2, low], by_x[1])
        self.high_own, high_x = plus(whole[0, high], by_y[0]), plus(whole[1, high], by_y[1])
        return self.swap(low_y, 4), self.swap(high_x, 2)

    def column(self, sides):
        return jnp.concatenate([self.plus(self.low_own, sides[0]), self.plus(self.high_own, sides[1])])


def hold(first, second):
    return lax.optimization_barrier((first, second))


def experts_routed(
    hidden_after_attention,
    expert_ids,
    expert_norm_gain,
    w_router,
    w_gate,
    w_up,
    w_down,
    grad_output,
):
    tok_count, d_model = hidden_after_attention.shape
    n_tensor = lax.axis_size("tensor")
    n_dp = lax.axis_size("dp")
    devices = n_dp * n_tensor
    second_norm_scale = root_mean_square_scale(hidden_after_attention)
    second_unit_rows = hidden_after_attention * second_norm_scale
    second_normalized = (second_unit_rows * expert_norm_gain).astype(jnp.bfloat16)
    experts = w_router.shape[1]
    topk = expert_ids.shape[1]
    exp_dev = w_gate.shape[0]
    most = 2 * ((tok_count * topk * 9 + experts * 16 - 1) // (experts * 16))
    route_probs = jax.nn.softmax(
        jnp.dot(second_normalized, w_router, preferred_element_type=jnp.float32), axis=-1
    )
    chosen = expert_ids[:, :, None] == jnp.arange(experts, dtype=jnp.int32)[None, None, :]
    gate_values = jnp.sum(jnp.where(chosen, route_probs[:, None, :], 0.0), axis=-1)
    flat_ids, pair_rank = slot_positions(expert_ids, experts)
    pair_slot = (flat_ids % exp_dev * n_dp + flat_ids // exp_dev) * most + pair_rank
    pair_count = tok_count * topk
    slot_count = exp_dev * n_dp * most
    slot_owner = (
        jnp.full((slot_count,), pair_count, jnp.int32)
        .at[pair_slot]
        .set(jnp.arange(pair_count, dtype=jnp.int32))
    )
    padded = jnp.concatenate([second_normalized, jnp.zeros((1, d_model), jnp.bfloat16)], axis=0)
    outgoing = padded[slot_owner // topk].reshape(exp_dev, n_dp, most, d_model)
    copies = jnp.broadcast_to(
        outgoing[:, :, None], (exp_dev, n_dp, n_tensor, most, d_model)
    ).reshape(exp_dev, devices, most, d_model)
    arrived = lax.all_to_all(copies, ("dp", "tensor"), split_axis=1, concat_axis=1, tiled=True)
    expert_rows = arrived.reshape(exp_dev, devices * most, d_model)
    gate_pre = jnp.einsum("erd,edf->erf", expert_rows, w_gate, preferred_element_type=jnp.float32)
    up_pre = jnp.einsum("erd,edf->erf", expert_rows, w_up, preferred_element_type=jnp.float32)
    gate_sigmoid = jax.nn.sigmoid(gate_pre)
    silu_gate = gate_pre * gate_sigmoid
    hidden = (silu_gate * up_pre).astype(jnp.bfloat16)
    partial_value = (
        jnp.einsum("erf,efd->erd", hidden, w_down, preferred_element_type=jnp.float32)
        .astype(jnp.bfloat16)
        .reshape(exp_dev, devices, most, d_model)
    )
    returned = lax.all_to_all(
        partial_value, ("dp", "tensor"), split_axis=1, concat_axis=1, tiled=True
    )
    expert_out = jnp.sum(
        returned.reshape(exp_dev, n_dp, n_tensor, most, d_model).astype(jnp.float32), axis=2
    ).reshape(slot_count, d_model)
    pair_out = expert_out[pair_slot].reshape(tok_count, topk, d_model)
    result = (hidden_after_attention + jnp.sum(gate_values[:, :, None] * pair_out, axis=1)).astype(
        jnp.bfloat16
    )
    cotangent = grad_output.astype(jnp.float32)
    grad_gates = jnp.sum(pair_out * cotangent[:, None, :], axis=-1)
    grad_pairs = (
        (gate_values[:, :, None] * cotangent[:, None, :])
        .astype(jnp.bfloat16)
        .reshape(pair_count, d_model)
    )
    grad_slots = jnp.concatenate([grad_pairs, jnp.zeros((1, d_model), jnp.bfloat16)], axis=0)[
        slot_owner
    ].reshape(exp_dev, n_dp, most, d_model)
    grad_copies = jnp.broadcast_to(
        grad_slots[:, :, None], (exp_dev, n_dp, n_tensor, most, d_model)
    ).reshape(exp_dev, devices, most, d_model)
    grad_arrived = lax.all_to_all(
        grad_copies, ("dp", "tensor"), split_axis=1, concat_axis=1, tiled=True
    )
    grad_rows = grad_arrived.reshape(exp_dev, devices * most, d_model)
    grad_hidden = jnp.einsum("erd,efd->erf", grad_rows, w_down, preferred_element_type=jnp.float32)
    grad_down = jnp.einsum("erf,erd->efd", hidden, grad_rows, preferred_element_type=jnp.float32)
    grad_gate_pre = (
        grad_hidden * up_pre * gate_sigmoid * (1.0 + gate_pre * (1.0 - gate_sigmoid))
    ).astype(jnp.bfloat16)
    grad_up_pre = (grad_hidden * silu_gate).astype(jnp.bfloat16)
    grad_gate = jnp.einsum(
        "erd,erf->edf", expert_rows, grad_gate_pre, preferred_element_type=jnp.float32
    )
    grad_up = jnp.einsum(
        "erd,erf->edf", expert_rows, grad_up_pre, preferred_element_type=jnp.float32
    )
    grad_expert_in = jnp.einsum(
        "erf,edf->erd", grad_gate_pre, w_gate, preferred_element_type=jnp.float32
    )
    grad_expert_in = grad_expert_in + jnp.einsum(
        "erf,edf->erd", grad_up_pre, w_up, preferred_element_type=jnp.float32
    )
    grad_expert_in = grad_expert_in.astype(jnp.bfloat16).reshape(exp_dev, devices, most, d_model)
    grad_back = lax.all_to_all(
        grad_expert_in, ("dp", "tensor"), split_axis=1, concat_axis=1, tiled=True
    )
    grad_slot_in = jnp.sum(
        grad_back.reshape(exp_dev, n_dp, n_tensor, most, d_model).astype(jnp.float32), axis=2
    ).reshape(slot_count, d_model)
    grad_second_normalized = jnp.sum(
        grad_slot_in[pair_slot].reshape(tok_count, topk, d_model), axis=1
    )
    grad_route = jnp.sum(jnp.where(chosen, grad_gates[:, :, None], 0.0), axis=1)
    grad_logits = (
        route_probs * (grad_route - jnp.sum(route_probs * grad_route, axis=-1, keepdims=True))
    ).astype(jnp.bfloat16)
    grad_router_part = jnp.einsum(
        "td,te->de", second_normalized, grad_logits, preferred_element_type=jnp.float32
    )
    grad_second_normalized = grad_second_normalized + jnp.einsum(
        "te,de->td", grad_logits, w_router, preferred_element_type=jnp.float32
    )
    grad_expert_share = jnp.sum(grad_second_normalized * second_unit_rows, axis=0)
    grad_second_unit_rows = grad_second_normalized * expert_norm_gain
    grad_hidden_one = (
        second_norm_scale
        * (
            grad_second_unit_rows
            - second_unit_rows
            * jnp.mean(grad_second_unit_rows * second_unit_rows, axis=-1, keepdims=True)
        )
        + cotangent
    )
    return (
        result,
        grad_hidden_one,
        grad_expert_share,
        grad_router_part,
        grad_gate,
        grad_up,
        grad_down,
    )


def experts_dense(
    hidden_after_attention,
    expert_ids,
    expert_norm_gain,
    w_router,
    w_gate,
    w_up,
    w_down,
    grad_output,
    all_cotangents,
):
    tok_count, d_model = hidden_after_attention.shape
    n_tensor = lax.axis_size("tensor")
    n_dp = lax.axis_size("dp")
    devices = n_dp * n_tensor
    everyone = ("dp", "tensor")
    second_norm_scale = root_mean_square_scale(hidden_after_attention)
    second_unit_rows = hidden_after_attention * second_norm_scale
    second_normalized = (second_unit_rows * expert_norm_gain).astype(jnp.bfloat16)
    experts = w_router.shape[1]
    exp_dev, _, width = w_gate.shape
    all_count = devices * tok_count
    expert_at = jnp.arange(experts, dtype=jnp.int32)

    chosen = jnp.any(expert_ids[:, :, None] == expert_at[None, None, :], axis=1)
    route_probs = jax.nn.softmax(
        jnp.dot(second_normalized, w_router, preferred_element_type=jnp.float32), axis=-1
    )
    gates = jnp.where(chosen, route_probs, 0.0).T

    down_rows = w_down.reshape(exp_dev * width, d_model)
    both = exp_dev * width
    all_rows, slopes, gated, tiles = gather_experts(
        second_normalized,
        gates,
        all_cotangents.reshape(devices, tok_count, d_model),
        w_gate,
        w_up,
        w_down,
        n_tensor,
        0,
    )
    all_rows, grad_pre = all_rows.reshape(all_count, d_model), slopes.reshape(all_count, 2 * both)
    gated_hidden = gated.reshape(all_count, both)
    lines = gated.reshape(n_dp, n_tensor * tok_count, both)

    def out_rows(places):
        picked = [
            lax.dynamic_index_in_dim(lines, lax.axis_index("dp") ^ k, axis=0, keepdims=False)
            for k in places
        ]
        return jnp.dot(
            jnp.concatenate(picked), down_rows, preferred_element_type=jnp.float32
        ).astype(jnp.bfloat16)

    spread = Spread(n_tensor, (tok_count, d_model))
    partner_rows = out_rows((1, 3, 5, 7))
    grad_in, gate_tiles = scatter_all(slopes, w_gate, w_up, tiles, n_tensor, 1)
    grad_in, partner_rows = hold(grad_in, partner_rows)
    theirs = spread.pair(out_rows((0, 2, 4, 6)), partner_rows)
    sides = spread.sides(theirs)
    grad_down = jnp.einsum(
        "tf,td->fd", gated_hidden, all_cotangents, preferred_element_type=jnp.float32
    ).reshape(exp_dev, width, d_model)
    grad_wide = jnp.einsum("td,tf->df", all_rows, grad_pre, preferred_element_type=jnp.float32)
    grad_gate = jnp.stack([grad_wide[:, e * width : (e + 1) * width] for e in range(exp_dev)])
    grad_up = jnp.stack([grad_wide[:, both + e * width : both + (e + 1) * width] for e in range(exp_dev)])

    grad_route = jnp.sum(gate_tiles[:, :exp_dev].reshape(n_dp, n_tensor, exp_dev, tok_count), axis=1)
    grad_route = jnp.where(chosen, grad_route.reshape(experts, tok_count).T, 0.0)
    cotangent = grad_output.astype(jnp.float32)
    grad_logits = (
        route_probs * (grad_route - jnp.sum(route_probs * grad_route, axis=-1, keepdims=True))
    ).astype(jnp.bfloat16)
    grad_router_part = jnp.einsum(
        "td,te->de", second_normalized, grad_logits, preferred_element_type=jnp.float32
    )
    grad_second_normalized = grad_in + jnp.einsum(
        "te,de->td", grad_logits, w_router, preferred_element_type=jnp.float32
    )
    grad_expert_share = jnp.sum(grad_second_normalized * second_unit_rows, axis=0)
    grad_second_unit_rows = grad_second_normalized * expert_norm_gain
    grad_hidden_one = (
        second_norm_scale
        * (
            grad_second_unit_rows
            - second_unit_rows
            * jnp.mean(grad_second_unit_rows * second_unit_rows, axis=-1, keepdims=True)
        )
        + cotangent
    )
    return (
        spread,
        sides,
        grad_hidden_one,
        grad_expert_share,
        grad_router_part,
        grad_gate,
        grad_up,
        grad_down,
    )


def local_gathered(
    tokens,
    file_ids,
    expert_ids,
    attention_norm_gain,
    w_query,
    w_key,
    w_value,
    query_gain,
    key_gain,
    w_output,
    expert_norm_gain,
    w_router,
    w_gate,
    w_up,
    w_down,
    grad_output,
):
    tok_count, d_model = tokens.shape
    n_tensor = lax.axis_size("tensor")
    n_dp = lax.axis_size("dp")
    devices = n_dp * n_tensor
    local_dim = w_query.shape[1]
    head_dim = HEAD_DIM
    local_heads = local_dim // head_dim
    seq_len = tok_count * n_tensor
    block_rows = min(512, seq_len)
    score_scale = 1.0 / math.sqrt(head_dim)
    file_row = file_ids[0]
    cosine, sine_table = rope_tables(seq_len, head_dim)
    input_tensors = tokens.astype(jnp.float32)
    first_norm_scale = root_mean_square_scale(input_tensors)
    first_unit_rows = input_tensors * first_norm_scale
    first_normalized = (first_unit_rows * attention_norm_gain).astype(jnp.bfloat16)
    normed_all = line_gather(first_normalized, n_tensor, 2).reshape(seq_len, d_model)
    all_cotangents = lax.all_gather(grad_output, ("dp", "tensor"), axis=0, tiled=True)
    query_raw = jnp.dot(normed_all, w_query, preferred_element_type=jnp.float32)
    key_raw = jnp.dot(normed_all, w_key, preferred_element_type=jnp.float32)
    value_rows = (
        jnp.dot(normed_all, w_value, preferred_element_type=jnp.float32)
        .astype(jnp.bfloat16)
        .reshape(seq_len, local_heads, head_dim)
    )
    query_total, key_total = line_total(
        jnp.stack([jnp.sum(query_raw * query_raw, axis=1), jnp.sum(key_raw * key_raw, axis=1)]), n_tensor, 6
    )
    query_scale = lax.rsqrt(query_total / d_model + EPSILON)[:, None]
    key_scale = lax.rsqrt(key_total / d_model + EPSILON)[:, None]
    query_hat = query_raw * query_scale
    key_hat = key_raw * key_scale
    queries = rotate(
        (query_hat * query_gain).reshape(seq_len, local_heads, head_dim), cosine, sine_table
    ).astype(jnp.bfloat16)
    key_rows = rotate(
        (key_hat * key_gain).reshape(seq_len, local_heads, head_dim), cosine, sine_table
    ).astype(jnp.bfloat16)
    block_start = 0
    scores = block_scores(queries, key_rows, file_row, block_start, score_scale)
    row_peak = jnp.max(scores, axis=-1, keepdims=True)
    log_total = row_peak + jnp.log(jnp.sum(jnp.exp(scores - row_peak), axis=-1, keepdims=True))
    attn_probs = jnp.exp(scores - log_total).astype(jnp.bfloat16)
    context_blocks = jnp.einsum(
        "hqk,khd->qhd", attn_probs, value_rows, preferred_element_type=jnp.float32
    )
    log_totals = [log_total]
    context = context_blocks.reshape(seq_len, local_dim).astype(jnp.bfloat16)
    attn_out = line_scatter(
        jnp.dot(context, w_output, preferred_element_type=jnp.float32)
        .astype(jnp.bfloat16)
        .reshape(n_tensor, tok_count, d_model),
        n_tensor,
        3,
    )
    hidden_after_attention = input_tensors + attn_out
    spread, sides, grad_hidden_one, grad_expert_share, grad_router_part, grad_gate, grad_up, grad_down = (
        experts_dense(
            hidden_after_attention,
            expert_ids,
            expert_norm_gain,
            w_router,
            w_gate,
            w_up,
            w_down,
            grad_output,
            all_cotangents,
        )
    )
    grad_attn = grad_hidden_one.astype(jnp.bfloat16)
    side_parts = jnp.concatenate([grad_router_part.T, grad_expert_share[None, :]])
    side_total = lax.psum(side_parts, ("dp", "tensor"))
    grad_attn, sides = hold(grad_attn, sides)
    sides = spread.side(sides)
    grad_attn_all = line_gather(grad_attn, n_tensor, 2)
    grad_attn_all, sides = hold(grad_attn_all, sides)
    sides = spread.last_side(sides)
    grad_attn_all = grad_attn_all.reshape(seq_len, d_model)
    grad_output_part = jnp.einsum(
        "sd,se->ed", context, grad_attn_all, preferred_element_type=jnp.float32
    )
    grad_context = (
        jnp.einsum("se,de->sd", grad_attn_all, w_output, preferred_element_type=jnp.float32)
        .astype(jnp.bfloat16)
        .reshape(seq_len, local_heads, head_dim)
    )
    grad_query_blocks = []
    grad_key_total = jnp.zeros((seq_len, local_heads, head_dim), jnp.float32)
    grad_value_total = jnp.zeros((seq_len, local_heads, head_dim), jnp.float32)
    for block_index, block_start in enumerate(range(0, seq_len, block_rows)):
        scores = block_scores(queries, key_rows, file_row, block_start, score_scale)
        probs_full = jnp.exp(scores - log_totals[block_index])
        probs_low = probs_full.astype(jnp.bfloat16)
        grad_value_total = jnp.einsum(
            "hqk,qhd->khd", probs_low, grad_context, preferred_element_type=jnp.float32
        )
        grad_probs = jnp.einsum(
            "qhd,khd->hqk", grad_context, value_rows, preferred_element_type=jnp.float32
        )
        row_shift = jnp.sum(probs_full * grad_probs, axis=-1, keepdims=True)
        grad_scores = (probs_full * (grad_probs - row_shift)).astype(jnp.bfloat16)
        grad_query_blocks.append(
            jnp.einsum("hqk,khd->qhd", grad_scores, key_rows, preferred_element_type=jnp.float32)
            * score_scale
        )
        grad_key_total = (
            jnp.einsum("hqk,qhd->khd", grad_scores, queries, preferred_element_type=jnp.float32)
            * score_scale
        )
    grad_query_normed = unrotate(grad_query_blocks[0], cosine, sine_table).reshape(
        seq_len, local_dim
    )
    grad_key_normed = unrotate(grad_key_total, cosine, sine_table).reshape(seq_len, local_dim)
    grad_qgain_part = jnp.sum(grad_query_normed * query_hat, axis=0)
    grad_kgain_part = jnp.sum(grad_key_normed * key_hat, axis=0)
    grad_query_hat = grad_query_normed * query_gain
    grad_key_hat = grad_key_normed * key_gain
    query_inner, key_inner = line_total(
        jnp.stack(
            [jnp.sum(grad_query_hat * query_hat, axis=1), jnp.sum(grad_key_hat * key_hat, axis=1)]
        ),
        n_tensor,
        6,
    )
    grad_query_raw = (
        query_scale * (grad_query_hat - query_hat * (query_inner / d_model)[:, None])
    ).astype(jnp.bfloat16)
    grad_key_raw = (key_scale * (grad_key_hat - key_hat * (key_inner / d_model)[:, None])).astype(
        jnp.bfloat16
    )
    grad_value_raw = grad_value_total.reshape(seq_len, local_dim).astype(jnp.bfloat16)
    grad_raw = jnp.concatenate([grad_query_raw, grad_key_raw, grad_value_raw], axis=1)
    w_raw = jnp.concatenate([w_query, w_key, w_value], axis=1)
    raw_part = jnp.einsum("sd,sf->df", normed_all, grad_raw, preferred_element_type=jnp.float32)
    row_part = jnp.einsum("sf,df->sd", grad_raw, w_raw, preferred_element_type=jnp.float32)
    column = spread.column(sides)
    mine = (jnp.arange(n_tensor) == lax.axis_index("tensor"))[:, None]
    gain_parts = jnp.stack(
        [
            jnp.zeros((d_model,), jnp.float32),
            jnp.where(mine, grad_qgain_part[None, :], 0.0).reshape(-1),
            jnp.where(mine, grad_kgain_part[None, :], 0.0).reshape(-1),
            jnp.zeros((d_model,), jnp.float32),
        ]
    )
    finished = finish_sums(
        raw_part.astype(jnp.bfloat16).reshape(n_dp * PIECES, -1, 3 * local_dim),
        grad_output_part.astype(jnp.bfloat16).reshape(n_dp * PIECES, -1, local_dim),
        row_part.astype(jnp.bfloat16).reshape(n_tensor, tok_count, d_model),
        column,
        first_unit_rows,
        gain_parts.reshape(8, -1),
        n_tensor,
        PIECES,
        4,
    )
    finished, side_total = hold(finished, side_total)
    total_query, total_key, total_value, total_output, grad_first_normalized, routed, gain_totals = finished
    total_router, total_ffn_gain = side_total[:-1].T, side_total[-1]
    total_query, total_key, total_value, total_output = (
        total.reshape(d_model, local_dim).astype(jnp.float32)
        for total in (total_query, total_key, total_value, total_output)
    )
    total_output = total_output.T
    grad_first_unit_rows = grad_first_normalized * attention_norm_gain
    grad_tokens = (
        first_norm_scale
        * (
            grad_first_unit_rows
            - first_unit_rows
            * jnp.mean(grad_first_unit_rows * first_unit_rows, axis=-1, keepdims=True)
        )
        + grad_hidden_one
    ).astype(jnp.bfloat16)
    result = (hidden_after_attention + routed).astype(jnp.bfloat16)
    gain_totals = gain_totals.reshape(4, d_model)
    total_attn_gain = gain_totals[0]
    own_gains = lax.dynamic_slice_in_dim(
        gain_totals, lax.axis_index("tensor") * local_dim, local_dim, axis=1
    )
    total_qgain, total_kgain = own_gains[1], own_gains[2]
    return (
        result,
        grad_tokens,
        total_query,
        total_key,
        total_value,
        total_output,
        total_qgain,
        total_kgain,
        total_attn_gain,
        total_ffn_gain,
        total_router,
        grad_gate,
        grad_up,
        grad_down,
    )


def local_routed(
    tokens,
    file_ids,
    expert_ids,
    attention_norm_gain,
    w_query,
    w_key,
    w_value,
    query_gain,
    key_gain,
    w_output,
    expert_norm_gain,
    w_router,
    w_gate,
    w_up,
    w_down,
    grad_output,
):
    tok_count, d_model = tokens.shape
    n_tensor = lax.axis_size("tensor")
    n_dp = lax.axis_size("dp")
    devices = n_dp * n_tensor
    local_dim = w_query.shape[1]
    head_dim = HEAD_DIM
    local_heads = local_dim // head_dim
    seq_len = tok_count * n_tensor
    block_rows = min(512, seq_len)
    score_scale = 1.0 / math.sqrt(head_dim)
    file_row = file_ids[0]
    cosine, sine_table = rope_tables(seq_len, head_dim)
    input_tensors = tokens.astype(jnp.float32)
    first_norm_scale = root_mean_square_scale(input_tensors)
    first_unit_rows = input_tensors * first_norm_scale
    first_normalized = (first_unit_rows * attention_norm_gain).astype(jnp.bfloat16)
    normed_all = lax.all_gather(first_normalized, "tensor", axis=0, tiled=True)
    query_raw = jnp.dot(normed_all, w_query, preferred_element_type=jnp.float32)
    key_raw = jnp.dot(normed_all, w_key, preferred_element_type=jnp.float32)
    value_rows = (
        jnp.dot(normed_all, w_value, preferred_element_type=jnp.float32)
        .astype(jnp.bfloat16)
        .reshape(seq_len, local_heads, head_dim)
    )
    query_total, key_total = lax.psum(
        (jnp.sum(query_raw * query_raw, axis=1), jnp.sum(key_raw * key_raw, axis=1)), "tensor"
    )
    query_scale = lax.rsqrt(query_total / d_model + EPSILON)[:, None]
    key_scale = lax.rsqrt(key_total / d_model + EPSILON)[:, None]
    query_hat = query_raw * query_scale
    key_hat = key_raw * key_scale
    queries = rotate(
        (query_hat * query_gain).reshape(seq_len, local_heads, head_dim), cosine, sine_table
    ).astype(jnp.bfloat16)
    key_rows = rotate(
        (key_hat * key_gain).reshape(seq_len, local_heads, head_dim), cosine, sine_table
    ).astype(jnp.bfloat16)
    block_start = 0
    scores = block_scores(queries, key_rows, file_row, block_start, score_scale)
    row_peak = jnp.max(scores, axis=-1, keepdims=True)
    log_total = row_peak + jnp.log(jnp.sum(jnp.exp(scores - row_peak), axis=-1, keepdims=True))
    attn_probs = jnp.exp(scores - log_total).astype(jnp.bfloat16)
    context_blocks = jnp.einsum(
        "hqk,khd->qhd", attn_probs, value_rows, preferred_element_type=jnp.float32
    )
    log_totals = [log_total]
    context = context_blocks.reshape(seq_len, local_dim).astype(jnp.bfloat16)
    attn_out = lax.psum_scatter(
        jnp.dot(context, w_output, preferred_element_type=jnp.float32).astype(jnp.bfloat16),
        "tensor",
        scatter_dimension=0,
        tiled=True,
    ).astype(jnp.float32)
    hidden_after_attention = input_tensors + attn_out
    result, grad_hidden_one, grad_expert_share, grad_router_part, grad_gate, grad_up, grad_down = (
        experts_routed(
            hidden_after_attention,
            expert_ids,
            expert_norm_gain,
            w_router,
            w_gate,
            w_up,
            w_down,
            grad_output,
        )
    )
    grad_attn = grad_hidden_one.astype(jnp.bfloat16)
    grad_attn_all = lax.all_gather(grad_attn, "tensor", axis=0, tiled=True)
    grad_output_part = jnp.einsum(
        "sd,se->de", context, grad_attn_all, preferred_element_type=jnp.float32
    )
    grad_context = (
        jnp.einsum("se,de->sd", grad_attn_all, w_output, preferred_element_type=jnp.float32)
        .astype(jnp.bfloat16)
        .reshape(seq_len, local_heads, head_dim)
    )
    grad_query_blocks = []
    grad_key_total = jnp.zeros((seq_len, local_heads, head_dim), jnp.float32)
    grad_value_total = jnp.zeros((seq_len, local_heads, head_dim), jnp.float32)
    for block_index, block_start in enumerate(range(0, seq_len, block_rows)):
        scores = block_scores(queries, key_rows, file_row, block_start, score_scale)
        probs_full = jnp.exp(scores - log_totals[block_index])
        probs_low = probs_full.astype(jnp.bfloat16)
        grad_value_total = jnp.einsum(
            "hqk,qhd->khd", probs_low, grad_context, preferred_element_type=jnp.float32
        )
        grad_probs = jnp.einsum(
            "qhd,khd->hqk", grad_context, value_rows, preferred_element_type=jnp.float32
        )
        row_shift = jnp.sum(probs_full * grad_probs, axis=-1, keepdims=True)
        grad_scores = (probs_full * (grad_probs - row_shift)).astype(jnp.bfloat16)
        grad_query_blocks.append(
            jnp.einsum("hqk,khd->qhd", grad_scores, key_rows, preferred_element_type=jnp.float32)
            * score_scale
        )
        grad_key_total = (
            jnp.einsum("hqk,qhd->khd", grad_scores, queries, preferred_element_type=jnp.float32)
            * score_scale
        )
    grad_query_normed = unrotate(grad_query_blocks[0], cosine, sine_table).reshape(
        seq_len, local_dim
    )
    grad_key_normed = unrotate(grad_key_total, cosine, sine_table).reshape(seq_len, local_dim)
    grad_qgain_part = jnp.sum(grad_query_normed * query_hat, axis=0)
    grad_kgain_part = jnp.sum(grad_key_normed * key_hat, axis=0)
    grad_query_hat = grad_query_normed * query_gain
    grad_key_hat = grad_key_normed * key_gain
    query_inner, key_inner = lax.psum(
        (jnp.sum(grad_query_hat * query_hat, axis=1), jnp.sum(grad_key_hat * key_hat, axis=1)),
        "tensor",
    )
    grad_query_raw = (
        query_scale * (grad_query_hat - query_hat * (query_inner / d_model)[:, None])
    ).astype(jnp.bfloat16)
    grad_key_raw = (key_scale * (grad_key_hat - key_hat * (key_inner / d_model)[:, None])).astype(
        jnp.bfloat16
    )
    grad_value_raw = grad_value_total.reshape(seq_len, local_dim).astype(jnp.bfloat16)
    grad_query_part = jnp.einsum(
        "sd,sf->df", normed_all, grad_query_raw, preferred_element_type=jnp.float32
    )
    grad_key_part = jnp.einsum(
        "sd,sf->df", normed_all, grad_key_raw, preferred_element_type=jnp.float32
    )
    grad_value_part = jnp.einsum(
        "sd,sf->df", normed_all, grad_value_raw, preferred_element_type=jnp.float32
    )
    summed = jnp.einsum("sf,df->sd", grad_query_raw, w_query, preferred_element_type=jnp.float32)
    summed = summed + jnp.einsum(
        "sf,df->sd", grad_key_raw, w_key, preferred_element_type=jnp.float32
    )
    grad_first_normalized = lax.psum_scatter(
        (
            summed
            + jnp.einsum("sf,df->sd", grad_value_raw, w_value, preferred_element_type=jnp.float32)
        ).astype(jnp.bfloat16),
        "tensor",
        scatter_dimension=0,
        tiled=True,
    ).astype(jnp.float32)
    grad_attention_share = jnp.sum(grad_first_normalized * first_unit_rows, axis=0)
    grad_first_unit_rows = grad_first_normalized * attention_norm_gain
    grad_tokens = (
        first_norm_scale
        * (
            grad_first_unit_rows
            - first_unit_rows
            * jnp.mean(grad_first_unit_rows * first_unit_rows, axis=-1, keepdims=True)
        )
        + grad_hidden_one
    ).astype(jnp.bfloat16)
    total_query, total_key, total_value, total_output, total_qgain, total_kgain = (
        lax.psum(grad_query_part.astype(jnp.bfloat16), "dp").astype(jnp.float32),
        lax.psum(grad_key_part.astype(jnp.bfloat16), "dp").astype(jnp.float32),
        lax.psum(grad_value_part.astype(jnp.bfloat16), "dp").astype(jnp.float32),
        lax.psum(grad_output_part.astype(jnp.bfloat16), "dp").astype(jnp.float32),
        lax.psum(grad_qgain_part.astype(jnp.bfloat16), "dp").astype(jnp.float32),
        lax.psum(grad_kgain_part.astype(jnp.bfloat16), "dp").astype(jnp.float32),
    )
    total_attn_gain, total_ffn_gain, total_router = lax.psum(
        (grad_attention_share, grad_expert_share, grad_router_part), ("dp", "tensor")
    )
    return (
        result,
        grad_tokens,
        total_query,
        total_key,
        total_value,
        total_output,
        total_qgain,
        total_kgain,
        total_attn_gain,
        total_ffn_gain,
        total_router,
        grad_gate,
        grad_up,
        grad_down,
    )


def solution(mesh):
    return jax.shard_map(
        local_gathered if mesh.shape["dp"] == 8 else local_routed,
        mesh=mesh,
        in_specs=(
            P(("dp", "tensor"), None),
            P("dp", None),
            P(("dp", "tensor"), None),
            P(),
            P(None, "tensor"),
            P(None, "tensor"),
            P(None, "tensor"),
            P("tensor"),
            P("tensor"),
            P("tensor", None),
            P(),
            P(),
            P("dp", None, "tensor"),
            P("dp", None, "tensor"),
            P("dp", "tensor", None),
            P(("dp", "tensor"), None),
        ),
        out_specs=(
            P(("dp", "tensor"), None),
            P(("dp", "tensor"), None),
            P(None, "tensor"),
            P(None, "tensor"),
            P(None, "tensor"),
            P("tensor", None),
            P("tensor"),
            P("tensor"),
            P(),
            P(),
            P(),
            P("dp", None, "tensor"),
            P("dp", None, "tensor"),
            P("dp", "tensor", None),
        ),
        check_vma=False,
    )
```
